32 devices in a mesh: rows: 8 (over z, y), tp: 4 (over x, core).
Axes of the slice: x: 2, y: 2, z: 4, core: 2. Of those that a mesh axis runs over, the one named last changes fastest.
Arguments:
- layer_input: bfloat16 [8, 1536, 1024], P('rows', 'tp'), may hold values from -6 to 6
- cotangent: bfloat16 [8, 1536, 1024], P('rows', 'tp'), may hold values from -6 to 6
- segments: int32 [8, 1536], P('rows'), may hold values from 0 to 23, as said below
- valid_frames: int32 [8, 1536], P('rows'), may hold values from 0 to 1, as said below
- gain_first: bfloat16 [1024], replicated, may hold values from 0.5 to 1.5
- up_first: bfloat16 [1024, 4096], P(None, 'tp'), may hold values from -0.1875 to 0.1875
- down_first: bfloat16 [4096, 1024], P('tp'), may hold values from -0.09375 to 0.09375
- gain_attend: bfloat16 [1024], replicated, may hold values from 0.5 to 1.5
- query_weight: bfloat16 [1024, 1024], P(None, 'tp'), may hold values from -0.1875 to 0.1875
- key_weight: bfloat16 [1024, 1024], P(None, 'tp'), may hold values from -0.1875 to 0.1875
- value_weight: bfloat16 [1024, 1024], P(None, 'tp'), may hold values from -0.1875 to 0.1875
- attend_out: bfloat16 [1024, 1024], P('tp'), may hold values from -0.75 to 0.75
- pos_weight: bfloat16 [1024, 1024], P(None, 'tp'), may hold values from -0.25 to 0.25
- content_bias: bfloat16 [8, 128], P('tp'), may hold values from -3 to 3
- position_bias: bfloat16 [8, 128], P('tp'), may hold values from -3 to 3
- gain_conv: bfloat16 [1024], replicated, may hold values from 0.5 to 1.5
- point_in: bfloat16 [1024, 2, 1024], P(None, None, 'tp'), may hold values from -0.1875 to 0.1875
- depth_kernel: bfloat16 [5, 1024], P(None, 'tp'), may hold values from -2.5 to 2.5
- gain_inner: bfloat16 [1024], P('tp'), may hold values from 0.5 to 1.5
- point_out: bfloat16 [1024, 1024], P('tp'), may hold values from -0.1875 to 0.1875
- gain_second: bfloat16 [1024], replicated, may hold values from 0.5 to 1.5
- up_second: bfloat16 [1024, 4096], P(None, 'tp'), may hold values from -0.1875 to 0.1875
- down_second: bfloat16 [4096, 1024], P('tp'), may hold values from -0.09375 to 0.09375
- gain_final: bfloat16 [1024], replicated, may hold values from 0.5 to 1.5
Outputs:
- layer_output: bfloat16 [8, 1536, 1024], P('rows', 'tp')
- input_grad: float32 [8, 1536, 1024], P('rows', 'tp')
- grad_gain_first: float32 [1024], replicated
- grad_up_first: float32 [1024, 4096], P(None, 'tp')
- grad_down_first: float32 [4096, 1024], P('tp')
- grad_gain_attend: float32 [1024], replicated
- grad_query_weight: float32 [1024, 1024], P(None, 'tp')
- grad_key_weight: float32 [1024, 1024], P(None, 'tp')
- grad_value_weight: float32 [1024, 1024], P(None, 'tp')
- grad_attend_out: float32 [1024, 1024], P('tp')
- grad_pos_weight: float32 [1024, 1024], P(None, 'tp')
- grad_content_bias: float32 [8, 128], P('tp')
- grad_position_bias: float32 [8, 128], P('tp')
- grad_gain_conv: float32 [1024], replicated
- grad_point_in: float32 [1024, 2, 1024], P(None, None, 'tp')
- grad_depth_kernel: float32 [5, 1024], P(None, 'tp')
- grad_gain_inner: float32 [1024], P('tp')
- grad_point_out: float32 [1024, 1024], P('tp')
- grad_gain_second: float32 [1024], replicated
- grad_up_second: float32 [1024, 4096], P(None, 'tp')
- grad_down_second: float32 [4096, 1024], P('tp')
- grad_gain_final: float32 [1024], replicated
The draws below stay inside these ranges and needn't reach their ends.
Inputs may be any that keep to these rules, and one draw needn't show every extreme that they name: `segments`: along each row, ids start at 0 and rise by one from utterance to utterance; padding slots, all at the row's end, carry the id one past the row's last utterance. Every utterance has at least 64 and at most 512 frames. `valid_frames`: 1 exactly on the slots of utterances; the padding slots of a row follow all of them.
All inputs are finite; a program needn't handle non-finite values.
Results may differ from the reference program's by a relative error of at most 0.025.
Values may be sent and summed in bfloat16 or wider, within the bound.
No kernel may reach another device: no remote copies, remote signals or barrier semaphores. Data moves between devices by JAX's collectives and lax.ppermute only.
A program may use at most 256 MiB of HBM per device.

```python
import math
import jax
import jax.numpy as jnp
from jax import lax

D = 1024
HEADS = 8
HEAD_DIM = 128
FF = 4096
CONV = 1024
KW = 5
SLOTS = 1536
QUERY_BLOCK = 512
SEG_MOST = 512
ROWS_DEV = 1
ROWS = 8


def packed_rows(key):
    shortest = max(SEG_MOST // 8, 1)
    count = SLOTS // shortest + 1
    lengths = jax.random.randint(jax.random.fold_in(key, 11), (ROWS, count), shortest, SEG_MOST + 1)
    first_row = (jnp.arange(ROWS, dtype=jnp.int32) == 0)[:, None]
    lengths = jnp.where(first_row, shortest, lengths).astype(jnp.int32)
    ends = jnp.cumsum(lengths, axis=1).astype(jnp.int32)
    kept = (ends <= SLOTS).astype(jnp.int32)
    place = jnp.arange(SLOTS, dtype=jnp.int32)
    finished = (ends[:, None, :] <= place[None, :, None]).astype(jnp.int32) * kept[:, None, :]
    segment = jnp.sum(finished, axis=2).astype(jnp.int32)
    filled = jnp.max(ends * kept, axis=1)
    valid = (place[None, :] < filled[:, None]).astype(jnp.int32)
    return (segment, valid)


def draw_segments(key, part):
    return packed_rows(key)[0]


def draw_valid_frames(key, part):
    return packed_rows(key)[1]


def level_of(rng, shape, cuts, smallest, high):
    def one(axis_at, shards_of):
        heights = jax.random.uniform(jax.random.fold_in(jax.random.fold_in(rng, 6), axis_at), (shards_of,), jnp.float32, smallest / len(cuts), high / len(cuts))
        return jnp.repeat(jnp.exp(heights), shape[axis_at] // shards_of).reshape((-1,) + (1,) * (len(shape) - axis_at - 1))

    loudness = one(*cuts[0])
    for cut in cuts[1:]:
        loudness = loudness * one(*cut)
    return loudness


def noise(own_key, shape, deviation, bound, cuts=(), kind=jnp.bfloat16):
    values = deviation * jax.random.normal(own_key, shape, jnp.float32)
    if cuts:
        values = values * level_of(own_key, shape, cuts, -0.22, 0.18)
    return jnp.clip(values, -bound, bound).astype(kind)


def setup_inputs(seed: int = 0) -> dict:
    key_list = jax.random.split(jax.random.key(seed), 25)
    layer_input = noise(key_list[0], (ROWS, SLOTS, D), 1.0, 6.0, ((0, 8), (1, 4)))
    cotangent = noise(key_list[1], (ROWS, SLOTS, D), 1.0, 6.0, ((0, 8), (1, 4)))
    segments = draw_segments(jax.random.fold_in(key_list[24], 71), 0)
    valid_frames = draw_valid_frames(jax.random.fold_in(key_list[24], 71), 0)
    gain_first = jnp.clip(1.0 + 0.1 * jax.random.normal(key_list[4], (D,), jnp.float32), 0.5, 1.5).astype(jnp.bfloat16)
    up_first = noise(key_list[5], (D, FF), D ** -0.5, 0.1875, ((1, 4),))
    down_first = noise(key_list[6], (FF, D), FF ** -0.5, 0.09375, ((0, 4),))
    gain_attend = jnp.clip(1.0 + 0.1 * jax.random.normal(key_list[7], (D,), jnp.float32), 0.5, 1.5).astype(jnp.bfloat16)
    query_weight = noise(key_list[8], (D, HEADS * HEAD_DIM), D ** -0.5, 0.1875, ((1, 4),))
    key_weight = noise(key_list[9], (D, HEADS * HEAD_DIM), D ** -0.5, 0.1875, ((1, 4),))
    value_weight = noise(key_list[10], (D, HEADS * HEAD_DIM), D ** -0.5, 0.1875, ((1, 4),))
    attend_out = noise(key_list[11], (HEADS * HEAD_DIM, D), (HEADS * HEAD_DIM // 16) ** -0.5, 0.75, ((0, 4),))
    pos_weight = noise(key_list[12], (D, HEADS * HEAD_DIM), (D // 2) ** -0.5, 0.25, ((1, 4),))
    content_bias = noise(key_list[13], (HEADS, HEAD_DIM), 0.5, 3.0, ((0, 4),))
    position_bias = noise(key_list[14], (HEADS, HEAD_DIM), 0.5, 3.0, ((0, 4),))
    gain_conv = jnp.clip(1.0 + 0.1 * jax.random.normal(key_list[15], (D,), jnp.float32), 0.5, 1.5).astype(jnp.bfloat16)
    point_in = noise(key_list[16], (D, 2, CONV), D ** -0.5, 0.1875, ((2, 4),))
    depth_kernel = noise(key_list[17], (KW, CONV), KW ** -0.5, 2.5, ((1, 4),))
    gain_inner = jnp.clip(1.0 + 0.1 * jax.random.normal(key_list[18], (CONV,), jnp.float32), 0.5, 1.5).astype(jnp.bfloat16)
    point_out = noise(key_list[19], (CONV, D), CONV ** -0.5, 0.1875, ((0, 4),))
    gain_second = jnp.clip(1.0 + 0.1 * jax.random.normal(key_list[20], (D,), jnp.float32), 0.5, 1.5).astype(jnp.bfloat16)
    up_second = noise(key_list[21], (D, FF), D ** -0.5, 0.1875, ((1, 4),))
    down_second = noise(key_list[22], (FF, D), FF ** -0.5, 0.09375, ((0, 4),))
    gain_final = jnp.clip(1.0 + 0.1 * jax.random.normal(key_list[23], (D,), jnp.float32), 0.5, 1.5).astype(jnp.bfloat16)
    return dict(layer_input=layer_input, cotangent=cotangent, segments=segments, valid_frames=valid_frames, gain_first=gain_first, up_first=up_first, down_first=down_first, gain_attend=gain_attend, query_weight=query_weight, key_weight=key_weight, value_weight=value_weight, attend_out=attend_out, pos_weight=pos_weight, content_bias=content_bias, position_bias=position_bias, gain_conv=gain_conv, point_in=point_in, depth_kernel=depth_kernel, gain_inner=gain_inner, point_out=point_out, gain_second=gain_second, up_second=up_second, down_second=down_second, gain_final=gain_final)


EPS = 1e-05
HIGH = lax.Precision.HIGHEST

@jax.custom_vjp
def low(v):
    return lax.optimization_barrier(v.astype(jnp.bfloat16)).astype(jnp.float32)

@jax.custom_vjp
def low_back(v):
    return v

def low_keep(v):
    return (low(v), None)

def low_pass(kept, grad):
    return (grad,)

def back_keep(v):
    return (v, None)

def back_low(kept, grad):
    return (low(grad),)
low.defvjp(low_keep, low_pass)
low_back.defvjp(back_keep, back_low)

def layer_norm(values, gain):
    mean = lax.optimization_barrier(jnp.mean(values, axis=-1, keepdims=True))
    centered = values - mean
    variance = lax.optimization_barrier(jnp.mean(centered * centered, axis=-1, keepdims=True))
    return centered * lax.rsqrt(variance + EPS) * gain

def product(left, right):
    return jnp.einsum('...d,df->...f', left, right, precision=HIGH)

def swish(values):
    return values * jax.nn.sigmoid(values)

def distance_table(slots, width):
    place = (slots - 1 - jnp.arange(2 * slots)).astype(jnp.float32)
    column = jnp.arange(width)
    rate = jnp.exp(-(column - column % 2).astype(jnp.float32) * (math.log(10000.0) / width))
    angle = place[:, None] * rate[None, :]
    return jnp.where(column[None, :] % 2 == 0, jnp.sin(angle), jnp.cos(angle))

def skew(grid, slots):
    heads, block, _ = grid.shape
    width = slots + block - 1
    flat = grid.reshape(heads, block * (width + 1))
    cut = lax.slice_in_dim(flat, block - 1, block - 1 + block * width, axis=1)
    return cut.reshape(heads, block, width)[:, :, :slots]

def shift_time(values, offset, fill):
    if offset == 0:
        return values
    filler = jnp.full(values.shape[:1] + (abs(offset),) + values.shape[2:], fill, values.dtype)
    if offset > 0:
        return jnp.concatenate([values[:, offset:], filler], 1)
    return jnp.concatenate([filler, values[:, :offset]], 1)

def neighbour_mask(segments, valid, offset):
    other_segment = shift_time(segments, offset, -1)
    other_valid = shift_time(valid, offset, 0)
    return ((other_segment == segments) & (other_valid == 1)).astype(jnp.float32)

def allow_block(segment_row, valid_row, start, block):
    slots = segment_row.shape[0]
    same = segment_row[start:start + block, None] == segment_row[None, :]
    itself = (jnp.arange(block) + start)[:, None] == jnp.arange(slots)[None, :]
    return same & ((valid_row[None, :] == 1) | itself)

def attention_block(q_content_b, q_position_b, key_row, value_row, window, allow):
    raw = jnp.einsum('qhd,khd->hqk', q_content_b, key_row, precision=HIGH)
    grid = jnp.einsum('qhd,whd->hqw', q_position_b, window, precision=HIGH)
    raw = low_back(raw + skew(grid, key_row.shape[0]))
    scores = jnp.where(allow[None], raw * HEAD_DIM ** (-0.5), -1e+30)
    top = lax.optimization_barrier(jnp.max(scores, axis=-1, keepdims=True))
    weights = jnp.exp(scores - top)
    probs = weights / lax.optimization_barrier(jnp.sum(weights, axis=-1, keepdims=True))
    return jnp.einsum('hqk,khd->qhd', low(probs), value_row, precision=HIGH)

def attention_row(q_content_row, q_position_row, key_row, value_row, rel, segment_row, valid_row):
    pieces = []
    for start in range(0, SLOTS, QUERY_BLOCK):
        window = lax.slice_in_dim(rel, SLOTS - QUERY_BLOCK - start, 2 * SLOTS - start, axis=0)
        allow = allow_block(segment_row, valid_row, start, QUERY_BLOCK)
        pieces.append(jax.checkpoint(attention_block)(q_content_row[start:start + QUERY_BLOCK], q_position_row[start:start + QUERY_BLOCK], key_row, value_row, window, allow))
    return jnp.concatenate(pieces, 0)

def feed_forward(values, gain, weight_up, weight_down):
    normed = low(layer_norm(values, gain))
    pre = low_back(product(normed, weight_up))
    act = low(swish(pre))
    return values + 0.5 * low_back(product(act, weight_down))

def attention(values, gain, query_weight, key_weight, value_weight, attend_out, pos_weight, content_bias, position_bias, segments, valid, table):
    count = values.shape[0]
    normed = low(layer_norm(values, gain))
    shape = (count, SLOTS, HEADS, HEAD_DIM)
    query = low_back(product(normed, query_weight)).reshape(shape)
    key = low(low_back(product(normed, key_weight))).reshape(shape)
    value = low(low_back(product(normed, value_weight))).reshape(shape)
    q_content = low(query + content_bias)
    q_position = low(query + position_bias)
    rel = low(low_back(product(table, pos_weight))).reshape(2 * SLOTS, HEADS, HEAD_DIM)
    rows_out = [attention_row(q_content[index], q_position[index], key[index], value[index], rel, segments[index], valid[index]) for index in range(count)]
    heads_out = low(low_back(jnp.stack(rows_out, 0))).reshape(count, SLOTS, HEADS * HEAD_DIM)
    return values + low_back(product(heads_out, attend_out))

def convolve(values, gain, point_in, depth_kernel, gain_inner, point_out, segments, valid):
    normed = low(layer_norm(values, gain))
    mixed = low_back(jnp.einsum('rld,dgc->rlgc', normed, point_in, precision=HIGH))
    glu = mixed[:, :, 0] * jax.nn.sigmoid(mixed[:, :, 1])
    depth = jnp.zeros_like(glu)
    for tap in range(KW):
        offset = tap - KW // 2
        depth = depth + depth_kernel[tap] * neighbour_mask(segments, valid, offset)[..., None] * shift_time(glu, offset, 0.0)
    inner = low(swish(layer_norm(depth, gain_inner)))
    return values + low_back(product(inner, point_out))

def group_forward(values, params, segments, valid, table):
    gain_first, up_first, down_first, gain_attend, query_weight, key_weight, value_weight, attend_out, pos_weight, content_bias, position_bias, gain_conv, point_in, depth_kernel, gain_inner, point_out, gain_second, up_second, down_second, gain_final = params
    values = feed_forward(values, gain_first, up_first, down_first)
    values = attention(values, gain_attend, query_weight, key_weight, value_weight, attend_out, pos_weight, content_bias, position_bias, segments, valid, table)
    values = convolve(values, gain_conv, point_in, depth_kernel, gain_inner, point_out, segments, valid)
    values = feed_forward(values, gain_second, up_second, down_second)
    return layer_norm(values, gain_final)

def reference(layer_input, cotangent, segments, valid_frames, gain_first, up_first, down_first, gain_attend, query_weight, key_weight, value_weight, attend_out, pos_weight, content_bias, position_bias, gain_conv, point_in, depth_kernel, gain_inner, point_out, gain_second, up_second, down_second, gain_final):
    params = tuple((weight.astype(jnp.float32) for weight in (gain_first, up_first, down_first, gain_attend, query_weight, key_weight, value_weight, attend_out, pos_weight, content_bias, position_bias, gain_conv, point_in, depth_kernel, gain_inner, point_out, gain_second, up_second, down_second, gain_final)))
    table = low(distance_table(SLOTS, D))
    groups = ROWS // ROWS_DEV

    def split(array):
        return array.reshape((groups, ROWS_DEV) + array.shape[1:])

    def one_group(total, item):
        group_input, group_cot, group_segments, group_valid = item

        def run(inputs, weights):
            return group_forward(inputs, weights, group_segments, group_valid, table)
        output, pull = jax.vjp(run, group_input.astype(jnp.float32), params)
        input_part, weight_parts = pull(group_cot.astype(jnp.float32))
        total = jax.tree.map(lambda left, right: left + right, total, weight_parts)
        return (total, (output.astype(jnp.bfloat16), input_part))
    start = jax.tree.map(jnp.zeros_like, params)
    total, (outputs, input_parts) = lax.scan(one_group, start, (split(layer_input), split(cotangent), split(segments), split(valid_frames)))
    return (outputs.reshape(layer_input.shape), input_parts.reshape(layer_input.shape), total[0], total[1], total[2], total[3], total[4], total[5], total[6], total[7], total[8], total[9], total[10], total[11], total[12], total[13], total[14], total[15], total[16], total[17], total[18], total[19])
```

```python
import functools
import math

import jax
import jax.numpy as jnp
from jax import lax
from jax.experimental import pallas as pl
from jax.experimental.pallas import tpu as pltpu
from jax.sharding import PartitionSpec as P

EPS = 1e-05
NEG = -1e30
F32 = jnp.float32
B16 = jnp.bfloat16
TQ = 128
TK = 384
HD = 128
STEP = 64
SM = pl.BlockSpec(memory_space=pltpu.SMEM)
VM = pl.BlockSpec(memory_space=pltpu.VMEM)

def dotx(a, b, ca, cb):
    return lax.dot_general(a, b, (((ca,), (cb,)), ((), ())), preferred_element_type=F32)

def skew_tile(grid):
    return pltpu.roll(grid, TK + 1, 1, stride=1, stride_axis=0)[:, :TK]

def unskew_flipped(flipped):
    wide = jnp.concatenate([flipped, jnp.zeros((TQ, TQ), F32)], axis=1)
    return pltpu.roll(wide, 0, 1, stride=1, stride_axis=0)

def attend_kernel(heads, spans, q_at, k_at, qc_ref, qp_ref, k_ref, v_ref, rel_ref, code_q_ref, code_k_ref,
                  out_ref, wide_ref, lse_ref):
    slots = qc_ref.shape[0]
    scale = HD ** -0.5
    blocks, tiles = slots // TQ, slots // TK

    def q_step(qb, _):
        at = pl.multiple_of(q_at[qb], TQ)
        true_at = pl.multiple_of(qb * TQ, TQ)
        code_q = code_q_ref[pl.ds(true_at, TQ), :]
        qc = [qc_ref[pl.ds(at, TQ), h * HD:(h + 1) * HD] for h in range(heads)]
        qp = [qp_ref[pl.ds(at, TQ), h * HD:(h + 1) * HD] for h in range(heads)]

        def k_step(kt, carry):
            ko = pl.multiple_of(k_at[kt], TQ)
            to = pl.multiple_of((blocks - 1 + kt * (TK // TQ) - qb) * TQ, TQ)
            mask = code_q == code_k_ref[kt]
            new = []
            for h in range(heads):
                lanes = slice(h * HD, (h + 1) * HD)
                top, total, acc = carry[h]
                grid = dotx(qp[h], rel_ref[pl.ds(to, TK + TQ), lanes], 1, 1)
                raw = dotx(qc[h], k_ref[pl.ds(ko, TK), lanes], 1, 1) + skew_tile(grid)
                scores = jnp.where(mask, raw * scale, NEG)
                top_new = jnp.maximum(top, jnp.max(scores, axis=1, keepdims=True))
                shrink = jnp.exp(top - top_new)
                weights = jnp.exp(scores - top_new)
                total = total * shrink + jnp.sum(weights, axis=1, keepdims=True)
                acc = acc * shrink + dotx(weights.astype(B16), v_ref[pl.ds(ko, TK), lanes], 1, 0)
                new.append((top_new, total, acc))
            return tuple(new)

        first = tuple((jnp.full((TQ, 1), NEG, F32), jnp.zeros((TQ, 1), F32), jnp.zeros((TQ, HD), F32))
                      for _ in range(heads))
        final = lax.fori_loop(spans[0, qb], spans[1, qb], k_step, first)
        for h in range(heads):
            lanes = slice(h * HD, (h + 1) * HD)
            top, total, acc = final[h]
            out = acc / total
            wide_ref[pl.ds(at, TQ), lanes] = out
            out_ref[pl.ds(at, TQ), lanes] = out.astype(B16)
            lse_ref[pl.ds(at, TQ), h:h + 1] = top + jnp.log(total)
        return 0

    lax.fori_loop(0, blocks, q_step, 0)

def attend_back_kernel(heads, spans, q_at, k_at, qc_ref, qp_ref, k_ref, v_ref, rel_ref, code_q_ref, code_k_ref,
                       d_out_ref, wide_ref, lse_ref,
                       dq_ref, dk_ref, dv_ref, drel_ref, bias_ref, dk_acc, dv_acc, drel_acc):
    slots = qc_ref.shape[0]
    scale = HD ** -0.5
    blocks, tiles = slots // TQ, slots // TK
    dk_acc[...] = jnp.zeros_like(dk_acc)
    dv_acc[...] = jnp.zeros_like(dv_acc)
    drel_acc[...] = jnp.zeros_like(drel_acc)
    bias_ref[...] = jnp.zeros_like(bias_ref)
    row = lax.broadcasted_iota(jnp.int32, (TQ, TQ), 0)
    column = lax.broadcasted_iota(jnp.int32, (TQ, TQ), 1)
    flip = (row + column == TQ - 1).astype(F32)
    flip_low = flip.astype(B16)

    def q_step(qb, _):
        at = pl.multiple_of(q_at[qb], TQ)
        true_at = pl.multiple_of(qb * TQ, TQ)
        code_q = code_q_ref[pl.ds(true_at, TQ), :]
        cols = [slice(h * HD, (h + 1) * HD) for h in range(heads)]
        qc = [qc_ref[pl.ds(at, TQ), c] for c in cols]
        qp = [qp_ref[pl.ds(at, TQ), c] for c in cols]
        qp_flipped = [dotx(flip_low, item, 1, 0).astype(B16) for item in qp]
        d_out = [d_out_ref[pl.ds(at, TQ), c] for c in cols]
        lse = [lse_ref[pl.ds(at, TQ), h:h + 1] for h in range(heads)]
        delta = [jnp.sum(d_out[h].astype(F32) * wide_ref[pl.ds(at, TQ), cols[h]], axis=1, keepdims=True)
                 for h in range(heads)]

        def k_step(kt, carry):
            ko = pl.multiple_of(k_at[kt], TQ)
            to = pl.multiple_of((blocks - 1 + kt * (TK // TQ) - qb) * TQ, TQ)
            mask = code_q == code_k_ref[kt]
            new = []
            for h in range(heads):
                lanes = cols[h]
                d_content, d_position = carry[h]
                window = rel_ref[pl.ds(to, TK + TQ), lanes]
                key = k_ref[pl.ds(ko, TK), lanes]
                grid = dotx(qp[h], window, 1, 1)
                raw = dotx(qc[h], key, 1, 1) + skew_tile(grid)
                probs = jnp.exp(jnp.where(mask, raw * scale - lse[h], NEG))
                d_probs = dotx(d_out[h], v_ref[pl.ds(ko, TK), lanes], 1, 1)
                d_raw = probs * (d_probs - delta[h]) * scale
                d_low = d_raw.astype(B16)
                d_grid = unskew_flipped(dotx(flip_low, d_low, 1, 0)).astype(B16)
                dv_acc[pl.ds(ko, TK), lanes] += dotx(probs.astype(B16), d_out[h], 0, 0)
                dk_acc[pl.ds(ko, TK), lanes] += dotx(d_low, qc[h], 0, 0)
                drel_acc[pl.ds(to, TK + TQ), lanes] += dotx(d_grid, qp_flipped[h], 0, 0)
                d_content = d_content + dotx(d_low, key, 1, 0)
                d_position = d_position + dotx(d_grid, window, 1, 0)
                new.append((d_content, d_position))
            return tuple(new)

        first = tuple((jnp.zeros((TQ, HD), F32),) * 2 for _ in range(heads))
        final = lax.fori_loop(spans[0, qb], spans[1, qb], k_step, first)
        for h in range(heads):
            d_content, d_position = final[h]
            d_position = lax.dot_general(flip, d_position, (((1,), (0,)), ((), ())),
                                         precision=lax.Precision.HIGHEST, preferred_element_type=F32)
            dq_ref[pl.ds(at, TQ), cols[h]] = (d_content + d_position).astype(B16)
            bias_ref[0:1, cols[h]] += jnp.sum(d_content, axis=0, keepdims=True)
            bias_ref[1:2, cols[h]] += jnp.sum(d_position, axis=0, keepdims=True)
        return 0

    lax.fori_loop(0, blocks, q_step, 0)
    dk_ref[...] = dk_acc[...].astype(B16)
    dv_ref[...] = dv_acc[...].astype(B16)
    drel_ref[...] = drel_acc[...].astype(B16)

def sds(s, d): return jax.ShapeDtypeStruct(s, d)

def attend(spans, q_at, k_at, qc, qp, k, v, rel, code_q, code_k):
    slots, width = qc.shape
    heads = width // HD
    return pl.pallas_call(
        functools.partial(attend_kernel, heads),
        out_shape=(sds((slots, width), B16), sds((slots, width), F32), sds((slots, heads), F32)),
        in_specs=[SM] * 3 + [VM] * 7, out_specs=(VM,) * 3,
        compiler_params=pltpu.CompilerParams(vmem_limit_bytes=40 << 20),
        cost_estimate=pl.CostEstimate(flops=int(4e9), bytes_accessed=int(9e6), transcendentals=int(2e6)),
    )(spans, q_at, k_at, qc, qp, k, v, rel, code_q, code_k)

def attend_back(spans, q_at, k_at, qc, qp, k, v, rel, code_q, code_k, d_out, wide, lse):
    slots, width = qc.shape
    heads = width // HD
    return pl.pallas_call(
        functools.partial(attend_back_kernel, heads),
        out_shape=(sds((slots, width), B16),) * 3 + (sds((2 * slots, width), B16), sds((8, width), F32)),
        in_specs=[SM] * 3 + [VM] * 10, out_specs=(VM,) * 5,
        scratch_shapes=[pltpu.VMEM((slots, width), F32), pltpu.VMEM((slots, width), F32), pltpu.VMEM((2 * slots, width), F32)],
        compiler_params=pltpu.CompilerParams(vmem_limit_bytes=48 << 20),
        cost_estimate=pl.CostEstimate(flops=int(12e9), bytes_accessed=int(12e6), transcendentals=int(2e6)),
    )(spans, q_at, k_at, qc, qp, k, v, rel, code_q, code_k, d_out, wide, lse)

def codes(segments, valid):
    slots = segments.shape[0]
    place = jnp.arange(slots, dtype=jnp.int32)
    code = jnp.where(valid == 1, segments, -1 - place)
    return code

def spans_of(code):
    slots = code.shape[0]
    same = code[:, None] == code[None, :]
    touch = jnp.any(same.reshape(slots // TQ, TQ, slots // TK, TK), axis=(1, 3))
    tiles = slots // TK
    idx = jnp.arange(tiles, dtype=jnp.int32)
    lo = jnp.min(jnp.where(touch, idx, tiles), axis=1)
    hi = jnp.max(jnp.where(touch, idx + 1, 0), axis=1)
    return jnp.stack([lo, hi], 0).astype(jnp.int32)


def normalize(values, gain):
    mean = jnp.mean(values, axis=-1, keepdims=True)
    centered = values - mean
    inverse = lax.rsqrt(jnp.mean(centered * centered, axis=-1, keepdims=True) + EPS)
    unit = centered * inverse
    return (unit * gain.astype(F32), unit, inverse)


def normalize_back(grad, unit, inverse, gain):
    scaled = grad * gain.astype(F32)
    first = jnp.mean(scaled, axis=-1, keepdims=True)
    second = jnp.mean(scaled * unit, axis=-1, keepdims=True)
    return (inverse * (scaled - first - unit * second), jnp.sum(grad * unit, axis=0))


def swish_slope(values):
    gate = jax.nn.sigmoid(values)
    return gate * (1.0 + values * (1.0 - gate))


def distance_table(slots, width, first):
    column = jnp.arange(width)
    even = (column % 2 == 0)[None, :]
    rate = jnp.exp(-(column - column % 2).astype(F32) * (math.log(10000.0) / width))
    coarse = (slots - 1 - STEP * jnp.arange(2 * slots // STEP)).astype(F32)[:, None] * rate[None, :]
    fine = jnp.arange(STEP).astype(F32)[:, None] * rate[None, :]
    sin_c, cos_c = jnp.sin(coarse), jnp.cos(coarse)
    with_cos = jnp.where(even, sin_c, cos_c)
    with_sin = jnp.where(even, -cos_c, sin_c)
    with_cos, with_sin, sin_f, cos_f = after((with_cos, with_sin, jnp.sin(fine), jnp.cos(fine)), first)
    table = with_cos[:, None, :] * cos_f[None] + with_sin[:, None, :] * sin_f[None]
    return table.reshape(2 * slots, width).astype(B16)


def dot(left, right, contract=(1, 0)):
    return lax.dot_general(
        left, right, (((contract[0],), (contract[1],)), ((), ())), preferred_element_type=F32
    )


def swap(values, distance):
    size = lax.axis_size("tp")
    return lax.ppermute(values, "tp", [(i, i ^ distance) for i in range(size)])


def distances():
    size = lax.axis_size("tp")
    return [1 << bit for bit in range(size.bit_length() - 1)]


def gather(own):
    slots = {0: own}
    for distance in reversed(distances()):
        for slot in list(slots):
            slots[slot ^ distance] = swap(slots[slot], distance)
    return [slots[slot] for slot in range(len(slots))]


def scatter(parts):
    parts = dict(enumerate(parts))
    sent = got = None
    for distance in distances():
        for slot in sorted(parts, reverse=True):
            if slot & distance:
                sent = parts.pop(slot).astype(B16)
                got = swap(sent, distance)
                parts[slot ^ distance] = parts[slot ^ distance].astype(F32) + got.astype(F32)
    return parts[0], (sent, got)


def after(values, *others):
    return lax.optimization_barrier((values, others))[0]


def halves(slots):
    half = len(slots) // 2
    return jnp.concatenate(slots[:half], 0), jnp.concatenate(slots[half:], 0)


def pieces(near, far, weight, contract):
    count = lax.axis_size("tp") // 2
    rows = near.shape[0] // count
    outs = {}
    for slot in reversed(range(2 * count)):
        source, place = (near, slot) if slot < count else (far, slot - count)
        outs[slot] = dot(source[place * rows : (place + 1) * rows], weight, contract)
    return [outs[slot] for slot in range(2 * count)]


def ring():
    size, mine = lax.axis_size("rows"), lax.axis_index("rows")
    order = list(range(0, size, 2)) + list(range(size - 1, 0, -2))
    place = jnp.where(mine % 2 == 0, mine // 2, size - (mine + 1) // 2)
    right = [(order[i], order[(i + 1) % size]) for i in range(size)]
    return size, place, right, [(there, here) for here, there in right]


def sum_ring(values, gates=(), early=()):
    size, place, right, left = ring()
    rows = values.shape[0] // size
    forward, back = size // 2, size - 1 - size // 2
    gates = dict(enumerate(gates))
    gate = lambda item, stage: after(item, gates[stage]) if gates.get(stage) is not None else item
    chunk = lambda k: lax.dynamic_slice_in_dim(values, ((place + k) % size) * rows, rows, 0)
    add = lambda got, own: (got.astype(F32) + own.astype(F32)).astype(B16)
    from_left = from_right = None
    for step in range(forward):
        own = gate(chunk(forward - step), step)
        from_left = lax.ppermute(own if step == 0 else add(from_left, own), "rows", right)
        if step < back:
            own = gate(chunk(step - back), step)
            from_right = lax.ppermute(own if step == 0 else add(from_right, own), "rows", left)
    out = jnp.zeros(values.shape, F32)
    own, out = after((gate(chunk(0), forward), out), early)
    total = own.astype(F32) + from_left.astype(F32)
    if back:
        total = total + from_right.astype(F32)
    total = total.astype(B16)
    put = lambda item, k: lax.dynamic_update_slice_in_dim(
        out, item.astype(F32), ((place + k) % size) * rows, 0
    )
    out = put(total, 0)
    from_left = from_right = total
    for step in range(forward):
        from_left = lax.ppermute(gate(from_left, forward + 1 + step), "rows", right)
        out = put(from_left, -1 - step)
        if step < back:
            from_right = lax.ppermute(gate(from_right, forward + 1 + step), "rows", left)
            out = put(from_right, 1 + step)
    return out


def sum_cube(values, axis):
    size = lax.axis_size(axis)
    if size & (size - 1):
        return lax.psum(values, axis)
    distance = 1
    while distance < size:
        values = values + lax.ppermute(values, axis, [(i, i ^ distance) for i in range(size)])
        distance *= 2
    return values


def halo(own, reach):
    size = lax.axis_size("tp")
    left = lax.ppermute(own[-reach:], "tp", [(i, i + 1) for i in range(size - 1)])
    right = lax.ppermute(own[:reach], "tp", [(i + 1, i) for i in range(size - 1)])
    return jnp.concatenate([left, own, right], 0)


def to_true(values):
    size, mine = lax.axis_size("tp"), lax.axis_index("tp")
    rows = values.shape[0] // size
    return jnp.concatenate(
        [lax.dynamic_slice_in_dim(values, (mine ^ k) * rows, rows, 0) for k in range(size)], 0
    )


def ffn_forward(values, gain, weight_up, weight_down):
    normed, unit, inverse = normalize(values, gain)
    near, far = halves(gather(normed.astype(B16)))
    pre = [dot(half, weight_up) for half in (near, far)]
    act = [(item * jax.nn.sigmoid(item)).astype(B16) for item in pre]
    total, (sent, _) = scatter(pieces(act[0], act[1], weight_down, (1, 0)))
    pre = [item.astype(B16) for item in pre]
    return (values + 0.5 * total, (unit, inverse, (near, far), pre, act), sent)


def ffn_backward(grad, kept, gain, weight_up, weight_down):
    unit, inverse, wide, pre, act = kept
    own = (0.5 * grad).astype(B16)
    cot = halves(gather(own))
    d_pre = [
        (dot(cot[half], weight_down, (1, 1)) * swish_slope(pre[half].astype(F32))).astype(B16)
        for half in (0, 1)
    ]
    d_norm, (sent, _) = scatter(pieces(d_pre[0], d_pre[1], weight_up, (1, 1)))
    d_in, grad_gain = normalize_back(d_norm, unit, inverse, gain)
    cot, d_pre = after((cot, d_pre), sent)
    grad_down = dot(jnp.concatenate(act, 0), jnp.concatenate(cot, 0), (0, 0))
    grad_up = dot(jnp.concatenate(wide, 0), jnp.concatenate(d_pre, 0), (0, 0))
    return (grad + d_in, grad_gain, (grad_up.astype(B16), grad_down.astype(B16)), (own, sent))


def places(slots):
    size, mine = lax.axis_size("tp"), lax.axis_index("tp")
    rows = slots // size
    if rows % TK:
        q_at = jnp.arange(slots // TQ, dtype=jnp.int32) * TQ
        k_at = jnp.arange(slots // TK, dtype=jnp.int32) * TK
        return q_at, k_at, True
    q_true = jnp.arange(slots // TQ, dtype=jnp.int32) * TQ
    k_true = jnp.arange(slots // TK, dtype=jnp.int32) * TK
    q_at = ((q_true // rows) ^ mine) * rows + q_true % rows
    k_at = ((k_true // rows) ^ mine) * rows + k_true % rows
    return q_at.astype(jnp.int32), k_at.astype(jnp.int32), False


def attend_forward(
    values, gain, weights, attend_out, content_bias, position_bias, code, spans, rel, prefetch
):
    slots = code.shape[0]
    width = attend_out.shape[0]
    q_at, k_at, reorder = places(slots)
    where = (spans, q_at, k_at)
    normed, unit, inverse = normalize(values, gain)
    near, far = halves(gather(normed.astype(B16)))
    far = after(far, rel, spans)
    fetched, arrived = prefetch(far)
    mixed = [dot(half, weights) for half in (near, far)]
    flat = lambda bias: bias.astype(F32).reshape(1, width)
    join = lambda items: jnp.concatenate(items, 0)
    q_content = join([(item[:, :width] + flat(content_bias)).astype(B16) for item in mixed])
    q_position = join([(item[:, :width] + flat(position_bias)).astype(B16) for item in mixed])
    key = join([item[:, width : 2 * width].astype(B16) for item in mixed])
    value = join([item[:, 2 * width :].astype(B16) for item in mixed])
    if reorder:
        q_content, q_position, key, value = map(to_true, (q_content, q_position, key, value))
    operands = (
        where
        + (q_content, q_position, key, value, rel)
        + (code.reshape(slots, 1), code.reshape(slots // TK, 1, TK))
    )
    heads_out, heads_wide, sums = attend(*operands)
    sent = after(to_true(heads_out) if reorder else heads_out, arrived)
    half = slots // 2
    total, _ = scatter(pieces(sent[:half], sent[half:], attend_out, (1, 0)))
    kept = (unit, inverse, (near, far), operands, heads_wide, sums, sent)
    return (values + total, kept, fetched)


def attend_backward(grad, cot, kept, gain, weights, attend_out, table, filler):
    unit, inverse, wide, operands, heads_wide, sums, sent = kept
    slots, width = sent.shape
    _, _, reorder = places(slots)
    cot = halves(gather(cot))
    d_heads = jnp.concatenate([dot(half, attend_out, (1, 1)).astype(B16) for half in cot], 0)
    if reorder:
        d_heads = to_true(d_heads)
    d_heads = after(d_heads, filler[0])
    d_query, d_key, d_value, d_rel, d_bias = attend_back(*operands, d_heads, heads_wide, sums)
    d_query, d_key, d_value = after((d_query, d_key, d_value), filler[1])
    if reorder:
        d_query, d_key, d_value = map(to_true, (d_query, d_key, d_value))
    d_all = jnp.concatenate([d_query, d_key, d_value], 1)
    half = slots // 2
    d_norm, (last, _) = scatter(pieces(d_all[:half], d_all[half:], weights, (1, 1)))
    d_in, grad_gain = normalize_back(d_norm, unit, inverse, gain)
    cot, d_all, d_rel = after((cot, d_all, d_rel), last)
    grad_out = dot(jnp.concatenate(cot, 0), sent, (0, 0))
    grad_all = dot(jnp.concatenate(wide, 0), d_all, (0, 0))
    grad_pos = dot(table, d_rel, (0, 0))
    grads = jnp.concatenate([item.astype(B16) for item in (grad_all, grad_pos, grad_out)], 1)
    return (grad + d_in, grad_gain, grads, d_bias[:2])


def conv_weights(point_in, depth_kernel, gain_inner, point_out, first):
    taps = depth_kernel.shape[0]
    own = after((point_in[:, 0], point_in[:, 1], point_out), first)
    small = gather(jnp.concatenate([depth_kernel, gain_inner[None]], 0))
    small = jnp.concatenate(small, 1).astype(F32)
    in_a, in_b, out = map(gather, own)
    arrived = [item[2::2] for item in (in_a, in_b, out)]
    in_a, in_b = jnp.concatenate(in_a, 1), jnp.concatenate(in_b, 1)
    return (in_a, in_b, small[:taps], small[taps], jnp.concatenate(out, 0)), arrived


def conv_masks(segments, valid, rows, taps):
    edge = 8
    reach = taps // 2
    base = lax.axis_index("tp") * rows + edge - reach
    wide_segments = jnp.pad(segments, edge, constant_values=-1)
    wide_valid = jnp.pad(valid, edge)
    own = lax.dynamic_slice_in_dim(wide_segments, base, rows + 2 * reach)
    masks = []
    for tap in range(taps):
        other = lax.dynamic_slice_in_dim(wide_segments, base + tap - reach, rows + 2 * reach)
        good = lax.dynamic_slice_in_dim(wide_valid, base + tap - reach, rows + 2 * reach)
        masks.append(((other == own) & (good == 1)).astype(F32)[:, None])
    return masks


def conv_forward(values, gain, full, masks):
    in_a, in_b, kernel, gain_inner, out = full
    rows = values.shape[0]
    taps = kernel.shape[0]
    reach = taps // 2
    normed, unit, inverse = normalize(values, gain)
    low = normed.astype(B16)
    wide = halo(low, 2 * reach)
    mixed_a = dot(wide, in_a)
    gate = jax.nn.sigmoid(dot(wide, in_b))
    glu = mixed_a * gate
    depth = 0.0
    for tap in range(taps):
        depth = depth + kernel[tap] * masks[tap] * glu[tap : tap + rows + 2 * reach]
    depth_norm, inner_unit, inner_inverse = normalize(depth, gain_inner)
    inner = (depth_norm * jax.nn.sigmoid(depth_norm)).astype(B16)
    own = slice(2 * reach, 2 * reach + rows)
    kept = (unit, inverse, low, mixed_a[own], gate[own], glu, inner_unit, inner_inverse, depth_norm, inner)
    return (values + dot(inner[reach : reach + rows], out), kept)


def conv_backward(grad, kept, gain, full, masks):
    unit, inverse, low, mixed_a, gate, glu, inner_unit, inner_inverse, depth_norm, inner = kept
    in_a, in_b, kernel, gain_inner, out = full
    rows = grad.shape[0]
    taps = kernel.shape[0]
    reach = taps // 2
    mine = slice(reach, reach + rows)
    cot = grad.astype(B16)
    d_act = dot(halo(cot, reach), out, (1, 1))
    d_depth_norm = d_act * swish_slope(depth_norm)
    grad_gain_inner = jnp.sum((d_depth_norm * inner_unit)[mine], axis=0)
    d_depth, _ = normalize_back(d_depth_norm, inner_unit, inner_inverse, gain_inner)
    d_glu = 0.0
    kernel_rows = []
    for tap in range(taps):
        weighted = d_depth * masks[tap]
        back = 2 * reach - tap
        d_glu = d_glu + kernel[tap] * weighted[back : back + rows]
        kernel_rows.append(jnp.sum(weighted[mine] * glu[reach + tap : reach + tap + rows], axis=0))
    d_a = (d_glu * gate).astype(B16)
    d_b = (d_glu * mixed_a * gate * (1.0 - gate)).astype(B16)
    d_norm = dot(d_a, in_a, (1, 1)) + dot(d_b, in_b, (1, 1))
    d_in, grad_gain = normalize_back(d_norm, unit, inverse, gain)
    grad = grad + d_in
    next_cot = grad.astype(B16)
    low, cot, d_a, d_b, inner = after((low, cot, d_a, d_b, inner), next_cot)
    size = lax.axis_size("tp")
    width = in_a.shape[1] // size
    parts, small_parts = [], []
    small = jnp.stack(kernel_rows + [grad_gain_inner], 0)
    for slot in range(size):
        cols = slice(slot * width, (slot + 1) * width)
        parts.append(
            jnp.concatenate(
                [
                    dot(low, d_a[:, cols], (0, 0)),
                    dot(low, d_b[:, cols], (0, 0)),
                    dot(cot, inner[mine][:, cols], (0, 0)),
                ],
                1,
            )
        )
        small_parts.append(small[:, cols])
    total, ends = scatter(parts)
    return (grad, next_cot, grad_gain, (total.astype(B16), scatter(small_parts)[0]), ends)


def body(
    layer_input,
    cotangent,
    segments,
    valid_frames,
    gain_first,
    up_first,
    down_first,
    gain_attend,
    query_weight,
    key_weight,
    value_weight,
    attend_out,
    pos_weight,
    content_bias,
    position_bias,
    gain_conv,
    point_in,
    depth_kernel,
    gain_inner,
    point_out,
    gain_second,
    up_second,
    down_second,
    gain_final,
):
    segment_row, valid_row = segments[0], valid_frames[0]
    weights = jnp.concatenate([query_weight, key_weight, value_weight], 1)
    width = query_weight.shape[1]
    taps = depth_kernel.shape[0]
    values = layer_input[0].astype(F32)
    rows = values.shape[0]
    slots = segment_row.shape[0]
    masks = conv_masks(segment_row, valid_row, rows, taps)
    code = codes(segment_row, valid_row)
    spans = spans_of(code)
    values, kept_first, sent = ffn_forward(values, gain_first, up_first, down_first)
    table = distance_table(slots, values.shape[1], sent)
    rel = dot(table, pos_weight).astype(B16)
    prefetch = functools.partial(conv_weights, point_in, depth_kernel, gain_inner, point_out)
    values, kept_attend, full = attend_forward(
        values, gain_attend, weights, attend_out, content_bias, position_bias, code, spans, rel, prefetch
    )
    values, kept_conv = conv_forward(values, gain_conv, full, masks)
    values, kept_second, _ = ffn_forward(values, gain_second, up_second, down_second)
    final, final_unit, final_inverse = normalize(values, gain_final)
    layer_output = final.astype(B16)
    grad, sum_final = normalize_back(cotangent[0].astype(F32), final_unit, final_inverse, gain_final)
    grad, sum_second, second_grads, _ = ffn_backward(
        grad, kept_second, gain_second, up_second, down_second
    )
    second_sum = lax.psum(second_grads, "rows")
    grad, cot, sum_conv, conv_grads, ends = conv_backward(grad, kept_conv, gain_conv, full, masks)
    grad, sum_attend, attend_grads, d_bias = attend_backward(
        grad, cot, kept_attend, gain_attend, weights, attend_out, table, ends
    )
    grad, sum_first, first_grads, marks = ffn_backward(
        grad, kept_first, gain_first, up_first, down_first
    )
    middle = jnp.concatenate([attend_grads, conv_grads[0]], 1)
    gates = (None, marks[0], marks[0], marks[1], marks[1])
    middle = sum_ring(middle, gates)
    attend_sum, conv_sum = middle[:, : 5 * width], middle[:, 5 * width :]
    second_up, second_down = [item.astype(F32) for item in second_sum]
    first_down = sum_ring(first_grads[1])
    first_up = sum_ring(first_grads[0], early=(second_up, second_down))
    first_sum = (first_up, first_down)
    gains = sum_cube(jnp.stack([sum_first, sum_attend, sum_conv, sum_second, sum_final]), "tp")
    small = jnp.concatenate([conv_grads[1], d_bias], 0)
    small_shape = small.shape
    pack = jnp.concatenate([gains.reshape(-1), small.reshape(-1)]).reshape(-1, width)
    pack = sum_cube(pack, "rows").reshape(-1)
    gains, small = pack[: gains.size].reshape(gains.shape), pack[gains.size :].reshape(small_shape)
    bias_shape = content_bias.shape
    return (
        layer_output[None],
        grad[None],
        gains[0],
        first_sum[0],
        first_sum[1],
        gains[1],
        attend_sum[:, :width],
        attend_sum[:, width : 2 * width],
        attend_sum[:, 2 * width : 3 * width],
        attend_sum[:, 4 * width :].T,
        attend_sum[:, 3 * width : 4 * width],
        small[taps + 1].reshape(bias_shape),
        small[taps + 2].reshape(bias_shape),
        gains[2],
        jnp.stack([conv_sum[:, :width], conv_sum[:, width : 2 * width]], 1),
        small[:taps],
        small[taps],
        conv_sum[:, 2 * width :].T,
        gains[3],
        second_up,
        second_down,
        gains[4],
    )


def solution(mesh):
    in_specs = (
        P("rows", "tp", None),
        P("rows", "tp", None),
        P("rows", None),
        P("rows", None),
        P(),
        P(None, "tp"),
        P("tp", None),
        P(),
        P(None, "tp"),
        P(None, "tp"),
        P(None, "tp"),
        P("tp", None),
        P(None, "tp"),
        P("tp", None),
        P("tp", None),
        P(),
        P(None, None, "tp"),
        P(None, "tp"),
        P("tp"),
        P("tp", None),
        P(),
        P(None, "tp"),
        P("tp", None),
        P(),
    )
    out_specs = (
        P("rows", "tp", None),
        P("rows", "tp", None),
        P(),
        P(None, "tp"),
        P("tp", None),
        P(),
        P(None, "tp"),
        P(None, "tp"),
        P(None, "tp"),
        P("tp", None),
        P(None, "tp"),
        P("tp", None),
        P("tp", None),
        P(),
        P(None, None, "tp"),
        P(None, "tp"),
        P("tp"),
        P("tp", None),
        P(),
        P(None, "tp"),
        P("tp", None),
        P(),
    )
    return jax.shard_map(body, mesh=mesh, in_specs=in_specs, out_specs=out_specs, check_vma=False)
```

```python
import functools
import math

import jax
import jax.numpy as jnp
from jax import lax
from jax.experimental import pallas as pl
from jax.experimental.pallas import tpu as pltpu
from jax.sharding import PartitionSpec as P

EPS = 1e-05
NEG = -1e30
F32 = jnp.float32
B16 = jnp.bfloat16
TQ = 128
TK = 384
HD = 128
STEP = 64
SM = pl.BlockSpec(memory_space=pltpu.SMEM)
VM = pl.BlockSpec(memory_space=pltpu.VMEM)

def dotx(a, b, ca, cb):
    return lax.dot_general(a, b, (((ca,), (cb,)), ((), ())), preferred_element_type=F32)

def skew_tile(grid):
    return pltpu.roll(grid, TK + 1, 1, stride=1, stride_axis=0)[:, :TK]

def unskew_flipped(flipped):
    wide = jnp.concatenate([flipped, jnp.zeros((TQ, TQ), F32)], axis=1)
    return pltpu.roll(wide, 0, 1, stride=1, stride_axis=0)

def attend_kernel(heads, spans, q_at, k_at, qc_ref, qp_ref, k_ref, v_ref, rel_ref, code_q_ref, code_k_ref,
                  out_ref, wide_ref, lse_ref):
    slots = qc_ref.shape[0]
    scale = HD ** -0.5
    blocks, tiles = slots // TQ, slots // TK

    def q_step(qb, _):
        at = pl.multiple_of(q_at[qb], TQ)
        true_at = pl.multiple_of(qb * TQ, TQ)
        code_q = code_q_ref[pl.ds(true_at, TQ), :]
        qc = [qc_ref[pl.ds(at, TQ), h * HD:(h + 1) * HD] for h in range(heads)]
        qp = [qp_ref[pl.ds(at, TQ), h * HD:(h + 1) * HD] for h in range(heads)]

        def k_step(kt, carry):
            ko = pl.multiple_of(k_at[kt], TQ)
            to = pl.multiple_of((blocks - 1 + kt * (TK // TQ) - qb) * TQ, TQ)
            mask = code_q == code_k_ref[kt]
            new = []
            for h in range(heads):
                lanes = slice(h * HD, (h + 1) * HD)
                top, total, acc = carry[h]
                grid = dotx(qp[h], rel_ref[pl.ds(to, TK + TQ), lanes], 1, 1)
                raw = dotx(qc[h], k_ref[pl.ds(ko, TK), lanes], 1, 1) + skew_tile(grid)
                scores = jnp.where(mask, raw * scale, NEG)
                top_new = jnp.maximum(top, jnp.max(scores, axis=1, keepdims=True))
                shrink = jnp.exp(top - top_new)
                weights = jnp.exp(scores - top_new)
                total = total * shrink + jnp.sum(weights, axis=1, keepdims=True)
                acc = acc * shrink + dotx(weights.astype(B16), v_ref[pl.ds(ko, TK), lanes], 1, 0)
                new.append((top_new, total, acc))
            return tuple(new)

        first = tuple((jnp.full((TQ, 1), NEG, F32), jnp.zeros((TQ, 1), F32), jnp.zeros((TQ, HD), F32))
                      for _ in range(heads))
        final = lax.fori_loop(spans[0, qb], spans[1, qb], k_step, first)
        for h in range(heads):
            lanes = slice(h * HD, (h + 1) * HD)
            top, total, acc = final[h]
            out = acc / total
            wide_ref[pl.ds(at, TQ), lanes] = out
            out_ref[pl.ds(at, TQ), lanes] = out.astype(B16)
            lse_ref[pl.ds(at, TQ), h:h + 1] = top + jnp.log(total)
        return 0

    lax.fori_loop(0, blocks, q_step, 0)

def attend_back_kernel(heads, spans, q_at, k_at, qc_ref, qp_ref, k_ref, v_ref, rel_ref, code_q_ref, code_k_ref,
                       d_out_ref, wide_ref, lse_ref,
                       dq_ref, dk_ref, dv_ref, drel_ref, bias_ref, dk_acc, dv_acc, drel_acc):
    slots = qc_ref.shape[0]
    scale = HD ** -0.5
    blocks, tiles = slots // TQ, slots // TK
    dk_acc[...] = jnp.zeros_like(dk_acc)
    dv_acc[...] = jnp.zeros_like(dv_acc)
    drel_acc[...] = jnp.zeros_like(drel_acc)
    bias_ref[...] = jnp.zeros_like(bias_ref)
    row = lax.broadcasted_iota(jnp.int32, (TQ, TQ), 0)
    column = lax.broadcasted_iota(jnp.int32, (TQ, TQ), 1)
    flip = (row + column == TQ - 1).astype(F32)
    flip_low = flip.astype(B16)

    def q_step(qb, _):
        at = pl.multiple_of(q_at[qb], TQ)
        true_at = pl.multiple_of(qb * TQ, TQ)
        code_q = code_q_ref[pl.ds(true_at, TQ), :]
        cols = [slice(h * HD, (h + 1) * HD) for h in range(heads)]
        qc = [qc_ref[pl.ds(at, TQ), c] for c in cols]
        qp = [qp_ref[pl.ds(at, TQ), c] for c in cols]
        qp_flipped = [dotx(flip_low, item, 1, 0).astype(B16) for item in qp]
        d_out = [d_out_ref[pl.ds(at, TQ), c] for c in cols]
        lse = [lse_ref[pl.ds(at, TQ), h:h + 1] for h in range(heads)]
        delta = [jnp.sum(d_out[h].astype(F32) * wide_ref[pl.ds(at, TQ), cols[h]], axis=1, keepdims=True)
                 for h in range(heads)]

        def k_step(kt, carry):
            ko = pl.multiple_of(k_at[kt], TQ)
            to = pl.multiple_of((blocks - 1 + kt * (TK // TQ) - qb) * TQ, TQ)
            mask = code_q == code_k_ref[kt]
            new = []
            for h in range(heads):
                lanes = cols[h]
                d_content, d_position = carry[h]
                window = rel_ref[pl.ds(to, TK + TQ), lanes]
                key = k_ref[pl.ds(ko, TK), lanes]
                grid = dotx(qp[h], window, 1, 1)
                raw = dotx(qc[h], key, 1, 1) + skew_tile(grid)
                probs = jnp.exp(jnp.where(mask, raw * scale - lse[h], NEG))
                d_probs = dotx(d_out[h], v_ref[pl.ds(ko, TK), lanes], 1, 1)
                d_raw = probs * (d_probs - delta[h]) * scale
                d_low = d_raw.astype(B16)
                d_grid = unskew_flipped(dotx(flip_low, d_low, 1, 0)).astype(B16)
                dv_acc[pl.ds(ko, TK), lanes] += dotx(probs.astype(B16), d_out[h], 0, 0)
                dk_acc[pl.ds(ko, TK), lanes] += dotx(d_low, qc[h], 0, 0)
                drel_acc[pl.ds(to, TK + TQ), lanes] += dotx(d_grid, qp_flipped[h], 0, 0)
                d_content = d_content + dotx(d_low, key, 1, 0)
                d_position = d_position + dotx(d_grid, window, 1, 0)
                new.append((d_content, d_position))
            return tuple(new)

        first = tuple((jnp.zeros((TQ, HD), F32),) * 2 for _ in range(heads))
        final = lax.fori_loop(spans[0, qb], spans[1, qb], k_step, first)
        for h in range(heads):
            d_content, d_position = final[h]
            d_position = lax.dot_general(flip, d_position, (((1,), (0,)), ((), ())),
                                         precision=lax.Precision.HIGHEST, preferred_element_type=F32)
            dq_ref[pl.ds(at, TQ), cols[h]] = (d_content + d_position).astype(B16)
            bias_ref[0:1, cols[h]] += jnp.sum(d_content, axis=0, keepdims=True)
            bias_ref[1:2, cols[h]] += jnp.sum(d_position, axis=0, keepdims=True)
        return 0

    lax.fori_loop(0, blocks, q_step, 0)
    dk_ref[...] = dk_acc[...].astype(B16)
    dv_ref[...] = dv_acc[...].astype(B16)
    drel_ref[...] = drel_acc[...].astype(B16)

def sds(s, d): return jax.ShapeDtypeStruct(s, d)

def attend(spans, q_at, k_at, qc, qp, k, v, rel, code_q, code_k):
    slots, width = qc.shape
    heads = width // HD
    return pl.pallas_call(
        functools.partial(attend_kernel, heads),
        out_shape=(sds((slots, width), B16), sds((slots, width), F32), sds((slots, heads), F32)),
        in_specs=[SM] * 3 + [VM] * 7, out_specs=(VM,) * 3,
        compiler_params=pltpu.CompilerParams(vmem_limit_bytes=40 << 20),
        cost_estimate=pl.CostEstimate(flops=int(4e9), bytes_accessed=int(9e6), transcendentals=int(2e6)),
    )(spans, q_at, k_at, qc, qp, k, v, rel, code_q, code_k)

def attend_back(spans, q_at, k_at, qc, qp, k, v, rel, code_q, code_k, d_out, wide, lse):
    slots, width = qc.shape
    heads = width // HD
    return pl.pallas_call(
        functools.partial(attend_back_kernel, heads),
        out_shape=(sds((slots, width), B16),) * 3 + (sds((2 * slots, width), B16), sds((8, width), F32)),
        in_specs=[SM] * 3 + [VM] * 10, out_specs=(VM,) * 5,
        scratch_shapes=[pltpu.VMEM((slots, width), F32), pltpu.VMEM((slots, width), F32), pltpu.VMEM((2 * slots, width), F32)],
        compiler_params=pltpu.CompilerParams(vmem_limit_bytes=48 << 20),
        cost_estimate=pl.CostEstimate(flops=int(12e9), bytes_accessed=int(12e6), transcendentals=int(2e6)),
    )(spans, q_at, k_at, qc, qp, k, v, rel, code_q, code_k, d_out, wide, lse)

def codes(segments, valid):
    slots = segments.shape[0]
    place = jnp.arange(slots, dtype=jnp.int32)
    code = jnp.where(valid == 1, segments, -1 - place)
    return code

def spans_of(code):
    slots = code.shape[0]
    same = code[:, None] == code[None, :]
    touch = jnp.any(same.reshape(slots // TQ, TQ, slots // TK, TK), axis=(1, 3))
    tiles = slots // TK
    idx = jnp.arange(tiles, dtype=jnp.int32)
    lo = jnp.min(jnp.where(touch, idx, tiles), axis=1)
    hi = jnp.max(jnp.where(touch, idx + 1, 0), axis=1)
    return jnp.stack([lo, hi], 0).astype(jnp.int32)


def normalize(values, gain):
    mean = jnp.mean(values, axis=-1, keepdims=True)
    centered = values - mean
    inverse = lax.rsqrt(jnp.mean(centered * centered, axis=-1, keepdims=True) + EPS)
    unit = centered * inverse
    return (unit * gain.astype(F32), unit, inverse)


def normalize_back(grad, unit, inverse, gain):
    scaled = grad * gain.astype(F32)
    first = jnp.mean(scaled, axis=-1, keepdims=True)
    second = jnp.mean(scaled * unit, axis=-1, keepdims=True)
    return (inverse * (scaled - first - unit * second), jnp.sum(grad * unit, axis=0))


def swish_slope(values):
    gate = jax.nn.sigmoid(values)
    return gate * (1.0 + values * (1.0 - gate))


def distance_table(slots, width, first):
    column = jnp.arange(width)
    even = (column % 2 == 0)[None, :]
    rate = jnp.exp(-(column - column % 2).astype(F32) * (math.log(10000.0) / width))
    coarse = (slots - 1 - STEP * jnp.arange(2 * slots // STEP)).astype(F32)[:, None] * rate[None, :]
    fine = jnp.arange(STEP).astype(F32)[:, None] * rate[None, :]
    sin_c, cos_c = jnp.sin(coarse), jnp.cos(coarse)
    with_cos = jnp.where(even, sin_c, cos_c)
    with_sin = jnp.where(even, -cos_c, sin_c)
    with_cos, with_sin, sin_f, cos_f = after((with_cos, with_sin, jnp.sin(fine), jnp.cos(fine)), first)
    table = with_cos[:, None, :] * cos_f[None] + with_sin[:, None, :] * sin_f[None]
    return table.reshape(2 * slots, width).astype(B16)


def dot(left, right, contract=(1, 0)):
    return lax.dot_general(
        left, right, (((contract[0],), (contract[1],)), ((), ())), preferred_element_type=F32
    )


def swap(values, distance):
    size = lax.axis_size("tp")
    return lax.ppermute(values, "tp", [(i, i ^ distance) for i in range(size)])


def distances():
    size = lax.axis_size("tp")
    return [1 << bit for bit in range(size.bit_length() - 1)]


def gather(own):
    slots = {0: own}
    for distance in reversed(distances()):
        for slot in list(slots):
            slots[slot ^ distance] = swap(slots[slot], distance)
    return [slots[slot] for slot in range(len(slots))]


def scatter(parts):
    parts = dict(enumerate(parts))
    sent = got = None
    for distance in distances():
        for slot in sorted(parts, reverse=True):
            if slot & distance:
                sent = parts.pop(slot).astype(B16)
                got = swap(sent, distance)
                parts[slot ^ distance] = parts[slot ^ distance].astype(F32) + got.astype(F32)
    return parts[0], (sent, got)


def after(values, *others):
    return lax.optimization_barrier((values, others))[0]


def halves(slots):
    half = len(slots) // 2
    return jnp.concatenate(slots[:half], 0), jnp.concatenate(slots[half:], 0)


def pieces(near, far, weight, contract):
    count = lax.axis_size("tp") // 2
    rows = near.shape[0] // count
    outs = {}
    for slot in reversed(range(2 * count)):
        source, place = (near, slot) if slot < count else (far, slot - count)
        outs[slot] = dot(source[place * rows : (place + 1) * rows], weight, contract)
    return [outs[slot] for slot in range(2 * count)]


def ring():
    size, mine = lax.axis_size("rows"), lax.axis_index("rows")
    order = list(range(0, size, 2)) + list(range(size - 1, 0, -2))
    place = jnp.where(mine % 2 == 0, mine // 2, size - (mine + 1) // 2)
    right = [(order[i], order[(i + 1) % size]) for i in range(size)]
    return size, place, right, [(there, here) for here, there in right]


def plain(piece):
    return piece


def turned(piece):
    return piece.T


def paired(piece):
    return piece.reshape(piece.shape[0], 2, piece.shape[1] // 2)


class RowSum:
    def __init__(self, values, parts, fill):
        self.size, self.place, self.right, self.left = ring()
        self.values, self.parts, self.fill = values, parts, fill
        self.rows = values.shape[0] // self.size
        self.half = self.rows // 2
        self.stages = self.size // 2
        self.steps = 2 * self.stages
        self.done = 0
        self.outs = None

    def chunk(self, k):
        at = ((self.place + k) % self.size) * self.rows
        return lax.dynamic_slice_in_dim(self.values, at, self.rows, 0)

    def send(self, to_right, to_left):
        self.from_left = lax.ppermute(to_right, "rows", self.right)
        self.from_right = lax.ppermute(to_left, "rows", self.left)
        return (to_right, to_left)

    def put(self, item, k, first=0):
        at = ((self.place + k) % self.size) * self.rows + first
        new, edge = [], 0
        for out, (width, form) in zip(self.outs, self.parts):
            piece = form(item[:, edge : edge + width].astype(F32))
            starts = [0] * out.ndim
            starts[out.ndim - 1 if form is turned else 0] = at
            new.append(lax.dynamic_update_slice(out, piece, starts))
            edge += width
        self.outs = new

    def step(self, gate=()):
        stage, stages, half = self.done, self.stages, self.half
        self.done += 1
        wide = lambda item: item.astype(F32)
        if stage == 0:
            first = after((self.chunk(stages)[:half], self.chunk(-stages)[half:]), gate)
            return self.send(*first)
        if stage <= stages:
            to_right, to_left = self.chunk(stages - stage), self.chunk(stage - stages)
            to_right, to_left = after((to_right, to_left), gate)
            to_right, to_left = wide(to_right), wide(to_left)
            from_left, from_right = wide(self.from_left), wide(self.from_right)
            if stage == 1:
                from_left = jnp.pad(from_left, ((0, self.rows - half), (0, 0)))
                from_right = jnp.pad(from_right, ((half, 0), (0, 0)))
            if stage < stages:
                to_right, to_left = to_right + from_left, to_left + from_right
                return self.send(to_right.astype(B16), to_left.astype(B16))
            total = (to_right + from_left + from_right).astype(B16)
            self.outs = []
            for width, form in self.parts:
                item = jax.eval_shape(form, jax.ShapeDtypeStruct((self.values.shape[0], width), F32))
                self.outs.append(jnp.full(item.shape, self.fill, F32))
            total, self.outs = after((total, self.outs))
            self.put(total, 0)
            to_right = to_left = total
        else:
            to_right, to_left = after((self.from_left, self.from_right), gate)
            self.put(to_right, stages - stage)
            self.put(to_left, stage - stages)
        if stage == 2 * stages - 1:
            to_right, to_left = to_right[:half], to_left[half:]
        return self.send(to_right, to_left)

    def finish(self):
        self.put(self.from_left, -self.stages)
        self.put(self.from_right, self.stages, self.half)
        return self.outs


class WholeSum(RowSum):
    def step(self, gate=()):
        self.done += 1
        if self.done == 1:
            self.total = lax.psum(after(self.values, gate), "rows").astype(F32)
        return ()

    def finish(self):
        edges = [sum(width for width, _ in self.parts[:k]) for k in range(len(self.parts) + 1)]
        return [
            form(self.total[:, edges[k] : edges[k + 1]]) for k, (_, form) in enumerate(self.parts)
        ]


def row_sum(values, parts, fill):
    kind = WholeSum if lax.axis_size("rows") % 2 else RowSum
    return kind(values, parts, float(fill))


def sum_cube(values, axis):
    size = lax.axis_size(axis)
    if size & (size - 1):
        return lax.psum(values, axis)
    distance = 1
    while distance < size:
        values = values + lax.ppermute(values, axis, [(i, i ^ distance) for i in range(size)])
        distance *= 2
    return values


def halo(own, reach):
    size = lax.axis_size("tp")
    left = lax.ppermute(own[-reach:], "tp", [(i, i + 1) for i in range(size - 1)])
    right = lax.ppermute(own[:reach], "tp", [(i + 1, i) for i in range(size - 1)])
    return jnp.concatenate([left, own, right], 0)


def to_true(values):
    size, mine = lax.axis_size("tp"), lax.axis_index("tp")
    rows = values.shape[0] // size
    return jnp.concatenate(
        [lax.dynamic_slice_in_dim(values, (mine ^ k) * rows, rows, 0) for k in range(size)], 0
    )


def ffn_forward(values, gain, weight_up, weight_down):
    normed, unit, inverse = normalize(values, gain)
    near, far = halves(gather(normed.astype(B16)))
    pre, act = [], []
    for half in (near, far):
        pre.append(dot(after(half, act), weight_up))
        act.append((pre[-1] * jax.nn.sigmoid(pre[-1])).astype(B16))
    total, (sent, _) = scatter(pieces(act[0], act[1], weight_down, (1, 0)))
    pre = [item.astype(B16) for item in pre]
    return (values + 0.5 * total, (unit, inverse, (near, far), pre, act), sent)


def ffn_backward(grad, kept, gain, weight_up, weight_down):
    unit, inverse, wide, pre, act = kept
    own = (0.5 * grad).astype(B16)
    cot = halves(gather(own))
    d_pre = []
    for half in (0, 1):
        d_act = dot(after(cot[half], d_pre), weight_down, (1, 1))
        d_pre.append((d_act * swish_slope(pre[half].astype(F32))).astype(B16))
    d_norm, (sent, _) = scatter(pieces(d_pre[0], d_pre[1], weight_up, (1, 1)))
    d_in, grad_gain = normalize_back(d_norm, unit, inverse, gain)
    cot, d_pre = after((cot, d_pre), sent)
    grad_down = dot(jnp.concatenate(act, 0), jnp.concatenate(cot, 0), (0, 0))
    grad_up = dot(jnp.concatenate(wide, 0), jnp.concatenate(d_pre, 0), (0, 0))
    return (grad + d_in, grad_gain, (grad_up.astype(B16), grad_down.astype(B16)), (own, sent))


def places(slots):
    size, mine = lax.axis_size("tp"), lax.axis_index("tp")
    rows = slots // size
    if rows % TK:
        q_at = jnp.arange(slots // TQ, dtype=jnp.int32) * TQ
        k_at = jnp.arange(slots // TK, dtype=jnp.int32) * TK
        return q_at, k_at, True
    q_true = jnp.arange(slots // TQ, dtype=jnp.int32) * TQ
    k_true = jnp.arange(slots // TK, dtype=jnp.int32) * TK
    q_at = ((q_true // rows) ^ mine) * rows + q_true % rows
    k_at = ((k_true // rows) ^ mine) * rows + k_true % rows
    return q_at.astype(jnp.int32), k_at.astype(jnp.int32), False


def attend_forward(
    values, gain, weights, attend_out, content_bias, position_bias, code, spans, rel, prefetch
):
    slots = code.shape[0]
    width = attend_out.shape[0]
    q_at, k_at, reorder = places(slots)
    where = (spans, q_at, k_at)
    normed, unit, inverse = normalize(values, gain)
    near, far = halves(gather(normed.astype(B16)))
    mixed = [dot(near, weights)]
    far = after(far, rel, spans, mixed)
    fetched, arrived = prefetch(far)
    mixed.append(dot(far, weights))
    flat = lambda bias: bias.astype(F32).reshape(1, width)
    join = lambda items: jnp.concatenate(items, 0)
    q_content = join([(item[:, :width] + flat(content_bias)).astype(B16) for item in mixed])
    q_position = join([(item[:, :width] + flat(position_bias)).astype(B16) for item in mixed])
    key = join([item[:, width : 2 * width].astype(B16) for item in mixed])
    value = join([item[:, 2 * width :].astype(B16) for item in mixed])
    if reorder:
        q_content, q_position, key, value = map(to_true, (q_content, q_position, key, value))
    operands = (
        where
        + (q_content, q_position, key, value, rel)
        + (code.reshape(slots, 1), code.reshape(slots // TK, 1, TK))
    )
    heads_out, heads_wide, sums = attend(*operands)
    sent = after(to_true(heads_out) if reorder else heads_out, arrived)
    half = slots // 2
    total, _ = scatter(pieces(sent[:half], sent[half:], attend_out, (1, 0)))
    kept = (unit, inverse, (near, far), operands, heads_wide, sums, sent)
    return (values + total, kept, fetched)


def attend_backward(grad, cot, kept, gain, weights, attend_out, table, filler):
    unit, inverse, wide, operands, heads_wide, sums, sent = kept
    slots, width = sent.shape
    _, _, reorder = places(slots)
    cot = halves(gather(cot))
    d_near = dot(cot[0], attend_out, (1, 1)).astype(B16)
    cot = (cot[0], after(cot[1], d_near))
    d_heads = jnp.concatenate([d_near, dot(cot[1], attend_out, (1, 1)).astype(B16)], 0)
    if reorder:
        d_heads = to_true(d_heads)
    d_heads = after(d_heads, filler[0])
    d_query, d_key, d_value, d_rel, d_bias = attend_back(*operands, d_heads, heads_wide, sums)
    d_query, d_key, d_value = after((d_query, d_key, d_value), filler[1])
    if reorder:
        d_query, d_key, d_value = map(to_true, (d_query, d_key, d_value))
    d_all = jnp.concatenate([d_query, d_key, d_value], 1)
    half = slots // 2
    d_norm, (last, _) = scatter(pieces(d_all[:half], d_all[half:], weights, (1, 1)))
    d_in, grad_gain = normalize_back(d_norm, unit, inverse, gain)
    cot, d_all, d_rel = after((cot, d_all, d_rel), last)
    grad_out = dot(jnp.concatenate(cot, 0), sent, (0, 0))
    grad_all = dot(jnp.concatenate(wide, 0), d_all, (0, 0))
    grad_pos = dot(table, d_rel, (0, 0))
    grads = jnp.concatenate([item.astype(B16) for item in (grad_all, grad_pos, grad_out)], 1)
    return (grad + d_in, grad_gain, grads, d_bias[:2])


def conv_weights(point_in, depth_kernel, gain_inner, point_out, first):
    taps = depth_kernel.shape[0]
    own = after((point_in[:, 0], point_in[:, 1], point_out), first)
    small = gather(jnp.concatenate([depth_kernel, gain_inner[None]], 0))
    small = jnp.concatenate(small, 1).astype(F32)
    in_a, in_b, out = map(gather, own)
    arrived = [item[2::2] for item in (in_a, in_b, out)]
    in_a, in_b = jnp.concatenate(in_a, 1), jnp.concatenate(in_b, 1)
    return (in_a, in_b, small[:taps], small[taps], jnp.concatenate(out, 0)), arrived


def conv_masks(segments, valid, rows, taps):
    edge = 8
    reach = taps // 2
    base = lax.axis_index("tp") * rows + edge - reach
    wide_segments = jnp.pad(segments, edge, constant_values=-1)
    wide_valid = jnp.pad(valid, edge)
    own = lax.dynamic_slice_in_dim(wide_segments, base, rows + 2 * reach)
    masks = []
    for tap in range(taps):
        other = lax.dynamic_slice_in_dim(wide_segments, base + tap - reach, rows + 2 * reach)
        good = lax.dynamic_slice_in_dim(wide_valid, base + tap - reach, rows + 2 * reach)
        masks.append(((other == own) & (good == 1)).astype(F32)[:, None])
    return masks


def conv_forward(values, gain, full, masks):
    in_a, in_b, kernel, gain_inner, out = full
    rows = values.shape[0]
    taps = kernel.shape[0]
    reach = taps // 2
    normed, unit, inverse = normalize(values, gain)
    low = normed.astype(B16)
    wide = halo(low, 2 * reach)
    mixed_a = dot(wide, in_a)
    gate = jax.nn.sigmoid(dot(wide, in_b))
    glu = mixed_a * gate
    depth = 0.0
    for tap in range(taps):
        depth = depth + kernel[tap] * masks[tap] * glu[tap : tap + rows + 2 * reach]
    depth_norm, inner_unit, inner_inverse = normalize(depth, gain_inner)
    inner = (depth_norm * jax.nn.sigmoid(depth_norm)).astype(B16)
    own = slice(2 * reach, 2 * reach + rows)
    kept = (unit, inverse, low, mixed_a[own], gate[own], glu, inner_unit, inner_inverse, depth_norm, inner)
    return (values + dot(inner[reach : reach + rows], out), kept)


def conv_backward(grad, kept, gain, full, masks):
    unit, inverse, low, mixed_a, gate, glu, inner_unit, inner_inverse, depth_norm, inner = kept
    in_a, in_b, kernel, gain_inner, out = full
    rows = grad.shape[0]
    taps = kernel.shape[0]
    reach = taps // 2
    mine = slice(reach, reach + rows)
    cot = grad.astype(B16)
    d_act = dot(halo(cot, reach), out, (1, 1))
    d_depth_norm = d_act * swish_slope(depth_norm)
    grad_gain_inner = jnp.sum((d_depth_norm * inner_unit)[mine], axis=0)
    d_depth, _ = normalize_back(d_depth_norm, inner_unit, inner_inverse, gain_inner)
    d_glu = 0.0
    kernel_rows = []
    for tap in range(taps):
        weighted = d_depth * masks[tap]
        back = 2 * reach - tap
        d_glu = d_glu + kernel[tap] * weighted[back : back + rows]
        kernel_rows.append(jnp.sum(weighted[mine] * glu[reach + tap : reach + tap + rows], axis=0))
    d_a = (d_glu * gate).astype(B16)
    d_b = (d_glu * mixed_a * gate * (1.0 - gate)).astype(B16)
    d_norm = dot(d_a, in_a, (1, 1)) + dot(d_b, in_b, (1, 1))
    d_in, grad_gain = normalize_back(d_norm, unit, inverse, gain)
    grad = grad + d_in
    next_cot = grad.astype(B16)
    low, cot, d_a, d_b, inner = after((low, cot, d_a, d_b, inner), next_cot)
    size = lax.axis_size("tp")
    width = in_a.shape[1] // size
    parts, small_parts = [], []
    grads = [
        dot(left, right, (0, 0)).astype(B16)
        for left, right in ((low, d_a), (low, d_b), (cot, inner[mine]))
    ]
    small = jnp.stack(kernel_rows + [grad_gain_inner], 0)
    for slot in range(size):
        cols = slice(slot * width, (slot + 1) * width)
        parts.append(jnp.concatenate([item[:, cols] for item in grads], 1))
        small_parts.append(small[:, cols])
    total, ends = scatter(parts)
    return (grad, next_cot, grad_gain, (total.astype(B16), scatter(small_parts)[0]), ends)


def body(
    layer_input,
    cotangent,
    segments,
    valid_frames,
    gain_first,
    up_first,
    down_first,
    gain_attend,
    query_weight,
    key_weight,
    value_weight,
    attend_out,
    pos_weight,
    content_bias,
    position_bias,
    gain_conv,
    point_in,
    depth_kernel,
    gain_inner,
    point_out,
    gain_second,
    up_second,
    down_second,
    gain_final,
):
    segment_row, valid_row = segments[0], valid_frames[0]
    weights = jnp.concatenate([query_weight, key_weight, value_weight], 1)
    width = query_weight.shape[1]
    taps = depth_kernel.shape[0]
    values = layer_input[0].astype(F32)
    rows = values.shape[0]
    slots = segment_row.shape[0]
    masks = conv_masks(segment_row, valid_row, rows, taps)
    code = codes(segment_row, valid_row)
    spans = spans_of(code)
    values, kept_first, sent = ffn_forward(values, gain_first, up_first, down_first)
    table = distance_table(slots, values.shape[1], sent)
    rel = dot(table, pos_weight).astype(B16)
    prefetch = functools.partial(conv_weights, point_in, depth_kernel, gain_inner, point_out)
    values, kept_attend, full = attend_forward(
        values, gain_attend, weights, attend_out, content_bias, position_bias, code, spans, rel, prefetch
    )
    values, kept_conv = conv_forward(values, gain_conv, full, masks)
    values, kept_second, _ = ffn_forward(values, gain_second, up_second, down_second)
    final, final_unit, final_inverse = normalize(values, gain_final)
    layer_output = final.astype(B16)
    grad, sum_final = normalize_back(cotangent[0].astype(F32), final_unit, final_inverse, gain_final)
    grad, sum_second, second_grads, _ = ffn_backward(
        grad, kept_second, gain_second, up_second, down_second
    )
    second_sum = lax.psum(second_grads, "rows")
    grad, cot, sum_conv, conv_grads, ends = conv_backward(grad, kept_conv, gain_conv, full, masks)
    grad, sum_attend, attend_grads, d_bias = attend_backward(
        grad, cot, kept_attend, gain_attend, weights, attend_out, table, ends
    )
    grad, sum_first, first_grads, marks = ffn_backward(
        grad, kept_first, gain_first, up_first, down_first
    )
    middle = jnp.concatenate([attend_grads, conv_grads[0]], 1)
    forms = [(width, plain)] * 4 + [(width, turned), (2 * width, paired), (width, turned)]
    middle = row_sum(middle, forms, 1)
    down = row_sum(first_grads[1], [(first_grads[1].shape[1], plain)], 2)
    up = row_sum(first_grads[0], [(first_grads[0].shape[1], plain)], 3)
    middle.step()
    token = middle.step(marks[1])
    for step in range(down.steps):
        token = down.step(token)
        token = up.step(token)
        if step == 2:
            second_sum = after(second_sum, token)
            second_up, second_down = [item.astype(F32) for item in second_sum]
            token = (token, second_up, second_down)
        if middle.done < middle.steps:
            token = middle.step(token)
    attend_sum = middle.finish()
    first_sum = up.finish() + down.finish()
    gains = sum_cube(jnp.stack([sum_first, sum_attend, sum_conv, sum_second, sum_final]), "tp")
    small = jnp.concatenate([conv_grads[1], d_bias], 0)
    small_shape = small.shape
    pack = jnp.concatenate([gains.reshape(-1), small.reshape(-1)]).reshape(-1, width)
    pack = sum_cube(pack, "rows").reshape(-1)
    gains, small = pack[: gains.size].reshape(gains.shape), pack[gains.size :].reshape(small_shape)
    bias_shape = content_bias.shape
    return (
        layer_output[None],
        grad[None],
        gains[0],
        first_sum[0],
        first_sum[1],
        gains[1],
        attend_sum[0],
        attend_sum[1],
        attend_sum[2],
        attend_sum[4],
        attend_sum[3],
        small[taps + 1].reshape(bias_shape),
        small[taps + 2].reshape(bias_shape),
        gains[2],
        attend_sum[5],
        small[:taps],
        small[taps],
        attend_sum[6],
        gains[3],
        second_up,
        second_down,
        gains[4],
    )


def solution(mesh):
    in_specs = (
        P("rows", "tp", None),
        P("rows", "tp", None),
        P("rows", None),
        P("rows", None),
        P(),
        P(None, "tp"),
        P("tp", None),
        P(),
        P(None, "tp"),
        P(None, "tp"),
        P(None, "tp"),
        P("tp", None),
        P(None, "tp"),
        P("tp", None),
        P("tp", None),
        P(),
        P(None, None, "tp"),
        P(None, "tp"),
        P("tp"),
        P("tp", None),
        P(),
        P(None, "tp"),
        P("tp", None),
        P(),
    )
    out_specs = (
        P("rows", "tp", None),
        P("rows", "tp", None),
        P(),
        P(None, "tp"),
        P("tp", None),
        P(),
        P(None, "tp"),
        P(None, "tp"),
        P(None, "tp"),
        P("tp", None),
        P(None, "tp"),
        P("tp", None),
        P("tp", None),
        P(),
        P(None, None, "tp"),
        P(None, "tp"),
        P("tp"),
        P("tp", None),
        P(),
        P(None, "tp"),
        P("tp", None),
        P(),
    )
    return jax.shard_map(body, mesh=mesh, in_specs=in_specs, out_specs=out_specs, check_vma=False)
```

```python
import functools
import math

import jax
import jax.numpy as jnp
from jax import lax
from jax.experimental import pallas as pl
from jax.experimental.pallas import tpu as pltpu
from jax.sharding import PartitionSpec as P

EPS = 1e-05
NEG = -1e30
F32 = jnp.float32
B16 = jnp.bfloat16
TQ = 128
TK = 384
HD = 128
STEP = 64
SM = pl.BlockSpec(memory_space=pltpu.SMEM)
VM = pl.BlockSpec(memory_space=pltpu.VMEM)

def dotx(a, b, ca, cb):
    return lax.dot_general(a, b, (((ca,), (cb,)), ((), ())), preferred_element_type=F32)

def skew_tile(grid):
    return pltpu.roll(grid, TK + 1, 1, stride=1, stride_axis=0)[:, :TK]

def unskew_flipped(flipped):
    wide = jnp.concatenate([flipped, jnp.zeros((TQ, TQ), F32)], axis=1)
    return pltpu.roll(wide, 0, 1, stride=1, stride_axis=0)

def attend_kernel(heads, spans, q_at, k_at, qc_ref, qp_ref, k_ref, v_ref, rel_ref, code_q_ref, code_k_ref,
                  out_ref, wide_ref, lse_ref):
    slots = qc_ref.shape[0]
    scale = HD ** -0.5
    blocks, tiles = slots // TQ, slots // TK

    def q_step(qb, _):
        at = pl.multiple_of(q_at[qb], TQ)
        true_at = pl.multiple_of(qb * TQ, TQ)
        code_q = code_q_ref[pl.ds(true_at, TQ), :]
        qc = [qc_ref[pl.ds(at, TQ), h * HD:(h + 1) * HD] for h in range(heads)]
        qp = [qp_ref[pl.ds(at, TQ), h * HD:(h + 1) * HD] for h in range(heads)]

        def k_step(kt, carry):
            ko = pl.multiple_of(k_at[kt], TQ)
            to = pl.multiple_of((blocks - 1 + kt * (TK // TQ) - qb) * TQ, TQ)
            mask = code_q == code_k_ref[kt]
            new = []
            for h in range(heads):
                lanes = slice(h * HD, (h + 1) * HD)
                top, total, acc = carry[h]
                grid = dotx(qp[h], rel_ref[pl.ds(to, TK + TQ), lanes], 1, 1)
                raw = dotx(qc[h], k_ref[pl.ds(ko, TK), lanes], 1, 1) + skew_tile(grid)
                scores = jnp.where(mask, raw * scale, NEG)
                top_new = jnp.maximum(top, jnp.max(scores, axis=1, keepdims=True))
                shrink = jnp.exp(top - top_new)
                weights = jnp.exp(scores - top_new)
                total = total * shrink + jnp.sum(weights, axis=1, keepdims=True)
                acc = acc * shrink + dotx(weights.astype(B16), v_ref[pl.ds(ko, TK), lanes], 1, 0)
                new.append((top_new, total, acc))
            return tuple(new)

        first = tuple((jnp.full((TQ, 1), NEG, F32), jnp.zeros((TQ, 1), F32), jnp.zeros((TQ, HD), F32))
                      for _ in range(heads))
        final = lax.fori_loop(spans[0, qb], spans[1, qb], k_step, first)
        for h in range(heads):
            lanes = slice(h * HD, (h + 1) * HD)
            top, total, acc = final[h]
            out = acc / total
            wide_ref[pl.ds(at, TQ), lanes] = out
            out_ref[pl.ds(at, TQ), lanes] = out.astype(B16)
            lse_ref[pl.ds(at, TQ), h:h + 1] = top + jnp.log(total)
        return 0

    lax.fori_loop(0, blocks, q_step, 0)

def attend_back_kernel(heads, spans, q_at, k_at, qc_ref, qp_ref, k_ref, v_ref, rel_ref, code_q_ref, code_k_ref,
                       d_out_ref, wide_ref, lse_ref,
                       all_ref, drel_ref, bias_ref, dk_acc, dv_acc, drel_acc):
    slots = qc_ref.shape[0]
    scale = HD ** -0.5
    blocks, tiles = slots // TQ, slots // TK
    dk_acc[...] = jnp.zeros_like(dk_acc)
    dv_acc[...] = jnp.zeros_like(dv_acc)
    drel_acc[...] = jnp.zeros_like(drel_acc)
    bias_ref[...] = jnp.zeros_like(bias_ref)
    row = lax.broadcasted_iota(jnp.int32, (TQ, TQ), 0)
    column = lax.broadcasted_iota(jnp.int32, (TQ, TQ), 1)
    flip = (row + column == TQ - 1).astype(F32)
    flip_low = flip.astype(B16)

    def q_step(qb, _):
        at = pl.multiple_of(q_at[qb], TQ)
        true_at = pl.multiple_of(qb * TQ, TQ)
        code_q = code_q_ref[pl.ds(true_at, TQ), :]
        cols = [slice(h * HD, (h + 1) * HD) for h in range(heads)]
        qc = [qc_ref[pl.ds(at, TQ), c] for c in cols]
        qp = [qp_ref[pl.ds(at, TQ), c] for c in cols]
        qp_flipped = [dotx(flip_low, item, 1, 0).astype(B16) for item in qp]
        d_out = [d_out_ref[pl.ds(at, TQ), c] for c in cols]
        lse = [lse_ref[pl.ds(at, TQ), h:h + 1] for h in range(heads)]
        delta = [jnp.sum(d_out[h].astype(F32) * wide_ref[pl.ds(at, TQ), cols[h]], axis=1, keepdims=True)
                 for h in range(heads)]

        def k_step(kt, carry):
            ko = pl.multiple_of(k_at[kt], TQ)
            to = pl.multiple_of((blocks - 1 + kt * (TK // TQ) - qb) * TQ, TQ)
            mask = code_q == code_k_ref[kt]
            new = []
            for h in range(heads):
                lanes = cols[h]
                d_content, d_position = carry[h]
                window = rel_ref[pl.ds(to, TK + TQ), lanes]
                key = k_ref[pl.ds(ko, TK), lanes]
                grid = dotx(qp[h], window, 1, 1)
                raw = dotx(qc[h], key, 1, 1) + skew_tile(grid)
                probs = jnp.exp(jnp.where(mask, raw * scale - lse[h], NEG))
                d_probs = dotx(d_out[h], v_ref[pl.ds(ko, TK), lanes], 1, 1)
                d_raw = probs * (d_probs - delta[h]) * scale
                d_low = d_raw.astype(B16)
                d_grid = unskew_flipped(dotx(flip_low, d_low, 1, 0)).astype(B16)
                dv_acc[pl.ds(ko, TK), lanes] += dotx(probs.astype(B16), d_out[h], 0, 0)
                dk_acc[pl.ds(ko, TK), lanes] += dotx(d_low, qc[h], 0, 0)
                drel_acc[pl.ds(to, TK + TQ), lanes] += dotx(d_grid, qp_flipped[h], 0, 0)
                d_content = d_content + dotx(d_low, key, 1, 0)
                d_position = d_position + dotx(d_grid, window, 1, 0)
                new.append((d_content, d_position))
            return tuple(new)

        first = tuple((jnp.zeros((TQ, HD), F32),) * 2 for _ in range(heads))
        final = lax.fori_loop(spans[0, qb], spans[1, qb], k_step, first)
        for h in range(heads):
            d_content, d_position = final[h]
            d_position = lax.dot_general(flip, d_position, (((1,), (0,)), ((), ())),
                                         precision=lax.Precision.HIGHEST, preferred_element_type=F32)
            all_ref[pl.ds(at, TQ), cols[h]] = (d_content + d_position).astype(B16)
            bias_ref[0:1, cols[h]] += jnp.sum(d_content, axis=0, keepdims=True)
            bias_ref[1:2, cols[h]] += jnp.sum(d_position, axis=0, keepdims=True)
        return 0

    lax.fori_loop(0, blocks, q_step, 0)
    width = dk_acc.shape[1]
    all_ref[:, width : 2 * width] = dk_acc[...].astype(B16)
    all_ref[:, 2 * width :] = dv_acc[...].astype(B16)
    drel_ref[...] = drel_acc[...].astype(B16)

def sds(s, d): return jax.ShapeDtypeStruct(s, d)

def attend(spans, q_at, k_at, qc, qp, k, v, rel, code_q, code_k):
    slots, width = qc.shape
    heads = width // HD
    return pl.pallas_call(
        functools.partial(attend_kernel, heads),
        out_shape=(sds((slots, width), B16), sds((slots, width), F32), sds((slots, heads), F32)),
        in_specs=[SM] * 3 + [VM] * 7, out_specs=(VM,) * 3,
        compiler_params=pltpu.CompilerParams(vmem_limit_bytes=40 << 20),
        cost_estimate=pl.CostEstimate(flops=int(4e9), bytes_accessed=int(9e6), transcendentals=int(2e6)),
    )(spans, q_at, k_at, qc, qp, k, v, rel, code_q, code_k)

def attend_back(spans, q_at, k_at, qc, qp, k, v, rel, code_q, code_k, d_out, wide, lse):
    slots, width = qc.shape
    heads = width // HD
    return pl.pallas_call(
        functools.partial(attend_back_kernel, heads),
        out_shape=(sds((slots, 3 * width), B16), sds((2 * slots, width), B16), sds((8, width), F32)),
        in_specs=[SM] * 3 + [VM] * 10, out_specs=(VM,) * 3,
        scratch_shapes=[pltpu.VMEM((slots, width), F32), pltpu.VMEM((slots, width), F32), pltpu.VMEM((2 * slots, width), F32)],
        compiler_params=pltpu.CompilerParams(vmem_limit_bytes=48 << 20),
        cost_estimate=pl.CostEstimate(flops=int(12e9), bytes_accessed=int(12e6), transcendentals=int(2e6)),
    )(spans, q_at, k_at, qc, qp, k, v, rel, code_q, code_k, d_out, wide, lse)

def codes(segments, valid):
    slots = segments.shape[0]
    place = jnp.arange(slots, dtype=jnp.int32)
    code = jnp.where(valid == 1, segments, -1 - place)
    return code

def spans_of(code):
    slots = code.shape[0]
    same = code[:, None] == code[None, :]
    touch = jnp.any(same.reshape(slots // TQ, TQ, slots // TK, TK), axis=(1, 3))
    tiles = slots // TK
    idx = jnp.arange(tiles, dtype=jnp.int32)
    lo = jnp.min(jnp.where(touch, idx, tiles), axis=1)
    hi = jnp.max(jnp.where(touch, idx + 1, 0), axis=1)
    return jnp.stack([lo, hi], 0).astype(jnp.int32)


def normalize(values, gain):
    mean = jnp.mean(values, axis=-1, keepdims=True)
    centered = values - mean
    inverse = lax.rsqrt(jnp.mean(centered * centered, axis=-1, keepdims=True) + EPS)
    unit = centered * inverse
    return (unit * gain.astype(F32), unit, inverse)


def normalize_back(grad, unit, inverse, gain):
    scaled = grad * gain.astype(F32)
    first = jnp.mean(scaled, axis=-1, keepdims=True)
    second = jnp.mean(scaled * unit, axis=-1, keepdims=True)
    return (inverse * (scaled - first - unit * second), jnp.sum(grad * unit, axis=0))


def swish_slope(values):
    gate = jax.nn.sigmoid(values)
    return gate * (1.0 + values * (1.0 - gate))


def distance_table(slots, width, first):
    column = jnp.arange(width)
    even = (column % 2 == 0)[None, :]
    rate = jnp.exp(-(column - column % 2).astype(F32) * (math.log(10000.0) / width))
    coarse = (slots - 1 - STEP * jnp.arange(2 * slots // STEP)).astype(F32)[:, None] * rate[None, :]
    fine = jnp.arange(STEP).astype(F32)[:, None] * rate[None, :]
    sin_c, cos_c = jnp.sin(coarse), jnp.cos(coarse)
    with_cos = jnp.where(even, sin_c, cos_c)
    with_sin = jnp.where(even, -cos_c, sin_c)
    with_cos, with_sin, sin_f, cos_f = after((with_cos, with_sin, jnp.sin(fine), jnp.cos(fine)), first)
    table = with_cos[:, None, :] * cos_f[None] + with_sin[:, None, :] * sin_f[None]
    return table.reshape(2 * slots, width).astype(B16)


def dot(left, right, contract=(1, 0)):
    return lax.dot_general(
        left, right, (((contract[0],), (contract[1],)), ((), ())), preferred_element_type=F32
    )


def swap(values, distance):
    size = lax.axis_size("tp")
    return lax.ppermute(values, "tp", [(i, i ^ distance) for i in range(size)])


def distances():
    size = lax.axis_size("tp")
    return [1 << bit for bit in range(size.bit_length() - 1)]


def gather(own):
    slots = {0: own}
    for distance in reversed(distances()):
        for slot in list(slots):
            slots[slot ^ distance] = swap(slots[slot], distance)
    return [slots[slot] for slot in range(len(slots))]


def scatter(parts, late=()):
    parts = dict(enumerate(parts))
    sent = got = None
    for distance in distances():
        for slot in sorted(parts, reverse=True):
            if slot & distance:
                sent = parts.pop(slot).astype(B16)
                if distance == distances()[-1]:
                    sent = after(sent, late)
                got = swap(sent, distance)
                parts[slot ^ distance] = parts[slot ^ distance].astype(F32) + got.astype(F32)
    return parts[0], (sent, got)


def after(values, *others):
    return lax.optimization_barrier((values, others))[0]


def spread(own, work, late=()):
    size = lax.axis_size("tp")
    far = swap(own, size // 2)
    slots = {0: own}
    for distance in reversed(distances()[:-1]):
        for slot in list(slots):
            slots[slot ^ distance] = swap(slots[slot], distance)
    outs = {slot: work(slot, slots[slot]) for slot in sorted(slots)}
    first = size // 2
    slots[first] = after(far, outs, late)
    arrived = slots[first]
    for distance in reversed(distances()[:-1]):
        for slot in [item for item in slots if item >= first]:
            slots[slot ^ distance] = swap(slots[slot], distance)
    for slot in range(first, size):
        outs[slot] = work(slot, slots[slot])
    ordered = lambda items: [items[slot] for slot in range(size)]
    return ordered(slots), ordered(outs), arrived


def join(items):
    return jnp.concatenate(items, 0)


def pieces(blocks, weight, contract, late=()):
    outs = {}
    for slot in reversed(range(len(blocks))):
        outs[slot] = dot(blocks[slot], weight, contract)
    return [outs[slot] for slot in range(len(blocks))]


def cut(values):
    size = lax.axis_size("tp")
    rows = values.shape[0] // size
    return [values[slot * rows : (slot + 1) * rows] for slot in range(size)]


def ring():
    size, mine = lax.axis_size("rows"), lax.axis_index("rows")
    order = list(range(0, size, 2)) + list(range(size - 1, 0, -2))
    place = jnp.where(mine % 2 == 0, mine // 2, size - (mine + 1) // 2)
    right = [(order[i], order[(i + 1) % size]) for i in range(size)]
    return size, place, right, [(there, here) for here, there in right]


def plain(piece):
    return piece


def turned(piece):
    return piece.T


def first_kernel(at, *refs):
    count = (len(refs) - 2) // 2
    refs[-2][...] = jnp.concatenate([ref[...] for ref in refs[:count]], 1)
    refs[-1][...] = jnp.concatenate([ref[...] for ref in refs[count:-2]], 1)


def pass_kernel(second, at, *refs):
    count = (len(refs) - 4) // 2
    from_left, from_right = (ref[...].astype(F32) for ref in refs[-4:-2])
    if second:
        top = pl.program_id(0) == 0
        from_left = jnp.where(top, from_left, 0.0)
        from_right = jnp.where(top, 0.0, from_right)
    own = jnp.concatenate([ref[...] for ref in refs[:count]], 1).astype(F32)
    refs[-2][...] = (own + from_left).astype(B16)
    own = jnp.concatenate([ref[...] for ref in refs[count:-4]], 1).astype(F32)
    refs[-1][...] = (own + from_right).astype(B16)


def total_kernel(split, at, *refs):
    count = len(refs) - 4
    own = jnp.concatenate([ref[...] for ref in refs[:count]], 1).astype(F32)
    from_left, from_right = (ref[...].astype(F32) for ref in refs[count : count + 2])
    half = refs[-1].shape[0]
    if split:
        refs[-2][...] = (own[:half] + from_left).astype(B16)
        refs[-1][...] = (own[half:] + from_right).astype(B16)
    else:
        total = (own + from_left + from_right).astype(B16)
        refs[-2][...] = total[:half]
        refs[-1][...] = total[half:]


def place_kernel(forms, spots, at, *refs):
    count = len(spots)
    outs, scratch = refs[count : count + len(forms)], list(refs[count + len(forms) :])
    half = refs[0].shape[0]
    held = [out if form is plain else scratch.pop(0) for out, form in zip(outs, forms)]
    widths = [item.shape[1] for item in held]
    size = held[0].shape[0] // (2 * half)
    for ref, (k, bottom) in zip(refs[:count], spots):
        start = pl.multiple_of(((at[0] + k + size) % size) * (2 * half) + bottom * half, half)
        edge = 0
        for item, width in zip(held, widths):
            item[pl.ds(start, half), :] = ref[:, edge : edge + width].astype(F32)
            edge += width
    for item, out, form in zip(held, outs, forms):
        if form is turned:
            out[...] = item[...].T


class RowSum:
    def __init__(self, arrays, parts):
        self.size, self.place, self.right, self.left = ring()
        self.arrays, self.parts = list(arrays), parts
        self.width = sum(item.shape[1] for item in arrays)
        self.rows = arrays[0].shape[0] // self.size
        self.half = self.rows // 2
        self.stages = self.size // 2
        self.steps = 2 * self.stages
        self.done = 0
        self.seen = []

    def call(self, kernel, at, blocks, extra, out_rows, grid, gate, out_blocks):
        arrays, extra = after((self.arrays, extra), gate)
        specs, operands = [], []
        for rows, index in blocks:
            for item in arrays:
                specs.append(pl.BlockSpec((rows, item.shape[1]), index))
                operands.append(item)
        for item, (rows, index) in zip(extra, out_blocks[1]):
            specs.append(pl.BlockSpec((rows, self.width), index))
            operands.append(item)
        rows, index = out_blocks[0]
        moved = sum(2 * rows * self.width for _ in range(4))
        return pl.pallas_call(
            kernel,
            grid_spec=pltpu.PrefetchScalarGridSpec(
                num_scalar_prefetch=1,
                grid=(grid,),
                in_specs=specs,
                out_specs=[pl.BlockSpec((rows, self.width), index)] * 2,
            ),
            out_shape=(sds((out_rows, self.width), B16),) * 2,
            cost_estimate=pl.CostEstimate(flops=moved, bytes_accessed=moved, transcendentals=0),
        )(at, *operands)

    def send(self, to_right, to_left):
        over = lambda items, way: [lax.ppermute(item, "rows", way) for item in items]
        self.from_left, self.from_right = over(to_right, self.right), over(to_left, self.left)
        return (to_right, to_left)

    def step(self, gate=()):
        stage, stages, half, rows = self.done, self.stages, self.half, self.rows
        self.done += 1
        ids = [(self.place + k) % self.size for k in (stages - stage, stage - stages)]
        at = jnp.stack(ids).astype(jnp.int32)
        whole = lambda i, at: (0, 0)
        if stage == 0:
            blocks = [(half, lambda i, at: (2 * at[0], 0)), (half, lambda i, at: (2 * at[1] + 1, 0))]
            out = self.call(first_kernel, at, blocks, [], half, 1, gate, ((half, whole), []))
            return self.send([out[0]], [out[1]])
        if stage < stages:
            blocks = [
                (half, lambda i, at: (2 * at[0] + i, 0)), (half, lambda i, at: (2 * at[1] + i, 0)),
            ]
            here = (half, lambda i, at: (i, 0))
            got = (half, whole) if stage == 1 else here
            kernel = functools.partial(pass_kernel, stage == 1)
            extra = self.from_left + self.from_right
            out = self.call(kernel, at, blocks, extra, rows, 2, gate, (here, [got, got]))
            return self.send([out[0]], [out[1]])
        if stage == stages:
            got = (half if stages == 1 else rows, whole)
            kernel = functools.partial(total_kernel, stages == 1)
            extra = self.from_left + self.from_right
            blocks = [(rows, lambda i, at: (at[0], 0))]
            out = self.call(kernel, at, blocks, extra, half, 1, gate, ((half, whole), [got, got]))
            to_right = to_left = list(out)
            self.see(to_right, 0)
        else:
            to_right, to_left = after((self.from_left, self.from_right), gate)
            self.see(to_right, stages - stage)
            self.see(to_left, stage - stages)
        if stage == 2 * stages - 1:
            to_right, to_left = to_right[:1], to_left[1:]
        return self.send(to_right, to_left)

    def see(self, pair, k):
        self.seen += [(pair[0], (k, 0)), (pair[1], (k, 1))]

    def finish(self, gate=()):
        self.seen += [(self.from_left[0], (-self.stages, 0)), (self.from_right[0], (self.stages, 1))]
        items = after([item for item, _ in self.seen], gate)
        spots = [((k + self.size) % self.size, bottom) for _, (k, bottom) in self.seen]
        forms = [form for _, form in self.parts]
        length = self.arrays[0].shape[0]
        shapes = [(length, width) if form is plain else (width, length) for width, form in self.parts]
        scratch = [pltpu.VMEM((length, width), F32) for width, form in self.parts if form is turned]
        moved = 6 * length * self.width
        return pl.pallas_call(
            functools.partial(place_kernel, forms, spots),
            out_shape=[sds(shape, F32) for shape in shapes],
            in_specs=[SM] + [VM] * len(items),
            out_specs=[VM] * len(shapes),
            scratch_shapes=scratch,
            compiler_params=pltpu.CompilerParams(vmem_limit_bytes=40 << 20),
            cost_estimate=pl.CostEstimate(flops=moved, bytes_accessed=moved, transcendentals=0),
        )(self.place.reshape(1).astype(jnp.int32), *items)


class WholeSum:
    def __init__(self, arrays, parts):
        self.arrays, self.parts, self.steps, self.done = list(arrays), parts, 1, 0

    def step(self, gate=()):
        self.done += 1
        values = after(jnp.concatenate(self.arrays, 1), gate)
        self.total = lax.psum(values, "rows").astype(F32)
        return ()

    def finish(self, gate=()):
        edges = [sum(width for width, _ in self.parts[:k]) for k in range(len(self.parts) + 1)]
        return [
            form(self.total[:, edges[k] : edges[k + 1]]) for k, (_, form) in enumerate(self.parts)
        ]


def row_sum(arrays, parts):
    size = lax.axis_size("rows")
    fits = size % 2 == 0 and arrays[0].shape[0] % (16 * size) == 0
    return (RowSum if fits else WholeSum)(arrays, parts)


class RowSums:
    def __init__(self, arrays, parts):
        if all(item.shape[0] == arrays[0].shape[0] for item in arrays):
            self.items = [row_sum(arrays, parts)]
        else:
            self.items = [row_sum([item], [part]) for item, part in zip(arrays, parts)]

    @property
    def left(self):
        return max(item.steps - item.done for item in self.items)

    def step(self, gate=()):
        for item in self.items:
            if item.done < item.steps:
                gate = item.step(gate)
        return gate

    def finish(self, gate=()):
        while self.left:
            gate = self.step(gate)
        return [out for item in self.items for out in item.finish(gate)]


def sum_cube(values, axis):
    size = lax.axis_size(axis)
    if size & (size - 1):
        return lax.psum(values, axis)
    distance = 1
    while distance < size:
        values = values + lax.ppermute(values, axis, [(i, i ^ distance) for i in range(size)])
        distance *= 2
    return values


def halo(own, reach):
    size = lax.axis_size("tp")
    left = lax.ppermute(own[-reach:], "tp", [(i, i + 1) for i in range(size - 1)])
    right = lax.ppermute(own[:reach], "tp", [(i + 1, i) for i in range(size - 1)])
    return jnp.concatenate([left, own, right], 0)


def to_true(values):
    size, mine = lax.axis_size("tp"), lax.axis_index("tp")
    rows = values.shape[0] // size
    return jnp.concatenate(
        [lax.dynamic_slice_in_dim(values, (mine ^ k) * rows, rows, 0) for k in range(size)], 0
    )


def ffn_forward(values, gain, weight_up, weight_down, prefetch=None):
    normed, unit, inverse = normalize(values, gain)

    def work(slot, block):
        pre = dot(block, weight_up)
        return (pre * jax.nn.sigmoid(pre)).astype(B16), pre.astype(B16)

    wide, outs, arrived = spread(normed.astype(B16), work)
    act, pre = [item[0] for item in outs], [item[1] for item in outs]
    fetched = ()
    parts = pieces(act, weight_down, (1, 0))
    if prefetch is not None:
        fetched = prefetch(arrived)
    total, (sent, _) = scatter(parts, fetched)
    return (values + 0.5 * total, (unit, inverse, wide, pre, act), sent, fetched)


def ffn_backward(grad, kept, gain, weight_up, weight_down, use=None, late=lambda own: ()):
    unit, inverse, wide, pre, act = kept
    own = (0.5 * grad).astype(B16)

    def work(slot, block):
        d_act = dot(block, weight_down, (1, 1))
        return (d_act * swish_slope(pre[slot].astype(F32))).astype(B16)

    cot, d_pre, _ = spread(own, work, late(own))
    d_norm, (sent, _) = scatter(pieces(d_pre, weight_up, (1, 1)))
    cot, d_pre = after((cot, d_pre), sent)
    grad_down = dot(join(act), join(cot), (0, 0)).astype(B16)
    grad_up = dot(join(wide), join(d_pre), (0, 0)).astype(B16)
    if use is not None:
        d_norm = after(d_norm, use((grad_up, grad_down)))
    d_in, grad_gain = normalize_back(d_norm, unit, inverse, gain)
    return (grad + d_in, grad_gain, (grad_up, grad_down), (own, sent))


def places(slots):
    size, mine = lax.axis_size("tp"), lax.axis_index("tp")
    rows = slots // size
    if rows % TK:
        q_at = jnp.arange(slots // TQ, dtype=jnp.int32) * TQ
        k_at = jnp.arange(slots // TK, dtype=jnp.int32) * TK
        return q_at, k_at, True
    q_true = jnp.arange(slots // TQ, dtype=jnp.int32) * TQ
    k_true = jnp.arange(slots // TK, dtype=jnp.int32) * TK
    q_at = ((q_true // rows) ^ mine) * rows + q_true % rows
    k_at = ((k_true // rows) ^ mine) * rows + k_true % rows
    return q_at.astype(jnp.int32), k_at.astype(jnp.int32), False


def attend_forward(
    values, gain, weights, attend_out, content_bias, position_bias, code, spans, rel, prefetch
):
    slots = code.shape[0]
    width = attend_out.shape[0]
    q_at, k_at, reorder = places(slots)
    where = (spans, q_at, k_at)
    normed, unit, inverse = normalize(values, gain)
    work = lambda slot, block: dot(block, weights)
    wide, mixed, first = spread(normed.astype(B16), work, (rel, spans))
    fetched, arrived = prefetch(first)
    flat = lambda bias: bias.astype(F32).reshape(1, width)
    q_content = join([(item[:, :width] + flat(content_bias)).astype(B16) for item in mixed])
    q_position = join([(item[:, :width] + flat(position_bias)).astype(B16) for item in mixed])
    key = join([item[:, width : 2 * width].astype(B16) for item in mixed])
    value = join([item[:, 2 * width :].astype(B16) for item in mixed])
    if reorder:
        q_content, q_position, key, value = map(to_true, (q_content, q_position, key, value))
    operands = (
        where
        + (q_content, q_position, key, value, rel)
        + (code.reshape(slots, 1), code.reshape(slots // TK, 1, TK))
    )
    heads_out, heads_wide, sums = attend(*operands)
    sent = after(to_true(heads_out) if reorder else heads_out, arrived)
    total, _ = scatter(pieces(cut(sent), attend_out, (1, 0)))
    kept = (unit, inverse, wide, operands, heads_wide, sums, sent)
    return (values + total, kept, fetched)


def attend_backward(grad, cot, kept, gain, weights, attend_out, table, filler, ring_step, use):
    unit, inverse, wide, operands, heads_wide, sums, sent = kept
    slots, width = sent.shape
    _, _, reorder = places(slots)
    work = lambda slot, block: dot(block, attend_out, (1, 1)).astype(B16)
    cot, d_heads, _ = spread(cot, work)
    d_heads = join(d_heads)
    if reorder:
        d_heads = to_true(d_heads)
    d_heads = after(d_heads, ring_step(filler[0]))
    d_all, d_rel, d_bias = attend_back(*operands, d_heads, heads_wide, sums)
    if reorder:
        d_all = to_true(d_all)
    d_all = after(d_all, filler[1])
    d_norm, (last, _) = scatter(pieces(cut(d_all), weights, (1, 1)))
    cot, d_all, d_rel = after((cot, d_all, d_rel), ring_step(last))
    grads = (
        dot(join(wide), d_all, (0, 0)),
        dot(table, d_rel, (0, 0)),
        dot(join(cot), sent, (0, 0)),
    )
    d_norm = after(d_norm, use([item.astype(B16) for item in grads]))
    d_in, grad_gain = normalize_back(d_norm, unit, inverse, gain)
    return (grad + d_in, grad_gain, d_bias[:2])


def conv_weights(own, first):
    slots = [gather(after(item, first)) for item in own]
    far = lax.axis_size("tp") // 2
    return slots, [item[far] for item in slots]


def conv_masks(segments, valid, rows, taps):
    edge = 8
    reach = taps // 2
    base = lax.axis_index("tp") * rows + edge - reach
    wide_segments = jnp.pad(segments, edge, constant_values=-1)
    wide_valid = jnp.pad(valid, edge)
    own = lax.dynamic_slice_in_dim(wide_segments, base, rows + 2 * reach)
    masks = []
    for tap in range(taps):
        other = lax.dynamic_slice_in_dim(wide_segments, base + tap - reach, rows + 2 * reach)
        good = lax.dynamic_slice_in_dim(wide_valid, base + tap - reach, rows + 2 * reach)
        masks.append(((other == own) & (good == 1)).astype(F32)[:, None])
    return masks


def conv_forward(values, gain, full, masks):
    in_a, in_b, kernel, gain_inner, out = full
    rows = values.shape[0]
    taps = kernel.shape[0]
    reach = taps // 2
    normed, unit, inverse = normalize(values, gain)
    low = normed.astype(B16)
    wide = halo(low, 2 * reach)
    mixed_a = dot(wide, in_a)
    gate = jax.nn.sigmoid(dot(wide, in_b))
    glu = mixed_a * gate
    depth = 0.0
    for tap in range(taps):
        depth = depth + kernel[tap] * masks[tap] * glu[tap : tap + rows + 2 * reach]
    depth_norm, inner_unit, inner_inverse = normalize(depth, gain_inner)
    inner = (depth_norm * jax.nn.sigmoid(depth_norm)).astype(B16)
    own = slice(2 * reach, 2 * reach + rows)
    kept = (unit, inverse, low, mixed_a[own], gate[own], glu, inner_unit, inner_inverse, depth_norm, inner)
    return (values + dot(inner[reach : reach + rows], out), kept)


def conv_backward(grad, kept, gain, full, masks, ring_step):
    unit, inverse, low, mixed_a, gate, glu, inner_unit, inner_inverse, depth_norm, inner = kept
    in_a, in_b, kernel, gain_inner, out = full
    rows = grad.shape[0]
    taps = kernel.shape[0]
    reach = taps // 2
    mine = slice(reach, reach + rows)
    cot = grad.astype(B16)
    d_act = dot(halo(cot, reach), out, (1, 1))
    d_depth_norm = after(d_act * swish_slope(depth_norm), ring_step(cot))
    grad_gain_inner = jnp.sum((d_depth_norm * inner_unit)[mine], axis=0)
    d_depth, _ = normalize_back(d_depth_norm, inner_unit, inner_inverse, gain_inner)
    d_depth = after(d_depth, ring_step(d_depth_norm))
    d_glu = 0.0
    kernel_rows = []
    for tap in range(taps):
        weighted = d_depth * masks[tap]
        back = 2 * reach - tap
        d_glu = d_glu + kernel[tap] * weighted[back : back + rows]
        kernel_rows.append(jnp.sum(weighted[mine] * glu[reach + tap : reach + tap + rows], axis=0))
    d_a = (d_glu * gate).astype(B16)
    d_b = (d_glu * mixed_a * gate * (1.0 - gate)).astype(B16)
    d_norm = dot(d_a, in_a, (1, 1)) + dot(d_b, in_b, (1, 1))
    d_in, grad_gain = normalize_back(d_norm, unit, inverse, gain)
    grad = grad + d_in
    next_cot = grad.astype(B16)
    low, cot, d_a, d_b, inner = after((low, cot, d_a, d_b, inner), ring_step(next_cot))
    size = lax.axis_size("tp")
    width = in_a.shape[1] // size
    parts, small_parts = [], []
    grads = [
        dot(left, right, (0, 0)).astype(B16)
        for left, right in ((low, d_a), (low, d_b), (cot, inner[mine]))
    ]
    grads = after(grads, ring_step(grads))
    small = jnp.stack(kernel_rows + [grad_gain_inner], 0)
    for slot in range(size):
        cols = slice(slot * width, (slot + 1) * width)
        parts.append(jnp.concatenate([item[:, cols] for item in grads], 1))
        small_parts.append(small[:, cols])
    total, ends = scatter(parts)
    return (grad, next_cot, grad_gain, (total.astype(B16), scatter(small_parts)[0]), ends)


def body(
    layer_input,
    cotangent,
    segments,
    valid_frames,
    gain_first,
    up_first,
    down_first,
    gain_attend,
    query_weight,
    key_weight,
    value_weight,
    attend_out,
    pos_weight,
    content_bias,
    position_bias,
    gain_conv,
    point_in,
    depth_kernel,
    gain_inner,
    point_out,
    gain_second,
    up_second,
    down_second,
    gain_final,
):
    segment_row, valid_row = segments[0], valid_frames[0]
    weights = jnp.concatenate([query_weight, key_weight, value_weight], 1)
    width = query_weight.shape[1]
    taps = depth_kernel.shape[0]
    small = gather(jnp.concatenate([depth_kernel, gain_inner[None]], 0))
    small = jnp.concatenate(small, 1).astype(F32)
    values = layer_input[0].astype(F32)
    rows = values.shape[0]
    slots = segment_row.shape[0]
    masks = conv_masks(segment_row, valid_row, rows, taps)
    code = codes(segment_row, valid_row)
    spans = spans_of(code)
    fetched = []

    def prefetch(first):
        slots, arrived = conv_weights([point_in[:, 0]], first)
        fetched.extend(slots)
        return arrived

    values, kept_first, sent, _ = ffn_forward(values, gain_first, up_first, down_first, prefetch)
    table = distance_table(slots, values.shape[1], sent)
    rel = dot(table, pos_weight).astype(B16)
    prefetch = functools.partial(conv_weights, (point_in[:, 1], point_out))
    values, kept_attend, others = attend_forward(
        values, gain_attend, weights, attend_out, content_bias, position_bias, code, spans, rel, prefetch
    )
    full = (
        jnp.concatenate(fetched[0], 1), jnp.concatenate(others[0], 1),
        small[:taps], small[taps], jnp.concatenate(others[1], 0),
    )
    values, kept_conv = conv_forward(values, gain_conv, full, masks)
    values, kept_second, _, _ = ffn_forward(values, gain_second, up_second, down_second)
    final, final_unit, final_inverse = normalize(values, gain_final)
    layer_output = final.astype(B16)
    grad, sum_final = normalize_back(cotangent[0].astype(F32), final_unit, final_inverse, gain_final)
    rings = {}
    lanes = lambda items: [(item.shape[1], plain) for item in items]

    def start_second(grads):
        rings["second"] = RowSums(grads, lanes(grads))
        return rings["second"].step()

    grad, sum_second, _, _ = ffn_backward(
        grad, kept_second, gain_second, up_second, down_second, start_second
    )
    second = rings["second"]
    step_second = lambda gate: second.step(gate)
    grad, cot, sum_conv, conv_grads, ends = conv_backward(
        grad, kept_conv, gain_conv, full, masks, step_second
    )

    def start_middle(grads):
        forms = [(width, plain)] * 4 + [(width, turned), (2 * width, plain), (width, turned)]
        rings["middle"] = row_sum(grads + [conv_grads[0]], forms)
        return second.step(rings["middle"].step())

    grad, sum_attend, d_bias = attend_backward(
        grad, cot, kept_attend, gain_attend, weights, attend_out, table, ends, step_second, start_middle
    )
    middle = rings["middle"]
    grad, sum_first, first_grads, marks = ffn_backward(
        grad, kept_first, gain_first, up_first, down_first, None, middle.step
    )
    first = RowSums(first_grads, lanes(first_grads))
    token = middle.step(marks[1])
    token = first.step(token)
    while middle.done < middle.steps:
        token = middle.step(token)
        if first.left > 1:
            token = first.step(token)
    second_up, second_down = second.finish(token)
    attend_sum = middle.finish(token)
    token = (attend_sum, second_up, second_down)
    first_sum = first.finish(token)
    gains = sum_cube(jnp.stack([sum_first, sum_attend, sum_conv, sum_second, sum_final]), "tp")
    small = jnp.concatenate([conv_grads[1], d_bias], 0)
    small_shape = small.shape
    pack = jnp.concatenate([gains.reshape(-1), small.reshape(-1)]).reshape(-1, width)
    pack = sum_cube(pack, "rows").reshape(-1)
    gains, small = pack[: gains.size].reshape(gains.shape), pack[gains.size :].reshape(small_shape)
    bias_shape = content_bias.shape
    return (
        layer_output[None],
        grad[None],
        gains[0],
        first_sum[0],
        first_sum[1],
        gains[1],
        attend_sum[0],
        attend_sum[1],
        attend_sum[2],
        attend_sum[4],
        attend_sum[3],
        small[taps + 1].reshape(bias_shape),
        small[taps + 2].reshape(bias_shape),
        gains[2],
        attend_sum[5].reshape(attend_sum[5].shape[0], 2, width),
        small[:taps],
        small[taps],
        attend_sum[6],
        gains[3],
        second_up,
        second_down,
        gains[4],
    )


def solution(mesh):
    in_specs = (
        P("rows", "tp", None),
        P("rows", "tp", None),
        P("rows", None),
        P("rows", None),
        P(),
        P(None, "tp"),
        P("tp", None),
        P(),
        P(None, "tp"),
        P(None, "tp"),
        P(None, "tp"),
        P("tp", None),
        P(None, "tp"),
        P("tp", None),
        P("tp", None),
        P(),
        P(None, None, "tp"),
        P(None, "tp"),
        P("tp"),
        P("tp", None),
        P(),
        P(None, "tp"),
        P("tp", None),
        P(),
    )
    out_specs = (
        P("rows", "tp", None),
        P("rows", "tp", None),
        P(),
        P(None, "tp"),
        P("tp", None),
        P(),
        P(None, "tp"),
        P(None, "tp"),
        P(None, "tp"),
        P("tp", None),
        P(None, "tp"),
        P("tp", None),
        P("tp", None),
        P(),
        P(None, None, "tp"),
        P(None, "tp"),
        P("tp"),
        P("tp", None),
        P(),
        P(None, "tp"),
        P("tp", None),
        P(),
    )
    return jax.shard_map(body, mesh=mesh, in_specs=in_specs, out_specs=out_specs, check_vma=False)
```

```python
import functools
import math

import jax
import jax.numpy as jnp
from jax import lax
from jax.experimental import pallas as pl
from jax.experimental.pallas import tpu as pltpu
from jax.sharding import PartitionSpec as P

EPS = 1e-05
NEG = -1e30
F32 = jnp.float32
B16 = jnp.bfloat16
TQ = 128
TK = 384
HD = 128
STEP = 64
SM = pl.BlockSpec(memory_space=pltpu.SMEM)
VM = pl.BlockSpec(memory_space=pltpu.VMEM)

def dotx(a, b, ca, cb):
    return lax.dot_general(a, b, (((ca,), (cb,)), ((), ())), preferred_element_type=F32)

def skew_tile(grid):
    return pltpu.roll(grid, TK + 1, 1, stride=1, stride_axis=0)[:, :TK]

def unskew_flipped(flipped):
    wide = jnp.concatenate([flipped, jnp.zeros((TQ, TQ), F32)], axis=1)
    return pltpu.roll(wide, 0, 1, stride=1, stride_axis=0)

def attend_kernel(heads, spans, q_at, k_at, qc_ref, qp_ref, k_ref, v_ref, rel_ref, code_q_ref, code_k_ref,
                  out_ref, wide_ref, lse_ref):
    slots = qc_ref.shape[0]
    scale = HD ** -0.5
    blocks, tiles = slots // TQ, slots // TK

    def q_step(qb, _):
        at = pl.multiple_of(q_at[qb], TQ)
        true_at = pl.multiple_of(qb * TQ, TQ)
        code_q = code_q_ref[pl.ds(true_at, TQ), :]
        qc = [qc_ref[pl.ds(at, TQ), h * HD:(h + 1) * HD] for h in range(heads)]
        qp = [qp_ref[pl.ds(at, TQ), h * HD:(h + 1) * HD] for h in range(heads)]

        def k_step(kt, carry):
            ko = pl.multiple_of(k_at[kt], TQ)
            to = pl.multiple_of((blocks - 1 + kt * (TK // TQ) - qb) * TQ, TQ)
            mask = code_q == code_k_ref[kt]
            new = []
            for h in range(heads):
                lanes = slice(h * HD, (h + 1) * HD)
                top, total, acc = carry[h]
                grid = dotx(qp[h], rel_ref[pl.ds(to, TK + TQ), lanes], 1, 1)
                raw = dotx(qc[h], k_ref[pl.ds(ko, TK), lanes], 1, 1) + skew_tile(grid)
                scores = jnp.where(mask, raw * scale, NEG)
                top_new = jnp.maximum(top, jnp.max(scores, axis=1, keepdims=True))
                shrink = jnp.exp(top - top_new)
                weights = jnp.exp(scores - top_new)
                total = total * shrink + jnp.sum(weights, axis=1, keepdims=True)
                acc = acc * shrink + dotx(weights.astype(B16), v_ref[pl.ds(ko, TK), lanes], 1, 0)
                new.append((top_new, total, acc))
            return tuple(new)

        first = tuple((jnp.full((TQ, 1), NEG, F32), jnp.zeros((TQ, 1), F32), jnp.zeros((TQ, HD), F32))
                      for _ in range(heads))
        final = lax.fori_loop(spans[0, qb], spans[1, qb], k_step, first)
        for h in range(heads):
            lanes = slice(h * HD, (h + 1) * HD)
            top, total, acc = final[h]
            out = acc / total
            wide_ref[pl.ds(at, TQ), lanes] = out
            out_ref[pl.ds(at, TQ), lanes] = out.astype(B16)
            lse_ref[pl.ds(at, TQ), h:h + 1] = top + jnp.log(total)
        return 0

    lax.fori_loop(0, blocks, q_step, 0)

def attend_back_kernel(heads, spans, q_at, k_at, qc_ref, qp_ref, k_ref, v_ref, rel_ref, code_q_ref, code_k_ref,
                       d_out_ref, wide_ref, lse_ref,
                       all_ref, drel_ref, bias_ref, dk_acc, dv_acc, drel_acc):
    slots = qc_ref.shape[0]
    scale = HD ** -0.5
    blocks, tiles = slots // TQ, slots // TK
    dk_acc[...] = jnp.zeros_like(dk_acc)
    dv_acc[...] = jnp.zeros_like(dv_acc)
    drel_acc[...] = jnp.zeros_like(drel_acc)
    bias_ref[...] = jnp.zeros_like(bias_ref)
    row = lax.broadcasted_iota(jnp.int32, (TQ, TQ), 0)
    column = lax.broadcasted_iota(jnp.int32, (TQ, TQ), 1)
    flip = (row + column == TQ - 1).astype(F32)
    flip_low = flip.astype(B16)

    def q_step(qb, _):
        at = pl.multiple_of(q_at[qb], TQ)
        true_at = pl.multiple_of(qb * TQ, TQ)
        code_q = code_q_ref[pl.ds(true_at, TQ), :]
        cols = [slice(h * HD, (h + 1) * HD) for h in range(heads)]
        qc = [qc_ref[pl.ds(at, TQ), c] for c in cols]
        qp = [qp_ref[pl.ds(at, TQ), c] for c in cols]
        qp_flipped = [dotx(flip_low, item, 1, 0).astype(B16) for item in qp]
        d_out = [d_out_ref[pl.ds(at, TQ), c] for c in cols]
        lse = [lse_ref[pl.ds(at, TQ), h:h + 1] for h in range(heads)]
        delta = [jnp.sum(d_out[h].astype(F32) * wide_ref[pl.ds(at, TQ), cols[h]], axis=1, keepdims=True)
                 for h in range(heads)]

        def k_step(kt, carry):
            ko = pl.multiple_of(k_at[kt], TQ)
            to = pl.multiple_of((blocks - 1 + kt * (TK // TQ) - qb) * TQ, TQ)
            mask = code_q == code_k_ref[kt]
            new = []
            for h in range(heads):
                lanes = cols[h]
                d_content, d_position = carry[h]
                window = rel_ref[pl.ds(to, TK + TQ), lanes]
                key = k_ref[pl.ds(ko, TK), lanes]
                grid = dotx(qp[h], window, 1, 1)
                raw = dotx(qc[h], key, 1, 1) + skew_tile(grid)
                probs = jnp.exp(jnp.where(mask, raw * scale - lse[h], NEG))
                d_probs = dotx(d_out[h], v_ref[pl.ds(ko, TK), lanes], 1, 1)
                d_raw = probs * (d_probs - delta[h]) * scale
                d_low = d_raw.astype(B16)
                d_grid = unskew_flipped(dotx(flip_low, d_low, 1, 0)).astype(B16)
                dv_acc[pl.ds(ko, TK), lanes] += dotx(probs.astype(B16), d_out[h], 0, 0)
                dk_acc[pl.ds(ko, TK), lanes] += dotx(d_low, qc[h], 0, 0)
                drel_acc[pl.ds(to, TK + TQ), lanes] += dotx(d_grid, qp_flipped[h], 0, 0)
                d_content = d_content + dotx(d_low, key, 1, 0)
                d_position = d_position + dotx(d_grid, window, 1, 0)
                new.append((d_content, d_position))
            return tuple(new)

        first = tuple((jnp.zeros((TQ, HD), F32),) * 2 for _ in range(heads))
        final = lax.fori_loop(spans[0, qb], spans[1, qb], k_step, first)
        for h in range(heads):
            d_content, d_position = final[h]
            d_position = lax.dot_general(flip, d_position, (((1,), (0,)), ((), ())),
                                         precision=lax.Precision.HIGHEST, preferred_element_type=F32)
            all_ref[pl.ds(at, TQ), cols[h]] = (d_content + d_position).astype(B16)
            bias_ref[0:1, cols[h]] += jnp.sum(d_content, axis=0, keepdims=True)
            bias_ref[1:2, cols[h]] += jnp.sum(d_position, axis=0, keepdims=True)
        return 0

    lax.fori_loop(0, blocks, q_step, 0)
    width = dk_acc.shape[1]
    all_ref[:, width : 2 * width] = dk_acc[...].astype(B16)
    all_ref[:, 2 * width :] = dv_acc[...].astype(B16)
    drel_ref[...] = drel_acc[...].astype(B16)

def sds(s, d): return jax.ShapeDtypeStruct(s, d)

def attend(spans, q_at, k_at, qc, qp, k, v, rel, code_q, code_k):
    slots, width = qc.shape
    heads = width // HD
    return pl.pallas_call(
        functools.partial(attend_kernel, heads),
        out_shape=(sds((slots, width), B16), sds((slots, width), F32), sds((slots, heads), F32)),
        in_specs=[SM] * 3 + [VM] * 7, out_specs=(VM,) * 3,
        compiler_params=pltpu.CompilerParams(vmem_limit_bytes=40 << 20),
        cost_estimate=pl.CostEstimate(flops=int(4e9), bytes_accessed=int(9e6), transcendentals=int(2e6)),
    )(spans, q_at, k_at, qc, qp, k, v, rel, code_q, code_k)

def attend_back(spans, q_at, k_at, qc, qp, k, v, rel, code_q, code_k, d_out, wide, lse):
    slots, width = qc.shape
    heads = width // HD
    return pl.pallas_call(
        functools.partial(attend_back_kernel, heads),
        out_shape=(sds((slots, 3 * width), B16), sds((2 * slots, width), B16), sds((8, width), F32)),
        in_specs=[SM] * 3 + [VM] * 10, out_specs=(VM,) * 3,
        scratch_shapes=[pltpu.VMEM((slots, width), F32), pltpu.VMEM((slots, width), F32), pltpu.VMEM((2 * slots, width), F32)],
        compiler_params=pltpu.CompilerParams(vmem_limit_bytes=48 << 20),
        cost_estimate=pl.CostEstimate(flops=int(1e6), bytes_accessed=int(1e6), transcendentals=0),
    )(spans, q_at, k_at, qc, qp, k, v, rel, code_q, code_k, d_out, wide, lse)

def codes(segments, valid):
    slots = segments.shape[0]
    place = jnp.arange(slots, dtype=jnp.int32)
    code = jnp.where(valid == 1, segments, -1 - place)
    return code

def spans_of(code):
    slots = code.shape[0]
    same = code[:, None] == code[None, :]
    touch = jnp.any(same.reshape(slots // TQ, TQ, slots // TK, TK), axis=(1, 3))
    tiles = slots // TK
    idx = jnp.arange(tiles, dtype=jnp.int32)
    lo = jnp.min(jnp.where(touch, idx, tiles), axis=1)
    hi = jnp.max(jnp.where(touch, idx + 1, 0), axis=1)
    return jnp.stack([lo, hi], 0).astype(jnp.int32)


def normalize(values, gain):
    mean = jnp.mean(values, axis=-1, keepdims=True)
    centered = values - mean
    inverse = lax.rsqrt(jnp.mean(centered * centered, axis=-1, keepdims=True) + EPS)
    unit = centered * inverse
    return (unit * gain.astype(F32), unit, inverse)


def normalize_back(grad, unit, inverse, gain):
    scaled = grad * gain.astype(F32)
    first = jnp.mean(scaled, axis=-1, keepdims=True)
    second = jnp.mean(scaled * unit, axis=-1, keepdims=True)
    return (inverse * (scaled - first - unit * second), jnp.sum(grad * unit, axis=0))


def swish_slope(values):
    gate = jax.nn.sigmoid(values)
    return gate * (1.0 + values * (1.0 - gate))


def distance_table(slots, width, first):
    column = jnp.arange(width)
    even = (column % 2 == 0)[None, :]
    rate = jnp.exp(-(column - column % 2).astype(F32) * (math.log(10000.0) / width))
    coarse = (slots - 1 - STEP * jnp.arange(2 * slots // STEP)).astype(F32)[:, None] * rate[None, :]
    fine = jnp.arange(STEP).astype(F32)[:, None] * rate[None, :]
    sin_c, cos_c = jnp.sin(coarse), jnp.cos(coarse)
    with_cos = jnp.where(even, sin_c, cos_c)
    with_sin = jnp.where(even, -cos_c, sin_c)
    with_cos, with_sin, sin_f, cos_f = after((with_cos, with_sin, jnp.sin(fine), jnp.cos(fine)), first)
    table = with_cos[:, None, :] * cos_f[None] + with_sin[:, None, :] * sin_f[None]
    return table.reshape(2 * slots, width).astype(B16)


def dot(left, right, contract=(1, 0)):
    return lax.dot_general(
        left, right, (((contract[0],), (contract[1],)), ((), ())), preferred_element_type=F32
    )


def swap(values, distance):
    size = lax.axis_size("tp")
    return lax.ppermute(values, "tp", [(i, i ^ distance) for i in range(size)])


def distances():
    size = lax.axis_size("tp")
    return [1 << bit for bit in range(size.bit_length() - 1)]


def gather(own):
    slots = {0: own}
    for distance in reversed(distances()):
        for slot in list(slots):
            slots[slot ^ distance] = swap(slots[slot], distance)
    return [slots[slot] for slot in range(len(slots))]


def scatter(parts, late=()):
    parts = dict(enumerate(parts))
    sent = got = None
    for distance in distances():
        for slot in sorted(parts, reverse=True):
            if slot & distance:
                sent = parts.pop(slot).astype(B16)
                if distance == distances()[-1]:
                    sent = after(sent, late)
                got = swap(sent, distance)
                parts[slot ^ distance] = parts[slot ^ distance].astype(F32) + got.astype(F32)
    return parts[0], (sent, got)


def after(values, *others):
    return lax.optimization_barrier((values, others))[0]


def spread(own, work, late=()):
    size = lax.axis_size("tp")
    first = size // 2
    far = swap(own, first)
    slots = {0: own}
    for distance in reversed(distances()[:-1]):
        for slot in list(slots):
            slots[slot ^ distance] = swap(slots[slot], distance)
    near = join([slots[slot] for slot in range(first)])
    outs = [work(0, near)]
    arrived = after(far, outs, late)
    slots = {0: arrived}
    for distance in reversed(distances()[:-1]):
        for slot in list(slots):
            slots[slot ^ distance] = swap(slots[slot], distance)
    far = join([slots[slot] for slot in range(first)])
    outs.append(work(1, far))
    return [near, far], outs, arrived


def join(items):
    return jnp.concatenate(items, 0)


def pieces(blocks, weight, contract, late=()):
    count = lax.axis_size("tp") // 2
    rows = blocks[0].shape[0] // count
    outs = {}
    for slot in reversed(range(2 * count)):
        place = slot % count
        block = blocks[slot // count][place * rows : (place + 1) * rows]
        outs[slot] = dot(block, weight, contract)
    return [outs[slot] for slot in range(2 * count)]


def cut(values):
    half = values.shape[0] // 2
    return [values[:half], values[half:]]


def ring():
    size, mine = lax.axis_size("rows"), lax.axis_index("rows")
    order = list(range(0, size, 2)) + list(range(size - 1, 0, -2))
    place = jnp.where(mine % 2 == 0, mine // 2, size - (mine + 1) // 2)
    right = [(order[i], order[(i + 1) % size]) for i in range(size)]
    return size, place, right, [(there, here) for here, there in right]


def plain(piece):
    return piece


def turned(piece):
    return piece.T


def first_kernel(at, *refs):
    count = (len(refs) - 2) // 2
    refs[-2][...] = jnp.concatenate([ref[...] for ref in refs[:count]], 1)
    refs[-1][...] = jnp.concatenate([ref[...] for ref in refs[count:-2]], 1)


def pass_kernel(second, at, *refs):
    count = (len(refs) - 4) // 2
    from_left, from_right = (ref[...].astype(F32) for ref in refs[-4:-2])
    if second:
        top = pl.program_id(0) == 0
        from_left = jnp.where(top, from_left, 0.0)
        from_right = jnp.where(top, 0.0, from_right)
    own = jnp.concatenate([ref[...] for ref in refs[:count]], 1).astype(F32)
    refs[-2][...] = (own + from_left).astype(B16)
    own = jnp.concatenate([ref[...] for ref in refs[count:-4]], 1).astype(F32)
    refs[-1][...] = (own + from_right).astype(B16)


def total_kernel(split, at, *refs):
    own = jnp.concatenate([ref[...] for ref in refs[:-3]], 1).astype(F32)
    from_left, from_right = (ref[...].astype(F32) for ref in refs[-3:-1])
    if split:
        refs[-1][...] = (own + jnp.concatenate([from_left, from_right], 0)).astype(B16)
    else:
        refs[-1][...] = (own + from_left + from_right).astype(B16)


def place_kernel(forms, spots, at, *refs):
    count = len(spots)
    outs, scratch = refs[count : count + len(forms)], list(refs[count + len(forms) :])
    half = refs[count - 1].shape[0]
    held = [out if form is plain else scratch.pop(0) for out, form in zip(outs, forms)]
    widths = [item.shape[1] for item in held]
    size = held[0].shape[0] // (2 * half)
    for ref, (k, bottom) in zip(refs[:count], spots):
        start = pl.multiple_of(((at[0] + k + size) % size) * (2 * half) + bottom * half, half)
        edge = 0
        for item, width in zip(held, widths):
            item[pl.ds(start, ref.shape[0]), :] = ref[:, edge : edge + width].astype(F32)
            edge += width
    for item, out, form in zip(held, outs, forms):
        if form is turned:
            out[...] = item[...].T


class RowSum:
    def __init__(self, arrays, parts):
        self.size, self.place, self.right, self.left = ring()
        self.arrays, self.parts = list(arrays), parts
        self.width = sum(item.shape[1] for item in arrays)
        self.rows = arrays[0].shape[0] // self.size
        self.half = self.rows // 2
        self.stages = self.size // 2
        self.steps = 2 * self.stages
        self.done = 0
        self.seen = []

    def call(self, kernel, at, blocks, extra, out_rows, grid, gate, out_blocks, count=2):
        arrays, extra = after((self.arrays, extra), gate)
        specs, operands = [], []
        for rows, index in blocks:
            for item in arrays:
                specs.append(pl.BlockSpec((rows, item.shape[1]), index))
                operands.append(item)
        for item, (rows, index) in zip(extra, out_blocks[1]):
            specs.append(pl.BlockSpec((rows, self.width), index))
            operands.append(item)
        rows, index = out_blocks[0]
        moved = sum(2 * rows * self.width for _ in range(4))
        return pl.pallas_call(
            kernel,
            grid_spec=pltpu.PrefetchScalarGridSpec(
                num_scalar_prefetch=1,
                grid=(grid,),
                in_specs=specs,
                out_specs=[pl.BlockSpec((rows, self.width), index)] * count,
            ),
            out_shape=(sds((out_rows, self.width), B16),) * count,
            cost_estimate=pl.CostEstimate(flops=moved, bytes_accessed=moved, transcendentals=0),
        )(at, *operands)

    def send(self, to_right, to_left):
        over = lambda items, way: [lax.ppermute(item, "rows", way) for item in items]
        self.from_left, self.from_right = over(to_right, self.right), over(to_left, self.left)
        return (to_right, to_left)

    def step(self, gate=()):
        stage, stages, half, rows = self.done, self.stages, self.half, self.rows
        self.done += 1
        ids = [(self.place + k) % self.size for k in (stages - stage, stage - stages)]
        at = jnp.stack(ids).astype(jnp.int32)
        whole = lambda i, at: (0, 0)
        if stage == 0:
            blocks = [(half, lambda i, at: (2 * at[0], 0)), (half, lambda i, at: (2 * at[1] + 1, 0))]
            out = self.call(first_kernel, at, blocks, [], half, 1, gate, ((half, whole), []))
            return self.send([out[0]], [out[1]])
        if stage < stages:
            blocks = [
                (half, lambda i, at: (2 * at[0] + i, 0)), (half, lambda i, at: (2 * at[1] + i, 0)),
            ]
            here = (half, lambda i, at: (i, 0))
            got = (half, whole) if stage == 1 else here
            kernel = functools.partial(pass_kernel, stage == 1)
            extra = self.from_left + self.from_right
            out = self.call(kernel, at, blocks, extra, rows, 2, gate, (here, [got, got]))
            return self.send([out[0]], [out[1]])
        if stage == stages:
            got = (half if stages == 1 else rows, whole)
            kernel = functools.partial(total_kernel, stages == 1)
            extra = self.from_left + self.from_right
            blocks = [(rows, lambda i, at: (at[0], 0))]
            blocks = [(half, lambda i, at: (2 * at[0] + i, 0))] if stages > 1 else blocks
            here = (half, lambda i, at: (i, 0)) if stages > 1 else (rows, whole)
            got = here if stages > 1 else got
            grid = 2 if stages > 1 else 1
            out = self.call(kernel, at, blocks, extra, rows, grid, gate, (here, [got, got]), 1)
            to_right = to_left = list(out)
            self.see(to_right, 0)
        else:
            to_right, to_left = after((self.from_left, self.from_right), gate)
            self.see(to_right, stages - stage)
            self.see(to_left, stage - stages)
        if stage == 2 * stages - 1:
            to_right, to_left = [to_right[0][:half]], [to_left[0][half:]]
        return self.send(to_right, to_left)

    def see(self, items, k):
        self.seen.append((items[0], (k, 0)))

    def finish(self, gate=()):
        self.seen += [(self.from_left[0], (-self.stages, 0)), (self.from_right[0], (self.stages, 1))]
        items = after([item for item, _ in self.seen], gate)
        spots = [((k + self.size) % self.size, bottom) for _, (k, bottom) in self.seen]
        forms = [form for _, form in self.parts]
        length = self.arrays[0].shape[0]
        shapes = [(length, width) if form is plain else (width, length) for width, form in self.parts]
        scratch = [pltpu.VMEM((length, width), F32) for width, form in self.parts if form is turned]
        moved = 6 * length * self.width
        return pl.pallas_call(
            functools.partial(place_kernel, forms, spots),
            out_shape=[sds(shape, F32) for shape in shapes],
            in_specs=[SM] + [VM] * len(items),
            out_specs=[VM] * len(shapes),
            scratch_shapes=scratch,
            compiler_params=pltpu.CompilerParams(vmem_limit_bytes=40 << 20),
            cost_estimate=pl.CostEstimate(flops=moved, bytes_accessed=moved, transcendentals=0),
        )(self.place.reshape(1).astype(jnp.int32), *items)


class WholeSum:
    def __init__(self, arrays, parts):
        self.arrays, self.parts, self.steps, self.done = list(arrays), parts, 1, 0

    def step(self, gate=()):
        self.done += 1
        values = after(jnp.concatenate(self.arrays, 1), gate)
        self.total = lax.psum(values, "rows").astype(F32)
        return ()

    def finish(self, gate=()):
        edges = [sum(width for width, _ in self.parts[:k]) for k in range(len(self.parts) + 1)]
        return [
            form(self.total[:, edges[k] : edges[k + 1]]) for k, (_, form) in enumerate(self.parts)
        ]


def row_sum(arrays, parts):
    size = lax.axis_size("rows")
    fits = size % 2 == 0 and arrays[0].shape[0] % (16 * size) == 0
    return (RowSum if fits else WholeSum)(arrays, parts)


def start_sum(arrays):
    if arrays[0].shape[0] == arrays[1].shape[0]:
        arrays = [jnp.concatenate(arrays, 1)]
    return [lax.psum_scatter(item, "rows", scatter_dimension=0, tiled=True) for item in arrays]


def end_sum(shares, width):
    whole = [lax.all_gather(item, "rows", axis=0, tiled=True) for item in shares]
    if len(whole) == 1:
        whole = [whole[0][:, :width], whole[0][:, width:]]
    return whole


class RowSums:
    def __init__(self, arrays, parts):
        if all(item.shape[0] == arrays[0].shape[0] for item in arrays):
            self.items = [row_sum(arrays, parts)]
        else:
            self.items = [row_sum([item], [part]) for item, part in zip(arrays, parts)]

    @property
    def done(self):
        return self.items[0].done

    @property
    def left(self):
        return max(item.steps - item.done for item in self.items)

    def step(self, gate=()):
        for item in self.items:
            if item.done < item.steps:
                gate = item.step(gate)
        return gate

    def finish(self, gate=()):
        while self.left:
            gate = self.step(gate)
        return [out for item in self.items for out in item.finish(gate)]


def sum_cube(values, axis):
    size = lax.axis_size(axis)
    if size & (size - 1):
        return lax.psum(values, axis)
    distance = 1
    while distance < size:
        values = values + lax.ppermute(values, axis, [(i, i ^ distance) for i in range(size)])
        distance *= 2
    return values


def halo(own, reach):
    size = lax.axis_size("tp")
    left = lax.ppermute(own[-reach:], "tp", [(i, i + 1) for i in range(size - 1)])
    right = lax.ppermute(own[:reach], "tp", [(i + 1, i) for i in range(size - 1)])
    return jnp.concatenate([left, own, right], 0)


def to_true(values):
    size, mine = lax.axis_size("tp"), lax.axis_index("tp")
    rows = values.shape[0] // size
    return jnp.concatenate(
        [lax.dynamic_slice_in_dim(values, (mine ^ k) * rows, rows, 0) for k in range(size)], 0
    )


def ffn_forward(values, gain, weight_up, weight_down, prefetch=None):
    normed, unit, inverse = normalize(values, gain)

    def work(slot, block):
        pre = dot(block, weight_up)
        return (pre * jax.nn.sigmoid(pre)).astype(B16), pre.astype(B16)

    wide, outs, arrived = spread(normed.astype(B16), work)
    act, pre = [item[0] for item in outs], [item[1] for item in outs]
    fetched = ()
    parts = pieces(act, weight_down, (1, 0))
    if prefetch is not None:
        fetched = prefetch(arrived)
    total, (sent, _) = scatter(parts, fetched)
    return (values + 0.5 * total, (unit, inverse, wide, pre, act), sent, fetched)


def ffn_backward(grad, kept, gain, weight_up, weight_down, use=None, late=lambda own: ()):
    unit, inverse, wide, pre, act = kept
    own = (0.5 * grad).astype(B16)

    def work(slot, block):
        d_act = dot(block, weight_down, (1, 1))
        return (d_act * swish_slope(pre[slot].astype(F32))).astype(B16)

    cot, d_pre, _ = spread(own, work, late(own))
    d_norm, (sent, _) = scatter(pieces(d_pre, weight_up, (1, 1)))
    cot, d_pre = after((cot, d_pre), sent)
    grad_down = dot(join(act), join(cot), (0, 0)).astype(B16)
    grad_up = dot(join(wide), join(d_pre), (0, 0)).astype(B16)
    if use is not None:
        d_norm = after(d_norm, use((grad_up, grad_down)))
    d_in, grad_gain = normalize_back(d_norm, unit, inverse, gain)
    return (grad + d_in, grad_gain, (grad_up, grad_down), (own, sent))


def places(slots):
    size, mine = lax.axis_size("tp"), lax.axis_index("tp")
    rows = slots // size
    if rows % TK:
        q_at = jnp.arange(slots // TQ, dtype=jnp.int32) * TQ
        k_at = jnp.arange(slots // TK, dtype=jnp.int32) * TK
        return q_at, k_at, True
    q_true = jnp.arange(slots // TQ, dtype=jnp.int32) * TQ
    k_true = jnp.arange(slots // TK, dtype=jnp.int32) * TK
    q_at = ((q_true // rows) ^ mine) * rows + q_true % rows
    k_at = ((k_true // rows) ^ mine) * rows + k_true % rows
    return q_at.astype(jnp.int32), k_at.astype(jnp.int32), False


def attend_forward(
    values, gain, weights, attend_out, content_bias, position_bias, code, spans, rel, prefetch
):
    slots = code.shape[0]
    width = attend_out.shape[0]
    q_at, k_at, reorder = places(slots)
    where = (spans, q_at, k_at)
    normed, unit, inverse = normalize(values, gain)
    work = lambda slot, block: dot(block, weights)
    wide, mixed, first = spread(normed.astype(B16), work, (rel, spans))
    fetched, arrived = prefetch(first)
    flat = lambda bias: bias.astype(F32).reshape(1, width)
    q_content = join([(item[:, :width] + flat(content_bias)).astype(B16) for item in mixed])
    q_position = join([(item[:, :width] + flat(position_bias)).astype(B16) for item in mixed])
    key = join([item[:, width : 2 * width].astype(B16) for item in mixed])
    value = join([item[:, 2 * width :].astype(B16) for item in mixed])
    if reorder:
        q_content, q_position, key, value = map(to_true, (q_content, q_position, key, value))
    operands = (
        where
        + (q_content, q_position, key, value, rel)
        + (code.reshape(slots, 1), code.reshape(slots // TK, 1, TK))
    )
    heads_out, heads_wide, sums = attend(*operands)
    sent = after(to_true(heads_out) if reorder else heads_out, arrived)
    total, _ = scatter(pieces(cut(sent), attend_out, (1, 0)))
    kept = (unit, inverse, wide, operands, heads_wide, sums, sent)
    return (values + total, kept, fetched)


def attend_backward(grad, cot, kept, gain, weights, attend_out, table, filler, use):
    unit, inverse, wide, operands, heads_wide, sums, sent = kept
    slots, width = sent.shape
    _, _, reorder = places(slots)
    work = lambda slot, block: dot(block, attend_out, (1, 1)).astype(B16)
    cot, d_heads, _ = spread(cot, work)
    d_heads = join(d_heads)
    if reorder:
        d_heads = to_true(d_heads)
    d_heads = after(d_heads, filler[0])
    d_all, d_rel, d_bias = attend_back(*operands, d_heads, heads_wide, sums)
    if reorder:
        d_all = to_true(d_all)
    d_all = after(d_all, filler[1])
    d_norm, (last, _) = scatter(pieces(cut(d_all), weights, (1, 1)))
    cot, d_all, d_rel = after((cot, d_all, d_rel), last)
    grads = (
        dot(join(wide), d_all, (0, 0)),
        dot(table, d_rel, (0, 0)),
        dot(join(cot), sent, (0, 0)),
    )
    d_norm = after(d_norm, use([item.astype(B16) for item in grads]))
    d_in, grad_gain = normalize_back(d_norm, unit, inverse, gain)
    return (grad + d_in, grad_gain, d_bias[:2])


def conv_weights(pick, own, first):
    slots = [gather(item) for item in pick(after(own, first))]
    far = lax.axis_size("tp") // 2
    return slots, [item[far] for item in slots]


def conv_masks(segments, valid, rows, taps):
    edge = 8
    reach = taps // 2
    base = lax.axis_index("tp") * rows + edge - reach
    wide_segments = jnp.pad(segments, edge, constant_values=-1)
    wide_valid = jnp.pad(valid, edge)
    own = lax.dynamic_slice_in_dim(wide_segments, base, rows + 2 * reach)
    masks = []
    for tap in range(taps):
        other = lax.dynamic_slice_in_dim(wide_segments, base + tap - reach, rows + 2 * reach)
        good = lax.dynamic_slice_in_dim(wide_valid, base + tap - reach, rows + 2 * reach)
        masks.append(((other == own) & (good == 1)).astype(F32)[:, None])
    return masks


def conv_forward(values, gain, full, masks):
    in_a, in_b, kernel, gain_inner, out = full
    rows = values.shape[0]
    taps = kernel.shape[0]
    reach = taps // 2
    normed, unit, inverse = normalize(values, gain)
    low = normed.astype(B16)
    wide = halo(low, 2 * reach)
    mixed_a = dot(wide, in_a)
    gate = jax.nn.sigmoid(dot(wide, in_b))
    glu = mixed_a * gate
    depth = 0.0
    for tap in range(taps):
        depth = depth + kernel[tap] * masks[tap] * glu[tap : tap + rows + 2 * reach]
    depth_norm, inner_unit, inner_inverse = normalize(depth, gain_inner)
    inner = (depth_norm * jax.nn.sigmoid(depth_norm)).astype(B16)
    own = slice(2 * reach, 2 * reach + rows)
    kept = (unit, inverse, low, mixed_a[own], gate[own], glu, inner_unit, inner_inverse, depth_norm, inner)
    return (values + dot(inner[reach : reach + rows], out), kept)


def conv_backward(grad, kept, gain, full, masks):
    unit, inverse, low, mixed_a, gate, glu, inner_unit, inner_inverse, depth_norm, inner = kept
    in_a, in_b, kernel, gain_inner, out = full
    rows = grad.shape[0]
    taps = kernel.shape[0]
    reach = taps // 2
    mine = slice(reach, reach + rows)
    cot = grad.astype(B16)
    d_act = dot(halo(cot, reach), out, (1, 1))
    d_depth_norm = d_act * swish_slope(depth_norm)
    grad_gain_inner = jnp.sum((d_depth_norm * inner_unit)[mine], axis=0)
    d_depth, _ = normalize_back(d_depth_norm, inner_unit, inner_inverse, gain_inner)
    d_glu = 0.0
    kernel_rows = []
    for tap in range(taps):
        weighted = d_depth * masks[tap]
        back = 2 * reach - tap
        d_glu = d_glu + kernel[tap] * weighted[back : back + rows]
        kernel_rows.append(jnp.sum(weighted[mine] * glu[reach + tap : reach + tap + rows], axis=0))
    d_a = (d_glu * gate).astype(B16)
    d_b = (d_glu * mixed_a * gate * (1.0 - gate)).astype(B16)
    d_norm = dot(d_a, in_a, (1, 1)) + dot(d_b, in_b, (1, 1))
    d_in, grad_gain = normalize_back(d_norm, unit, inverse, gain)
    grad = grad + d_in
    next_cot = grad.astype(B16)
    low, cot, d_a, d_b, inner = after((low, cot, d_a, d_b, inner), next_cot)
    size = lax.axis_size("tp")
    width = in_a.shape[1] // size
    parts, small_parts = [], []
    grads = [
        dot(left, right, (0, 0)).astype(B16)
        for left, right in ((low, d_a), (low, d_b), (cot, inner[mine]))
    ]
    small = jnp.stack(kernel_rows + [grad_gain_inner], 0)
    for slot in range(size):
        cols = slice(slot * width, (slot + 1) * width)
        parts.append(jnp.concatenate([item[:, cols] for item in grads], 1))
        small_parts.append(small[:, cols])
    total, ends = scatter(parts)
    return (grad, next_cot, grad_gain, (total.astype(B16), scatter(small_parts)[0]), ends)


def body(
    layer_input,
    cotangent,
    segments,
    valid_frames,
    gain_first,
    up_first,
    down_first,
    gain_attend,
    query_weight,
    key_weight,
    value_weight,
    attend_out,
    pos_weight,
    content_bias,
    position_bias,
    gain_conv,
    point_in,
    depth_kernel,
    gain_inner,
    point_out,
    gain_second,
    up_second,
    down_second,
    gain_final,
):
    width = query_weight.shape[1]
    taps = depth_kernel.shape[0]
    values = layer_input[0].astype(F32)
    rows = values.shape[0]
    slots = segments.shape[1]
    fetched = []

    def prefetch(first):
        slots, arrived = conv_weights(lambda own: [own[:, 0]], point_in, first)
        fetched.extend(slots)
        return arrived

    values, kept_first, sent, _ = ffn_forward(values, gain_first, up_first, down_first, prefetch)
    segment_row, valid_row = after((segments[0], valid_frames[0]), sent)
    code = codes(segment_row, valid_row)
    spans = spans_of(code)
    weights = jnp.concatenate(after((query_weight, key_weight, value_weight), sent), 1)
    table = distance_table(slots, values.shape[1], sent)
    rel = dot(table, pos_weight).astype(B16)
    pick = lambda own: [own[0][:, 1], own[1]]
    prefetch = functools.partial(conv_weights, pick, (point_in, point_out))
    values, kept_attend, others = attend_forward(
        values, gain_attend, weights, attend_out, content_bias, position_bias, code, spans, rel, prefetch
    )
    ready = kept_attend[2][1]
    masks = conv_masks(*after((segment_row, valid_row), ready), rows, taps)
    small = gather(after(jnp.concatenate([depth_kernel, gain_inner[None]], 0), ready))
    small = jnp.concatenate(small, 1).astype(F32)
    full = (
        jnp.concatenate(fetched[0], 1), jnp.concatenate(others[0], 1),
        small[:taps], small[taps], jnp.concatenate(others[1], 0),
    )
    values, kept_conv = conv_forward(values, gain_conv, full, masks)
    values, kept_second, _, _ = ffn_forward(values, gain_second, up_second, down_second)
    final, final_unit, final_inverse = normalize(values, gain_final)
    layer_output = final.astype(B16)
    grad, sum_final = normalize_back(cotangent[0].astype(F32), final_unit, final_inverse, gain_final)
    held = {}
    lanes = lambda items: [(item.shape[1], plain) for item in items]

    def start_second(grads):
        held["second"] = start_sum(grads)
        return grads

    grad, sum_second, _, _ = ffn_backward(
        grad, kept_second, gain_second, up_second, down_second, start_second
    )
    grad, cot, sum_conv, conv_grads, ends = conv_backward(grad, kept_conv, gain_conv, full, masks)
    ends = (ends[0], (ends[1], held["second"]))

    def start_middle(grads):
        forms = [(width, plain)] * 4 + [(width, turned), (2 * width, plain), (width, turned)]
        held["middle"] = row_sum(grads + [conv_grads[0]], forms)
        return held["middle"].step()

    grad, sum_attend, d_bias = attend_backward(
        grad, cot, kept_attend, gain_attend, weights, attend_out, table, ends, start_middle
    )
    second_sum = end_sum(held["second"], up_second.shape[1])
    middle = held["middle"]

    def fill(own):
        own, sums = after((own, (sum_attend, sum_conv, sum_second, sum_final)), own)
        return jnp.stack(sums), conv_grads[1]

    grad, sum_first, first_grads, marks = ffn_backward(
        grad, kept_first, gain_first, up_first, down_first, None, fill
    )
    first = RowSums(first_grads, lanes(first_grads))
    token = middle.step(marks[1])
    token = first.step(token)
    while middle.done < middle.steps:
        token = middle.step(token)
        if first.left > 1:
            token = first.step(token)
        if first.done == 3:
            token = (token, grad)
        if first.done == 5:
            second_sum = after(second_sum, token)
            second_up, second_down = [item.astype(F32) for item in second_sum]
            token = (token, second_up, second_down)
    attend_sum = middle.finish(token)
    first_sum = first.finish(attend_sum)
    gains = sum_cube(jnp.stack([sum_first, sum_attend, sum_conv, sum_second, sum_final]), "tp")
    small = jnp.concatenate([conv_grads[1], d_bias], 0)
    small_shape = small.shape
    pack = jnp.concatenate([gains.reshape(-1), small.reshape(-1)]).reshape(-1, width)
    pack = sum_cube(pack, "rows").reshape(-1)
    gains, small = pack[: gains.size].reshape(gains.shape), pack[gains.size :].reshape(small_shape)
    bias_shape = content_bias.shape
    return (
        layer_output[None],
        grad[None],
        gains[0],
        first_sum[0],
        first_sum[1],
        gains[1],
        attend_sum[0],
        attend_sum[1],
        attend_sum[2],
        attend_sum[4],
        attend_sum[3],
        small[taps + 1].reshape(bias_shape),
        small[taps + 2].reshape(bias_shape),
        gains[2],
        attend_sum[5].reshape(attend_sum[5].shape[0], 2, width),
        small[:taps],
        small[taps],
        attend_sum[6],
        gains[3],
        second_up,
        second_down,
        gains[4],
    )


def solution(mesh):
    in_specs = (
        P("rows", "tp", None),
        P("rows", "tp", None),
        P("rows", None),
        P("rows", None),
        P(),
        P(None, "tp"),
        P("tp", None),
        P(),
        P(None, "tp"),
        P(None, "tp"),
        P(None, "tp"),
        P("tp", None),
        P(None, "tp"),
        P("tp", None),
        P("tp", None),
        P(),
        P(None, None, "tp"),
        P(None, "tp"),
        P("tp"),
        P("tp", None),
        P(),
        P(None, "tp"),
        P("tp", None),
        P(),
    )
    out_specs = (
        P("rows", "tp", None),
        P("rows", "tp", None),
        P(),
        P(None, "tp"),
        P("tp", None),
        P(),
        P(None, "tp"),
        P(None, "tp"),
        P(None, "tp"),
        P("tp", None),
        P(None, "tp"),
        P("tp", None),
        P("tp", None),
        P(),
        P(None, None, "tp"),
        P(None, "tp"),
        P("tp"),
        P("tp", None),
        P(),
        P(None, "tp"),
        P("tp", None),
        P(),
    )
    return jax.shard_map(body, mesh=mesh, in_specs=in_specs, out_specs=out_specs, check_vma=False)
```

```python
import functools
import math

import jax
import jax.numpy as jnp
from jax import lax
from jax.experimental import pallas as pl
from jax.experimental.pallas import tpu as pltpu
from jax.sharding import PartitionSpec as P

EPS = 1e-05
NEG = -1e30
F32 = jnp.float32
B16 = jnp.bfloat16
TQ = 128
TK = 384
HD = 128
STEP = 64
LINK_BYTES = 60_000_000
SM = pl.BlockSpec(memory_space=pltpu.SMEM)
VM = pl.BlockSpec(memory_space=pltpu.VMEM)

def dotx(a, b, ca, cb):
    return lax.dot_general(a, b, (((ca,), (cb,)), ((), ())), preferred_element_type=F32)

def skew_tile(grid):
    return pltpu.roll(grid, TK + 1, 1, stride=1, stride_axis=0)[:, :TK]

def unskew_flipped(flipped):
    wide = jnp.concatenate([flipped, jnp.zeros((TQ, TQ), F32)], axis=1)
    return pltpu.roll(wide, 0, 1, stride=1, stride_axis=0)

def attend_kernel(heads, spans, q_at, k_at, qc_ref, qp_ref, k_ref, v_ref, rel_ref, code_q_ref, code_k_ref,
                  out_ref, wide_ref, lse_ref):
    slots = qc_ref.shape[0]
    scale = HD ** -0.5
    blocks, tiles = slots // TQ, slots // TK

    def q_step(qb, _):
        at = pl.multiple_of(q_at[qb], TQ)
        true_at = pl.multiple_of(qb * TQ, TQ)
        code_q = code_q_ref[pl.ds(true_at, TQ), :]
        qc = [qc_ref[pl.ds(at, TQ), h * HD:(h + 1) * HD] for h in range(heads)]
        qp = [qp_ref[pl.ds(at, TQ), h * HD:(h + 1) * HD] for h in range(heads)]

        def k_step(kt, carry):
            ko = pl.multiple_of(k_at[kt], TQ)
            to = pl.multiple_of((blocks - 1 + kt * (TK // TQ) - qb) * TQ, TQ)
            mask = code_q == code_k_ref[kt]
            new = []
            for h in range(heads):
                lanes = slice(h * HD, (h + 1) * HD)
                top, total, acc = carry[h]
                grid = dotx(qp[h], rel_ref[pl.ds(to, TK + TQ), lanes], 1, 1)
                raw = dotx(qc[h], k_ref[pl.ds(ko, TK), lanes], 1, 1) + skew_tile(grid)
                scores = jnp.where(mask, raw * scale, NEG)
                top_new = jnp.maximum(top, jnp.max(scores, axis=1, keepdims=True))
                shrink = jnp.exp(top - top_new)
                weights = jnp.exp(scores - top_new)
                total = total * shrink + jnp.sum(weights, axis=1, keepdims=True)
                acc = acc * shrink + dotx(weights.astype(B16), v_ref[pl.ds(ko, TK), lanes], 1, 0)
                new.append((top_new, total, acc))
            return tuple(new)

        first = tuple((jnp.full((TQ, 1), NEG, F32), jnp.zeros((TQ, 1), F32), jnp.zeros((TQ, HD), F32))
                      for _ in range(heads))
        final = lax.fori_loop(spans[0, qb], spans[1, qb], k_step, first)
        for h in range(heads):
            lanes = slice(h * HD, (h + 1) * HD)
            top, total, acc = final[h]
            out = acc / total
            wide_ref[pl.ds(at, TQ), lanes] = out
            out_ref[pl.ds(at, TQ), lanes] = out.astype(B16)
            lse_ref[pl.ds(at, TQ), h:h + 1] = top + jnp.log(total)
        return 0

    lax.fori_loop(0, blocks, q_step, 0)

def attend_back_kernel(heads, spans, q_at, k_at, qc_ref, qp_ref, k_ref, v_ref, rel_ref, code_q_ref, code_k_ref,
                       d_out_ref, wide_ref, lse_ref,
                       all_ref, drel_ref, bias_ref, dk_acc, dv_acc, drel_acc):
    slots = qc_ref.shape[0]
    scale = HD ** -0.5
    blocks, tiles = slots // TQ, slots // TK
    dk_acc[...] = jnp.zeros_like(dk_acc)
    dv_acc[...] = jnp.zeros_like(dv_acc)
    drel_acc[...] = jnp.zeros_like(drel_acc)
    bias_ref[...] = jnp.zeros_like(bias_ref)
    row = lax.broadcasted_iota(jnp.int32, (TQ, TQ), 0)
    column = lax.broadcasted_iota(jnp.int32, (TQ, TQ), 1)
    flip = (row + column == TQ - 1).astype(F32)
    flip_low = flip.astype(B16)

    def q_step(qb, _):
        at = pl.multiple_of(q_at[qb], TQ)
        true_at = pl.multiple_of(qb * TQ, TQ)
        code_q = code_q_ref[pl.ds(true_at, TQ), :]
        cols = [slice(h * HD, (h + 1) * HD) for h in range(heads)]
        qc = [qc_ref[pl.ds(at, TQ), c] for c in cols]
        qp = [qp_ref[pl.ds(at, TQ), c] for c in cols]
        qp_flipped = [dotx(flip_low, item, 1, 0).astype(B16) for item in qp]
        d_out = [d_out_ref[pl.ds(at, TQ), c] for c in cols]
        lse = [lse_ref[pl.ds(at, TQ), h:h + 1] for h in range(heads)]
        delta = [jnp.sum(d_out[h].astype(F32) * wide_ref[pl.ds(at, TQ), cols[h]], axis=1, keepdims=True)
                 for h in range(heads)]

        def k_step(kt, carry):
            ko = pl.multiple_of(k_at[kt], TQ)
            to = pl.multiple_of((blocks - 1 + kt * (TK // TQ) - qb) * TQ, TQ)
            mask = code_q == code_k_ref[kt]
            new = []
            for h in range(heads):
                lanes = cols[h]
                d_content, d_position = carry[h]
                window = rel_ref[pl.ds(to, TK + TQ), lanes]
                key = k_ref[pl.ds(ko, TK), lanes]
                grid = dotx(qp[h], window, 1, 1)
                raw = dotx(qc[h], key, 1, 1) + skew_tile(grid)
                probs = jnp.exp(jnp.where(mask, raw * scale - lse[h], NEG))
                d_probs = dotx(d_out[h], v_ref[pl.ds(ko, TK), lanes], 1, 1)
                d_raw = probs * (d_probs - delta[h]) * scale
                d_low = d_raw.astype(B16)
                d_grid = unskew_flipped(dotx(flip_low, d_low, 1, 0)).astype(B16)
                dv_acc[pl.ds(ko, TK), lanes] += dotx(probs.astype(B16), d_out[h], 0, 0)
                dk_acc[pl.ds(ko, TK), lanes] += dotx(d_low, qc[h], 0, 0)
                drel_acc[pl.ds(to, TK + TQ), lanes] += dotx(d_grid, qp_flipped[h], 0, 0)
                d_content = d_content + dotx(d_low, key, 1, 0)
                d_position = d_position + dotx(d_grid, window, 1, 0)
                new.append((d_content, d_position))
            return tuple(new)

        first = tuple((jnp.zeros((TQ, HD), F32),) * 2 for _ in range(heads))
        final = lax.fori_loop(spans[0, qb], spans[1, qb], k_step, first)
        for h in range(heads):
            d_content, d_position = final[h]
            d_position = lax.dot_general(flip, d_position, (((1,), (0,)), ((), ())),
                                         precision=lax.Precision.HIGHEST, preferred_element_type=F32)
            all_ref[pl.ds(at, TQ), cols[h]] = (d_content + d_position).astype(B16)
            bias_ref[0:1, cols[h]] += jnp.sum(d_content, axis=0, keepdims=True)
            bias_ref[1:2, cols[h]] += jnp.sum(d_position, axis=0, keepdims=True)
        return 0

    lax.fori_loop(0, blocks, q_step, 0)
    width = dk_acc.shape[1]
    all_ref[:, width : 2 * width] = dk_acc[...].astype(B16)
    all_ref[:, 2 * width :] = dv_acc[...].astype(B16)
    drel_ref[...] = drel_acc[...].astype(B16)

def sds(s, d): return jax.ShapeDtypeStruct(s, d)

def attend(spans, q_at, k_at, qc, qp, k, v, rel, code_q, code_k):
    slots, width = qc.shape
    heads = width // HD
    return pl.pallas_call(
        functools.partial(attend_kernel, heads),
        out_shape=(sds((slots, width), B16), sds((slots, width), F32), sds((slots, heads), F32)),
        in_specs=[SM] * 3 + [VM] * 7, out_specs=(VM,) * 3,
        compiler_params=pltpu.CompilerParams(vmem_limit_bytes=40 << 20),
        cost_estimate=pl.CostEstimate(flops=int(4e9), bytes_accessed=int(9e6), transcendentals=int(2e6)),
    )(spans, q_at, k_at, qc, qp, k, v, rel, code_q, code_k)

def attend_back(spans, q_at, k_at, qc, qp, k, v, rel, code_q, code_k, d_out, wide, lse):
    slots, width = qc.shape
    heads = width // HD
    return pl.pallas_call(
        functools.partial(attend_back_kernel, heads),
        out_shape=(sds((slots, 3 * width), B16), sds((2 * slots, width), B16), sds((8, width), F32)),
        in_specs=[SM] * 3 + [VM] * 10, out_specs=(VM,) * 3,
        scratch_shapes=[pltpu.VMEM((slots, width), F32), pltpu.VMEM((slots, width), F32), pltpu.VMEM((2 * slots, width), F32)],
        compiler_params=pltpu.CompilerParams(vmem_limit_bytes=48 << 20),
        cost_estimate=pl.CostEstimate(flops=int(1e6), bytes_accessed=int(1e6), transcendentals=0),
    )(spans, q_at, k_at, qc, qp, k, v, rel, code_q, code_k, d_out, wide, lse)

def codes(segments, valid):
    slots = segments.shape[0]
    place = jnp.arange(slots, dtype=jnp.int32)
    code = jnp.where(valid == 1, segments, -1 - place)
    return code

def spans_of(code):
    slots = code.shape[0]
    same = code[:, None] == code[None, :]
    touch = jnp.any(same.reshape(slots // TQ, TQ, slots // TK, TK), axis=(1, 3))
    tiles = slots // TK
    idx = jnp.arange(tiles, dtype=jnp.int32)
    lo = jnp.min(jnp.where(touch, idx, tiles), axis=1)
    hi = jnp.max(jnp.where(touch, idx + 1, 0), axis=1)
    return jnp.stack([lo, hi], 0).astype(jnp.int32)


def normalize(values, gain):
    mean = jnp.mean(values, axis=-1, keepdims=True)
    centered = values - mean
    inverse = lax.rsqrt(jnp.mean(centered * centered, axis=-1, keepdims=True) + EPS)
    unit = centered * inverse
    return (unit * gain.astype(F32), unit, inverse)


def normalize_back(grad, unit, inverse, gain):
    scaled = grad * gain.astype(F32)
    first = jnp.mean(scaled, axis=-1, keepdims=True)
    second = jnp.mean(scaled * unit, axis=-1, keepdims=True)
    return (inverse * (scaled - first - unit * second), (grad, unit))


def gain_sums(pairs, gate):
    return jnp.stack([jnp.sum(grad * unit, axis=0) for grad, unit in after(pairs, gate)])


def swish_slope(values):
    gate = jax.nn.sigmoid(values)
    return gate * (1.0 + values * (1.0 - gate))


def distance_table(slots, width, first):
    column = jnp.arange(width)
    even = (column % 2 == 0)[None, :]
    rate = jnp.exp(-(column - column % 2).astype(F32) * (math.log(10000.0) / width))
    coarse = (slots - 1 - STEP * jnp.arange(2 * slots // STEP)).astype(F32)[:, None] * rate[None, :]
    fine = jnp.arange(STEP).astype(F32)[:, None] * rate[None, :]
    sin_c, cos_c = jnp.sin(coarse), jnp.cos(coarse)
    with_cos = jnp.where(even, sin_c, cos_c)
    with_sin = jnp.where(even, -cos_c, sin_c)
    with_cos, with_sin, sin_f, cos_f = after((with_cos, with_sin, jnp.sin(fine), jnp.cos(fine)), first)
    table = with_cos[:, None, :] * cos_f[None] + with_sin[:, None, :] * sin_f[None]
    return table.reshape(2 * slots, width).astype(B16)


def dot(left, right, contract=(1, 0)):
    return lax.dot_general(
        left, right, (((contract[0],), (contract[1],)), ((), ())), preferred_element_type=F32
    )


def swap(values, distance):
    size = lax.axis_size("tp")
    return lax.ppermute(values, "tp", [(i, i ^ distance) for i in range(size)])


def distances():
    size = lax.axis_size("tp")
    return [1 << bit for bit in range(size.bit_length() - 1)]


def gather(own):
    slots = {0: own}
    for distance in reversed(distances()):
        for slot in list(slots):
            slots[slot ^ distance] = swap(slots[slot], distance)
    return [slots[slot] for slot in range(len(slots))]


def scatter(parts, late=()):
    parts = dict(enumerate(parts))
    sent = got = None
    for distance in distances():
        for slot in sorted(parts, reverse=True):
            if slot & distance:
                sent = parts.pop(slot).astype(B16)
                if distance == distances()[-1]:
                    sent = after(sent, late)
                got = swap(sent, distance)
                parts[slot ^ distance] = parts[slot ^ distance].astype(F32) + got.astype(F32)
    return parts[0], (sent, got)


def after(values, *others):
    return lax.optimization_barrier((values, others))[0]


def join_kernel(*refs):
    rows = refs[0].shape[0]
    for place, ref in enumerate(refs[:-1]):
        refs[-1][place * rows : (place + 1) * rows] = ref[...]


def halves(slots, weight=1):
    half = len(slots) // 2
    rows, width = slots[0].shape
    far = pl.pallas_call(
        join_kernel,
        out_shape=sds((half * rows, width), slots[0].dtype),
        in_specs=[VM] * half,
        out_specs=VM,
        cost_estimate=pl.CostEstimate(flops=0, bytes_accessed=weight * LINK_BYTES, transcendentals=0),
    )(*slots[half:])
    return jnp.concatenate(slots[:half], 0), far


def pieces(near, far, weight, contract):
    count = lax.axis_size("tp") // 2
    rows = near.shape[0] // count
    outs = {}
    for slot in reversed(range(2 * count)):
        source, place = (near, slot) if slot < count else (far, slot - count)
        outs[slot] = dot(source[place * rows : (place + 1) * rows], weight, contract)
    return [outs[slot] for slot in range(2 * count)]


def ring():
    size, mine = lax.axis_size("rows"), lax.axis_index("rows")
    order = list(range(0, size, 2)) + list(range(size - 1, 0, -2))
    place = jnp.where(mine % 2 == 0, mine // 2, size - (mine + 1) // 2)
    right = [(order[i], order[(i + 1) % size]) for i in range(size)]
    return size, place, right, [(there, here) for here, there in right]


def plain(piece):
    return piece


def turned(piece):
    return piece.T


def first_kernel(at, *refs):
    count = (len(refs) - 2) // 2
    refs[-2][...] = jnp.concatenate([ref[...] for ref in refs[:count]], 1)
    refs[-1][...] = jnp.concatenate([ref[...] for ref in refs[count:-2]], 1)


def pass_kernel(second, at, *refs):
    count = (len(refs) - 4) // 2
    from_left, from_right = (ref[...].astype(F32) for ref in refs[-4:-2])
    if second:
        top = pl.program_id(0) == 0
        from_left = jnp.where(top, from_left, 0.0)
        from_right = jnp.where(top, 0.0, from_right)
    own = jnp.concatenate([ref[...] for ref in refs[:count]], 1).astype(F32)
    refs[-2][...] = (own + from_left).astype(B16)
    own = jnp.concatenate([ref[...] for ref in refs[count:-4]], 1).astype(F32)
    refs[-1][...] = (own + from_right).astype(B16)


def total_kernel(split, at, *refs):
    own = jnp.concatenate([ref[...] for ref in refs[:-3]], 1).astype(F32)
    from_left, from_right = (ref[...].astype(F32) for ref in refs[-3:-1])
    if split:
        refs[-1][...] = (own + jnp.concatenate([from_left, from_right], 0)).astype(B16)
    else:
        refs[-1][...] = (own + from_left + from_right).astype(B16)


def place_kernel(spots, spans, at, *refs):
    count = len(spots)
    outs, held = refs[count : count + len(spans)], refs[-1]
    half = refs[count - 1].shape[0]
    size = held.shape[0] // (2 * half)
    for ref, (k, bottom) in zip(refs[:count], spots):
        start = ((at[0] + k) % size) * (2 * half) + bottom * half
        start = pl.multiple_of(start, half)
        held[pl.ds(start, ref.shape[0]), :] = ref[...].astype(F32)
    for out, (low, high, form) in zip(outs, spans):
        here = (pl.program_id(0) >= low) & (pl.program_id(0) < high)

        @pl.when(here)
        def _(out=out, form=form):
            out[...] = form(held[...])


class RowSum:
    def __init__(self, arrays, parts):
        self.size, self.place, self.right, self.left = ring()
        self.arrays, self.parts = list(arrays), parts
        self.width = sum(item.shape[1] for item in arrays)
        self.rows = arrays[0].shape[0] // self.size
        self.half = self.rows // 2
        self.stages = self.size // 2
        self.steps = 2 * self.stages
        self.done = 0
        self.seen = []

    def call(self, kernel, at, blocks, extra, out_rows, grid, gate, out_blocks, count=2):
        arrays, extra = after((self.arrays, extra), gate)
        specs, operands = [], []
        for rows, index in blocks:
            for item in arrays:
                specs.append(pl.BlockSpec((rows, item.shape[1]), index))
                operands.append(item)
        for item, (rows, index) in zip(extra, out_blocks[1]):
            specs.append(pl.BlockSpec((rows, self.width), index))
            operands.append(item)
        rows, index = out_blocks[0]
        moved = sum(2 * rows * self.width for _ in range(4))
        return pl.pallas_call(
            kernel,
            grid_spec=pltpu.PrefetchScalarGridSpec(
                num_scalar_prefetch=1,
                grid=(grid,),
                in_specs=specs,
                out_specs=[pl.BlockSpec((rows, self.width), index)] * count,
            ),
            out_shape=(sds((out_rows, self.width), B16),) * count,
            cost_estimate=pl.CostEstimate(flops=moved, bytes_accessed=moved, transcendentals=0),
        )(at, *operands)

    def send(self, to_right, to_left):
        over = lambda items, way: [lax.ppermute(item, "rows", way) for item in items]
        self.from_left, self.from_right = over(to_right, self.right), over(to_left, self.left)
        return (to_right, to_left)

    def step(self, gate=()):
        stage, stages, half, rows = self.done, self.stages, self.half, self.rows
        self.done += 1
        ids = [(self.place + k) % self.size for k in (stages - stage, stage - stages)]
        at = jnp.stack(ids).astype(jnp.int32)
        whole = lambda i, at: (0, 0)
        if stage == 0:
            blocks = [(half, lambda i, at: (2 * at[0], 0)), (half, lambda i, at: (2 * at[1] + 1, 0))]
            out = self.call(first_kernel, at, blocks, [], half, 1, gate, ((half, whole), []))
            return self.send([out[0]], [out[1]])
        if stage < stages:
            blocks = [
                (half, lambda i, at: (2 * at[0] + i, 0)), (half, lambda i, at: (2 * at[1] + i, 0)),
            ]
            here = (half, lambda i, at: (i, 0))
            got = (half, whole) if stage == 1 else here
            kernel = functools.partial(pass_kernel, stage == 1)
            extra = self.from_left + self.from_right
            out = self.call(kernel, at, blocks, extra, rows, 2, gate, (here, [got, got]))
            return self.send([out[0]], [out[1]])
        if stage == stages:
            got = (half if stages == 1 else rows, whole)
            kernel = functools.partial(total_kernel, stages == 1)
            extra = self.from_left + self.from_right
            blocks = [(rows, lambda i, at: (at[0], 0))]
            blocks = [(half, lambda i, at: (2 * at[0] + i, 0))] if stages > 1 else blocks
            here = (half, lambda i, at: (i, 0)) if stages > 1 else (rows, whole)
            got = here if stages > 1 else got
            grid = 2 if stages > 1 else 1
            out = self.call(kernel, at, blocks, extra, rows, grid, gate, (here, [got, got]), 1)
            to_right = to_left = list(out)
            self.see(to_right, 0)
        else:
            to_right, to_left = after((self.from_left, self.from_right), gate)
            self.see(to_right, stages - stage)
            self.see(to_left, stage - stages)
        if stage == 2 * stages - 1:
            to_right, to_left = [to_right[0][:half]], [to_left[0][half:]]
        return self.send(to_right, to_left)

    def see(self, items, k):
        self.seen.append((items[0], (k, 0)))

    def finish(self, gate=()):
        self.seen += [(self.from_left[0], (-self.stages, 0)), (self.from_right[0], (self.stages, 1))]
        items = after([item for item, _ in self.seen], gate)
        spots = [((k + self.size) % self.size, bottom) for _, (k, bottom) in self.seen]
        length = self.arrays[0].shape[0]
        step = math.gcd(*[width for width, _ in self.parts])
        spans, specs, shapes, low = [], [], [], 0
        for width, form in self.parts:
            count = width // step
            spans.append((low, low + count, form))

            def column(i, at, low=low, count=count):
                return jnp.clip(i - low, 0, count - 1)

            if form is turned:
                shapes.append((width, length))
                specs.append(pl.BlockSpec((step, length), lambda i, at, f=column: (f(i, at), 0)))
            else:
                shapes.append((length, width))
                specs.append(pl.BlockSpec((length, step), lambda i, at, f=column: (0, f(i, at))))
            low += count
        moved = 6 * length * self.width
        return pl.pallas_call(
            functools.partial(place_kernel, spots, spans),
            grid_spec=pltpu.PrefetchScalarGridSpec(
                num_scalar_prefetch=1,
                grid=(low,),
                in_specs=[pl.BlockSpec((item.shape[0], step), lambda i, at: (0, i)) for item in items],
                out_specs=specs,
                scratch_shapes=[pltpu.VMEM((length, step), F32)],
            ),
            out_shape=[sds(shape, F32) for shape in shapes],
            compiler_params=pltpu.CompilerParams(vmem_limit_bytes=40 << 20),
            cost_estimate=pl.CostEstimate(flops=moved, bytes_accessed=moved, transcendentals=0),
        )(self.place.reshape(1).astype(jnp.int32), *items)


class WholeSum:
    def __init__(self, arrays, parts):
        self.arrays, self.parts, self.steps, self.done = list(arrays), parts, 1, 0

    def step(self, gate=()):
        self.done += 1
        values = after(jnp.concatenate(self.arrays, 1), gate)
        self.total = lax.psum(values, "rows").astype(F32)
        return ()

    def finish(self, gate=()):
        edges = [sum(width for width, _ in self.parts[:k]) for k in range(len(self.parts) + 1)]
        return [
            form(self.total[:, edges[k] : edges[k + 1]]) for k, (_, form) in enumerate(self.parts)
        ]


def row_sum(arrays, parts):
    size = lax.axis_size("rows")
    fits = size % 2 == 0 and arrays[0].shape[0] % (16 * size) == 0
    return (RowSum if fits else WholeSum)(arrays, parts)


def start_sum(arrays):
    if arrays[0].shape[1] == arrays[1].shape[1]:
        arrays = [jnp.concatenate(arrays, 0)]
    return [lax.psum_scatter(item, "rows", scatter_dimension=0, tiled=True) for item in arrays]


def end_sum(shares):
    return [lax.all_gather(item, "rows", axis=0, tiled=True) for item in shares]


def split_sum(whole, rows):
    if len(whole) == 1:
        whole = [whole[0][:rows], whole[0][rows:]]
    return [item.astype(F32) for item in whole]


class RowSums:
    def __init__(self, arrays, parts):
        if all(item.shape[0] == arrays[0].shape[0] for item in arrays):
            self.items = [row_sum(arrays, parts)]
        else:
            self.items = [row_sum([item], [part]) for item, part in zip(arrays, parts)]

    @property
    def done(self):
        return self.items[0].done

    @property
    def left(self):
        return max(item.steps - item.done for item in self.items)

    def step(self, gate=()):
        for item in self.items:
            if item.done < item.steps:
                gate = item.step(gate)
        return gate

    def finish(self, gate=()):
        while self.left:
            gate = self.step(gate)
        return [out for item in self.items for out in item.finish(gate)]


def sum_cube(values, axis):
    size = lax.axis_size(axis)
    if size & (size - 1):
        return lax.psum(values, axis)
    distance = 1
    while distance < size:
        values = values + lax.ppermute(values, axis, [(i, i ^ distance) for i in range(size)])
        distance *= 2
    return values


def halo(own, reach):
    size = lax.axis_size("tp")
    left = lax.ppermute(own[-reach:], "tp", [(i, i + 1) for i in range(size - 1)])
    right = lax.ppermute(own[:reach], "tp", [(i + 1, i) for i in range(size - 1)])
    return jnp.concatenate([left, own, right], 0)


def to_true(values):
    size, mine = lax.axis_size("tp"), lax.axis_index("tp")
    rows = values.shape[0] // size
    return jnp.concatenate(
        [lax.dynamic_slice_in_dim(values, (mine ^ k) * rows, rows, 0) for k in range(size)], 0
    )


def ffn_forward(values, gain, weight_up, weight_down):
    normed, unit, inverse = normalize(values, gain)
    near, far = halves(gather(normed.astype(B16)))
    pre, act = [], []
    for half in (near, far):
        pre.append(dot(half, weight_up))
        act.append((pre[-1] * jax.nn.sigmoid(pre[-1])).astype(B16))
    total, (sent, _) = scatter(pieces(act[0], act[1], weight_down, (1, 0)))
    pre = [item.astype(B16) for item in pre]
    return (values + 0.5 * total, (unit, inverse, (near, far), pre, act), sent)


def ffn_backward(grad, kept, gain, weight_up, weight_down, use=None):
    unit, inverse, wide, pre, act = kept
    own = (0.5 * grad).astype(B16)
    cot = halves(gather(own))
    d_pre = []
    for half in (0, 1):
        d_act = dot(cot[half], weight_down, (1, 1))
        d_pre.append((d_act * swish_slope(pre[half].astype(F32))).astype(B16))
    d_norm, (sent, _) = scatter(pieces(d_pre[0], d_pre[1], weight_up, (1, 1)))
    cot, d_pre = after((cot, d_pre), sent)
    grad_down = dot(jnp.concatenate(act, 0), jnp.concatenate(cot, 0), (0, 0))
    grad_up = dot(jnp.concatenate(wide, 0), jnp.concatenate(d_pre, 0), (0, 0))
    grads = (grad_up.astype(B16), grad_down.astype(B16))
    if use is not None:
        d_norm = after(d_norm, use(grads))
    d_in, grad_gain = normalize_back(d_norm, unit, inverse, gain)
    return (grad + d_in, grad_gain, grads, (own, sent))


def places(slots):
    size, mine = lax.axis_size("tp"), lax.axis_index("tp")
    rows = slots // size
    if rows % TK:
        q_at = jnp.arange(slots // TQ, dtype=jnp.int32) * TQ
        k_at = jnp.arange(slots // TK, dtype=jnp.int32) * TK
        return q_at, k_at, True
    q_true = jnp.arange(slots // TQ, dtype=jnp.int32) * TQ
    k_true = jnp.arange(slots // TK, dtype=jnp.int32) * TK
    q_at = ((q_true // rows) ^ mine) * rows + q_true % rows
    k_at = ((k_true // rows) ^ mine) * rows + k_true % rows
    return q_at.astype(jnp.int32), k_at.astype(jnp.int32), False


def attend_forward(
    values, gain, weights, attend_out, content_bias, position_bias, code, spans, rel, prefetch
):
    slots = code.shape[0]
    width = attend_out.shape[0]
    q_at, k_at, reorder = places(slots)
    where = (spans, q_at, k_at)
    normed, unit, inverse = normalize(values, gain)
    near, far = halves(gather(normed.astype(B16)))
    mixed = [dot(near, weights)]
    far = after(far, rel, spans)
    fetched, arrived = prefetch(far)
    mixed.append(dot(far, weights))
    flat = lambda bias: bias.astype(F32).reshape(1, width)
    join = lambda items: jnp.concatenate(items, 0)
    q_content = join([(item[:, :width] + flat(content_bias)).astype(B16) for item in mixed])
    q_position = join([(item[:, :width] + flat(position_bias)).astype(B16) for item in mixed])
    key = join([item[:, width : 2 * width].astype(B16) for item in mixed])
    value = join([item[:, 2 * width :].astype(B16) for item in mixed])
    if reorder:
        q_content, q_position, key, value = map(to_true, (q_content, q_position, key, value))
    operands = (
        where
        + (q_content, q_position, key, value, rel)
        + (code.reshape(slots, 1), code.reshape(slots // TK, 1, TK))
    )
    heads_out, heads_wide, sums = attend(*operands)
    sent = after(to_true(heads_out) if reorder else heads_out, arrived)
    half = slots // 2
    total, _ = scatter(pieces(sent[:half], sent[half:], attend_out, (1, 0)))
    kept = (unit, inverse, (near, far), operands, heads_wide, sums, sent)
    return (values + total, kept, fetched)


def attend_backward(grad, cot, kept, gain, weights, attend_out, table, filler):
    unit, inverse, wide, operands, heads_wide, sums, sent = kept
    slots, width = sent.shape
    _, _, reorder = places(slots)
    d_near = dot(cot[0], attend_out, (1, 1)).astype(B16)
    d_heads = jnp.concatenate([d_near, dot(cot[1], attend_out, (1, 1)).astype(B16)], 0)
    if reorder:
        d_heads = to_true(d_heads)
    d_heads = after(d_heads, filler[0])
    d_all, d_rel, d_bias = attend_back(*operands, d_heads, heads_wide, sums)
    if reorder:
        d_all = to_true(d_all)
    d_all = after(d_all, filler[1])
    half = slots // 2
    d_norm, (last, _) = scatter(pieces(d_all[:half], d_all[half:], weights, (1, 1)))
    d_in, grad_gain = normalize_back(d_norm, unit, inverse, gain)
    cot, d_all, d_rel = after((cot, d_all, d_rel), last)
    grad_out = dot(jnp.concatenate(cot, 0), sent, (0, 0))
    grad_all = dot(jnp.concatenate(wide, 0), d_all, (0, 0))
    grad_pos = dot(table, d_rel, (0, 0))
    grads = [item.astype(B16) for item in (grad_all, grad_pos, grad_out)]
    return (grad + d_in, grad_gain, grads, d_bias[:2])


def conv_weights(point_in, depth_kernel, gain_inner, point_out, first):
    taps = depth_kernel.shape[0]
    own = after((point_in[:, 0], point_in[:, 1], point_out), first)
    small = gather(jnp.concatenate([depth_kernel, gain_inner[None]], 0))
    small = jnp.concatenate(small, 1).astype(F32)
    in_a, in_b, out = map(gather, own)
    arrived = [item[2::2] for item in (in_a, in_b, out)]
    in_a, in_b = jnp.concatenate(in_a, 1), jnp.concatenate(in_b, 1)
    return (in_a, in_b, small[:taps], small[taps], jnp.concatenate(out, 0)), arrived


def conv_masks(segments, valid, rows, taps):
    edge = 8
    reach = taps // 2
    base = lax.axis_index("tp") * rows + edge - reach
    wide_segments = jnp.pad(segments, edge, constant_values=-1)
    wide_valid = jnp.pad(valid, edge)
    own = lax.dynamic_slice_in_dim(wide_segments, base, rows + 2 * reach)
    masks = []
    for tap in range(taps):
        other = lax.dynamic_slice_in_dim(wide_segments, base + tap - reach, rows + 2 * reach)
        good = lax.dynamic_slice_in_dim(wide_valid, base + tap - reach, rows + 2 * reach)
        masks.append(((other == own) & (good == 1)).astype(F32)[:, None])
    return masks


def conv_forward(values, gain, full, masks):
    in_a, in_b, kernel, gain_inner, out = full
    rows = values.shape[0]
    taps = kernel.shape[0]
    reach = taps // 2
    normed, unit, inverse = normalize(values, gain)
    low = normed.astype(B16)
    wide = halo(low, 2 * reach)
    mixed_a = dot(wide, in_a)
    gate = jax.nn.sigmoid(dot(wide, in_b))
    glu = mixed_a * gate
    depth = 0.0
    for tap in range(taps):
        depth = depth + kernel[tap] * masks[tap] * glu[tap : tap + rows + 2 * reach]
    depth_norm, inner_unit, inner_inverse = normalize(depth, gain_inner)
    inner = (depth_norm * jax.nn.sigmoid(depth_norm)).astype(B16)
    own = slice(2 * reach, 2 * reach + rows)
    kept = (unit, inverse, low, mixed_a[own], gate[own], glu, inner_unit, inner_inverse, depth_norm, inner)
    return (values + dot(inner[reach : reach + rows], out), kept)


def conv_backward(grad, kept, gain, full, masks):
    unit, inverse, low, mixed_a, gate, glu, inner_unit, inner_inverse, depth_norm, inner = kept
    in_a, in_b, kernel, gain_inner, out = full
    rows = grad.shape[0]
    taps = kernel.shape[0]
    reach = taps // 2
    mine = slice(reach, reach + rows)
    cot = grad.astype(B16)
    d_act = dot(halo(cot, reach), out, (1, 1))
    d_depth_norm = d_act * swish_slope(depth_norm)
    grad_gain_inner = jnp.sum((d_depth_norm * inner_unit)[mine], axis=0)
    d_depth, _ = normalize_back(d_depth_norm, inner_unit, inner_inverse, gain_inner)
    d_glu = 0.0
    kernel_rows = []
    for tap in range(taps):
        weighted = d_depth * masks[tap]
        back = 2 * reach - tap
        d_glu = d_glu + kernel[tap] * weighted[back : back + rows]
        kernel_rows.append(jnp.sum(weighted[mine] * glu[reach + tap : reach + tap + rows], axis=0))
    d_a = (d_glu * gate).astype(B16)
    d_b = (d_glu * mixed_a * gate * (1.0 - gate)).astype(B16)
    d_norm = dot(d_a, in_a, (1, 1)) + dot(d_b, in_b, (1, 1))
    d_in, grad_gain = normalize_back(d_norm, unit, inverse, gain)
    grad = grad + d_in
    slots = gather(grad.astype(B16))
    next_cot = halves(slots, 3)
    low, cot, d_a, d_b, inner = after((low, cot, d_a, d_b, inner), slots[1])
    size = lax.axis_size("tp")
    width = in_a.shape[1] // size
    parts, small_parts = [], []
    grads = [
        dot(left, right, (0, 0)).astype(B16)
        for left, right in ((low, d_a), (low, d_b), (cot, inner[mine]))
    ]
    small = jnp.stack(kernel_rows + [grad_gain_inner], 0)
    for slot in range(size):
        cols = slice(slot * width, (slot + 1) * width)
        parts.append(jnp.concatenate([item[:, cols] for item in grads], 1))
        small_parts.append(small[:, cols])
    total, ends = scatter(parts, next_cot[1])
    return (grad, next_cot, grad_gain, (total.astype(B16), scatter(small_parts)[0]), ends)


def body(
    layer_input,
    cotangent,
    segments,
    valid_frames,
    gain_first,
    up_first,
    down_first,
    gain_attend,
    query_weight,
    key_weight,
    value_weight,
    attend_out,
    pos_weight,
    content_bias,
    position_bias,
    gain_conv,
    point_in,
    depth_kernel,
    gain_inner,
    point_out,
    gain_second,
    up_second,
    down_second,
    gain_final,
):
    segment_row, valid_row = segments[0], valid_frames[0]
    weights = jnp.concatenate([query_weight, key_weight, value_weight], 1)
    width = query_weight.shape[1]
    taps = depth_kernel.shape[0]
    values = layer_input[0].astype(F32)
    rows = values.shape[0]
    slots = segment_row.shape[0]
    masks = conv_masks(segment_row, valid_row, rows, taps)
    code = codes(segment_row, valid_row)
    spans = spans_of(code)
    values, kept_first, sent = ffn_forward(values, gain_first, up_first, down_first)
    table = distance_table(slots, values.shape[1], sent)
    rel = dot(table, pos_weight).astype(B16)
    prefetch = functools.partial(conv_weights, point_in, depth_kernel, gain_inner, point_out)
    values, kept_attend, full = attend_forward(
        values, gain_attend, weights, attend_out, content_bias, position_bias, code, spans, rel, prefetch
    )
    values, kept_conv = conv_forward(values, gain_conv, full, masks)
    values, kept_second, _ = ffn_forward(values, gain_second, up_second, down_second)
    final, final_unit, final_inverse = normalize(values, gain_final)
    layer_output = final.astype(B16)
    grad, sum_final = normalize_back(cotangent[0].astype(F32), final_unit, final_inverse, gain_final)
    held = {}

    def start_second(grads):
        held["second"] = start_sum(grads)
        return grads

    grad, sum_second, _, _ = ffn_backward(
        grad, kept_second, gain_second, up_second, down_second, start_second
    )
    grad, cot, sum_conv, conv_grads, ends = conv_backward(grad, kept_conv, gain_conv, full, masks)
    ends = (ends[0], (ends[1], held["second"]))
    grad, sum_attend, attend_grads, d_bias = attend_backward(
        grad, cot, kept_attend, gain_attend, weights, attend_out, table, ends
    )
    second_sum = end_sum(held["second"])
    grad, sum_first, first_grads, marks = ffn_backward(
        grad, kept_first, gain_first, up_first, down_first
    )
    pairs = (sum_first, sum_attend, sum_conv, sum_second, sum_final)
    gains = sum_cube(gain_sums(pairs, marks[1]), "tp")
    small = jnp.concatenate([conv_grads[1], d_bias], 0)
    small_shape = small.shape
    pack = jnp.concatenate([gains.reshape(-1), small.reshape(-1)]).reshape(-1, width)
    pack = sum_cube(pack, "rows")
    forms = [(width, plain)] * 4 + [(width, turned), (2 * width, plain), (width, turned)]
    middle = row_sum(attend_grads + [conv_grads[0]], forms)
    first = RowSums(first_grads, [(item.shape[1], plain) for item in first_grads])
    middle.step()
    token = middle.step(marks[1])
    token = first.step(token)
    second_sum = after(second_sum, token)
    token = second_sum
    while middle.done < middle.steps:
        token = middle.step(token)
        if first.left > 1:
            token = first.step(token)
        if first.done == 3:
            token = (token, grad)
        if first.done == 5:
            second_up, second_down = split_sum(after(second_sum, token), up_second.shape[0])
            token = (token, second_up, second_down, pack)
    attend_sum = middle.finish(token)
    first_sum = first.finish(attend_sum)
    pack = pack.reshape(-1)
    gains, small = pack[: gains.size].reshape(gains.shape), pack[gains.size :].reshape(small_shape)
    bias_shape = content_bias.shape
    return (
        layer_output[None],
        grad[None],
        gains[0],
        first_sum[0],
        first_sum[1],
        gains[1],
        attend_sum[0],
        attend_sum[1],
        attend_sum[2],
        attend_sum[4],
        attend_sum[3],
        small[taps + 1].reshape(bias_shape),
        small[taps + 2].reshape(bias_shape),
        gains[2],
        attend_sum[5].reshape(attend_sum[5].shape[0], 2, width),
        small[:taps],
        small[taps],
        attend_sum[6],
        gains[3],
        second_up,
        second_down,
        gains[4],
    )


def solution(mesh):
    in_specs = (
        P("rows", "tp", None),
        P("rows", "tp", None),
        P("rows", None),
        P("rows", None),
        P(),
        P(None, "tp"),
        P("tp", None),
        P(),
        P(None, "tp"),
        P(None, "tp"),
        P(None, "tp"),
        P("tp", None),
        P(None, "tp"),
        P("tp", None),
        P("tp", None),
        P(),
        P(None, None, "tp"),
        P(None, "tp"),
        P("tp"),
        P("tp", None),
        P(),
        P(None, "tp"),
        P("tp", None),
        P(),
    )
    out_specs = (
        P("rows", "tp", None),
        P("rows", "tp", None),
        P(),
        P(None, "tp"),
        P("tp", None),
        P(),
        P(None, "tp"),
        P(None, "tp"),
        P(None, "tp"),
        P("tp", None),
        P(None, "tp"),
        P("tp", None),
        P("tp", None),
        P(),
        P(None, None, "tp"),
        P(None, "tp"),
        P("tp"),
        P("tp", None),
        P(),
        P(None, "tp"),
        P("tp", None),
        P(),
    )
    return jax.shard_map(body, mesh=mesh, in_specs=in_specs, out_specs=out_specs, check_vma=False)
```

```python
import functools
import math

import jax
import jax.numpy as jnp
from jax import lax
from jax.experimental import pallas as pl
from jax.experimental.pallas import tpu as pltpu
from jax.sharding import PartitionSpec as P

EPS = 1e-05
NEG = -1e30
F32 = jnp.float32
B16 = jnp.bfloat16
TQ = 128
TK = 384
HD = 128
STEP = 64
LINK_BYTES = 180_000_000
SM = pl.BlockSpec(memory_space=pltpu.SMEM)
VM = pl.BlockSpec(memory_space=pltpu.VMEM)

def dotx(a, b, ca, cb):
    return lax.dot_general(a, b, (((ca,), (cb,)), ((), ())), preferred_element_type=F32)

def skew_tile(grid):
    return pltpu.roll(grid, TK + 1, 1, stride=1, stride_axis=0)[:, :TK]

def unskew_flipped(flipped):
    wide = jnp.concatenate([flipped, jnp.zeros((TQ, TQ), F32)], axis=1)
    return pltpu.roll(wide, 0, 1, stride=1, stride_axis=0)

def attend_kernel(heads, spans, q_at, k_at, qc_ref, qp_ref, k_ref, v_ref, rel_ref, code_q_ref, code_k_ref,
                  out_ref, wide_ref, lse_ref):
    slots = qc_ref.shape[0]
    scale = HD ** -0.5
    blocks, tiles = slots // TQ, slots // TK

    def q_step(qb, _):
        at = pl.multiple_of(q_at[qb], TQ)
        true_at = pl.multiple_of(qb * TQ, TQ)
        code_q = code_q_ref[pl.ds(true_at, TQ), :]
        qc = [qc_ref[pl.ds(at, TQ), h * HD:(h + 1) * HD] for h in range(heads)]
        qp = [qp_ref[pl.ds(at, TQ), h * HD:(h + 1) * HD] for h in range(heads)]

        def k_step(kt, carry):
            ko = pl.multiple_of(k_at[kt], TQ)
            to = pl.multiple_of((blocks - 1 + kt * (TK // TQ) - qb) * TQ, TQ)
            mask = code_q == code_k_ref[kt]
            new = []
            for h in range(heads):
                lanes = slice(h * HD, (h + 1) * HD)
                top, total, acc = carry[h]
                grid = dotx(qp[h], rel_ref[pl.ds(to, TK + TQ), lanes], 1, 1)
                raw = dotx(qc[h], k_ref[pl.ds(ko, TK), lanes], 1, 1) + skew_tile(grid)
                scores = jnp.where(mask, raw * scale, NEG)
                top_new = jnp.maximum(top, jnp.max(scores, axis=1, keepdims=True))
                shrink = jnp.exp(top - top_new)
                weights = jnp.exp(scores - top_new)
                total = total * shrink + jnp.sum(weights, axis=1, keepdims=True)
                acc = acc * shrink + dotx(weights.astype(B16), v_ref[pl.ds(ko, TK), lanes], 1, 0)
                new.append((top_new, total, acc))
            return tuple(new)

        first = tuple((jnp.full((TQ, 1), NEG, F32), jnp.zeros((TQ, 1), F32), jnp.zeros((TQ, HD), F32))
                      for _ in range(heads))
        final = lax.fori_loop(spans[0, qb], spans[1, qb], k_step, first)
        for h in range(heads):
            lanes = slice(h * HD, (h + 1) * HD)
            top, total, acc = final[h]
            out = acc / total
            wide_ref[pl.ds(at, TQ), lanes] = out
            out_ref[pl.ds(at, TQ), lanes] = out.astype(B16)
            lse_ref[pl.ds(at, TQ), h:h + 1] = top + jnp.log(total)
        return 0

    lax.fori_loop(0, blocks, q_step, 0)

def attend_back_kernel(heads, spans, q_at, k_at, qc_ref, qp_ref, k_ref, v_ref, rel_ref, code_q_ref, code_k_ref,
                       d_out_ref, wide_ref, lse_ref,
                       all_ref, drel_ref, bias_ref, dk_acc, dv_acc, drel_acc):
    slots = qc_ref.shape[0]
    scale = HD ** -0.5
    blocks, tiles = slots // TQ, slots // TK
    dk_acc[...] = jnp.zeros_like(dk_acc)
    dv_acc[...] = jnp.zeros_like(dv_acc)
    drel_acc[...] = jnp.zeros_like(drel_acc)
    bias_ref[...] = jnp.zeros_like(bias_ref)
    row = lax.broadcasted_iota(jnp.int32, (TQ, TQ), 0)
    column = lax.broadcasted_iota(jnp.int32, (TQ, TQ), 1)
    flip = (row + column == TQ - 1).astype(F32)
    flip_low = flip.astype(B16)

    def q_step(qb, _):
        at = pl.multiple_of(q_at[qb], TQ)
        true_at = pl.multiple_of(qb * TQ, TQ)
        code_q = code_q_ref[pl.ds(true_at, TQ), :]
        cols = [slice(h * HD, (h + 1) * HD) for h in range(heads)]
        qc = [qc_ref[pl.ds(at, TQ), c] for c in cols]
        qp = [qp_ref[pl.ds(at, TQ), c] for c in cols]
        qp_flipped = [dotx(flip_low, item, 1, 0).astype(B16) for item in qp]
        d_out = [d_out_ref[pl.ds(at, TQ), c] for c in cols]
        lse = [lse_ref[pl.ds(at, TQ), h:h + 1] for h in range(heads)]
        delta = [jnp.sum(d_out[h].astype(F32) * wide_ref[pl.ds(at, TQ), cols[h]], axis=1, keepdims=True)
                 for h in range(heads)]

        def k_step(kt, carry):
            ko = pl.multiple_of(k_at[kt], TQ)
            to = pl.multiple_of((blocks - 1 + kt * (TK // TQ) - qb) * TQ, TQ)
            mask = code_q == code_k_ref[kt]
            new = []
            for h in range(heads):
                lanes = cols[h]
                d_content, d_position = carry[h]
                window = rel_ref[pl.ds(to, TK + TQ), lanes]
                key = k_ref[pl.ds(ko, TK), lanes]
                grid = dotx(qp[h], window, 1, 1)
                raw = dotx(qc[h], key, 1, 1) + skew_tile(grid)
                probs = jnp.exp(jnp.where(mask, raw * scale - lse[h], NEG))
                d_probs = dotx(d_out[h], v_ref[pl.ds(ko, TK), lanes], 1, 1)
                d_raw = probs * (d_probs - delta[h]) * scale
                d_low = d_raw.astype(B16)
                d_grid = unskew_flipped(dotx(flip_low, d_low, 1, 0)).astype(B16)
                dv_acc[pl.ds(ko, TK), lanes] += dotx(probs.astype(B16), d_out[h], 0, 0)
                dk_acc[pl.ds(ko, TK), lanes] += dotx(d_low, qc[h], 0, 0)
                drel_acc[pl.ds(to, TK + TQ), lanes] += dotx(d_grid, qp_flipped[h], 0, 0)
                d_content = d_content + dotx(d_low, key, 1, 0)
                d_position = d_position + dotx(d_grid, window, 1, 0)
                new.append((d_content, d_position))
            return tuple(new)

        first = tuple((jnp.zeros((TQ, HD), F32),) * 2 for _ in range(heads))
        final = lax.fori_loop(spans[0, qb], spans[1, qb], k_step, first)
        for h in range(heads):
            d_content, d_position = final[h]
            d_position = lax.dot_general(flip, d_position, (((1,), (0,)), ((), ())),
                                         precision=lax.Precision.HIGHEST, preferred_element_type=F32)
            all_ref[pl.ds(at, TQ), cols[h]] = (d_content + d_position).astype(B16)
            bias_ref[0:1, cols[h]] += jnp.sum(d_content, axis=0, keepdims=True)
            bias_ref[1:2, cols[h]] += jnp.sum(d_position, axis=0, keepdims=True)
        return 0

    lax.fori_loop(0, blocks, q_step, 0)
    width = dk_acc.shape[1]
    all_ref[:, width : 2 * width] = dk_acc[...].astype(B16)
    all_ref[:, 2 * width :] = dv_acc[...].astype(B16)
    drel_ref[...] = drel_acc[...].astype(B16)

def sds(s, d): return jax.ShapeDtypeStruct(s, d)

def attend(spans, q_at, k_at, qc, qp, k, v, rel, code_q, code_k):
    slots, width = qc.shape
    heads = width // HD
    return pl.pallas_call(
        functools.partial(attend_kernel, heads),
        out_shape=(sds((slots, width), B16), sds((slots, width), F32), sds((slots, heads), F32)),
        in_specs=[SM] * 3 + [VM] * 7, out_specs=(VM,) * 3,
        compiler_params=pltpu.CompilerParams(vmem_limit_bytes=40 << 20),
        cost_estimate=pl.CostEstimate(flops=int(4e9), bytes_accessed=int(9e6), transcendentals=int(2e6)),
    )(spans, q_at, k_at, qc, qp, k, v, rel, code_q, code_k)

def attend_back(spans, q_at, k_at, qc, qp, k, v, rel, code_q, code_k, d_out, wide, lse):
    slots, width = qc.shape
    heads = width // HD
    return pl.pallas_call(
        functools.partial(attend_back_kernel, heads),
        out_shape=(sds((slots, 3 * width), B16), sds((2 * slots, width), B16), sds((8, width), F32)),
        in_specs=[SM] * 3 + [VM] * 10, out_specs=(VM,) * 3,
        scratch_shapes=[pltpu.VMEM((slots, width), F32), pltpu.VMEM((slots, width), F32), pltpu.VMEM((2 * slots, width), F32)],
        compiler_params=pltpu.CompilerParams(vmem_limit_bytes=48 << 20),
        cost_estimate=pl.CostEstimate(flops=int(1e6), bytes_accessed=int(1e6), transcendentals=0),
    )(spans, q_at, k_at, qc, qp, k, v, rel, code_q, code_k, d_out, wide, lse)

def codes(segments, valid):
    slots = segments.shape[0]
    place = jnp.arange(slots, dtype=jnp.int32)
    code = jnp.where(valid == 1, segments, -1 - place)
    return code

def spans_of(code):
    slots = code.shape[0]
    same = code[:, None] == code[None, :]
    touch = jnp.any(same.reshape(slots // TQ, TQ, slots // TK, TK), axis=(1, 3))
    tiles = slots // TK
    idx = jnp.arange(tiles, dtype=jnp.int32)
    lo = jnp.min(jnp.where(touch, idx, tiles), axis=1)
    hi = jnp.max(jnp.where(touch, idx + 1, 0), axis=1)
    return jnp.stack([lo, hi], 0).astype(jnp.int32)


def normalize(values, gain):
    mean = jnp.mean(values, axis=-1, keepdims=True)
    centered = values - mean
    inverse = lax.rsqrt(jnp.mean(centered * centered, axis=-1, keepdims=True) + EPS)
    unit = centered * inverse
    return (unit * gain.astype(F32), unit, inverse)


def normalize_back(grad, unit, inverse, gain):
    scaled = grad * gain.astype(F32)
    first = jnp.mean(scaled, axis=-1, keepdims=True)
    second = jnp.mean(scaled * unit, axis=-1, keepdims=True)
    return (inverse * (scaled - first - unit * second), (grad, unit))


def gain_sums(pairs, gate):
    return jnp.stack([jnp.sum(grad * unit, axis=0) for grad, unit in after(pairs, gate)])


def swish_slope(values):
    gate = jax.nn.sigmoid(values)
    return gate * (1.0 + values * (1.0 - gate))


def distance_table(slots, width, first):
    column = jnp.arange(width)
    even = (column % 2 == 0)[None, :]
    rate = jnp.exp(-(column - column % 2).astype(F32) * (math.log(10000.0) / width))
    coarse = (slots - 1 - STEP * jnp.arange(2 * slots // STEP)).astype(F32)[:, None] * rate[None, :]
    fine = jnp.arange(STEP).astype(F32)[:, None] * rate[None, :]
    sin_c, cos_c = jnp.sin(coarse), jnp.cos(coarse)
    with_cos = jnp.where(even, sin_c, cos_c)
    with_sin = jnp.where(even, -cos_c, sin_c)
    with_cos, with_sin, sin_f, cos_f = after((with_cos, with_sin, jnp.sin(fine), jnp.cos(fine)), first)
    table = with_cos[:, None, :] * cos_f[None] + with_sin[:, None, :] * sin_f[None]
    return table.reshape(2 * slots, width).astype(B16)


def dot(left, right, contract=(1, 0)):
    return lax.dot_general(
        left, right, (((contract[0],), (contract[1],)), ((), ())), preferred_element_type=F32
    )


def swap(values, distance):
    size = lax.axis_size("tp")
    return lax.ppermute(values, "tp", [(i, i ^ distance) for i in range(size)])


def distances():
    size = lax.axis_size("tp")
    return [1 << bit for bit in range(size.bit_length() - 1)]


def same_kernel(block_ref, out_ref):
    pass


def arrived(block):
    spec = pl.BlockSpec(memory_space=pl.ANY)
    return pl.pallas_call(
        same_kernel,
        in_specs=[spec],
        out_specs=spec,
        out_shape=jax.ShapeDtypeStruct(block.shape, block.dtype),
        input_output_aliases={0: 0},
        cost_estimate=pl.CostEstimate(flops=0, bytes_accessed=LINK_BYTES, transcendentals=0),
    )(block)


def gather(own, first=False, late=()):
    slots = {0: own}
    for distance in reversed(distances()):
        for slot in list(slots):
            slots[slot ^ distance] = swap(slots[slot], distance)
    last = len(slots) - 1
    if first:
        slots[last] = after(arrived(slots[last]), late)
    return [slots[slot] for slot in range(len(slots))]


def scatter(parts, late=(), add=True):
    parts = dict(enumerate(parts))
    sent = got = None
    for distance in distances():
        for slot in sorted(parts, reverse=True):
            if slot & distance:
                sent = parts.pop(slot).astype(B16)
                if distance == distances()[-1]:
                    sent = after(sent, late)
                got = swap(sent, distance)
                if add or distance != distances()[-1]:
                    parts[slot ^ distance] = parts[slot ^ distance].astype(F32) + got.astype(F32)
    return parts[0], (sent, got)


def after(values, *others):
    return lax.optimization_barrier((values, others))[0]


def halves(slots):
    half = len(slots) // 2
    return jnp.concatenate(slots[:half], 0), jnp.concatenate(slots[half:], 0)


def pieces(near, far, weight, contract):
    count = lax.axis_size("tp") // 2
    rows = near.shape[0] // count
    outs = {}
    for slot in reversed(range(2 * count)):
        source, place = (near, slot) if slot < count else (far, slot - count)
        outs[slot] = dot(source[place * rows : (place + 1) * rows], weight, contract)
    return [outs[slot] for slot in range(2 * count)]


def ring():
    size, mine = lax.axis_size("rows"), lax.axis_index("rows")
    order = list(range(0, size, 2)) + list(range(size - 1, 0, -2))
    place = jnp.where(mine % 2 == 0, mine // 2, size - (mine + 1) // 2)
    right = [(order[i], order[(i + 1) % size]) for i in range(size)]
    return size, place, right, [(there, here) for here, there in right]


def plain(piece):
    return piece


def turned(piece):
    return piece.T


def first_kernel(at, *refs):
    count = (len(refs) - 2) // 2
    refs[-2][...] = jnp.concatenate([ref[...] for ref in refs[:count]], 1)
    refs[-1][...] = jnp.concatenate([ref[...] for ref in refs[count:-2]], 1)


def pass_kernel(second, at, *refs):
    count = (len(refs) - 4) // 2
    from_left, from_right = (ref[...].astype(F32) for ref in refs[-4:-2])
    if second:
        top = pl.program_id(0) == 0
        from_left = jnp.where(top, from_left, 0.0)
        from_right = jnp.where(top, 0.0, from_right)
    own = jnp.concatenate([ref[...] for ref in refs[:count]], 1).astype(F32)
    refs[-2][...] = (own + from_left).astype(B16)
    own = jnp.concatenate([ref[...] for ref in refs[count:-4]], 1).astype(F32)
    refs[-1][...] = (own + from_right).astype(B16)


def total_kernel(split, at, *refs):
    own = jnp.concatenate([ref[...] for ref in refs[:-3]], 1).astype(F32)
    from_left, from_right = (ref[...].astype(F32) for ref in refs[-3:-1])
    if split:
        refs[-1][...] = (own + jnp.concatenate([from_left, from_right], 0)).astype(B16)
    else:
        refs[-1][...] = (own + from_left + from_right).astype(B16)


def place_kernel(spots, spans, at, *refs):
    count = len(spots)
    outs, held = refs[count : count + len(spans)], refs[-1]
    half = refs[count - 1].shape[0]
    size = held.shape[0] // (2 * half)
    for ref, (k, bottom) in zip(refs[:count], spots):
        start = ((at[0] + k) % size) * (2 * half) + bottom * half
        start = pl.multiple_of(start, half)
        held[pl.ds(start, ref.shape[0]), :] = ref[...].astype(F32)
    for out, (low, high, form) in zip(outs, spans):
        here = (pl.program_id(0) >= low) & (pl.program_id(0) < high)

        @pl.when(here)
        def _(out=out, form=form):
            out[...] = form(held[...])


class RowSum:
    def __init__(self, arrays, parts):
        self.size, self.place, self.right, self.left = ring()
        self.arrays, self.parts = list(arrays), parts
        self.width = sum(item.shape[1] for item in arrays)
        self.rows = arrays[0].shape[0] // self.size
        self.half = self.rows // 2
        self.stages = self.size // 2
        self.steps = 2 * self.stages
        self.done = 0
        self.seen = []

    def call(self, kernel, at, blocks, extra, out_rows, grid, gate, out_blocks, count=2):
        arrays, extra = after((self.arrays, extra), gate)
        specs, operands = [], []
        for rows, index in blocks:
            for item in arrays:
                specs.append(pl.BlockSpec((rows, item.shape[1]), index))
                operands.append(item)
        for item, (rows, index) in zip(extra, out_blocks[1]):
            specs.append(pl.BlockSpec((rows, self.width), index))
            operands.append(item)
        rows, index = out_blocks[0]
        moved = sum(2 * rows * self.width for _ in range(4))
        return pl.pallas_call(
            kernel,
            grid_spec=pltpu.PrefetchScalarGridSpec(
                num_scalar_prefetch=1,
                grid=(grid,),
                in_specs=specs,
                out_specs=[pl.BlockSpec((rows, self.width), index)] * count,
            ),
            out_shape=(sds((out_rows, self.width), B16),) * count,
            cost_estimate=pl.CostEstimate(flops=moved, bytes_accessed=moved, transcendentals=0),
        )(at, *operands)

    def send(self, to_right, to_left):
        over = lambda items, way: [lax.ppermute(item, "rows", way) for item in items]
        self.from_left, self.from_right = over(to_right, self.right), over(to_left, self.left)
        return (to_right, to_left)

    def step(self, gate=()):
        stage, stages, half, rows = self.done, self.stages, self.half, self.rows
        self.done += 1
        ids = [(self.place + k) % self.size for k in (stages - stage, stage - stages)]
        at = jnp.stack(ids).astype(jnp.int32)
        whole = lambda i, at: (0, 0)
        if stage == 0:
            blocks = [(half, lambda i, at: (2 * at[0], 0)), (half, lambda i, at: (2 * at[1] + 1, 0))]
            out = self.call(first_kernel, at, blocks, [], half, 1, gate, ((half, whole), []))
            return self.send([out[0]], [out[1]])
        if stage < stages:
            blocks = [
                (half, lambda i, at: (2 * at[0] + i, 0)), (half, lambda i, at: (2 * at[1] + i, 0)),
            ]
            here = (half, lambda i, at: (i, 0))
            got = (half, whole) if stage == 1 else here
            kernel = functools.partial(pass_kernel, stage == 1)
            extra = self.from_left + self.from_right
            out = self.call(kernel, at, blocks, extra, rows, 2, gate, (here, [got, got]))
            return self.send([out[0]], [out[1]])
        if stage == stages:
            got = (half if stages == 1 else rows, whole)
            kernel = functools.partial(total_kernel, stages == 1)
            extra = self.from_left + self.from_right
            blocks = [(rows, lambda i, at: (at[0], 0))]
            blocks = [(half, lambda i, at: (2 * at[0] + i, 0))] if stages > 1 else blocks
            here = (half, lambda i, at: (i, 0)) if stages > 1 else (rows, whole)
            got = here if stages > 1 else got
            grid = 2 if stages > 1 else 1
            out = self.call(kernel, at, blocks, extra, rows, grid, gate, (here, [got, got]), 1)
            to_right = to_left = list(out)
            self.see(to_right, 0)
        else:
            to_right, to_left = after((self.from_left, self.from_right), gate)
            self.see(to_right, stages - stage)
            self.see(to_left, stage - stages)
        if stage == 2 * stages - 1:
            to_right, to_left = [to_right[0][:half]], [to_left[0][half:]]
        return self.send(to_right, to_left)

    def see(self, items, k):
        self.seen.append((items[0], (k, 0)))

    def finish(self, gate=()):
        self.seen += [(self.from_left[0], (-self.stages, 0)), (self.from_right[0], (self.stages, 1))]
        items = after([item for item, _ in self.seen], gate)
        spots = [((k + self.size) % self.size, bottom) for _, (k, bottom) in self.seen]
        length = self.arrays[0].shape[0]
        step = math.gcd(*[width for width, _ in self.parts])
        spans, specs, shapes, low = [], [], [], 0
        for width, form in self.parts:
            count = width // step
            spans.append((low, low + count, form))

            def column(i, at, low=low, count=count):
                return jnp.clip(i - low, 0, count - 1)

            if form is turned:
                shapes.append((width, length))
                specs.append(pl.BlockSpec((step, length), lambda i, at, f=column: (f(i, at), 0)))
            else:
                shapes.append((length, width))
                specs.append(pl.BlockSpec((length, step), lambda i, at, f=column: (0, f(i, at))))
            low += count
        moved = 6 * length * self.width
        return pl.pallas_call(
            functools.partial(place_kernel, spots, spans),
            grid_spec=pltpu.PrefetchScalarGridSpec(
                num_scalar_prefetch=1,
                grid=(low,),
                in_specs=[pl.BlockSpec((item.shape[0], step), lambda i, at: (0, i)) for item in items],
                out_specs=specs,
                scratch_shapes=[pltpu.VMEM((length, step), F32)],
            ),
            out_shape=[sds(shape, F32) for shape in shapes],
            compiler_params=pltpu.CompilerParams(vmem_limit_bytes=60 << 20),
            cost_estimate=pl.CostEstimate(flops=moved, bytes_accessed=moved, transcendentals=0),
        )(self.place.reshape(1).astype(jnp.int32), *items)


class WholeSum:
    def __init__(self, arrays, parts):
        self.arrays, self.parts, self.steps, self.done = list(arrays), parts, 1, 0

    def step(self, gate=()):
        self.done += 1
        values = after(jnp.concatenate(self.arrays, 1), gate)
        self.total = lax.psum(values, "rows").astype(F32)
        return ()

    def finish(self, gate=()):
        edges = [sum(width for width, _ in self.parts[:k]) for k in range(len(self.parts) + 1)]
        return [
            form(self.total[:, edges[k] : edges[k + 1]]) for k, (_, form) in enumerate(self.parts)
        ]


def row_sum(arrays, parts):
    size = lax.axis_size("rows")
    fits = size % 2 == 0 and arrays[0].shape[0] % (16 * size) == 0
    return (RowSum if fits else WholeSum)(arrays, parts)


def start_sum(arrays):
    if arrays[0].shape[1] == arrays[1].shape[1]:
        arrays = [jnp.concatenate(arrays, 0)]
    return [lax.psum_scatter(item, "rows", scatter_dimension=0, tiled=True) for item in arrays]


def end_sum(shares):
    return [lax.all_gather(item, "rows", axis=0, tiled=True) for item in shares]


def split_sum(whole, rows):
    if len(whole) == 1:
        whole = [whole[0][:rows], whole[0][rows:]]
    return [item.astype(F32) for item in whole]


class RowSums:
    def __init__(self, arrays, parts):
        if all(item.shape[0] == arrays[0].shape[0] for item in arrays):
            self.items = [row_sum(arrays, parts)]
        else:
            self.items = [row_sum([item], [part]) for item, part in zip(arrays, parts)]

    @property
    def done(self):
        return self.items[0].done

    @property
    def left(self):
        return max(item.steps - item.done for item in self.items)

    def step(self, gate=()):
        for item in self.items:
            if item.done < item.steps:
                gate = item.step(gate)
        return gate

    def finish(self, gate=()):
        while self.left:
            gate = self.step(gate)
        return [out for item in self.items for out in item.finish(gate)]


def sum_cube(values, axis):
    size = lax.axis_size(axis)
    if size & (size - 1):
        return lax.psum(values, axis)
    distance = 1
    while distance < size:
        values = values + lax.ppermute(values, axis, [(i, i ^ distance) for i in range(size)])
        distance *= 2
    return values


def halo(own, reach):
    size = lax.axis_size("tp")
    left = lax.ppermute(own[-reach:], "tp", [(i, i + 1) for i in range(size - 1)])
    right = lax.ppermute(own[:reach], "tp", [(i + 1, i) for i in range(size - 1)])
    return jnp.concatenate([left, own, right], 0)


def to_true(values):
    size, mine = lax.axis_size("tp"), lax.axis_index("tp")
    rows = values.shape[0] // size
    return jnp.concatenate(
        [lax.dynamic_slice_in_dim(values, (mine ^ k) * rows, rows, 0) for k in range(size)], 0
    )


def ffn_forward(values, gain, weight_up, weight_down):
    normed, unit, inverse = normalize(values, gain)
    near, far = halves(gather(normed.astype(B16)))
    pre, act = [], []
    for half in (near, far):
        pre.append(dot(after(half, act), weight_up))
        act.append((pre[-1] * jax.nn.sigmoid(pre[-1])).astype(B16))
    total, (sent, _) = scatter(pieces(act[0], act[1], weight_down, (1, 0)))
    pre = [item.astype(B16) for item in pre]
    return (values + 0.5 * total, (unit, inverse, (near, far), pre, act), sent)


def ffn_backward(grad, kept, gain, weight_up, weight_down, use=None, fill=None):
    unit, inverse, wide, pre, act = kept
    own = (0.5 * grad).astype(B16)
    cot = halves(gather(own) if fill is None else gather(own, True, fill(own)))
    d_pre = []
    for half in (0, 1):
        d_act = dot(after(cot[half], d_pre), weight_down, (1, 1))
        d_pre.append((d_act * swish_slope(pre[half].astype(F32))).astype(B16))
    d_norm, (sent, _) = scatter(pieces(d_pre[0], d_pre[1], weight_up, (1, 1)))
    cot, d_pre = after((cot, d_pre), sent)
    grad_down = dot(jnp.concatenate(act, 0), jnp.concatenate(cot, 0), (0, 0))
    grad_up = dot(jnp.concatenate(wide, 0), jnp.concatenate(d_pre, 0), (0, 0))
    grads = (grad_up.astype(B16), grad_down.astype(B16))
    if use is not None:
        d_norm = after(d_norm, use(grads))
    d_in, grad_gain = normalize_back(d_norm, unit, inverse, gain)
    return (grad + d_in, grad_gain, grads, (own, sent))


def places(slots):
    size, mine = lax.axis_size("tp"), lax.axis_index("tp")
    rows = slots // size
    if rows % TK:
        q_at = jnp.arange(slots // TQ, dtype=jnp.int32) * TQ
        k_at = jnp.arange(slots // TK, dtype=jnp.int32) * TK
        return q_at, k_at, True
    q_true = jnp.arange(slots // TQ, dtype=jnp.int32) * TQ
    k_true = jnp.arange(slots // TK, dtype=jnp.int32) * TK
    q_at = ((q_true // rows) ^ mine) * rows + q_true % rows
    k_at = ((k_true // rows) ^ mine) * rows + k_true % rows
    return q_at.astype(jnp.int32), k_at.astype(jnp.int32), False


def attend_forward(
    values, gain, weights, attend_out, content_bias, position_bias, code, spans, rel, prefetch
):
    slots = code.shape[0]
    width = attend_out.shape[0]
    q_at, k_at, reorder = places(slots)
    where = (spans, q_at, k_at)
    normed, unit, inverse = normalize(values, gain)
    near, far = halves(gather(normed.astype(B16)))
    mixed = [dot(near, weights)]
    far = after(far, rel, spans, mixed)
    fetched, arrived = prefetch(far)
    mixed.append(dot(far, weights))
    flat = lambda bias: bias.astype(F32).reshape(1, width)
    join = lambda items: jnp.concatenate(items, 0)
    q_content = join([(item[:, :width] + flat(content_bias)).astype(B16) for item in mixed])
    q_position = join([(item[:, :width] + flat(position_bias)).astype(B16) for item in mixed])
    key = join([item[:, width : 2 * width].astype(B16) for item in mixed])
    value = join([item[:, 2 * width :].astype(B16) for item in mixed])
    if reorder:
        q_content, q_position, key, value = map(to_true, (q_content, q_position, key, value))
    operands = (
        where
        + (q_content, q_position, key, value, rel)
        + (code.reshape(slots, 1), code.reshape(slots // TK, 1, TK))
    )
    heads_out, heads_wide, sums = attend(*operands)
    sent = after(to_true(heads_out) if reorder else heads_out, arrived)
    half = slots // 2
    total, _ = scatter(pieces(sent[:half], sent[half:], attend_out, (1, 0)))
    kept = (unit, inverse, (near, far), operands, heads_wide, sums, sent)
    return (values + total, kept, fetched)


def attend_backward(grad, cot, kept, gain, weights, attend_out, table, filler, use):
    unit, inverse, wide, operands, heads_wide, sums, sent = kept
    slots, width = sent.shape
    _, _, reorder = places(slots)
    cot = halves(cot)
    d_near = dot(cot[0], attend_out, (1, 1)).astype(B16)
    cot = (cot[0], after(cot[1], d_near))
    d_heads = jnp.concatenate([d_near, dot(cot[1], attend_out, (1, 1)).astype(B16)], 0)
    if reorder:
        d_heads = to_true(d_heads)
    d_heads = after(d_heads, filler[0])
    d_all, d_rel, d_bias = attend_back(*operands, d_heads, heads_wide, sums)
    if reorder:
        d_all = to_true(d_all)
    d_all = after(d_all, filler[1])
    half = slots // 2
    d_norm, (last, _) = scatter(pieces(d_all[:half], d_all[half:], weights, (1, 1)))
    cot, d_all, d_rel = after((cot, d_all, d_rel), last)
    grad_out = dot(jnp.concatenate(cot, 0), sent, (0, 0))
    grad_all = dot(jnp.concatenate(wide, 0), d_all, (0, 0))
    grad_pos = dot(table, d_rel, (0, 0))
    grads = [item.astype(B16) for item in (grad_all, grad_pos, grad_out)]
    d_norm = after(d_norm, use(grads, last))
    d_in, grad_gain = normalize_back(d_norm, unit, inverse, gain)
    return (grad + d_in, grad_gain, d_bias[:2])


def conv_weights(point_in, depth_kernel, gain_inner, point_out, first):
    taps = depth_kernel.shape[0]
    own = after((point_in[:, 0], point_in[:, 1], point_out), first)
    small = gather(jnp.concatenate([depth_kernel, gain_inner[None]], 0))
    small = jnp.concatenate(small, 1).astype(F32)
    in_a, in_b, out = map(gather, own)
    arrived = [item[2::2] for item in (in_a, in_b, out)]
    in_a, in_b = jnp.concatenate(in_a, 1), jnp.concatenate(in_b, 1)
    return (in_a, in_b, small[:taps], small[taps], jnp.concatenate(out, 0)), arrived


def conv_masks(segments, valid, rows, taps):
    edge = 8
    reach = taps // 2
    base = lax.axis_index("tp") * rows + edge - reach
    wide_segments = jnp.pad(segments, edge, constant_values=-1)
    wide_valid = jnp.pad(valid, edge)
    own = lax.dynamic_slice_in_dim(wide_segments, base, rows + 2 * reach)
    masks = []
    for tap in range(taps):
        other = lax.dynamic_slice_in_dim(wide_segments, base + tap - reach, rows + 2 * reach)
        good = lax.dynamic_slice_in_dim(wide_valid, base + tap - reach, rows + 2 * reach)
        masks.append(((other == own) & (good == 1)).astype(F32)[:, None])
    return masks


def conv_forward(values, gain, full, masks):
    in_a, in_b, kernel, gain_inner, out = full
    rows = values.shape[0]
    taps = kernel.shape[0]
    reach = taps // 2
    normed, unit, inverse = normalize(values, gain)
    low = normed.astype(B16)
    wide = halo(low, 2 * reach)
    mixed_a = dot(wide, in_a)
    gate = jax.nn.sigmoid(dot(wide, in_b))
    glu = mixed_a * gate
    depth = 0.0
    for tap in range(taps):
        depth = depth + kernel[tap] * masks[tap] * glu[tap : tap + rows + 2 * reach]
    depth_norm, inner_unit, inner_inverse = normalize(depth, gain_inner)
    inner = (depth_norm * jax.nn.sigmoid(depth_norm)).astype(B16)
    own = slice(2 * reach, 2 * reach + rows)
    kept = (unit, inverse, low, mixed_a[own], gate[own], glu, inner_unit, inner_inverse, depth_norm, inner)
    return (values + dot(inner[reach : reach + rows], out), kept)


def conv_backward(grad, kept, gain, full, masks):
    unit, inverse, low, mixed_a, gate, glu, inner_unit, inner_inverse, depth_norm, inner = kept
    in_a, in_b, kernel, gain_inner, out = full
    rows = grad.shape[0]
    taps = kernel.shape[0]
    reach = taps // 2
    mine = slice(reach, reach + rows)
    cot = grad.astype(B16)
    d_act = dot(halo(cot, reach), out, (1, 1))
    d_depth_norm = d_act * swish_slope(depth_norm)
    d_depth, _ = normalize_back(d_depth_norm, inner_unit, inner_inverse, gain_inner)
    d_glu = 0.0
    for tap in range(taps):
        weighted = d_depth * masks[tap]
        back = 2 * reach - tap
        d_glu = d_glu + kernel[tap] * weighted[back : back + rows]
    d_a = (d_glu * gate).astype(B16)
    d_b = (d_glu * mixed_a * gate * (1.0 - gate)).astype(B16)
    d_norm = dot(d_a, in_a, (1, 1)) + dot(d_b, in_b, (1, 1))
    d_in, grad_gain = normalize_back(d_norm, unit, inverse, gain)
    grad = grad + d_in
    slots = gather(grad.astype(B16), True)
    low, cot, d_a, d_b, inner = after((low, cot, d_a, d_b, inner), slots[1])
    size = lax.axis_size("tp")
    width = in_a.shape[1] // size
    parts = []
    grads = [
        dot(left, right, (0, 0)).astype(B16)
        for left, right in ((low, d_a), (low, d_b), (cot, inner[mine]))
    ]

    def small_grads(gate):
        d_own, norm_own = after((d_depth[mine], d_depth_norm[mine]), gate)
        sums = []
        for tap in range(taps):
            near = d_own * masks[tap][mine]
            sums.append(jnp.sum(near * glu[reach + tap : reach + tap + rows], axis=0))
        sums.append(jnp.sum(norm_own * inner_unit[mine], axis=0))
        small = jnp.stack(sums, 0)
        return scatter([small[:, k * width : (k + 1) * width] for k in range(size)])[0]

    for slot in range(size):
        cols = slice(slot * width, (slot + 1) * width)
        parts.append(jnp.concatenate([item[:, cols] for item in grads], 1))
    total, ends = scatter(parts, slots[-1], False)
    return (grad, slots, grad_gain, (total, small_grads), ends)


def body(
    layer_input,
    cotangent,
    segments,
    valid_frames,
    gain_first,
    up_first,
    down_first,
    gain_attend,
    query_weight,
    key_weight,
    value_weight,
    attend_out,
    pos_weight,
    content_bias,
    position_bias,
    gain_conv,
    point_in,
    depth_kernel,
    gain_inner,
    point_out,
    gain_second,
    up_second,
    down_second,
    gain_final,
):
    segment_row, valid_row = segments[0], valid_frames[0]
    weights = jnp.concatenate([query_weight, key_weight, value_weight], 1)
    width = query_weight.shape[1]
    taps = depth_kernel.shape[0]
    values = layer_input[0].astype(F32)
    rows = values.shape[0]
    slots = segment_row.shape[0]
    masks = conv_masks(segment_row, valid_row, rows, taps)
    code = codes(segment_row, valid_row)
    spans = spans_of(code)
    values, kept_first, sent = ffn_forward(values, gain_first, up_first, down_first)
    table = distance_table(slots, values.shape[1], sent)
    rel = dot(table, pos_weight).astype(B16)
    prefetch = functools.partial(conv_weights, point_in, depth_kernel, gain_inner, point_out)
    values, kept_attend, full = attend_forward(
        values, gain_attend, weights, attend_out, content_bias, position_bias, code, spans, rel, prefetch
    )
    values, kept_conv = conv_forward(values, gain_conv, full, masks)
    values, kept_second, _ = ffn_forward(values, gain_second, up_second, down_second)
    final, final_unit, final_inverse = normalize(values, gain_final)
    layer_output = final.astype(B16)
    grad, sum_final = normalize_back(cotangent[0].astype(F32), final_unit, final_inverse, gain_final)
    held = {}

    def start_second(grads):
        held["second"] = start_sum(grads)
        return grads

    grad, sum_second, _, _ = ffn_backward(
        grad, kept_second, gain_second, up_second, down_second, start_second
    )
    grad, cot, sum_conv, conv_grads, ends = conv_backward(grad, kept_conv, gain_conv, full, masks)
    ends = (ends[0], (ends, held["second"]))

    def start_middle(grads, last):
        own, got = after((conv_grads[0], ends[1][0][1]), last)
        total = (own.astype(F32) + got.astype(F32)).astype(B16)
        forms = [(width, plain)] * 4 + [(width, turned), (2 * width, plain), (width, turned)]
        held["middle"] = row_sum(grads + [total], forms)
        return held["middle"].step()

    grad, sum_attend, d_bias = attend_backward(
        grad, cot, kept_attend, gain_attend, weights, attend_out, table, ends, start_middle
    )
    middle = held["middle"]
    second_sum = end_sum(held["second"])
    grad, sum_first, first_grads, marks = ffn_backward(
        grad, kept_first, gain_first, up_first, down_first, None, middle.step
    )
    first = RowSums(first_grads, [(item.shape[1], plain) for item in first_grads])
    token = middle.step(marks[1])
    token = first.step(token)
    second_sum = after(second_sum, token)
    token = second_sum
    while middle.done < middle.steps:
        token = middle.step(token)
        if first.left > 1:
            token = first.step(token)
        if first.done == 3:
            token = (token, grad)
        if first.done == 5:
            second_up, second_down = split_sum(after(second_sum, token), up_second.shape[0])
            token = (token, second_up, second_down)
    while first.left:
        token = first.step(token)
    pairs = (sum_first, sum_attend, sum_conv, sum_second, sum_final)
    gains = sum_cube(gain_sums(pairs, marks[1]), "tp")
    small = jnp.concatenate([conv_grads[1](marks[1]), d_bias], 0)
    small_shape = small.shape
    pack = jnp.concatenate([gains.reshape(-1), small.reshape(-1)]).reshape(-1, width)
    pack = sum_cube(after(pack, token), "rows")
    attend_sum = middle.finish(token)
    first_sum = first.finish(attend_sum)
    pack = pack.reshape(-1)
    gains, small = pack[: gains.size].reshape(gains.shape), pack[gains.size :].reshape(small_shape)
    bias_shape = content_bias.shape
    return (
        layer_output[None],
        grad[None],
        gains[0],
        first_sum[0],
        first_sum[1],
        gains[1],
        attend_sum[0],
        attend_sum[1],
        attend_sum[2],
        attend_sum[4],
        attend_sum[3],
        small[taps + 1].reshape(bias_shape),
        small[taps + 2].reshape(bias_shape),
        gains[2],
        attend_sum[5].reshape(attend_sum[5].shape[0], 2, width),
        small[:taps],
        small[taps],
        attend_sum[6],
        gains[3],
        second_up,
        second_down,
        gains[4],
    )


def solution(mesh):
    in_specs = (
        P("rows", "tp", None),
        P("rows", "tp", None),
        P("rows", None),
        P("rows", None),
        P(),
        P(None, "tp"),
        P("tp", None),
        P(),
        P(None, "tp"),
        P(None, "tp"),
        P(None, "tp"),
        P("tp", None),
        P(None, "tp"),
        P("tp", None),
        P("tp", None),
        P(),
        P(None, None, "tp"),
        P(None, "tp"),
        P("tp"),
        P("tp", None),
        P(),
        P(None, "tp"),
        P("tp", None),
        P(),
    )
    out_specs = (
        P("rows", "tp", None),
        P("rows", "tp", None),
        P(),
        P(None, "tp"),
        P("tp", None),
        P(),
        P(None, "tp"),
        P(None, "tp"),
        P(None, "tp"),
        P("tp", None),
        P(None, "tp"),
        P("tp", None),
        P("tp", None),
        P(),
        P(None, None, "tp"),
        P(None, "tp"),
        P("tp"),
        P("tp", None),
        P(),
        P(None, "tp"),
        P("tp", None),
        P(),
    )
    return jax.shard_map(body, mesh=mesh, in_specs=in_specs, out_specs=out_specs, check_vma=False)
```

```python
import functools
import math

import jax
import jax.numpy as jnp
from jax import lax
from jax.experimental import pallas as pl
from jax.experimental.pallas import tpu as pltpu
from jax.sharding import PartitionSpec as P

EPS = 1e-05
NEG = -1e30
F32 = jnp.float32
B16 = jnp.bfloat16
TQ = 128
TK = 384
HD = 128
STEP = 64
LINK_BYTES = 180_000_000
SM = pl.BlockSpec(memory_space=pltpu.SMEM)
VM = pl.BlockSpec(memory_space=pltpu.VMEM)

def dotx(a, b, ca, cb):
    return lax.dot_general(a, b, (((ca,), (cb,)), ((), ())), preferred_element_type=F32)

def skew_tile(grid):
    return pltpu.roll(grid, TK + 1, 1, stride=1, stride_axis=0)[:, :TK]

def unskew_flipped(flipped):
    wide = jnp.concatenate([flipped, jnp.zeros((TQ, TQ), F32)], axis=1)
    return pltpu.roll(wide, 0, 1, stride=1, stride_axis=0)

def attend_kernel(heads, spans, q_at, k_at, qc_ref, qp_ref, k_ref, v_ref, rel_ref, code_q_ref, code_k_ref,
                  out_ref, wide_ref, lse_ref):
    slots = qc_ref.shape[0]
    scale = HD ** -0.5
    blocks, tiles = slots // TQ, slots // TK

    def q_step(qb, _):
        at = pl.multiple_of(q_at[qb], TQ)
        true_at = pl.multiple_of(qb * TQ, TQ)
        code_q = code_q_ref[pl.ds(true_at, TQ), :]
        qc = [qc_ref[pl.ds(at, TQ), h * HD:(h + 1) * HD] for h in range(heads)]
        qp = [qp_ref[pl.ds(at, TQ), h * HD:(h + 1) * HD] for h in range(heads)]

        def k_step(kt, carry):
            ko = pl.multiple_of(k_at[kt], TQ)
            to = pl.multiple_of((blocks - 1 + kt * (TK // TQ) - qb) * TQ, TQ)
            mask = code_q == code_k_ref[kt]
            new = []
            for h in range(heads):
                lanes = slice(h * HD, (h + 1) * HD)
                top, total, acc = carry[h]
                grid = dotx(qp[h], rel_ref[pl.ds(to, TK + TQ), lanes], 1, 1)
                raw = dotx(qc[h], k_ref[pl.ds(ko, TK), lanes], 1, 1) + skew_tile(grid)
                scores = jnp.where(mask, raw * scale, NEG)
                top_new = jnp.maximum(top, jnp.max(scores, axis=1, keepdims=True))
                shrink = jnp.exp(top - top_new)
                weights = jnp.exp(scores - top_new)
                total = total * shrink + jnp.sum(weights, axis=1, keepdims=True)
                acc = acc * shrink + dotx(weights.astype(B16), v_ref[pl.ds(ko, TK), lanes], 1, 0)
                new.append((top_new, total, acc))
            return tuple(new)

        first = tuple((jnp.full((TQ, 1), NEG, F32), jnp.zeros((TQ, 1), F32), jnp.zeros((TQ, HD), F32))
                      for _ in range(heads))
        final = lax.fori_loop(spans[0, qb], spans[1, qb], k_step, first)
        for h in range(heads):
            lanes = slice(h * HD, (h + 1) * HD)
            top, total, acc = final[h]
            out = acc / total
            wide_ref[pl.ds(at, TQ), lanes] = out
            out_ref[pl.ds(at, TQ), lanes] = out.astype(B16)
            lse_ref[pl.ds(at, TQ), h:h + 1] = top + jnp.log(total)
        return 0

    lax.fori_loop(0, blocks, q_step, 0)

def attend_back_kernel(heads, spans, q_at, k_at, qc_ref, qp_ref, k_ref, v_ref, rel_ref, code_q_ref, code_k_ref,
                       d_out_ref, wide_ref, lse_ref,
                       all_ref, drel_ref, bias_ref, dk_acc, dv_acc, drel_acc):
    slots = qc_ref.shape[0]
    scale = HD ** -0.5
    blocks, tiles = slots // TQ, slots // TK
    dk_acc[...] = jnp.zeros_like(dk_acc)
    dv_acc[...] = jnp.zeros_like(dv_acc)
    drel_acc[...] = jnp.zeros_like(drel_acc)
    bias_ref[...] = jnp.zeros_like(bias_ref)
    row = lax.broadcasted_iota(jnp.int32, (TQ, TQ), 0)
    column = lax.broadcasted_iota(jnp.int32, (TQ, TQ), 1)
    flip = (row + column == TQ - 1).astype(F32)
    flip_low = flip.astype(B16)

    def q_step(qb, _):
        at = pl.multiple_of(q_at[qb], TQ)
        true_at = pl.multiple_of(qb * TQ, TQ)
        code_q = code_q_ref[pl.ds(true_at, TQ), :]
        cols = [slice(h * HD, (h + 1) * HD) for h in range(heads)]
        qc = [qc_ref[pl.ds(at, TQ), c] for c in cols]
        qp = [qp_ref[pl.ds(at, TQ), c] for c in cols]
        qp_flipped = [dotx(flip_low, item, 1, 0).astype(B16) for item in qp]
        d_out = [d_out_ref[pl.ds(at, TQ), c] for c in cols]
        lse = [lse_ref[pl.ds(at, TQ), h:h + 1] for h in range(heads)]
        delta = [jnp.sum(d_out[h].astype(F32) * wide_ref[pl.ds(at, TQ), cols[h]], axis=1, keepdims=True)
                 for h in range(heads)]

        def k_step(kt, carry):
            ko = pl.multiple_of(k_at[kt], TQ)
            to = pl.multiple_of((blocks - 1 + kt * (TK // TQ) - qb) * TQ, TQ)
            mask = code_q == code_k_ref[kt]
            new = []
            for h in range(heads):
                lanes = cols[h]
                d_content, d_position = carry[h]
                window = rel_ref[pl.ds(to, TK + TQ), lanes]
                key = k_ref[pl.ds(ko, TK), lanes]
                grid = dotx(qp[h], window, 1, 1)
                raw = dotx(qc[h], key, 1, 1) + skew_tile(grid)
                probs = jnp.exp(jnp.where(mask, raw * scale - lse[h], NEG))
                d_probs = dotx(d_out[h], v_ref[pl.ds(ko, TK), lanes], 1, 1)
                d_raw = probs * (d_probs - delta[h]) * scale
                d_low = d_raw.astype(B16)
                d_grid = unskew_flipped(dotx(flip_low, d_low, 1, 0)).astype(B16)
                dv_acc[pl.ds(ko, TK), lanes] += dotx(probs.astype(B16), d_out[h], 0, 0)
                dk_acc[pl.ds(ko, TK), lanes] += dotx(d_low, qc[h], 0, 0)
                drel_acc[pl.ds(to, TK + TQ), lanes] += dotx(d_grid, qp_flipped[h], 0, 0)
                d_content = d_content + dotx(d_low, key, 1, 0)
                d_position = d_position + dotx(d_grid, window, 1, 0)
                new.append((d_content, d_position))
            return tuple(new)

        first = tuple((jnp.zeros((TQ, HD), F32),) * 2 for _ in range(heads))
        final = lax.fori_loop(spans[0, qb], spans[1, qb], k_step, first)
        for h in range(heads):
            d_content, d_position = final[h]
            d_position = lax.dot_general(flip, d_position, (((1,), (0,)), ((), ())),
                                         precision=lax.Precision.HIGHEST, preferred_element_type=F32)
            all_ref[pl.ds(at, TQ), cols[h]] = (d_content + d_position).astype(B16)
            bias_ref[0:1, cols[h]] += jnp.sum(d_content, axis=0, keepdims=True)
            bias_ref[1:2, cols[h]] += jnp.sum(d_position, axis=0, keepdims=True)
        return 0

    lax.fori_loop(0, blocks, q_step, 0)
    width = dk_acc.shape[1]
    all_ref[:, width : 2 * width] = dk_acc[...].astype(B16)
    all_ref[:, 2 * width :] = dv_acc[...].astype(B16)
    drel_ref[...] = drel_acc[...].astype(B16)

def sds(s, d): return jax.ShapeDtypeStruct(s, d)

def attend(spans, q_at, k_at, qc, qp, k, v, rel, code_q, code_k):
    slots, width = qc.shape
    heads = width // HD
    return pl.pallas_call(
        functools.partial(attend_kernel, heads),
        out_shape=(sds((slots, width), B16), sds((slots, width), F32), sds((slots, heads), F32)),
        in_specs=[SM] * 3 + [VM] * 7, out_specs=(VM,) * 3,
        compiler_params=pltpu.CompilerParams(vmem_limit_bytes=40 << 20),
        cost_estimate=pl.CostEstimate(flops=int(4e9), bytes_accessed=int(9e6), transcendentals=int(2e6)),
    )(spans, q_at, k_at, qc, qp, k, v, rel, code_q, code_k)

def attend_back(spans, q_at, k_at, qc, qp, k, v, rel, code_q, code_k, d_out, wide, lse):
    slots, width = qc.shape
    heads = width // HD
    return pl.pallas_call(
        functools.partial(attend_back_kernel, heads),
        out_shape=(sds((slots, 3 * width), B16), sds((2 * slots, width), B16), sds((8, width), F32)),
        in_specs=[SM] * 3 + [VM] * 10, out_specs=(VM,) * 3,
        scratch_shapes=[pltpu.VMEM((slots, width), F32), pltpu.VMEM((slots, width), F32), pltpu.VMEM((2 * slots, width), F32)],
        compiler_params=pltpu.CompilerParams(vmem_limit_bytes=48 << 20),
        cost_estimate=pl.CostEstimate(flops=int(1e6), bytes_accessed=int(1e6), transcendentals=0),
    )(spans, q_at, k_at, qc, qp, k, v, rel, code_q, code_k, d_out, wide, lse)

def codes(segments, valid):
    slots = segments.shape[0]
    place = jnp.arange(slots, dtype=jnp.int32)
    code = jnp.where(valid == 1, segments, -1 - place)
    return code

def spans_of(code):
    slots = code.shape[0]
    same = code[:, None] == code[None, :]
    touch = jnp.any(same.reshape(slots // TQ, TQ, slots // TK, TK), axis=(1, 3))
    tiles = slots // TK
    idx = jnp.arange(tiles, dtype=jnp.int32)
    lo = jnp.min(jnp.where(touch, idx, tiles), axis=1)
    hi = jnp.max(jnp.where(touch, idx + 1, 0), axis=1)
    return jnp.stack([lo, hi], 0).astype(jnp.int32)


def normalize(values, gain):
    mean = jnp.mean(values, axis=-1, keepdims=True)
    centered = values - mean
    inverse = lax.rsqrt(jnp.mean(centered * centered, axis=-1, keepdims=True) + EPS)
    unit = centered * inverse
    return (unit * gain.astype(F32), unit, inverse)


def normalize_back(grad, unit, inverse, gain):
    scaled = grad * gain.astype(F32)
    first = jnp.mean(scaled, axis=-1, keepdims=True)
    second = jnp.mean(scaled * unit, axis=-1, keepdims=True)
    return (inverse * (scaled - first - unit * second), (grad, unit))


def gain_sums(pairs, gate):
    return jnp.stack([jnp.sum(grad * unit, axis=0) for grad, unit in after(pairs, gate)])


def swish_slope(values):
    gate = jax.nn.sigmoid(values)
    return gate * (1.0 + values * (1.0 - gate))


def distance_table(slots, width, first):
    column = jnp.arange(width)
    even = (column % 2 == 0)[None, :]
    rate = jnp.exp(-(column - column % 2).astype(F32) * (math.log(10000.0) / width))
    coarse = (slots - 1 - STEP * jnp.arange(2 * slots // STEP)).astype(F32)[:, None] * rate[None, :]
    fine = jnp.arange(STEP).astype(F32)[:, None] * rate[None, :]
    sin_c, cos_c = jnp.sin(coarse), jnp.cos(coarse)
    with_cos = jnp.where(even, sin_c, cos_c)
    with_sin = jnp.where(even, -cos_c, sin_c)
    with_cos, with_sin, sin_f, cos_f = after((with_cos, with_sin, jnp.sin(fine), jnp.cos(fine)), first)
    table = with_cos[:, None, :] * cos_f[None] + with_sin[:, None, :] * sin_f[None]
    return table.reshape(2 * slots, width).astype(B16)


def dot(left, right, contract=(1, 0)):
    return lax.dot_general(
        left, right, (((contract[0],), (contract[1],)), ((), ())), preferred_element_type=F32
    )


def swap(values, distance):
    size = lax.axis_size("tp")
    return lax.ppermute(values, "tp", [(i, i ^ distance) for i in range(size)])


def distances():
    size = lax.axis_size("tp")
    return [1 << bit for bit in range(size.bit_length() - 1)]


def same_kernel(block_ref, out_ref):
    pass


def arrived(block):
    spec = pl.BlockSpec(memory_space=pl.ANY)
    return pl.pallas_call(
        same_kernel,
        in_specs=[spec],
        out_specs=spec,
        out_shape=jax.ShapeDtypeStruct(block.shape, block.dtype),
        input_output_aliases={0: 0},
        cost_estimate=pl.CostEstimate(flops=0, bytes_accessed=LINK_BYTES, transcendentals=0),
    )(block)


def gather(own, first=False, late=()):
    slots = {0: own}
    for distance in reversed(distances()):
        for slot in list(slots):
            slots[slot ^ distance] = swap(slots[slot], distance)
    last = len(slots) - 1
    if first:
        slots[last] = after(arrived(slots[last]), late)
    return [slots[slot] for slot in range(len(slots))]


def scatter(parts, late=(), add=True):
    parts = dict(enumerate(parts))
    sent = got = None
    for distance in distances():
        for slot in sorted(parts, reverse=True):
            if slot & distance:
                sent = parts.pop(slot).astype(B16)
                if distance == distances()[-1]:
                    sent = after(sent, late)
                got = swap(sent, distance)
                if add or distance != distances()[-1]:
                    parts[slot ^ distance] = parts[slot ^ distance].astype(F32) + got.astype(F32)
    return parts[0], (sent, got)


def after(values, *others):
    return lax.optimization_barrier((values, others))[0]


def halves(slots):
    half = len(slots) // 2
    return jnp.concatenate(slots[:half], 0), jnp.concatenate(slots[half:], 0)


def pieces(near, far, weight, contract):
    count = lax.axis_size("tp") // 2
    rows = near.shape[0] // count
    outs = {}
    for slot in reversed(range(2 * count)):
        source, place = (near, slot) if slot < count else (far, slot - count)
        outs[slot] = dot(source[place * rows : (place + 1) * rows], weight, contract)
    return [outs[slot] for slot in range(2 * count)]


def ring():
    size, mine = lax.axis_size("rows"), lax.axis_index("rows")
    order = list(range(0, size, 2)) + list(range(size - 1, 0, -2))
    place = jnp.where(mine % 2 == 0, mine // 2, size - (mine + 1) // 2)
    right = [(order[i], order[(i + 1) % size]) for i in range(size)]
    return size, place, right, [(there, here) for here, there in right]


def plain(piece):
    return piece


def turned(piece):
    return piece.T


def first_kernel(at, *refs):
    count = (len(refs) - 2) // 2
    refs[-2][...] = jnp.concatenate([ref[...] for ref in refs[:count]], 1)
    refs[-1][...] = jnp.concatenate([ref[...] for ref in refs[count:-2]], 1)


def pass_kernel(second, at, *refs):
    count = (len(refs) - 4) // 2
    from_left, from_right = (ref[...].astype(F32) for ref in refs[-4:-2])
    if second:
        top = pl.program_id(0) == 0
        from_left = jnp.where(top, from_left, 0.0)
        from_right = jnp.where(top, 0.0, from_right)
    own = jnp.concatenate([ref[...] for ref in refs[:count]], 1).astype(F32)
    refs[-2][...] = (own + from_left).astype(B16)
    own = jnp.concatenate([ref[...] for ref in refs[count:-4]], 1).astype(F32)
    refs[-1][...] = (own + from_right).astype(B16)


def total_kernel(split, at, *refs):
    own = jnp.concatenate([ref[...] for ref in refs[:-3]], 1).astype(F32)
    from_left, from_right = (ref[...].astype(F32) for ref in refs[-3:-1])
    if split:
        refs[-1][...] = (own + jnp.concatenate([from_left, from_right], 0)).astype(B16)
    else:
        refs[-1][...] = (own + from_left + from_right).astype(B16)


def place_kernel(spots, spans, at, *refs):
    count = len(spots)
    outs, held = refs[count : count + len(spans)], refs[-1]
    half = refs[count - 1].shape[0]
    size = held.shape[0] // (2 * half)
    for ref, (k, bottom) in zip(refs[:count], spots):
        start = ((at[0] + k) % size) * (2 * half) + bottom * half
        start = pl.multiple_of(start, half)
        held[pl.ds(start, ref.shape[0]), :] = ref[...].astype(F32)
    for out, (low, high, form) in zip(outs, spans):
        here = (pl.program_id(0) >= low) & (pl.program_id(0) < high)

        @pl.when(here)
        def _(out=out, form=form):
            out[...] = form(held[...])


class RowSum:
    def __init__(self, arrays, parts):
        self.size, self.place, self.right, self.left = ring()
        self.arrays, self.parts = list(arrays), parts
        self.width = sum(item.shape[1] for item in arrays)
        self.rows = arrays[0].shape[0] // self.size
        self.half = self.rows // 2
        self.stages = self.size // 2
        self.steps = 2 * self.stages
        self.done = 0
        self.seen = []

    def call(self, kernel, at, blocks, extra, out_rows, grid, gate, out_blocks, count=2):
        arrays, extra = after((self.arrays, extra), gate)
        specs, operands = [], []
        for rows, index in blocks:
            for item in arrays:
                specs.append(pl.BlockSpec((rows, item.shape[1]), index))
                operands.append(item)
        for item, (rows, index) in zip(extra, out_blocks[1]):
            specs.append(pl.BlockSpec((rows, self.width), index))
            operands.append(item)
        rows, index = out_blocks[0]
        moved = sum(2 * rows * self.width for _ in range(4))
        return pl.pallas_call(
            kernel,
            grid_spec=pltpu.PrefetchScalarGridSpec(
                num_scalar_prefetch=1,
                grid=(grid,),
                in_specs=specs,
                out_specs=[pl.BlockSpec((rows, self.width), index)] * count,
            ),
            out_shape=(sds((out_rows, self.width), B16),) * count,
            cost_estimate=pl.CostEstimate(flops=moved, bytes_accessed=moved, transcendentals=0),
        )(at, *operands)

    def send(self, to_right, to_left):
        over = lambda items, way: [lax.ppermute(item, "rows", way) for item in items]
        self.from_left, self.from_right = over(to_right, self.right), over(to_left, self.left)
        return (to_right, to_left)

    def step(self, gate=()):
        stage, stages, half, rows = self.done, self.stages, self.half, self.rows
        self.done += 1
        ids = [(self.place + k) % self.size for k in (stages - stage, stage - stages)]
        at = jnp.stack(ids).astype(jnp.int32)
        whole = lambda i, at: (0, 0)
        if stage == 0:
            blocks = [(half, lambda i, at: (2 * at[0], 0)), (half, lambda i, at: (2 * at[1] + 1, 0))]
            out = self.call(first_kernel, at, blocks, [], half, 1, gate, ((half, whole), []))
            return self.send([out[0]], [out[1]])
        if stage < stages:
            blocks = [
                (half, lambda i, at: (2 * at[0] + i, 0)), (half, lambda i, at: (2 * at[1] + i, 0)),
            ]
            here = (half, lambda i, at: (i, 0))
            got = (half, whole) if stage == 1 else here
            kernel = functools.partial(pass_kernel, stage == 1)
            extra = self.from_left + self.from_right
            out = self.call(kernel, at, blocks, extra, rows, 2, gate, (here, [got, got]))
            return self.send([out[0]], [out[1]])
        if stage == stages:
            got = (half if stages == 1 else rows, whole)
            kernel = functools.partial(total_kernel, stages == 1)
            extra = self.from_left + self.from_right
            blocks = [(rows, lambda i, at: (at[0], 0))]
            blocks = [(half, lambda i, at: (2 * at[0] + i, 0))] if stages > 1 else blocks
            here = (half, lambda i, at: (i, 0)) if stages > 1 else (rows, whole)
            got = here if stages > 1 else got
            grid = 2 if stages > 1 else 1
            out = self.call(kernel, at, blocks, extra, rows, grid, gate, (here, [got, got]), 1)
            to_right = to_left = list(out)
            self.see(to_right, 0)
        else:
            to_right, to_left = after((self.from_left, self.from_right), gate)
            self.see(to_right, stages - stage)
            self.see(to_left, stage - stages)
        if stage == 2 * stages - 1:
            to_right, to_left = [to_right[0][:half]], [to_left[0][half:]]
        return self.send(to_right, to_left)

    def came(self):
        return self.from_left + self.from_right

    def see(self, items, k):
        self.seen.append((items[0], (k, 0)))

    def finish(self, gate=()):
        self.seen += [(self.from_left[0], (-self.stages, 0)), (self.from_right[0], (self.stages, 1))]
        items = after([item for item, _ in self.seen], gate)
        spots = [((k + self.size) % self.size, bottom) for _, (k, bottom) in self.seen]
        length = self.arrays[0].shape[0]
        step = math.gcd(*[width for width, _ in self.parts])
        spans, specs, shapes, low = [], [], [], 0
        for width, form in self.parts:
            count = width // step
            spans.append((low, low + count, form))

            def column(i, at, low=low, count=count):
                return jnp.clip(i - low, 0, count - 1)

            if form is turned:
                shapes.append((width, length))
                specs.append(pl.BlockSpec((step, length), lambda i, at, f=column: (f(i, at), 0)))
            else:
                shapes.append((length, width))
                specs.append(pl.BlockSpec((length, step), lambda i, at, f=column: (0, f(i, at))))
            low += count
        moved = 6 * length * self.width
        return pl.pallas_call(
            functools.partial(place_kernel, spots, spans),
            grid_spec=pltpu.PrefetchScalarGridSpec(
                num_scalar_prefetch=1,
                grid=(low,),
                in_specs=[pl.BlockSpec((item.shape[0], step), lambda i, at: (0, i)) for item in items],
                out_specs=specs,
                scratch_shapes=[pltpu.VMEM((length, step), F32)],
            ),
            out_shape=[sds(shape, F32) for shape in shapes],
            compiler_params=pltpu.CompilerParams(vmem_limit_bytes=60 << 20),
            cost_estimate=pl.CostEstimate(flops=moved, bytes_accessed=moved, transcendentals=0),
        )(self.place.reshape(1).astype(jnp.int32), *items)


class WholeSum:
    came = staticmethod(lambda: ())

    def __init__(self, arrays, parts):
        self.arrays, self.parts, self.steps, self.done = list(arrays), parts, 1, 0

    def step(self, gate=()):
        self.done += 1
        values = after(jnp.concatenate(self.arrays, 1), gate)
        self.total = lax.psum(values, "rows").astype(F32)
        return ()

    def finish(self, gate=()):
        edges = [sum(width for width, _ in self.parts[:k]) for k in range(len(self.parts) + 1)]
        return [
            form(self.total[:, edges[k] : edges[k + 1]]) for k, (_, form) in enumerate(self.parts)
        ]


def row_sum(arrays, parts):
    size = lax.axis_size("rows")
    fits = size % 2 == 0 and arrays[0].shape[0] % (16 * size) == 0
    return (RowSum if fits else WholeSum)(arrays, parts)


def start_sum(arrays):
    if arrays[0].shape[1] == arrays[1].shape[1]:
        arrays = [jnp.concatenate(arrays, 0)]
    return [lax.psum_scatter(item, "rows", scatter_dimension=0, tiled=True) for item in arrays]


def end_sum(shares):
    return [lax.all_gather(item, "rows", axis=0, tiled=True) for item in shares]


def split_sum(whole, rows):
    if len(whole) == 1:
        whole = [whole[0][:rows], whole[0][rows:]]
    return [item.astype(F32) for item in whole]


class RowSums:
    def __init__(self, arrays, parts):
        if all(item.shape[0] == arrays[0].shape[0] for item in arrays):
            self.items = [row_sum(arrays, parts)]
        else:
            self.items = [row_sum([item], [part]) for item, part in zip(arrays, parts)]

    def came(self):
        return [item.came() for item in self.items]

    @property
    def done(self):
        return self.items[0].done

    @property
    def left(self):
        return max(item.steps - item.done for item in self.items)

    def step(self, gate=()):
        for item in self.items:
            if item.done < item.steps:
                gate = item.step(gate)
        return gate

    def finish(self, gate=()):
        while self.left:
            gate = self.step(gate)
        return [out for item in self.items for out in item.finish(gate)]


def sum_cube(values, axis, late=()):
    size = lax.axis_size(axis)
    if size & (size - 1):
        return lax.psum(values, axis)
    distance = 1
    while distance < size:
        values = values + lax.ppermute(values, axis, [(i, i ^ distance) for i in range(size)])
        values = after(values, late)
        distance *= 2
    return values


def halo(own, reach):
    size = lax.axis_size("tp")
    left = lax.ppermute(own[-reach:], "tp", [(i, i + 1) for i in range(size - 1)])
    right = lax.ppermute(own[:reach], "tp", [(i + 1, i) for i in range(size - 1)])
    return jnp.concatenate([left, own, right], 0)


def to_true(values):
    size, mine = lax.axis_size("tp"), lax.axis_index("tp")
    rows = values.shape[0] // size
    return jnp.concatenate(
        [lax.dynamic_slice_in_dim(values, (mine ^ k) * rows, rows, 0) for k in range(size)], 0
    )


def ffn_forward(values, gain, weight_up, weight_down):
    normed, unit, inverse = normalize(values, gain)
    near, far = halves(gather(normed.astype(B16), True))
    pre, act = [], []
    for half in (near, far):
        pre.append(dot(after(half, act), weight_up))
        act.append((pre[-1] * jax.nn.sigmoid(pre[-1])).astype(B16))
    total, (sent, _) = scatter(pieces(act[0], act[1], weight_down, (1, 0)))
    pre = [item.astype(B16) for item in pre]
    return (values + 0.5 * total, (unit, inverse, (near, far), pre, act), sent)


def ffn_backward(grad, kept, gain, weight_up, weight_down, use=None):
    unit, inverse, wide, pre, act = kept
    own = (0.5 * grad).astype(B16)
    cot = halves(gather(own, True))
    d_pre = []
    for half in (0, 1):
        d_act = dot(after(cot[half], d_pre), weight_down, (1, 1))
        d_pre.append((d_act * swish_slope(pre[half].astype(F32))).astype(B16))
    d_norm, (sent, _) = scatter(pieces(d_pre[0], d_pre[1], weight_up, (1, 1)))
    cot, d_pre = after((cot, d_pre), sent)
    grad_down = dot(jnp.concatenate(act, 0), jnp.concatenate(cot, 0), (0, 0))
    grad_up = dot(jnp.concatenate(wide, 0), jnp.concatenate(d_pre, 0), (0, 0))
    grads = (grad_up.astype(B16), grad_down.astype(B16))
    if use is not None:
        d_norm = after(d_norm, use(grads))
    d_in, grad_gain = normalize_back(d_norm, unit, inverse, gain)
    return (grad + d_in, grad_gain, grads, (own, sent))


def places(slots):
    size, mine = lax.axis_size("tp"), lax.axis_index("tp")
    rows = slots // size
    if rows % TK:
        q_at = jnp.arange(slots // TQ, dtype=jnp.int32) * TQ
        k_at = jnp.arange(slots // TK, dtype=jnp.int32) * TK
        return q_at, k_at, True
    q_true = jnp.arange(slots // TQ, dtype=jnp.int32) * TQ
    k_true = jnp.arange(slots // TK, dtype=jnp.int32) * TK
    q_at = ((q_true // rows) ^ mine) * rows + q_true % rows
    k_at = ((k_true // rows) ^ mine) * rows + k_true % rows
    return q_at.astype(jnp.int32), k_at.astype(jnp.int32), False


def attend_forward(
    values, gain, weights, attend_out, content_bias, position_bias, code, spans, rel, prefetch
):
    slots = code.shape[0]
    width = attend_out.shape[0]
    q_at, k_at, reorder = places(slots)
    where = (spans, q_at, k_at)
    normed, unit, inverse = normalize(values, gain)
    slots_in = gather(normed.astype(B16), True, (rel, spans))
    near, far = halves(slots_in)
    mixed = [dot(near, weights)]
    far = after(far, mixed)
    fetched, came = prefetch(slots_in[len(slots_in) // 2])
    mixed.append(dot(far, weights))
    flat = lambda bias: bias.astype(F32).reshape(1, width)
    join = lambda items: jnp.concatenate(items, 0)
    q_content = join([(item[:, :width] + flat(content_bias)).astype(B16) for item in mixed])
    q_position = join([(item[:, :width] + flat(position_bias)).astype(B16) for item in mixed])
    key = join([item[:, width : 2 * width].astype(B16) for item in mixed])
    value = join([item[:, 2 * width :].astype(B16) for item in mixed])
    if reorder:
        q_content, q_position, key, value = map(to_true, (q_content, q_position, key, value))
    operands = (
        where
        + (q_content, q_position, key, value, rel)
        + (code.reshape(slots, 1), code.reshape(slots // TK, 1, TK))
    )
    heads_out, heads_wide, sums = attend(*operands)
    sent = after(to_true(heads_out) if reorder else heads_out, came)
    half = slots // 2
    total, _ = scatter(pieces(sent[:half], sent[half:], attend_out, (1, 0)))
    kept = (unit, inverse, (near, far), operands, heads_wide, sums, sent)
    return (values + total, kept, fetched)


def attend_backward(grad, cot, kept, gain, weights, attend_out, table, filler, use):
    unit, inverse, wide, operands, heads_wide, sums, sent = kept
    slots, width = sent.shape
    _, _, reorder = places(slots)
    cot = halves(cot)
    d_near = dot(cot[0], attend_out, (1, 1)).astype(B16)
    cot = (cot[0], after(cot[1], d_near))
    d_heads = jnp.concatenate([d_near, dot(cot[1], attend_out, (1, 1)).astype(B16)], 0)
    if reorder:
        d_heads = to_true(d_heads)
    d_heads = after(d_heads, filler[0])
    d_all, d_rel, d_bias = attend_back(*operands, d_heads, heads_wide, sums)
    if reorder:
        d_all = to_true(d_all)
    d_all = after(d_all, filler[1])
    half = slots // 2
    d_norm, (last, _) = scatter(pieces(d_all[:half], d_all[half:], weights, (1, 1)))
    cot, d_all, d_rel = after((cot, d_all, d_rel), last)
    grad_out = dot(jnp.concatenate(cot, 0), sent, (0, 0))
    grad_all = dot(jnp.concatenate(wide, 0), d_all, (0, 0))
    grad_pos = dot(table, d_rel, (0, 0))
    grads = [item.astype(B16) for item in (grad_all, grad_pos, grad_out)]
    d_norm = after(d_norm, use(grads, last))
    d_in, grad_gain = normalize_back(d_norm, unit, inverse, gain)
    return (grad + d_in, grad_gain, d_bias[:2])


def conv_weights(point_in, depth_kernel, gain_inner, point_out, first):
    taps = depth_kernel.shape[0]
    own = after((point_in[:, 0], point_in[:, 1], point_out), first)
    small = gather(jnp.concatenate([depth_kernel, gain_inner[None]], 0))
    small = jnp.concatenate(small, 1).astype(F32)
    in_a, in_b, out = map(gather, own)
    arrived = [item[2::2] for item in (in_a, in_b, out)]
    in_a, in_b = jnp.concatenate(in_a, 1), jnp.concatenate(in_b, 1)
    return (in_a, in_b, small[:taps], small[taps], jnp.concatenate(out, 0)), arrived


def conv_masks(segments, valid, rows, taps):
    edge = 8
    reach = taps // 2
    base = lax.axis_index("tp") * rows + edge - reach
    wide_segments = jnp.pad(segments, edge, constant_values=-1)
    wide_valid = jnp.pad(valid, edge)
    own = lax.dynamic_slice_in_dim(wide_segments, base, rows + 2 * reach)
    masks = []
    for tap in range(taps):
        other = lax.dynamic_slice_in_dim(wide_segments, base + tap - reach, rows + 2 * reach)
        good = lax.dynamic_slice_in_dim(wide_valid, base + tap - reach, rows + 2 * reach)
        masks.append(((other == own) & (good == 1)).astype(F32)[:, None])
    return masks


def conv_forward(values, gain, full, masks):
    in_a, in_b, kernel, gain_inner, out = full
    rows = values.shape[0]
    taps = kernel.shape[0]
    reach = taps // 2
    normed, unit, inverse = normalize(values, gain)
    low = normed.astype(B16)
    wide = halo(low, 2 * reach)
    mixed_a = dot(wide, in_a)
    gate = jax.nn.sigmoid(dot(wide, in_b))
    glu = mixed_a * gate
    depth = 0.0
    for tap in range(taps):
        depth = depth + kernel[tap] * masks[tap] * glu[tap : tap + rows + 2 * reach]
    depth_norm, inner_unit, inner_inverse = normalize(depth, gain_inner)
    inner = (depth_norm * jax.nn.sigmoid(depth_norm)).astype(B16)
    own = slice(2 * reach, 2 * reach + rows)
    kept = (unit, inverse, low, mixed_a[own], gate[own], glu, inner_unit, inner_inverse, depth_norm, inner)
    return (values + dot(inner[reach : reach + rows], out), kept)


def conv_backward(grad, kept, gain, full, masks):
    unit, inverse, low, mixed_a, gate, glu, inner_unit, inner_inverse, depth_norm, inner = kept
    in_a, in_b, kernel, gain_inner, out = full
    rows = grad.shape[0]
    taps = kernel.shape[0]
    reach = taps // 2
    mine = slice(reach, reach + rows)
    cot = grad.astype(B16)
    d_act = dot(halo(cot, reach), out, (1, 1))
    d_depth_norm = d_act * swish_slope(depth_norm)
    d_depth, _ = normalize_back(d_depth_norm, inner_unit, inner_inverse, gain_inner)
    d_glu = 0.0
    for tap in range(taps):
        weighted = d_depth * masks[tap]
        back = 2 * reach - tap
        d_glu = d_glu + kernel[tap] * weighted[back : back + rows]
    d_a = (d_glu * gate).astype(B16)
    d_b = (d_glu * mixed_a * gate * (1.0 - gate)).astype(B16)
    d_norm = dot(d_a, in_a, (1, 1)) + dot(d_b, in_b, (1, 1))
    d_in, grad_gain = normalize_back(d_norm, unit, inverse, gain)
    grad = grad + d_in
    slots = gather(grad.astype(B16), True)
    low, cot, d_a, d_b, inner = after((low, cot, d_a, d_b, inner), slots[1])
    size = lax.axis_size("tp")
    width = in_a.shape[1] // size
    parts = []
    grads = [
        dot(left, right, (0, 0)).astype(B16)
        for left, right in ((low, d_a), (low, d_b), (cot, inner[mine]))
    ]

    def small_grads(gate):
        d_own, norm_own = after((d_depth[mine], d_depth_norm[mine]), gate)
        sums = []
        for tap in range(taps):
            near = d_own * masks[tap][mine]
            sums.append(jnp.sum(near * glu[reach + tap : reach + tap + rows], axis=0))
        sums.append(jnp.sum(norm_own * inner_unit[mine], axis=0))
        small = jnp.stack(sums, 0)
        return scatter([small[:, k * width : (k + 1) * width] for k in range(size)])[0]

    for slot in range(size):
        cols = slice(slot * width, (slot + 1) * width)
        parts.append(jnp.concatenate([item[:, cols] for item in grads], 1))
    total, ends = scatter(parts, slots[-1], False)
    return (grad, slots, grad_gain, (total, small_grads), ends)


def body(
    layer_input,
    cotangent,
    segments,
    valid_frames,
    gain_first,
    up_first,
    down_first,
    gain_attend,
    query_weight,
    key_weight,
    value_weight,
    attend_out,
    pos_weight,
    content_bias,
    position_bias,
    gain_conv,
    point_in,
    depth_kernel,
    gain_inner,
    point_out,
    gain_second,
    up_second,
    down_second,
    gain_final,
):
    segment_row, valid_row = segments[0], valid_frames[0]
    weights = jnp.concatenate([query_weight, key_weight, value_weight], 1)
    width = query_weight.shape[1]
    taps = depth_kernel.shape[0]
    values = layer_input[0].astype(F32)
    rows = values.shape[0]
    slots = segment_row.shape[0]
    masks = conv_masks(segment_row, valid_row, rows, taps)
    code = codes(segment_row, valid_row)
    spans = spans_of(code)
    values, kept_first, sent = ffn_forward(values, gain_first, up_first, down_first)
    table = distance_table(slots, values.shape[1], sent)
    rel = dot(table, pos_weight).astype(B16)
    prefetch = functools.partial(conv_weights, point_in, depth_kernel, gain_inner, point_out)
    values, kept_attend, full = attend_forward(
        values, gain_attend, weights, attend_out, content_bias, position_bias, code, spans, rel, prefetch
    )
    values, kept_conv = conv_forward(values, gain_conv, full, masks)
    values, kept_second, _ = ffn_forward(values, gain_second, up_second, down_second)
    final, final_unit, final_inverse = normalize(values, gain_final)
    layer_output = final.astype(B16)
    grad, sum_final = normalize_back(cotangent[0].astype(F32), final_unit, final_inverse, gain_final)
    held = {}

    def start_second(grads):
        held["second"] = start_sum(grads)
        return grads

    grad, sum_second, _, _ = ffn_backward(
        grad, kept_second, gain_second, up_second, down_second, start_second
    )
    grad, cot, sum_conv, conv_grads, ends = conv_backward(grad, kept_conv, gain_conv, full, masks)
    ends = (ends[0], (ends, held["second"]))

    def start_middle(grads, last):
        own, got = after((conv_grads[0], ends[1][0][1]), last)
        total = (own.astype(F32) + got.astype(F32)).astype(B16)
        forms = [(width, plain)] * 4 + [(width, turned), (2 * width, plain), (width, turned)]
        held["middle"] = row_sum(grads + [total], forms)
        return held["middle"].step()

    grad, sum_attend, d_bias = attend_backward(
        grad, cot, kept_attend, gain_attend, weights, attend_out, table, ends, start_middle
    )
    middle = held["middle"]
    second_sum = end_sum(held["second"])
    grad, sum_first, first_grads, marks = ffn_backward(
        grad, kept_first, gain_first, up_first, down_first
    )
    first = RowSums(first_grads, [(item.shape[1], plain) for item in first_grads])
    token = middle.step(marks[1])
    token = middle.step(first.step(token))
    second_sum = after(second_sum, token)
    token = second_sum
    while middle.done < middle.steps:
        token = middle.step(token)
        if first.left > 1:
            token = first.step(token)
        if first.done == 3:
            token = (token, grad)
        if first.done == 5:
            second_up, second_down = split_sum(after(second_sum, token), up_second.shape[0])
            token = (token, second_up, second_down)
    while first.left:
        gate = (token, middle.came()) if first.left == 1 else token
        token = first.step(gate)
    pairs = (sum_first, sum_attend, sum_conv, sum_second, sum_final)
    gains = sum_cube(gain_sums(pairs, marks[1]), "tp")
    small = jnp.concatenate([conv_grads[1](marks[1]), d_bias], 0)
    small_shape = small.shape
    pack = jnp.concatenate([gains.reshape(-1), small.reshape(-1)]).reshape(-1, width)
    pack = sum_cube(after(pack, token), "rows", first.came())
    attend_sum = middle.finish(token)
    first_sum = first.finish(attend_sum)
    pack = pack.reshape(-1)
    gains, small = pack[: gains.size].reshape(gains.shape), pack[gains.size :].reshape(small_shape)
    bias_shape = content_bias.shape
    return (
        layer_output[None],
        grad[None],
        gains[0],
        first_sum[0],
        first_sum[1],
        gains[1],
        attend_sum[0],
        attend_sum[1],
        attend_sum[2],
        attend_sum[4],
        attend_sum[3],
        small[taps + 1].reshape(bias_shape),
        small[taps + 2].reshape(bias_shape),
        gains[2],
        attend_sum[5].reshape(attend_sum[5].shape[0], 2, width),
        small[:taps],
        small[taps],
        attend_sum[6],
        gains[3],
        second_up,
        second_down,
        gains[4],
    )


def solution(mesh):
    in_specs = (
        P("rows", "tp", None),
        P("rows", "tp", None),
        P("rows", None),
        P("rows", None),
        P(),
        P(None, "tp"),
        P("tp", None),
        P(),
        P(None, "tp"),
        P(None, "tp"),
        P(None, "tp"),
        P("tp", None),
        P(None, "tp"),
        P("tp", None),
        P("tp", None),
        P(),
        P(None, None, "tp"),
        P(None, "tp"),
        P("tp"),
        P("tp", None),
        P(),
        P(None, "tp"),
        P("tp", None),
        P(),
    )
    out_specs = (
        P("rows", "tp", None),
        P("rows", "tp", None),
        P(),
        P(None, "tp"),
        P("tp", None),
        P(),
        P(None, "tp"),
        P(None, "tp"),
        P(None, "tp"),
        P("tp", None),
        P(None, "tp"),
        P("tp", None),
        P("tp", None),
        P(),
        P(None, None, "tp"),
        P(None, "tp"),
        P("tp"),
        P("tp", None),
        P(),
        P(None, "tp"),
        P("tp", None),
        P(),
    )
    return jax.shard_map(body, mesh=mesh, in_specs=in_specs, out_specs=out_specs, check_vma=False)
```

```python
import functools
import math

import jax
import jax.numpy as jnp
from jax import lax
from jax.experimental import pallas as pl
from jax.experimental.pallas import tpu as pltpu
from jax.sharding import PartitionSpec as P

EPS = 1e-05
NEG = -1e30
F32 = jnp.float32
B16 = jnp.bfloat16
TQ = 128
TK = 384
HD = 128
STEP = 64
LINK_BYTES = 180_000_000
SM = pl.BlockSpec(memory_space=pltpu.SMEM)
VM = pl.BlockSpec(memory_space=pltpu.VMEM)

def dotx(a, b, ca, cb):
    return lax.dot_general(a, b, (((ca,), (cb,)), ((), ())), preferred_element_type=F32)

def skew_tile(grid):
    return pltpu.roll(grid, TK + 1, 1, stride=1, stride_axis=0)[:, :TK]

def unskew_flipped(flipped):
    wide = jnp.concatenate([flipped, jnp.zeros((TQ, TQ), F32)], axis=1)
    return pltpu.roll(wide, 0, 1, stride=1, stride_axis=0)

def attend_kernel(heads, spans, q_at, k_at, qc_ref, qp_ref, k_ref, v_ref, rel_ref, code_q_ref, code_k_ref,
                  out_ref, wide_ref, lse_ref):
    slots = qc_ref.shape[0]
    scale = HD ** -0.5
    blocks, tiles = slots // TQ, slots // TK

    def q_step(qb, _):
        at = pl.multiple_of(q_at[qb], TQ)
        true_at = pl.multiple_of(qb * TQ, TQ)
        code_q = code_q_ref[pl.ds(true_at, TQ), :]
        qc = [qc_ref[pl.ds(at, TQ), h * HD:(h + 1) * HD] for h in range(heads)]
        qp = [qp_ref[pl.ds(at, TQ), h * HD:(h + 1) * HD] for h in range(heads)]

        def k_step(kt, carry):
            ko = pl.multiple_of(k_at[kt], TQ)
            to = pl.multiple_of((blocks - 1 + kt * (TK // TQ) - qb) * TQ, TQ)
            mask = code_q == code_k_ref[kt]
            new = []
            for h in range(heads):
                lanes = slice(h * HD, (h + 1) * HD)
                top, total, acc = carry[h]
                grid = dotx(qp[h], rel_ref[pl.ds(to, TK + TQ), lanes], 1, 1)
                raw = dotx(qc[h], k_ref[pl.ds(ko, TK), lanes], 1, 1) + skew_tile(grid)
                scores = jnp.where(mask, raw * scale, NEG)
                top_new = jnp.maximum(top, jnp.max(scores, axis=1, keepdims=True))
                shrink = jnp.exp(top - top_new)
                weights = jnp.exp(scores - top_new)
                total = total * shrink + jnp.sum(weights, axis=1, keepdims=True)
                acc = acc * shrink + dotx(weights.astype(B16), v_ref[pl.ds(ko, TK), lanes], 1, 0)
                new.append((top_new, total, acc))
            return tuple(new)

        first = tuple((jnp.full((TQ, 1), NEG, F32), jnp.zeros((TQ, 1), F32), jnp.zeros((TQ, HD), F32))
                      for _ in range(heads))
        final = lax.fori_loop(spans[0, qb], spans[1, qb], k_step, first)
        for h in range(heads):
            lanes = slice(h * HD, (h + 1) * HD)
            top, total, acc = final[h]
            out = acc / total
            wide_ref[pl.ds(at, TQ), lanes] = out
            out_ref[pl.ds(at, TQ), lanes] = out.astype(B16)
            lse_ref[pl.ds(at, TQ), h:h + 1] = top + jnp.log(total)
        return 0

    lax.fori_loop(0, blocks, q_step, 0)

def attend_back_kernel(heads, spans, q_at, k_at, qc_ref, qp_ref, k_ref, v_ref, rel_ref, code_q_ref, code_k_ref,
                       d_out_ref, wide_ref, lse_ref,
                       all_ref, drel_ref, bias_ref, dk_acc, dv_acc, drel_acc):
    slots = qc_ref.shape[0]
    scale = HD ** -0.5
    blocks, tiles = slots // TQ, slots // TK
    dk_acc[...] = jnp.zeros_like(dk_acc)
    dv_acc[...] = jnp.zeros_like(dv_acc)
    drel_acc[...] = jnp.zeros_like(drel_acc)
    bias_ref[...] = jnp.zeros_like(bias_ref)
    row = lax.broadcasted_iota(jnp.int32, (TQ, TQ), 0)
    column = lax.broadcasted_iota(jnp.int32, (TQ, TQ), 1)
    flip = (row + column == TQ - 1).astype(F32)
    flip_low = flip.astype(B16)

    def q_step(qb, _):
        at = pl.multiple_of(q_at[qb], TQ)
        true_at = pl.multiple_of(qb * TQ, TQ)
        code_q = code_q_ref[pl.ds(true_at, TQ), :]
        cols = [slice(h * HD, (h + 1) * HD) for h in range(heads)]
        qc = [qc_ref[pl.ds(at, TQ), c] for c in cols]
        qp = [qp_ref[pl.ds(at, TQ), c] for c in cols]
        qp_flipped = [dotx(flip_low, item, 1, 0).astype(B16) for item in qp]
        d_out = [d_out_ref[pl.ds(at, TQ), c] for c in cols]
        lse = [lse_ref[pl.ds(at, TQ), h:h + 1] for h in range(heads)]
        delta = [jnp.sum(d_out[h].astype(F32) * wide_ref[pl.ds(at, TQ), cols[h]], axis=1, keepdims=True)
                 for h in range(heads)]

        def k_step(kt, carry):
            ko = pl.multiple_of(k_at[kt], TQ)
            to = pl.multiple_of((blocks - 1 + kt * (TK // TQ) - qb) * TQ, TQ)
            mask = code_q == code_k_ref[kt]
            new = []
            for h in range(heads):
                lanes = cols[h]
                d_content, d_position = carry[h]
                window = rel_ref[pl.ds(to, TK + TQ), lanes]
                key = k_ref[pl.ds(ko, TK), lanes]
                grid = dotx(qp[h], window, 1, 1)
                raw = dotx(qc[h], key, 1, 1) + skew_tile(grid)
                probs = jnp.exp(jnp.where(mask, raw * scale - lse[h], NEG))
                d_probs = dotx(d_out[h], v_ref[pl.ds(ko, TK), lanes], 1, 1)
                d_raw = probs * (d_probs - delta[h]) * scale
                d_low = d_raw.astype(B16)
                d_grid = unskew_flipped(dotx(flip_low, d_low, 1, 0)).astype(B16)
                dv_acc[pl.ds(ko, TK), lanes] += dotx(probs.astype(B16), d_out[h], 0, 0)
                dk_acc[pl.ds(ko, TK), lanes] += dotx(d_low, qc[h], 0, 0)
                drel_acc[pl.ds(to, TK + TQ), lanes] += dotx(d_grid, qp_flipped[h], 0, 0)
                d_content = d_content + dotx(d_low, key, 1, 0)
                d_position = d_position + dotx(d_grid, window, 1, 0)
                new.append((d_content, d_position))
            return tuple(new)

        first = tuple((jnp.zeros((TQ, HD), F32),) * 2 for _ in range(heads))
        final = lax.fori_loop(spans[0, qb], spans[1, qb], k_step, first)
        for h in range(heads):
            d_content, d_position = final[h]
            d_position = lax.dot_general(flip, d_position, (((1,), (0,)), ((), ())),
                                         precision=lax.Precision.HIGHEST, preferred_element_type=F32)
            all_ref[pl.ds(at, TQ), cols[h]] = (d_content + d_position).astype(B16)
            bias_ref[0:1, cols[h]] += jnp.sum(d_content, axis=0, keepdims=True)
            bias_ref[1:2, cols[h]] += jnp.sum(d_position, axis=0, keepdims=True)
        return 0

    lax.fori_loop(0, blocks, q_step, 0)
    width = dk_acc.shape[1]
    all_ref[:, width : 2 * width] = dk_acc[...].astype(B16)
    all_ref[:, 2 * width :] = dv_acc[...].astype(B16)
    drel_ref[...] = drel_acc[...].astype(B16)

def sds(s, d): return jax.ShapeDtypeStruct(s, d)

def attend(spans, q_at, k_at, qc, qp, k, v, rel, code_q, code_k):
    slots, width = qc.shape
    heads = width // HD
    return pl.pallas_call(
        functools.partial(attend_kernel, heads),
        out_shape=(sds((slots, width), B16), sds((slots, width), F32), sds((slots, heads), F32)),
        in_specs=[SM] * 3 + [VM] * 7, out_specs=(VM,) * 3,
        compiler_params=pltpu.CompilerParams(vmem_limit_bytes=40 << 20),
        cost_estimate=pl.CostEstimate(flops=int(4e9), bytes_accessed=int(9e6), transcendentals=int(2e6)),
    )(spans, q_at, k_at, qc, qp, k, v, rel, code_q, code_k)

def attend_back(spans, q_at, k_at, qc, qp, k, v, rel, code_q, code_k, d_out, wide, lse):
    slots, width = qc.shape
    heads = width // HD
    return pl.pallas_call(
        functools.partial(attend_back_kernel, heads),
        out_shape=(sds((slots, 3 * width), B16), sds((2 * slots, width), B16), sds((8, width), F32)),
        in_specs=[SM] * 3 + [VM] * 10, out_specs=(VM,) * 3,
        scratch_shapes=[pltpu.VMEM((slots, width), F32), pltpu.VMEM((slots, width), F32), pltpu.VMEM((2 * slots, width), F32)],
        compiler_params=pltpu.CompilerParams(vmem_limit_bytes=48 << 20),
        cost_estimate=pl.CostEstimate(flops=int(1e6), bytes_accessed=int(1e6), transcendentals=0),
    )(spans, q_at, k_at, qc, qp, k, v, rel, code_q, code_k, d_out, wide, lse)

def codes(segments, valid):
    slots = segments.shape[0]
    place = jnp.arange(slots, dtype=jnp.int32)
    code = jnp.where(valid == 1, segments, -1 - place)
    return code

def spans_of(code):
    slots = code.shape[0]
    same = code[:, None] == code[None, :]
    touch = jnp.any(same.reshape(slots // TQ, TQ, slots // TK, TK), axis=(1, 3))
    tiles = slots // TK
    idx = jnp.arange(tiles, dtype=jnp.int32)
    lo = jnp.min(jnp.where(touch, idx, tiles), axis=1)
    hi = jnp.max(jnp.where(touch, idx + 1, 0), axis=1)
    return jnp.stack([lo, hi], 0).astype(jnp.int32)


def normalize(values, gain):
    mean = jnp.mean(values, axis=-1, keepdims=True)
    centered = values - mean
    inverse = lax.rsqrt(jnp.mean(centered * centered, axis=-1, keepdims=True) + EPS)
    unit = centered * inverse
    return (unit * gain.astype(F32), unit, inverse)


def normalize_back(grad, unit, inverse, gain):
    scaled = grad * gain.astype(F32)
    first = jnp.mean(scaled, axis=-1, keepdims=True)
    second = jnp.mean(scaled * unit, axis=-1, keepdims=True)
    return (inverse * (scaled - first - unit * second), (grad, unit))


def gain_sums(pairs, gate):
    return jnp.stack([jnp.sum(grad * unit, axis=0) for grad, unit in after(pairs, gate)])


def swish_slope(values):
    gate = jax.nn.sigmoid(values)
    return gate * (1.0 + values * (1.0 - gate))


def distance_table(slots, width, first):
    column = jnp.arange(width)
    even = (column % 2 == 0)[None, :]
    rate = jnp.exp(-(column - column % 2).astype(F32) * (math.log(10000.0) / width))
    coarse = (slots - 1 - STEP * jnp.arange(2 * slots // STEP)).astype(F32)[:, None] * rate[None, :]
    fine = jnp.arange(STEP).astype(F32)[:, None] * rate[None, :]
    sin_c, cos_c = jnp.sin(coarse), jnp.cos(coarse)
    with_cos = jnp.where(even, sin_c, cos_c)
    with_sin = jnp.where(even, -cos_c, sin_c)
    with_cos, with_sin, sin_f, cos_f = after((with_cos, with_sin, jnp.sin(fine), jnp.cos(fine)), first)
    table = with_cos[:, None, :] * cos_f[None] + with_sin[:, None, :] * sin_f[None]
    return table.reshape(2 * slots, width).astype(B16)


def dot(left, right, contract=(1, 0)):
    return lax.dot_general(
        left, right, (((contract[0],), (contract[1],)), ((), ())), preferred_element_type=F32
    )


def swap(values, distance):
    size = lax.axis_size("tp")
    return lax.ppermute(values, "tp", [(i, i ^ distance) for i in range(size)])


def distances():
    size = lax.axis_size("tp")
    return [1 << bit for bit in range(size.bit_length() - 1)]


def same_kernel(block_ref, out_ref):
    pass


def arrived(block):
    spec = pl.BlockSpec(memory_space=pl.ANY)
    return pl.pallas_call(
        same_kernel,
        in_specs=[spec],
        out_specs=spec,
        out_shape=jax.ShapeDtypeStruct(block.shape, block.dtype),
        input_output_aliases={0: 0},
        cost_estimate=pl.CostEstimate(flops=0, bytes_accessed=LINK_BYTES, transcendentals=0),
    )(block)


def gather(own, first=False, late=()):
    slots = {0: own}
    for distance in reversed(distances()):
        for slot in list(slots):
            slots[slot ^ distance] = swap(slots[slot], distance)
            if distance == distances()[-1]:
                slots[slot ^ distance] = after(slots[slot ^ distance], late)
    last = len(slots) - 1
    if first:
        slots[last] = arrived(slots[last])
    return [slots[slot] for slot in range(len(slots))]


def scatter(parts, late=(), add=True):
    parts = dict(enumerate(parts))
    sent = got = None
    for distance in distances():
        for slot in sorted(parts, reverse=True):
            if slot & distance:
                sent = parts.pop(slot).astype(B16)
                if distance == distances()[-1]:
                    sent = after(sent, late)
                got = swap(sent, distance)
                if add or distance != distances()[-1]:
                    parts[slot ^ distance] = parts[slot ^ distance].astype(F32) + got.astype(F32)
    return parts[0], (sent, got)


def after(values, *others):
    return lax.optimization_barrier((values, others))[0]


def halves(slots):
    half = len(slots) // 2
    return jnp.concatenate(slots[:half], 0), jnp.concatenate(slots[half:], 0)


def pieces(near, far, weight, contract):
    count = lax.axis_size("tp") // 2
    rows = near.shape[0] // count
    outs = {}
    for slot in reversed(range(2 * count)):
        source, place = (near, slot) if slot < count else (far, slot - count)
        outs[slot] = dot(source[place * rows : (place + 1) * rows], weight, contract)
    return [outs[slot] for slot in range(2 * count)]


def ring():
    size, mine = lax.axis_size("rows"), lax.axis_index("rows")
    order = list(range(0, size, 2)) + list(range(size - 1, 0, -2))
    place = jnp.where(mine % 2 == 0, mine // 2, size - (mine + 1) // 2)
    right = [(order[i], order[(i + 1) % size]) for i in range(size)]
    return size, place, right, [(there, here) for here, there in right]


def plain(piece):
    return piece


def turned(piece):
    return piece.T


def first_kernel(at, *refs):
    count = (len(refs) - 2) // 2
    refs[-2][...] = jnp.concatenate([ref[...] for ref in refs[:count]], 1)
    refs[-1][...] = jnp.concatenate([ref[...] for ref in refs[count:-2]], 1)


def pass_kernel(second, at, *refs):
    count = (len(refs) - 4) // 2
    from_left, from_right = (ref[...].astype(F32) for ref in refs[-4:-2])
    if second:
        top = pl.program_id(0) == 0
        from_left = jnp.where(top, from_left, 0.0)
        from_right = jnp.where(top, 0.0, from_right)
    own = jnp.concatenate([ref[...] for ref in refs[:count]], 1).astype(F32)
    refs[-2][...] = (own + from_left).astype(B16)
    own = jnp.concatenate([ref[...] for ref in refs[count:-4]], 1).astype(F32)
    refs[-1][...] = (own + from_right).astype(B16)


def total_kernel(split, at, *refs):
    own = jnp.concatenate([ref[...] for ref in refs[:-3]], 1).astype(F32)
    from_left, from_right = (ref[...].astype(F32) for ref in refs[-3:-1])
    if split:
        refs[-1][...] = (own + jnp.concatenate([from_left, from_right], 0)).astype(B16)
    else:
        refs[-1][...] = (own + from_left + from_right).astype(B16)


def place_kernel(spots, spans, at, *refs):
    count = len(spots)
    outs, held = refs[count : count + len(spans)], refs[-1]
    half = refs[count - 1].shape[0]
    size = held.shape[0] // (2 * half)
    for ref, (k, bottom) in zip(refs[:count], spots):
        start = ((at[0] + k) % size) * (2 * half) + bottom * half
        start = pl.multiple_of(start, half)
        held[pl.ds(start, ref.shape[0]), :] = ref[...].astype(F32)
    for out, (low, high, form) in zip(outs, spans):
        here = (pl.program_id(0) >= low) & (pl.program_id(0) < high)

        @pl.when(here)
        def _(out=out, form=form):
            out[...] = form(held[...])


class RowSum:
    def __init__(self, arrays, parts):
        self.size, self.place, self.right, self.left = ring()
        self.arrays, self.parts = list(arrays), parts
        self.width = sum(item.shape[1] for item in arrays)
        self.rows = arrays[0].shape[0] // self.size
        self.half = self.rows // 2
        self.stages = self.size // 2
        self.steps = 2 * self.stages
        self.done = 0
        self.seen = []

    def call(self, kernel, at, blocks, extra, out_rows, grid, gate, out_blocks, count=2):
        arrays, extra = after((self.arrays, extra), gate)
        specs, operands = [], []
        for rows, index in blocks:
            for item in arrays:
                specs.append(pl.BlockSpec((rows, item.shape[1]), index))
                operands.append(item)
        for item, (rows, index) in zip(extra, out_blocks[1]):
            specs.append(pl.BlockSpec((rows, self.width), index))
            operands.append(item)
        rows, index = out_blocks[0]
        moved = sum(2 * rows * self.width for _ in range(4))
        return pl.pallas_call(
            kernel,
            grid_spec=pltpu.PrefetchScalarGridSpec(
                num_scalar_prefetch=1,
                grid=(grid,),
                in_specs=specs,
                out_specs=[pl.BlockSpec((rows, self.width), index)] * count,
            ),
            out_shape=(sds((out_rows, self.width), B16),) * count,
            cost_estimate=pl.CostEstimate(flops=moved, bytes_accessed=moved, transcendentals=0),
        )(at, *operands)

    def send(self, to_right, to_left):
        over = lambda items, way: [lax.ppermute(item, "rows", way) for item in items]
        self.from_left, self.from_right = over(to_right, self.right), over(to_left, self.left)
        return (to_right, to_left)

    def step(self, gate=()):
        stage, stages, half, rows = self.done, self.stages, self.half, self.rows
        self.done += 1
        ids = [(self.place + k) % self.size for k in (stages - stage, stage - stages)]
        at = jnp.stack(ids).astype(jnp.int32)
        whole = lambda i, at: (0, 0)
        if stage == 0:
            blocks = [(half, lambda i, at: (2 * at[0], 0)), (half, lambda i, at: (2 * at[1] + 1, 0))]
            out = self.call(first_kernel, at, blocks, [], half, 1, gate, ((half, whole), []))
            return self.send([out[0]], [out[1]])
        if stage < stages:
            blocks = [
                (half, lambda i, at: (2 * at[0] + i, 0)), (half, lambda i, at: (2 * at[1] + i, 0)),
            ]
            here = (half, lambda i, at: (i, 0))
            got = (half, whole) if stage == 1 else here
            kernel = functools.partial(pass_kernel, stage == 1)
            extra = self.from_left + self.from_right
            out = self.call(kernel, at, blocks, extra, rows, 2, gate, (here, [got, got]))
            return self.send([out[0]], [out[1]])
        if stage == stages:
            got = (half if stages == 1 else rows, whole)
            kernel = functools.partial(total_kernel, stages == 1)
            extra = self.from_left + self.from_right
            blocks = [(rows, lambda i, at: (at[0], 0))]
            blocks = [(half, lambda i, at: (2 * at[0] + i, 0))] if stages > 1 else blocks
            here = (half, lambda i, at: (i, 0)) if stages > 1 else (rows, whole)
            got = here if stages > 1 else got
            grid = 2 if stages > 1 else 1
            out = self.call(kernel, at, blocks, extra, rows, grid, gate, (here, [got, got]), 1)
            to_right = to_left = list(out)
            self.see(to_right, 0)
        else:
            to_right, to_left = after((self.from_left, self.from_right), gate)
            self.see(to_right, stages - stage)
            self.see(to_left, stage - stages)
        if stage == 2 * stages - 1:
            to_right, to_left = [to_right[0][:half]], [to_left[0][half:]]
        return self.send(to_right, to_left)

    def came(self):
        return self.from_left + self.from_right

    def see(self, items, k):
        self.seen.append((items[0], (k, 0)))

    def finish(self, gate=()):
        self.seen += [(self.from_left[0], (-self.stages, 0)), (self.from_right[0], (self.stages, 1))]
        items = after([item for item, _ in self.seen], gate)
        spots = [((k + self.size) % self.size, bottom) for _, (k, bottom) in self.seen]
        length = self.arrays[0].shape[0]
        step = math.gcd(*[width for width, _ in self.parts])
        spans, specs, shapes, low = [], [], [], 0
        for width, form in self.parts:
            count = width // step
            spans.append((low, low + count, form))

            def column(i, at, low=low, count=count):
                return jnp.clip(i - low, 0, count - 1)

            if form is turned:
                shapes.append((width, length))
                specs.append(pl.BlockSpec((step, length), lambda i, at, f=column: (f(i, at), 0)))
            else:
                shapes.append((length, width))
                specs.append(pl.BlockSpec((length, step), lambda i, at, f=column: (0, f(i, at))))
            low += count
        moved = 6 * length * self.width
        return pl.pallas_call(
            functools.partial(place_kernel, spots, spans),
            grid_spec=pltpu.PrefetchScalarGridSpec(
                num_scalar_prefetch=1,
                grid=(low,),
                in_specs=[pl.BlockSpec((item.shape[0], step), lambda i, at: (0, i)) for item in items],
                out_specs=specs,
                scratch_shapes=[pltpu.VMEM((length, step), F32)],
            ),
            out_shape=[sds(shape, F32) for shape in shapes],
            compiler_params=pltpu.CompilerParams(vmem_limit_bytes=60 << 20),
            cost_estimate=pl.CostEstimate(flops=moved, bytes_accessed=moved, transcendentals=0),
        )(self.place.reshape(1).astype(jnp.int32), *items)


class WholeSum:
    came = staticmethod(lambda: ())

    def __init__(self, arrays, parts):
        self.arrays, self.parts, self.steps, self.done = list(arrays), parts, 1, 0

    def step(self, gate=()):
        self.done += 1
        values = after(jnp.concatenate(self.arrays, 1), gate)
        self.total = lax.psum(values, "rows").astype(F32)
        return ()

    def finish(self, gate=()):
        edges = [sum(width for width, _ in self.parts[:k]) for k in range(len(self.parts) + 1)]
        return [
            form(self.total[:, edges[k] : edges[k + 1]]) for k, (_, form) in enumerate(self.parts)
        ]


def row_sum(arrays, parts):
    size = lax.axis_size("rows")
    fits = size % 2 == 0 and arrays[0].shape[0] % (16 * size) == 0
    return (RowSum if fits else WholeSum)(arrays, parts)


def start_sum(arrays):
    if arrays[0].shape[1] == arrays[1].shape[1]:
        arrays = [jnp.concatenate(arrays, 0)]
    return [lax.psum_scatter(item, "rows", scatter_dimension=0, tiled=True) for item in arrays]


def end_sum(shares):
    return [lax.all_gather(item, "rows", axis=0, tiled=True) for item in shares]


def split_sum(whole, rows):
    if len(whole) == 1:
        whole = [whole[0][:rows], whole[0][rows:]]
    return [item.astype(F32) for item in whole]


class RowSums:
    def __init__(self, arrays, parts):
        if all(item.shape[0] == arrays[0].shape[0] for item in arrays):
            self.items = [row_sum(arrays, parts)]
        else:
            self.items = [row_sum([item], [part]) for item, part in zip(arrays, parts)]

    def came(self):
        return [item.came() for item in self.items]

    @property
    def done(self):
        return self.items[0].done

    @property
    def left(self):
        return max(item.steps - item.done for item in self.items)

    def step(self, gate=()):
        for item in self.items:
            if item.done < item.steps:
                gate = item.step(gate)
        return gate

    def finish(self, gate=()):
        while self.left:
            gate = self.step(gate)
        return [out for item in self.items for out in item.finish(gate)]


def sum_cube(values, axis):
    size = lax.axis_size(axis)
    if size & (size - 1):
        return lax.psum(values, axis)
    distance = 1
    while distance < size:
        values = values + lax.ppermute(values, axis, [(i, i ^ distance) for i in range(size)])
        distance *= 2
    return values


def halo(own, reach):
    size = lax.axis_size("tp")
    left = lax.ppermute(own[-reach:], "tp", [(i, i + 1) for i in range(size - 1)])
    right = lax.ppermute(own[:reach], "tp", [(i + 1, i) for i in range(size - 1)])
    return jnp.concatenate([left, own, right], 0)


def to_true(values):
    size, mine = lax.axis_size("tp"), lax.axis_index("tp")
    rows = values.shape[0] // size
    return jnp.concatenate(
        [lax.dynamic_slice_in_dim(values, (mine ^ k) * rows, rows, 0) for k in range(size)], 0
    )


def ffn_forward(values, gain, weight_up, weight_down):
    normed, unit, inverse = normalize(values, gain)
    near, far = halves(gather(normed.astype(B16)))
    pre, act = [], []
    for half in (near, far):
        pre.append(dot(after(half, act), weight_up))
        act.append((pre[-1] * jax.nn.sigmoid(pre[-1])).astype(B16))
    total, (sent, _) = scatter(pieces(act[0], act[1], weight_down, (1, 0)))
    pre = [item.astype(B16) for item in pre]
    return (values + 0.5 * total, (unit, inverse, (near, far), pre, act), sent)


def ffn_backward(grad, kept, gain, weight_up, weight_down, use=None, fill=None):
    unit, inverse, wide, pre, act = kept
    own = (0.5 * grad).astype(B16)
    cot = halves(gather(own) if fill is None else gather(own, False, fill(own)))
    d_pre = []
    for half in (0, 1):
        d_act = dot(after(cot[half], d_pre), weight_down, (1, 1))
        d_pre.append((d_act * swish_slope(pre[half].astype(F32))).astype(B16))
    d_norm, (sent, _) = scatter(pieces(d_pre[0], d_pre[1], weight_up, (1, 1)))
    cot, d_pre = after((cot, d_pre), sent)
    grad_down = dot(jnp.concatenate(act, 0), jnp.concatenate(cot, 0), (0, 0))
    grad_up = dot(jnp.concatenate(wide, 0), jnp.concatenate(d_pre, 0), (0, 0))
    grads = (grad_up.astype(B16), grad_down.astype(B16))
    if use is not None:
        d_norm = after(d_norm, use(grads))
    d_in, grad_gain = normalize_back(d_norm, unit, inverse, gain)
    return (grad + d_in, grad_gain, grads, (own, sent))


def places(slots):
    size, mine = lax.axis_size("tp"), lax.axis_index("tp")
    rows = slots // size
    if rows % TK:
        q_at = jnp.arange(slots // TQ, dtype=jnp.int32) * TQ
        k_at = jnp.arange(slots // TK, dtype=jnp.int32) * TK
        return q_at, k_at, True
    q_true = jnp.arange(slots // TQ, dtype=jnp.int32) * TQ
    k_true = jnp.arange(slots // TK, dtype=jnp.int32) * TK
    q_at = ((q_true // rows) ^ mine) * rows + q_true % rows
    k_at = ((k_true // rows) ^ mine) * rows + k_true % rows
    return q_at.astype(jnp.int32), k_at.astype(jnp.int32), False


def attend_forward(
    values, gain, weights, attend_out, content_bias, position_bias, code, spans, rel, prefetch
):
    slots = code.shape[0]
    width = attend_out.shape[0]
    q_at, k_at, reorder = places(slots)
    where = (spans, q_at, k_at)
    normed, unit, inverse = normalize(values, gain)
    slots_in = gather(normed.astype(B16))
    near, far = halves(slots_in)
    mixed = [dot(near, weights)]
    far = after(far, rel, spans, mixed)
    fetched, came = prefetch(slots_in[len(slots_in) // 2])
    mixed.append(dot(far, weights))
    flat = lambda bias: bias.astype(F32).reshape(1, width)
    join = lambda items: jnp.concatenate(items, 0)
    q_content = join([(item[:, :width] + flat(content_bias)).astype(B16) for item in mixed])
    q_position = join([(item[:, :width] + flat(position_bias)).astype(B16) for item in mixed])
    key = join([item[:, width : 2 * width].astype(B16) for item in mixed])
    value = join([item[:, 2 * width :].astype(B16) for item in mixed])
    if reorder:
        q_content, q_position, key, value = map(to_true, (q_content, q_position, key, value))
    operands = (
        where
        + (q_content, q_position, key, value, rel)
        + (code.reshape(slots, 1), code.reshape(slots // TK, 1, TK))
    )
    heads_out, heads_wide, sums = attend(*operands)
    sent = after(to_true(heads_out) if reorder else heads_out, came)
    half = slots // 2
    total, _ = scatter(pieces(sent[:half], sent[half:], attend_out, (1, 0)))
    kept = (unit, inverse, (near, far), operands, heads_wide, sums, sent)
    return (values + total, kept, fetched)


def attend_backward(grad, cot, kept, gain, weights, attend_out, table, filler, use):
    unit, inverse, wide, operands, heads_wide, sums, sent = kept
    slots, width = sent.shape
    _, _, reorder = places(slots)
    cot = halves(cot)
    d_near = dot(cot[0], attend_out, (1, 1)).astype(B16)
    cot = (cot[0], after(cot[1], d_near))
    d_heads = jnp.concatenate([d_near, dot(cot[1], attend_out, (1, 1)).astype(B16)], 0)
    if reorder:
        d_heads = to_true(d_heads)
    d_heads = after(d_heads, filler[0])
    d_all, d_rel, d_bias = attend_back(*operands, d_heads, heads_wide, sums)
    if reorder:
        d_all = to_true(d_all)
    d_all = after(d_all, filler[1])
    half = slots // 2
    d_norm, (last, _) = scatter(pieces(d_all[:half], d_all[half:], weights, (1, 1)))
    cot, d_all, d_rel = after((cot, d_all, d_rel), last)
    grad_out = dot(jnp.concatenate(cot, 0), sent, (0, 0))
    grad_all = dot(jnp.concatenate(wide, 0), d_all, (0, 0))
    grad_pos = dot(table, d_rel, (0, 0))
    grads = [item.astype(B16) for item in (grad_all, grad_pos, grad_out)]
    d_norm = after(d_norm, use(grads, last))
    d_in, grad_gain = normalize_back(d_norm, unit, inverse, gain)
    return (grad + d_in, grad_gain, d_bias[:2])


def conv_weights(point_in, depth_kernel, gain_inner, point_out, first):
    taps = depth_kernel.shape[0]
    own = after((point_in[:, 0], point_in[:, 1], point_out), first)
    small = gather(jnp.concatenate([depth_kernel, gain_inner[None]], 0))
    small = jnp.concatenate(small, 1).astype(F32)
    in_a, in_b, out = map(gather, own)
    arrived = [item[2::2] for item in (in_a, in_b, out)]
    in_a, in_b = jnp.concatenate(in_a, 1), jnp.concatenate(in_b, 1)
    return (in_a, in_b, small[:taps], small[taps], jnp.concatenate(out, 0)), arrived


def conv_masks(segments, valid, rows, taps):
    edge = 8
    reach = taps // 2
    base = lax.axis_index("tp") * rows + edge - reach
    wide_segments = jnp.pad(segments, edge, constant_values=-1)
    wide_valid = jnp.pad(valid, edge)
    own = lax.dynamic_slice_in_dim(wide_segments, base, rows + 2 * reach)
    masks = []
    for tap in range(taps):
        other = lax.dynamic_slice_in_dim(wide_segments, base + tap - reach, rows + 2 * reach)
        good = lax.dynamic_slice_in_dim(wide_valid, base + tap - reach, rows + 2 * reach)
        masks.append(((other == own) & (good == 1)).astype(F32)[:, None])
    return masks


def conv_forward(values, gain, full, masks):
    in_a, in_b, kernel, gain_inner, out = full
    rows = values.shape[0]
    taps = kernel.shape[0]
    reach = taps // 2
    normed, unit, inverse = normalize(values, gain)
    low = normed.astype(B16)
    wide = halo(low, 2 * reach)
    mixed_a = dot(wide, in_a)
    gate = jax.nn.sigmoid(dot(wide, in_b))
    glu = mixed_a * gate
    depth = 0.0
    for tap in range(taps):
        depth = depth + kernel[tap] * masks[tap] * glu[tap : tap + rows + 2 * reach]
    depth_norm, inner_unit, inner_inverse = normalize(depth, gain_inner)
    inner = (depth_norm * jax.nn.sigmoid(depth_norm)).astype(B16)
    own = slice(2 * reach, 2 * reach + rows)
    kept = (unit, inverse, low, mixed_a[own], gate[own], glu, inner_unit, inner_inverse, depth_norm, inner)
    return (values + dot(inner[reach : reach + rows], out), kept)


def conv_backward(grad, kept, gain, full, masks):
    unit, inverse, low, mixed_a, gate, glu, inner_unit, inner_inverse, depth_norm, inner = kept
    in_a, in_b, kernel, gain_inner, out = full
    rows = grad.shape[0]
    taps = kernel.shape[0]
    reach = taps // 2
    mine = slice(reach, reach + rows)
    cot = grad.astype(B16)
    d_act = dot(halo(cot, reach), out, (1, 1))
    d_depth_norm = d_act * swish_slope(depth_norm)
    d_depth, _ = normalize_back(d_depth_norm, inner_unit, inner_inverse, gain_inner)
    d_glu = 0.0
    for tap in range(taps):
        weighted = d_depth * masks[tap]
        back = 2 * reach - tap
        d_glu = d_glu + kernel[tap] * weighted[back : back + rows]
    d_a = (d_glu * gate).astype(B16)
    d_b = (d_glu * mixed_a * gate * (1.0 - gate)).astype(B16)
    d_norm = dot(d_a, in_a, (1, 1)) + dot(d_b, in_b, (1, 1))
    d_in, grad_gain = normalize_back(d_norm, unit, inverse, gain)
    grad = grad + d_in
    slots = gather(grad.astype(B16), True)
    low, cot, d_a, d_b, inner = after((low, cot, d_a, d_b, inner), slots[1])
    size = lax.axis_size("tp")
    width = in_a.shape[1] // size
    parts = []
    grads = [
        dot(left, right, (0, 0)).astype(B16)
        for left, right in ((low, d_a), (low, d_b), (cot, inner[mine]))
    ]

    def small_grads(gate):
        d_own, norm_own = after((d_depth[mine], d_depth_norm[mine]), gate)
        sums = []
        for tap in range(taps):
            near = d_own * masks[tap][mine]
            sums.append(jnp.sum(near * glu[reach + tap : reach + tap + rows], axis=0))
        sums.append(jnp.sum(norm_own * inner_unit[mine], axis=0))
        small, here = jnp.stack(sums, 0), lax.axis_index("tp")
        places = [(k ^ here) * width for k in range(size)]
        return jnp.concatenate([lax.dynamic_slice_in_dim(small, at, width, 1) for at in places], 1)

    for slot in range(size):
        cols = slice(slot * width, (slot + 1) * width)
        parts.append(jnp.concatenate([item[:, cols] for item in grads], 1))
    total, ends = scatter(parts, slots[-1], False)
    return (grad, slots, grad_gain, (total, small_grads), ends)


def body(
    layer_input,
    cotangent,
    segments,
    valid_frames,
    gain_first,
    up_first,
    down_first,
    gain_attend,
    query_weight,
    key_weight,
    value_weight,
    attend_out,
    pos_weight,
    content_bias,
    position_bias,
    gain_conv,
    point_in,
    depth_kernel,
    gain_inner,
    point_out,
    gain_second,
    up_second,
    down_second,
    gain_final,
):
    segment_row, valid_row = segments[0], valid_frames[0]
    weights = jnp.concatenate([query_weight, key_weight, value_weight], 1)
    width = query_weight.shape[1]
    taps = depth_kernel.shape[0]
    values = layer_input[0].astype(F32)
    rows = values.shape[0]
    slots = segment_row.shape[0]
    masks = conv_masks(segment_row, valid_row, rows, taps)
    code = codes(segment_row, valid_row)
    spans = spans_of(code)
    values, kept_first, sent = ffn_forward(values, gain_first, up_first, down_first)
    table = distance_table(slots, values.shape[1], sent)
    rel = dot(table, pos_weight).astype(B16)
    prefetch = functools.partial(conv_weights, point_in, depth_kernel, gain_inner, point_out)
    values, kept_attend, full = attend_forward(
        values, gain_attend, weights, attend_out, content_bias, position_bias, code, spans, rel, prefetch
    )
    values, kept_conv = conv_forward(values, gain_conv, full, masks)
    values, kept_second, _ = ffn_forward(values, gain_second, up_second, down_second)
    final, final_unit, final_inverse = normalize(values, gain_final)
    layer_output = final.astype(B16)
    grad, sum_final = normalize_back(cotangent[0].astype(F32), final_unit, final_inverse, gain_final)
    held = {}

    def start_second(grads):
        held["second"] = start_sum(grads)
        return grads

    grad, sum_second, _, _ = ffn_backward(
        grad, kept_second, gain_second, up_second, down_second, start_second
    )
    grad, cot, sum_conv, conv_grads, ends = conv_backward(grad, kept_conv, gain_conv, full, masks)
    ends = (ends[0], (ends, held["second"]))

    def start_middle(grads, last):
        own, got = after((conv_grads[0], ends[1][0][1]), last)
        total = (own.astype(F32) + got.astype(F32)).astype(B16)
        forms = [(width, plain)] * 4 + [(width, turned), (2 * width, plain), (width, turned)]
        held["middle"] = row_sum(grads + [total], forms)
        return held["middle"].step()

    grad, sum_attend, d_bias = attend_backward(
        grad, cot, kept_attend, gain_attend, weights, attend_out, table, ends, start_middle
    )
    middle = held["middle"]
    second_sum = end_sum(held["second"])

    def fill(own):
        pairs = (sum_attend, sum_conv, sum_second, sum_final)
        held["small"] = [gain_sums(pairs, own), conv_grads[1](own)]
        return held["small"]

    grad, sum_first, first_grads, marks = ffn_backward(
        grad, kept_first, gain_first, up_first, down_first, None, fill
    )
    first = RowSums(first_grads, [(item.shape[1], plain) for item in first_grads])
    token = middle.step(marks[1])
    token = first.step(token)
    second_sum = after(second_sum, token)
    token = second_sum
    while middle.done < middle.steps:
        token = middle.step(token)
        if first.left > 1:
            token = first.step(token)
        if first.done == 3:
            token = (token, grad)
        if first.done == 5:
            second_up, second_down = split_sum(after(second_sum, token), up_second.shape[0])
            token = (token, second_up, second_down)
    while first.left:
        gate = (token, middle.came()) if first.left == 1 else token
        token = first.step(gate)
    at = lax.axis_index("tp") * width
    bias = jnp.zeros((2, lax.axis_size("tp") * width), F32)
    bias = lax.dynamic_update_slice_in_dim(bias, d_bias, at, 1)
    pack = jnp.concatenate([gain_sums((sum_first,), marks[1])] + held["small"] + [bias], 0)
    pack = sum_cube(after(pack, token), "tp")
    pack = sum_cube(after(pack, first.came()), "rows")
    attend_sum = middle.finish(token)
    first_sum = first.finish(attend_sum)
    gains, small = pack[:5], lax.dynamic_slice_in_dim(pack[5:], at, width, 1)
    bias_shape = content_bias.shape
    return (
        layer_output[None],
        grad[None],
        gains[0],
        first_sum[0],
        first_sum[1],
        gains[1],
        attend_sum[0],
        attend_sum[1],
        attend_sum[2],
        attend_sum[4],
        attend_sum[3],
        small[taps + 1].reshape(bias_shape),
        small[taps + 2].reshape(bias_shape),
        gains[2],
        attend_sum[5].reshape(attend_sum[5].shape[0], 2, width),
        small[:taps],
        small[taps],
        attend_sum[6],
        gains[3],
        second_up,
        second_down,
        gains[4],
    )


def solution(mesh):
    in_specs = (
        P("rows", "tp", None),
        P("rows", "tp", None),
        P("rows", None),
        P("rows", None),
        P(),
        P(None, "tp"),
        P("tp", None),
        P(),
        P(None, "tp"),
        P(None, "tp"),
        P(None, "tp"),
        P("tp", None),
        P(None, "tp"),
        P("tp", None),
        P("tp", None),
        P(),
        P(None, None, "tp"),
        P(None, "tp"),
        P("tp"),
        P("tp", None),
        P(),
        P(None, "tp"),
        P("tp", None),
        P(),
    )
    out_specs = (
        P("rows", "tp", None),
        P("rows", "tp", None),
        P(),
        P(None, "tp"),
        P("tp", None),
        P(),
        P(None, "tp"),
        P(None, "tp"),
        P(None, "tp"),
        P("tp", None),
        P(None, "tp"),
        P("tp", None),
        P("tp", None),
        P(),
        P(None, None, "tp"),
        P(None, "tp"),
        P("tp"),
        P("tp", None),
        P(),
        P(None, "tp"),
        P("tp", None),
        P(),
    )
    return jax.shard_map(body, mesh=mesh, in_specs=in_specs, out_specs=out_specs, check_vma=False)
```

```python
import functools
import math

import jax
import jax.numpy as jnp
from jax import lax
from jax.experimental import pallas as pl
from jax.experimental.pallas import tpu as pltpu
from jax.sharding import PartitionSpec as P

EPS = 1e-05
NEG = -1e30
F32 = jnp.float32
B16 = jnp.bfloat16
TQ = 384
TK = 384
HD = 128
STEP = 64
LINK_BYTES = 180_000_000
SM = pl.BlockSpec(memory_space=pltpu.SMEM)
VM = pl.BlockSpec(memory_space=pltpu.VMEM)

def dotx(a, b, ca, cb):
    return lax.dot_general(a, b, (((ca,), (cb,)), ((), ())), preferred_element_type=F32)

def skew_tile(grid):
    return pltpu.roll(grid, TK + 1, 1, stride=1, stride_axis=0)[:, :TK]

def unskew_flipped(flipped):
    wide = jnp.concatenate([flipped, jnp.zeros((TQ, TQ), F32)], axis=1)
    return pltpu.roll(wide, 0, 1, stride=1, stride_axis=0)

def attend_kernel(heads, spans, q_at, k_at, qc_ref, qp_ref, k_ref, v_ref, rel_ref, code_q_ref, code_k_ref,
                  out_ref, wide_ref, lse_ref):
    slots = qc_ref.shape[0]
    scale = HD ** -0.5
    blocks, tiles = slots // TQ, slots // TK

    def q_step(qb, _):
        at = pl.multiple_of(q_at[qb], TQ)
        true_at = pl.multiple_of(qb * TQ, TQ)
        code_q = code_q_ref[pl.ds(true_at, TQ), :]
        qc = [qc_ref[pl.ds(at, TQ), h * HD:(h + 1) * HD] for h in range(heads)]
        qp = [qp_ref[pl.ds(at, TQ), h * HD:(h + 1) * HD] for h in range(heads)]

        def k_step(kt, carry):
            ko = pl.multiple_of(k_at[kt], TQ)
            to = pl.multiple_of((blocks - 1 + kt * (TK // TQ) - qb) * TQ, TQ)
            mask = code_q == code_k_ref[kt]
            new = []
            for h in range(heads):
                lanes = slice(h * HD, (h + 1) * HD)
                top, total, acc = carry[h]
                grid = dotx(qp[h], rel_ref[pl.ds(to, TK + TQ), lanes], 1, 1)
                raw = dotx(qc[h], k_ref[pl.ds(ko, TK), lanes], 1, 1) + skew_tile(grid)
                scores = jnp.where(mask, raw * scale, NEG)
                top_new = jnp.maximum(top, jnp.max(scores, axis=1, keepdims=True))
                shrink = jnp.exp(top - top_new)
                weights = jnp.exp(scores - top_new)
                total = total * shrink + jnp.sum(weights, axis=1, keepdims=True)
                acc = acc * shrink + dotx(weights.astype(B16), v_ref[pl.ds(ko, TK), lanes], 1, 0)
                new.append((top_new, total, acc))
            return tuple(new)

        first = tuple((jnp.full((TQ, 1), NEG, F32), jnp.zeros((TQ, 1), F32), jnp.zeros((TQ, HD), F32))
                      for _ in range(heads))
        final = lax.fori_loop(spans[0, qb], spans[1, qb], k_step, first)
        for h in range(heads):
            lanes = slice(h * HD, (h + 1) * HD)
            top, total, acc = final[h]
            out = acc / total
            wide_ref[pl.ds(at, TQ), lanes] = out
            out_ref[pl.ds(at, TQ), lanes] = out.astype(B16)
            lse_ref[pl.ds(at, TQ), h:h + 1] = top + jnp.log(total)
        return 0

    lax.fori_loop(0, blocks, q_step, 0)

def attend_back_kernel(heads, spans, q_at, k_at, qc_ref, qp_ref, k_ref, v_ref, rel_ref, code_q_ref, code_k_ref,
                       d_out_ref, wide_ref, lse_ref,
                       all_ref, drel_ref, bias_ref, dk_acc, dv_acc, drel_acc):
    slots = qc_ref.shape[0]
    scale = HD ** -0.5
    blocks, tiles = slots // TQ, slots // TK
    dk_acc[...] = jnp.zeros_like(dk_acc)
    dv_acc[...] = jnp.zeros_like(dv_acc)
    drel_acc[...] = jnp.zeros_like(drel_acc)
    bias_ref[...] = jnp.zeros_like(bias_ref)
    row = lax.broadcasted_iota(jnp.int32, (TQ, TQ), 0)
    column = lax.broadcasted_iota(jnp.int32, (TQ, TQ), 1)
    flip = (row + column == TQ - 1).astype(F32)
    flip_low = flip.astype(B16)

    def q_step(qb, _):
        at = pl.multiple_of(q_at[qb], TQ)
        true_at = pl.multiple_of(qb * TQ, TQ)
        code_q = code_q_ref[pl.ds(true_at, TQ), :]
        cols = [slice(h * HD, (h + 1) * HD) for h in range(heads)]
        qc = [qc_ref[pl.ds(at, TQ), c] for c in cols]
        qp = [qp_ref[pl.ds(at, TQ), c] for c in cols]
        qp_turned = [dotx(item, flip_low, 0, 0).astype(B16) for item in qp]
        d_out = [d_out_ref[pl.ds(at, TQ), c] for c in cols]
        qc_turned = [item.T for item in qc]
        d_out_turned = [item.T for item in d_out]
        lse = [lse_ref[pl.ds(at, TQ), h:h + 1] for h in range(heads)]
        delta = [jnp.sum(d_out[h].astype(F32) * wide_ref[pl.ds(at, TQ), cols[h]], axis=1, keepdims=True)
                 for h in range(heads)]

        def k_step(kt, carry):
            ko = pl.multiple_of(k_at[kt], TQ)
            to = pl.multiple_of((blocks - 1 + kt * (TK // TQ) - qb) * TQ, TQ)
            mask = code_q == code_k_ref[kt]
            new = []
            for h in range(heads):
                lanes = cols[h]
                d_content, d_position = carry[h]
                window = rel_ref[pl.ds(to, TK + TQ), lanes]
                key = k_ref[pl.ds(ko, TK), lanes]
                grid = dotx(qp[h], window, 1, 1)
                raw = dotx(qc[h], key, 1, 1) + skew_tile(grid)
                probs = jnp.exp(jnp.where(mask, raw * scale - lse[h], NEG))
                d_probs = dotx(d_out[h], v_ref[pl.ds(ko, TK), lanes], 1, 1)
                d_raw = probs * (d_probs - delta[h]) * scale
                d_low = d_raw.astype(B16)
                d_grid = unskew_flipped(dotx(flip_low, d_low, 1, 0)).astype(B16)
                dv_acc[lanes, pl.ds(ko, TK)] += dotx(d_out_turned[h], probs.astype(B16), 1, 0)
                dk_acc[lanes, pl.ds(ko, TK)] += dotx(qc_turned[h], d_low, 1, 0)
                drel_acc[lanes, pl.ds(to, TK + TQ)] += dotx(qp_turned[h], d_grid, 1, 0)
                d_content = d_content + dotx(d_low, key, 1, 0)
                d_position = d_position + dotx(d_grid, window, 1, 0)
                new.append((d_content, d_position))
            return tuple(new)

        first = tuple((jnp.zeros((TQ, HD), F32),) * 2 for _ in range(heads))
        final = lax.fori_loop(spans[0, qb], spans[1, qb], k_step, first)
        for h in range(heads):
            d_content, d_position = final[h]
            d_position = lax.dot_general(flip, d_position, (((1,), (0,)), ((), ())),
                                         precision=lax.Precision.HIGHEST, preferred_element_type=F32)
            all_ref[pl.ds(at, TQ), cols[h]] = (d_content + d_position).astype(B16)
            bias_ref[0:1, cols[h]] += jnp.sum(d_content, axis=0, keepdims=True)
            bias_ref[1:2, cols[h]] += jnp.sum(d_position, axis=0, keepdims=True)
        return 0

    lax.fori_loop(0, blocks, q_step, 0)
    width = dk_acc.shape[0]
    all_ref[:, width : 2 * width] = dk_acc[...].astype(B16).T
    all_ref[:, 2 * width :] = dv_acc[...].astype(B16).T
    drel_ref[...] = drel_acc[...].astype(B16).T

def sds(s, d): return jax.ShapeDtypeStruct(s, d)

def attend(spans, q_at, k_at, qc, qp, k, v, rel, code_q, code_k):
    slots, width = qc.shape
    heads = width // HD
    return pl.pallas_call(
        functools.partial(attend_kernel, heads),
        out_shape=(sds((slots, width), B16), sds((slots, width), F32), sds((slots, heads), F32)),
        in_specs=[SM] * 3 + [VM] * 7, out_specs=(VM,) * 3,
        compiler_params=pltpu.CompilerParams(vmem_limit_bytes=40 << 20),
        cost_estimate=pl.CostEstimate(flops=int(4e9), bytes_accessed=int(9e6), transcendentals=int(2e6)),
    )(spans, q_at, k_at, qc, qp, k, v, rel, code_q, code_k)

def attend_back(spans, q_at, k_at, qc, qp, k, v, rel, code_q, code_k, d_out, wide, lse):
    slots, width = qc.shape
    heads = width // HD
    return pl.pallas_call(
        functools.partial(attend_back_kernel, heads),
        out_shape=(sds((slots, 3 * width), B16), sds((2 * slots, width), B16), sds((8, width), F32)),
        in_specs=[SM] * 3 + [VM] * 10, out_specs=(VM,) * 3,
        scratch_shapes=[pltpu.VMEM((width, slots), F32), pltpu.VMEM((width, slots), F32), pltpu.VMEM((width, 2 * slots), F32)],
        compiler_params=pltpu.CompilerParams(vmem_limit_bytes=48 << 20),
        cost_estimate=pl.CostEstimate(flops=int(1e6), bytes_accessed=int(1e6), transcendentals=0),
    )(spans, q_at, k_at, qc, qp, k, v, rel, code_q, code_k, d_out, wide, lse)

def codes(segments, valid):
    slots = segments.shape[0]
    place = jnp.arange(slots, dtype=jnp.int32)
    code = jnp.where(valid == 1, segments, -1 - place)
    return code

def spans_of(code):
    slots = code.shape[0]
    same = code[:, None] == code[None, :]
    touch = jnp.any(same.reshape(slots // TQ, TQ, slots // TK, TK), axis=(1, 3))
    tiles = slots // TK
    idx = jnp.arange(tiles, dtype=jnp.int32)
    lo = jnp.min(jnp.where(touch, idx, tiles), axis=1)
    hi = jnp.max(jnp.where(touch, idx + 1, 0), axis=1)
    return jnp.stack([lo, hi], 0).astype(jnp.int32)


def normalize(values, gain):
    mean = jnp.mean(values, axis=-1, keepdims=True)
    centered = values - mean
    inverse = lax.rsqrt(jnp.mean(centered * centered, axis=-1, keepdims=True) + EPS)
    unit = centered * inverse
    return (unit * gain.astype(F32), unit, inverse)


def normalize_back(grad, unit, inverse, gain):
    scaled = grad * gain.astype(F32)
    first = jnp.mean(scaled, axis=-1, keepdims=True)
    second = jnp.mean(scaled * unit, axis=-1, keepdims=True)
    return (inverse * (scaled - first - unit * second), (grad, unit))


def gain_sums(pairs, gate):
    return jnp.stack([jnp.sum(grad * unit, axis=0) for grad, unit in after(pairs, gate)])


def swish_slope(values):
    gate = jax.nn.sigmoid(values)
    return gate * (1.0 + values * (1.0 - gate))


def distance_table(slots, width, first):
    column = jnp.arange(width)
    even = (column % 2 == 0)[None, :]
    rate = jnp.exp(-(column - column % 2).astype(F32) * (math.log(10000.0) / width))
    coarse = (slots - 1 - STEP * jnp.arange(2 * slots // STEP)).astype(F32)[:, None] * rate[None, :]
    fine = jnp.arange(STEP).astype(F32)[:, None] * rate[None, :]
    sin_c, cos_c = jnp.sin(coarse), jnp.cos(coarse)
    with_cos = jnp.where(even, sin_c, cos_c)
    with_sin = jnp.where(even, -cos_c, sin_c)
    with_cos, with_sin, sin_f, cos_f = after((with_cos, with_sin, jnp.sin(fine), jnp.cos(fine)), first)
    table = with_cos[:, None, :] * cos_f[None] + with_sin[:, None, :] * sin_f[None]
    return table.reshape(2 * slots, width).astype(B16)


def dot(left, right, contract=(1, 0)):
    return lax.dot_general(
        left, right, (((contract[0],), (contract[1],)), ((), ())), preferred_element_type=F32
    )


def swap(values, distance):
    size = lax.axis_size("tp")
    return lax.ppermute(values, "tp", [(i, i ^ distance) for i in range(size)])


def distances():
    size = lax.axis_size("tp")
    return [1 << bit for bit in range(size.bit_length() - 1)]


def same_kernel(block_ref, out_ref):
    pass


def arrived(block):
    spec = pl.BlockSpec(memory_space=pl.ANY)
    return pl.pallas_call(
        same_kernel,
        in_specs=[spec],
        out_specs=spec,
        out_shape=jax.ShapeDtypeStruct(block.shape, block.dtype),
        input_output_aliases={0: 0},
        cost_estimate=pl.CostEstimate(flops=0, bytes_accessed=LINK_BYTES, transcendentals=0),
    )(block)


def gather(own, first=False, late=()):
    slots = {0: own}
    for distance in reversed(distances()):
        for slot in list(slots):
            slots[slot ^ distance] = swap(slots[slot], distance)
    last = len(slots) - 1
    if first:
        slots[last] = after(arrived(slots[last]), late)
    return [slots[slot] for slot in range(len(slots))]


def scatter(parts, late=(), add=True):
    parts = dict(enumerate(parts))
    sent = got = None
    for distance in distances():
        for slot in sorted(parts, reverse=True):
            if slot & distance:
                sent = parts.pop(slot).astype(B16)
                if distance == distances()[-1]:
                    sent = after(sent, late)
                got = swap(sent, distance)
                if add or distance != distances()[-1]:
                    parts[slot ^ distance] = parts[slot ^ distance].astype(F32) + got.astype(F32)
    return parts[0], (sent, got)


def after(values, *others):
    return lax.optimization_barrier((values, others))[0]


def halves(slots):
    half = len(slots) // 2
    return jnp.concatenate(slots[:half], 0), jnp.concatenate(slots[half:], 0)


def pieces(near, far, weight, contract):
    count = lax.axis_size("tp") // 2
    rows = near.shape[0] // count
    outs = {}
    for slot in reversed(range(2 * count)):
        source, place = (near, slot) if slot < count else (far, slot - count)
        outs[slot] = dot(source[place * rows : (place + 1) * rows], weight, contract)
    return [outs[slot] for slot in range(2 * count)]


def ring():
    size, mine = lax.axis_size("rows"), lax.axis_index("rows")
    order = list(range(0, size, 2)) + list(range(size - 1, 0, -2))
    place = jnp.where(mine % 2 == 0, mine // 2, size - (mine + 1) // 2)
    right = [(order[i], order[(i + 1) % size]) for i in range(size)]
    return size, place, right, [(there, here) for here, there in right]


def plain(piece):
    return piece


def turned(piece):
    return piece.T


def first_kernel(at, *refs):
    count = (len(refs) - 2) // 2
    refs[-2][...] = jnp.concatenate([ref[...] for ref in refs[:count]], 1)
    refs[-1][...] = jnp.concatenate([ref[...] for ref in refs[count:-2]], 1)


def pass_kernel(second, at, *refs):
    count = (len(refs) - 4) // 2
    from_left, from_right = (ref[...].astype(F32) for ref in refs[-4:-2])
    if second:
        top = pl.program_id(0) == 0
        from_left = jnp.where(top, from_left, 0.0)
        from_right = jnp.where(top, 0.0, from_right)
    own = jnp.concatenate([ref[...] for ref in refs[:count]], 1).astype(F32)
    refs[-2][...] = (own + from_left).astype(B16)
    own = jnp.concatenate([ref[...] for ref in refs[count:-4]], 1).astype(F32)
    refs[-1][...] = (own + from_right).astype(B16)


def total_kernel(split, at, *refs):
    own = jnp.concatenate([ref[...] for ref in refs[:-3]], 1).astype(F32)
    from_left, from_right = (ref[...].astype(F32) for ref in refs[-3:-1])
    if split:
        refs[-1][...] = (own + jnp.concatenate([from_left, from_right], 0)).astype(B16)
    else:
        refs[-1][...] = (own + from_left + from_right).astype(B16)


def place_kernel(spots, spans, at, *refs):
    count = len(spots)
    outs, held = refs[count : count + len(spans)], refs[-1]
    half = refs[count - 1].shape[0]
    size = held.shape[0] // (2 * half)
    for ref, (k, bottom) in zip(refs[:count], spots):
        start = ((at[0] + k) % size) * (2 * half) + bottom * half
        start = pl.multiple_of(start, half)
        held[pl.ds(start, ref.shape[0]), :] = ref[...].astype(F32)
    for out, (low, high, form) in zip(outs, spans):
        here = (pl.program_id(0) >= low) & (pl.program_id(0) < high)

        @pl.when(here)
        def _(out=out, form=form):
            out[...] = form(held[...])


class RowSum:
    def __init__(self, arrays, parts):
        self.size, self.place, self.right, self.left = ring()
        self.arrays, self.parts = list(arrays), parts
        self.width = sum(item.shape[1] for item in arrays)
        self.rows = arrays[0].shape[0] // self.size
        self.half = self.rows // 2
        self.stages = self.size // 2
        self.steps = 2 * self.stages
        self.done = 0
        self.seen = []

    def call(self, kernel, at, blocks, extra, out_rows, grid, gate, out_blocks, count=2):
        arrays, extra = after((self.arrays, extra), gate)
        specs, operands = [], []
        for rows, index in blocks:
            for item in arrays:
                specs.append(pl.BlockSpec((rows, item.shape[1]), index))
                operands.append(item)
        for item, (rows, index) in zip(extra, out_blocks[1]):
            specs.append(pl.BlockSpec((rows, self.width), index))
            operands.append(item)
        rows, index = out_blocks[0]
        moved = sum(2 * rows * self.width for _ in range(4))
        return pl.pallas_call(
            kernel,
            grid_spec=pltpu.PrefetchScalarGridSpec(
                num_scalar_prefetch=1,
                grid=(grid,),
                in_specs=specs,
                out_specs=[pl.BlockSpec((rows, self.width), index)] * count,
            ),
            out_shape=(sds((out_rows, self.width), B16),) * count,
            cost_estimate=pl.CostEstimate(flops=moved, bytes_accessed=moved, transcendentals=0),
        )(at, *operands)

    def send(self, to_right, to_left):
        over = lambda items, way: [lax.ppermute(item, "rows", way) for item in items]
        self.from_left, self.from_right = over(to_right, self.right), over(to_left, self.left)
        return (to_right, to_left)

    def step(self, gate=()):
        stage, stages, half, rows = self.done, self.stages, self.half, self.rows
        self.done += 1
        ids = [(self.place + k) % self.size for k in (stages - stage, stage - stages)]
        at = jnp.stack(ids).astype(jnp.int32)
        whole = lambda i, at: (0, 0)
        if stage == 0:
            blocks = [(half, lambda i, at: (2 * at[0], 0)), (half, lambda i, at: (2 * at[1] + 1, 0))]
            out = self.call(first_kernel, at, blocks, [], half, 1, gate, ((half, whole), []))
            return self.send([out[0]], [out[1]])
        if stage < stages:
            blocks = [
                (half, lambda i, at: (2 * at[0] + i, 0)), (half, lambda i, at: (2 * at[1] + i, 0)),
            ]
            here = (half, lambda i, at: (i, 0))
            got = (half, whole) if stage == 1 else here
            kernel = functools.partial(pass_kernel, stage == 1)
            extra = self.from_left + self.from_right
            out = self.call(kernel, at, blocks, extra, rows, 2, gate, (here, [got, got]))
            return self.send([out[0]], [out[1]])
        if stage == stages:
            got = (half if stages == 1 else rows, whole)
            kernel = functools.partial(total_kernel, stages == 1)
            extra = self.from_left + self.from_right
            blocks = [(rows, lambda i, at: (at[0], 0))]
            blocks = [(half, lambda i, at: (2 * at[0] + i, 0))] if stages > 1 else blocks
            here = (half, lambda i, at: (i, 0)) if stages > 1 else (rows, whole)
            got = here if stages > 1 else got
            grid = 2 if stages > 1 else 1
            out = self.call(kernel, at, blocks, extra, rows, grid, gate, (here, [got, got]), 1)
            to_right = to_left = list(out)
            self.see(to_right, 0)
        else:
            to_right, to_left = after((self.from_left, self.from_right), gate)
            self.see(to_right, stages - stage)
            self.see(to_left, stage - stages)
        if stage == 2 * stages - 1:
            to_right, to_left = [to_right[0][:half]], [to_left[0][half:]]
        return self.send(to_right, to_left)

    def see(self, items, k):
        self.seen.append((items[0], (k, 0)))

    def finish(self, gate=()):
        self.seen += [(self.from_left[0], (-self.stages, 0)), (self.from_right[0], (self.stages, 1))]
        items = after([item for item, _ in self.seen], gate)
        spots = [((k + self.size) % self.size, bottom) for _, (k, bottom) in self.seen]
        length = self.arrays[0].shape[0]
        step = math.gcd(*[width for width, _ in self.parts])
        spans, specs, shapes, low = [], [], [], 0
        for width, form in self.parts:
            count = width // step
            spans.append((low, low + count, form))

            def column(i, at, low=low, count=count):
                return jnp.clip(i - low, 0, count - 1)

            if form is turned:
                shapes.append((width, length))
                specs.append(pl.BlockSpec((step, length), lambda i, at, f=column: (f(i, at), 0)))
            else:
                shapes.append((length, width))
                specs.append(pl.BlockSpec((length, step), lambda i, at, f=column: (0, f(i, at))))
            low += count
        moved = 6 * length * self.width
        return pl.pallas_call(
            functools.partial(place_kernel, spots, spans),
            grid_spec=pltpu.PrefetchScalarGridSpec(
                num_scalar_prefetch=1,
                grid=(low,),
                in_specs=[pl.BlockSpec((item.shape[0], step), lambda i, at: (0, i)) for item in items],
                out_specs=specs,
                scratch_shapes=[pltpu.VMEM((length, step), F32)],
            ),
            out_shape=[sds(shape, F32) for shape in shapes],
            compiler_params=pltpu.CompilerParams(vmem_limit_bytes=60 << 20),
            cost_estimate=pl.CostEstimate(flops=moved, bytes_accessed=moved, transcendentals=0),
        )(self.place.reshape(1).astype(jnp.int32), *items)


class WholeSum:
    def __init__(self, arrays, parts):
        self.arrays, self.parts, self.steps, self.done = list(arrays), parts, 1, 0

    def step(self, gate=()):
        self.done += 1
        values = after(jnp.concatenate(self.arrays, 1), gate)
        self.total = lax.psum(values, "rows").astype(F32)
        return ()

    def finish(self, gate=()):
        edges = [sum(width for width, _ in self.parts[:k]) for k in range(len(self.parts) + 1)]
        return [
            form(self.total[:, edges[k] : edges[k + 1]]) for k, (_, form) in enumerate(self.parts)
        ]


def row_sum(arrays, parts):
    size = lax.axis_size("rows")
    fits = size % 2 == 0 and arrays[0].shape[0] % (16 * size) == 0
    return (RowSum if fits else WholeSum)(arrays, parts)


def start_sum(arrays):
    if arrays[0].shape[1] == arrays[1].shape[1]:
        arrays = [jnp.concatenate(arrays, 0)]
    return [lax.psum_scatter(item, "rows", scatter_dimension=0, tiled=True) for item in arrays]


def end_sum(shares):
    return [lax.all_gather(item, "rows", axis=0, tiled=True) for item in shares]


def split_sum(whole, rows):
    if len(whole) == 1:
        whole = [whole[0][:rows], whole[0][rows:]]
    return [item.astype(F32) for item in whole]


class RowSums:
    def __init__(self, arrays, parts):
        if all(item.shape[0] == arrays[0].shape[0] for item in arrays):
            self.items = [row_sum(arrays, parts)]
        else:
            self.items = [row_sum([item], [part]) for item, part in zip(arrays, parts)]

    @property
    def done(self):
        return self.items[0].done

    @property
    def left(self):
        return max(item.steps - item.done for item in self.items)

    def step(self, gate=()):
        for item in self.items:
            if item.done < item.steps:
                gate = item.step(gate)
        return gate

    def finish(self, gate=()):
        while self.left:
            gate = self.step(gate)
        return [out for item in self.items for out in item.finish(gate)]


def sum_cube(values, axis):
    size = lax.axis_size(axis)
    if size & (size - 1):
        return lax.psum(values, axis)
    distance = 1
    while distance < size:
        values = values + lax.ppermute(values, axis, [(i, i ^ distance) for i in range(size)])
        distance *= 2
    return values


def halo(own, reach):
    size = lax.axis_size("tp")
    left = lax.ppermute(own[-reach:], "tp", [(i, i + 1) for i in range(size - 1)])
    right = lax.ppermute(own[:reach], "tp", [(i + 1, i) for i in range(size - 1)])
    return jnp.concatenate([left, own, right], 0)


def to_true(values):
    size, mine = lax.axis_size("tp"), lax.axis_index("tp")
    rows = values.shape[0] // size
    return jnp.concatenate(
        [lax.dynamic_slice_in_dim(values, (mine ^ k) * rows, rows, 0) for k in range(size)], 0
    )


def ffn_forward(values, gain, weight_up, weight_down):
    normed, unit, inverse = normalize(values, gain)
    near, far = halves(gather(normed.astype(B16)))
    pre, act = [], []
    for half in (near, far):
        pre.append(dot(after(half, act), weight_up))
        act.append((pre[-1] * jax.nn.sigmoid(pre[-1])).astype(B16))
    total, (sent, _) = scatter(pieces(act[0], act[1], weight_down, (1, 0)))
    pre = [item.astype(B16) for item in pre]
    return (values + 0.5 * total, (unit, inverse, (near, far), pre, act), sent)


def ffn_backward(grad, kept, gain, weight_up, weight_down, use=None, fill=None):
    unit, inverse, wide, pre, act = kept
    own = (0.5 * grad).astype(B16)
    cot = halves(gather(own) if fill is None else gather(own, True, fill(own)))
    d_pre = []
    for half in (0, 1):
        d_act = dot(after(cot[half], d_pre), weight_down, (1, 1))
        d_pre.append((d_act * swish_slope(pre[half].astype(F32))).astype(B16))
    d_norm, (sent, _) = scatter(pieces(d_pre[0], d_pre[1], weight_up, (1, 1)))
    cot, d_pre = after((cot, d_pre), sent)
    grad_down = dot(jnp.concatenate(act, 0), jnp.concatenate(cot, 0), (0, 0))
    grad_up = dot(jnp.concatenate(wide, 0), jnp.concatenate(d_pre, 0), (0, 0))
    grads = (grad_up.astype(B16), grad_down.astype(B16))
    if use is not None:
        d_norm = after(d_norm, use(grads))
    d_in, grad_gain = normalize_back(d_norm, unit, inverse, gain)
    return (grad + d_in, grad_gain, grads, (own, sent))


def places(slots):
    size, mine = lax.axis_size("tp"), lax.axis_index("tp")
    rows = slots // size
    if rows % TK:
        q_at = jnp.arange(slots // TQ, dtype=jnp.int32) * TQ
        k_at = jnp.arange(slots // TK, dtype=jnp.int32) * TK
        return q_at, k_at, True
    q_true = jnp.arange(slots // TQ, dtype=jnp.int32) * TQ
    k_true = jnp.arange(slots // TK, dtype=jnp.int32) * TK
    q_at = ((q_true // rows) ^ mine) * rows + q_true % rows
    k_at = ((k_true // rows) ^ mine) * rows + k_true % rows
    return q_at.astype(jnp.int32), k_at.astype(jnp.int32), False


def attend_forward(
    values, gain, weights, attend_out, content_bias, position_bias, code, spans, rel, prefetch
):
    slots = code.shape[0]
    width = attend_out.shape[0]
    q_at, k_at, reorder = places(slots)
    where = (spans, q_at, k_at)
    normed, unit, inverse = normalize(values, gain)
    near, far = halves(gather(normed.astype(B16)))
    mixed = [dot(near, weights)]
    far = after(far, rel, spans, mixed)
    fetched, arrived = prefetch(far)
    mixed.append(dot(far, weights))
    flat = lambda bias: bias.astype(F32).reshape(1, width)
    join = lambda items: jnp.concatenate(items, 0)
    q_content = join([(item[:, :width] + flat(content_bias)).astype(B16) for item in mixed])
    q_position = join([(item[:, :width] + flat(position_bias)).astype(B16) for item in mixed])
    key = join([item[:, width : 2 * width].astype(B16) for item in mixed])
    value = join([item[:, 2 * width :].astype(B16) for item in mixed])
    if reorder:
        q_content, q_position, key, value = map(to_true, (q_content, q_position, key, value))
    operands = (
        where
        + (q_content, q_position, key, value, rel)
        + (code.reshape(slots, 1), code.reshape(slots // TK, 1, TK))
    )
    heads_out, heads_wide, sums = attend(*operands)
    sent = after(to_true(heads_out) if reorder else heads_out, arrived)
    half = slots // 2
    total, _ = scatter(pieces(sent[:half], sent[half:], attend_out, (1, 0)))
    kept = (unit, inverse, (near, far), operands, heads_wide, sums, sent)
    return (values + total, kept, fetched)


def attend_backward(grad, cot, kept, gain, weights, attend_out, table, filler, use):
    unit, inverse, wide, operands, heads_wide, sums, sent = kept
    slots, width = sent.shape
    _, _, reorder = places(slots)
    cot = halves(cot)
    d_near = dot(cot[0], attend_out, (1, 1)).astype(B16)
    cot = (cot[0], after(cot[1], d_near))
    d_heads = jnp.concatenate([d_near, dot(cot[1], attend_out, (1, 1)).astype(B16)], 0)
    if reorder:
        d_heads = to_true(d_heads)
    d_heads = after(d_heads, filler[0])
    d_all, d_rel, d_bias = attend_back(*operands, d_heads, heads_wide, sums)
    if reorder:
        d_all = to_true(d_all)
    d_all = after(d_all, filler[1])
    half = slots // 2
    d_norm, (last, _) = scatter(pieces(d_all[:half], d_all[half:], weights, (1, 1)))
    cot, d_all, d_rel = after((cot, d_all, d_rel), last)
    grad_out = dot(jnp.concatenate(cot, 0), sent, (0, 0))
    grad_all = dot(jnp.concatenate(wide, 0), d_all, (0, 0))
    grad_pos = dot(table, d_rel, (0, 0))
    grads = [item.astype(B16) for item in (grad_all, grad_pos, grad_out)]
    d_norm = after(d_norm, use(grads, last))
    d_in, grad_gain = normalize_back(d_norm, unit, inverse, gain)
    return (grad + d_in, grad_gain, d_bias[:2])


def conv_weights(point_in, depth_kernel, gain_inner, point_out, first):
    taps = depth_kernel.shape[0]
    own = after((point_in[:, 0], point_in[:, 1], point_out), first)
    small = gather(jnp.concatenate([depth_kernel, gain_inner[None]], 0))
    small = jnp.concatenate(small, 1).astype(F32)
    in_a, in_b, out = map(gather, own)
    arrived = [item[2::2] for item in (in_a, in_b, out)]
    in_a, in_b = jnp.concatenate(in_a, 1), jnp.concatenate(in_b, 1)
    return (in_a, in_b, small[:taps], small[taps], jnp.concatenate(out, 0)), arrived


def conv_masks(segments, valid, rows, taps):
    edge = 8
    reach = taps // 2
    base = lax.axis_index("tp") * rows + edge - reach
    wide_segments = jnp.pad(segments, edge, constant_values=-1)
    wide_valid = jnp.pad(valid, edge)
    own = lax.dynamic_slice_in_dim(wide_segments, base, rows + 2 * reach)
    masks = []
    for tap in range(taps):
        other = lax.dynamic_slice_in_dim(wide_segments, base + tap - reach, rows + 2 * reach)
        good = lax.dynamic_slice_in_dim(wide_valid, base + tap - reach, rows + 2 * reach)
        masks.append(((other == own) & (good == 1)).astype(F32)[:, None])
    return masks


def conv_forward(values, gain, full, masks):
    in_a, in_b, kernel, gain_inner, out = full
    rows = values.shape[0]
    taps = kernel.shape[0]
    reach = taps // 2
    normed, unit, inverse = normalize(values, gain)
    low = normed.astype(B16)
    wide = halo(low, 2 * reach)
    mixed_a = dot(wide, in_a)
    gate = jax.nn.sigmoid(dot(wide, in_b))
    glu = mixed_a * gate
    depth = 0.0
    for tap in range(taps):
        depth = depth + kernel[tap] * masks[tap] * glu[tap : tap + rows + 2 * reach]
    depth_norm, inner_unit, inner_inverse = normalize(depth, gain_inner)
    inner = (depth_norm * jax.nn.sigmoid(depth_norm)).astype(B16)
    own = slice(2 * reach, 2 * reach + rows)
    kept = (unit, inverse, low, mixed_a[own], gate[own], glu, inner_unit, inner_inverse, depth_norm, inner)
    return (values + dot(inner[reach : reach + rows], out), kept)


def conv_backward(grad, kept, gain, full, masks):
    unit, inverse, low, mixed_a, gate, glu, inner_unit, inner_inverse, depth_norm, inner = kept
    in_a, in_b, kernel, gain_inner, out = full
    rows = grad.shape[0]
    taps = kernel.shape[0]
    reach = taps // 2
    mine = slice(reach, reach + rows)
    cot = grad.astype(B16)
    d_act = dot(halo(cot, reach), out, (1, 1))
    d_depth_norm = d_act * swish_slope(depth_norm)
    d_depth, _ = normalize_back(d_depth_norm, inner_unit, inner_inverse, gain_inner)
    d_glu = 0.0
    for tap in range(taps):
        weighted = d_depth * masks[tap]
        back = 2 * reach - tap
        d_glu = d_glu + kernel[tap] * weighted[back : back + rows]
    d_a = (d_glu * gate).astype(B16)
    d_b = (d_glu * mixed_a * gate * (1.0 - gate)).astype(B16)
    d_norm = dot(d_a, in_a, (1, 1)) + dot(d_b, in_b, (1, 1))
    d_in, grad_gain = normalize_back(d_norm, unit, inverse, gain)
    grad = grad + d_in
    slots = gather(grad.astype(B16), True)
    low, cot, d_a, d_b, inner = after((low, cot, d_a, d_b, inner), slots[1])
    size = lax.axis_size("tp")
    width = in_a.shape[1] // size
    parts = []
    grads = [
        dot(left, right, (0, 0)).astype(B16)
        for left, right in ((low, d_a), (low, d_b), (cot, inner[mine]))
    ]

    def small_grads(gate):
        d_own, norm_own = after((d_depth[mine], d_depth_norm[mine]), gate)
        sums = []
        for tap in range(taps):
            near = d_own * masks[tap][mine]
            sums.append(jnp.sum(near * glu[reach + tap : reach + tap + rows], axis=0))
        sums.append(jnp.sum(norm_own * inner_unit[mine], axis=0))
        small = jnp.stack(sums, 0)
        return scatter([small[:, k * width : (k + 1) * width] for k in range(size)])[0]

    for slot in range(size):
        cols = slice(slot * width, (slot + 1) * width)
        parts.append(jnp.concatenate([item[:, cols] for item in grads], 1))
    total, ends = scatter(parts, slots[-1], False)
    return (grad, slots, grad_gain, (total, small_grads), ends)


def body(
    layer_input,
    cotangent,
    segments,
    valid_frames,
    gain_first,
    up_first,
    down_first,
    gain_attend,
    query_weight,
    key_weight,
    value_weight,
    attend_out,
    pos_weight,
    content_bias,
    position_bias,
    gain_conv,
    point_in,
    depth_kernel,
    gain_inner,
    point_out,
    gain_second,
    up_second,
    down_second,
    gain_final,
):
    segment_row, valid_row = segments[0], valid_frames[0]
    weights = jnp.concatenate([query_weight, key_weight, value_weight], 1)
    width = query_weight.shape[1]
    taps = depth_kernel.shape[0]
    values = layer_input[0].astype(F32)
    rows = values.shape[0]
    slots = segment_row.shape[0]
    masks = conv_masks(segment_row, valid_row, rows, taps)
    code = codes(segment_row, valid_row)
    spans = spans_of(code)
    values, kept_first, sent = ffn_forward(values, gain_first, up_first, down_first)
    table = distance_table(slots, values.shape[1], sent)
    rel = dot(table, pos_weight).astype(B16)
    prefetch = functools.partial(conv_weights, point_in, depth_kernel, gain_inner, point_out)
    values, kept_attend, full = attend_forward(
        values, gain_attend, weights, attend_out, content_bias, position_bias, code, spans, rel, prefetch
    )
    values, kept_conv = conv_forward(values, gain_conv, full, masks)
    values, kept_second, _ = ffn_forward(values, gain_second, up_second, down_second)
    final, final_unit, final_inverse = normalize(values, gain_final)
    layer_output = final.astype(B16)
    grad, sum_final = normalize_back(cotangent[0].astype(F32), final_unit, final_inverse, gain_final)
    held = {}

    def start_second(grads):
        held["second"] = start_sum(grads)
        return grads

    grad, sum_second, _, _ = ffn_backward(
        grad, kept_second, gain_second, up_second, down_second, start_second
    )
    grad, cot, sum_conv, conv_grads, ends = conv_backward(grad, kept_conv, gain_conv, full, masks)
    ends = (ends[0], (ends, held["second"]))

    def start_middle(grads, last):
        own, got = after((conv_grads[0], ends[1][0][1]), last)
        total = (own.astype(F32) + got.astype(F32)).astype(B16)
        forms = [(width, plain)] * 4 + [(width, turned), (2 * width, plain), (width, turned)]
        held["middle"] = row_sum(grads + [total], forms)
        return held["middle"].step()

    grad, sum_attend, d_bias = attend_backward(
        grad, cot, kept_attend, gain_attend, weights, attend_out, table, ends, start_middle
    )
    middle = held["middle"]
    second_sum = end_sum(held["second"])
    grad, sum_first, first_grads, marks = ffn_backward(
        grad, kept_first, gain_first, up_first, down_first, None, middle.step
    )
    first = RowSums(first_grads, [(item.shape[1], plain) for item in first_grads])
    token = middle.step(marks[1])
    token = first.step(token)
    second_sum = after(second_sum, token)
    token = second_sum
    while middle.done < middle.steps:
        token = middle.step(token)
        if first.left > 1:
            token = first.step(token)
        if first.done == 3:
            token = (token, grad)
        if first.done == 5:
            second_up, second_down = split_sum(after(second_sum, token), up_second.shape[0])
            token = (token, second_up, second_down)
    while first.left:
        token = first.step(token)
    pairs = (sum_first, sum_attend, sum_conv, sum_second, sum_final)
    gains = sum_cube(gain_sums(pairs, marks[1]), "tp")
    small = jnp.concatenate([conv_grads[1](marks[1]), d_bias], 0)
    small_shape = small.shape
    pack = jnp.concatenate([gains.reshape(-1), small.reshape(-1)]).reshape(-1, width)
    pack = sum_cube(after(pack, token), "rows")
    attend_sum = middle.finish(token)
    first_sum = first.finish(attend_sum)
    pack = pack.reshape(-1)
    gains, small = pack[: gains.size].reshape(gains.shape), pack[gains.size :].reshape(small_shape)
    bias_shape = content_bias.shape
    return (
        layer_output[None],
        grad[None],
        gains[0],
        first_sum[0],
        first_sum[1],
        gains[1],
        attend_sum[0],
        attend_sum[1],
        attend_sum[2],
        attend_sum[4],
        attend_sum[3],
        small[taps + 1].reshape(bias_shape),
        small[taps + 2].reshape(bias_shape),
        gains[2],
        attend_sum[5].reshape(attend_sum[5].shape[0], 2, width),
        small[:taps],
        small[taps],
        attend_sum[6],
        gains[3],
        second_up,
        second_down,
        gains[4],
    )


def solution(mesh):
    in_specs = (
        P("rows", "tp", None),
        P("rows", "tp", None),
        P("rows", None),
        P("rows", None),
        P(),
        P(None, "tp"),
        P("tp", None),
        P(),
        P(None, "tp"),
        P(None, "tp"),
        P(None, "tp"),
        P("tp", None),
        P(None, "tp"),
        P("tp", None),
        P("tp", None),
        P(),
        P(None, None, "tp"),
        P(None, "tp"),
        P("tp"),
        P("tp", None),
        P(),
        P(None, "tp"),
        P("tp", None),
        P(),
    )
    out_specs = (
        P("rows", "tp", None),
        P("rows", "tp", None),
        P(),
        P(None, "tp"),
        P("tp", None),
        P(),
        P(None, "tp"),
        P(None, "tp"),
        P(None, "tp"),
        P("tp", None),
        P(None, "tp"),
        P("tp", None),
        P("tp", None),
        P(),
        P(None, None, "tp"),
        P(None, "tp"),
        P("tp"),
        P("tp", None),
        P(),
        P(None, "tp"),
        P("tp", None),
        P(),
    )
    return jax.shard_map(body, mesh=mesh, in_specs=in_specs, out_specs=out_specs, check_vma=False)
```

```python
import functools
import math

import jax
import jax.numpy as jnp
from jax import lax
from jax.experimental import pallas as pl
from jax.experimental.pallas import tpu as pltpu
from jax.sharding import PartitionSpec as P

EPS = 1e-05
NEG = -1e30
F32 = jnp.float32
B16 = jnp.bfloat16
TQ = 384
TK = 384
HD = 128
STEP = 64
LINK_BYTES = 180_000_000
SM = pl.BlockSpec(memory_space=pltpu.SMEM)
VM = pl.BlockSpec(memory_space=pltpu.VMEM)

def dotx(a, b, ca, cb):
    return lax.dot_general(a, b, (((ca,), (cb,)), ((), ())), preferred_element_type=F32)

def skew_tile(grid):
    return pltpu.roll(grid, TK + 1, 1, stride=1, stride_axis=0)[:, :TK]

def unskew_flipped(flipped):
    wide = jnp.concatenate([flipped, jnp.zeros((TQ, TQ), F32)], axis=1)
    return pltpu.roll(wide, 0, 1, stride=1, stride_axis=0)

def attend_kernel(heads, spans, q_at, k_at, qc_ref, qp_ref, k_ref, v_ref, rel_ref, code_q_ref, code_k_ref,
                  out_ref, wide_ref, lse_ref):
    slots = qc_ref.shape[0]
    scale = HD ** -0.5
    blocks, tiles = slots // TQ, slots // TK

    def q_step(qb, _):
        at = pl.multiple_of(q_at[qb], TQ)
        true_at = pl.multiple_of(qb * TQ, TQ)
        code_q = code_q_ref[pl.ds(true_at, TQ), :]
        qc = [qc_ref[pl.ds(at, TQ), h * HD:(h + 1) * HD] for h in range(heads)]
        qp = [qp_ref[pl.ds(at, TQ), h * HD:(h + 1) * HD] for h in range(heads)]

        def k_step(kt, carry):
            ko = pl.multiple_of(k_at[kt], TQ)
            to = pl.multiple_of((blocks - 1 + kt * (TK // TQ) - qb) * TQ, TQ)
            mask = code_q == code_k_ref[kt]
            new = []
            for h in range(heads):
                lanes = slice(h * HD, (h + 1) * HD)
                top, total, acc = carry[h]
                grid = dotx(qp[h], rel_ref[pl.ds(to, TK + TQ), lanes], 1, 1)
                raw = dotx(qc[h], k_ref[pl.ds(ko, TK), lanes], 1, 1) + skew_tile(grid)
                scores = jnp.where(mask, raw * scale, NEG)
                top_new = jnp.maximum(top, jnp.max(scores, axis=1, keepdims=True))
                shrink = jnp.exp(top - top_new)
                weights = jnp.exp(scores - top_new)
                total = total * shrink + jnp.sum(weights, axis=1, keepdims=True)
                acc = acc * shrink + dotx(weights.astype(B16), v_ref[pl.ds(ko, TK), lanes], 1, 0)
                new.append((top_new, total, acc))
            return tuple(new)

        first = tuple((jnp.full((TQ, 1), NEG, F32), jnp.zeros((TQ, 1), F32), jnp.zeros((TQ, HD), F32))
                      for _ in range(heads))
        final = lax.fori_loop(spans[0, qb], spans[1, qb], k_step, first)
        for h in range(heads):
            lanes = slice(h * HD, (h + 1) * HD)
            top, total, acc = final[h]
            out = acc / total
            wide_ref[pl.ds(at, TQ), lanes] = out
            out_ref[pl.ds(at, TQ), lanes] = out.astype(B16)
            lse_ref[pl.ds(at, TQ), h:h + 1] = top + jnp.log(total)
        return 0

    lax.fori_loop(0, blocks, q_step, 0)

def attend_back_kernel(heads, spans, q_at, k_at, qc_ref, qp_ref, k_ref, v_ref, rel_ref, code_q_ref, code_k_ref,
                       d_out_ref, wide_ref, lse_ref,
                       all_ref, drel_ref, bias_ref, dk_acc, dv_acc, drel_acc):
    slots = qc_ref.shape[0]
    scale = HD ** -0.5
    blocks, tiles = slots // TQ, slots // TK
    dk_acc[...] = jnp.zeros_like(dk_acc)
    dv_acc[...] = jnp.zeros_like(dv_acc)
    drel_acc[...] = jnp.zeros_like(drel_acc)
    bias_ref[...] = jnp.zeros_like(bias_ref)
    row = lax.broadcasted_iota(jnp.int32, (TQ, TQ), 0)
    column = lax.broadcasted_iota(jnp.int32, (TQ, TQ), 1)
    flip = (row + column == TQ - 1).astype(F32)
    flip_low = flip.astype(B16)

    def q_step(qb, _):
        at = pl.multiple_of(q_at[qb], TQ)
        true_at = pl.multiple_of(qb * TQ, TQ)
        code_q = code_q_ref[pl.ds(true_at, TQ), :]
        cols = [slice(h * HD, (h + 1) * HD) for h in range(heads)]
        qc = [qc_ref[pl.ds(at, TQ), c] for c in cols]
        qp = [qp_ref[pl.ds(at, TQ), c] for c in cols]
        qp_turned = [dotx(item, flip_low, 0, 0).astype(B16) for item in qp]
        d_out = [d_out_ref[pl.ds(at, TQ), c] for c in cols]
        qc_turned = [item.T for item in qc]
        d_out_turned = [item.T for item in d_out]
        lse = [lse_ref[pl.ds(at, TQ), h:h + 1] for h in range(heads)]
        delta = [jnp.sum(d_out[h].astype(F32) * wide_ref[pl.ds(at, TQ), cols[h]], axis=1, keepdims=True)
                 for h in range(heads)]

        def k_step(kt, carry):
            ko = pl.multiple_of(k_at[kt], TQ)
            to = pl.multiple_of((blocks - 1 + kt * (TK // TQ) - qb) * TQ, TQ)
            mask = code_q == code_k_ref[kt]
            new = []
            for h in range(heads):
                lanes = cols[h]
                d_content, d_position = carry[h]
                window = rel_ref[pl.ds(to, TK + TQ), lanes]
                key = k_ref[pl.ds(ko, TK), lanes]
                grid = dotx(qp[h], window, 1, 1)
                raw = dotx(qc[h], key, 1, 1) + skew_tile(grid)
                probs = jnp.exp(jnp.where(mask, raw * scale - lse[h], NEG))
                d_probs = dotx(d_out[h], v_ref[pl.ds(ko, TK), lanes], 1, 1)
                d_raw = probs * (d_probs - delta[h]) * scale
                d_low = d_raw.astype(B16)
                d_grid = unskew_flipped(dotx(flip_low, d_low, 1, 0)).astype(B16)
                dv_acc[lanes, pl.ds(ko, TK)] += dotx(d_out_turned[h], probs.astype(B16), 1, 0)
                dk_acc[lanes, pl.ds(ko, TK)] += dotx(qc_turned[h], d_low, 1, 0)
                drel_acc[lanes, pl.ds(to, TK + TQ)] += dotx(qp_turned[h], d_grid, 1, 0)
                d_content = d_content + dotx(d_low, key, 1, 0)
                d_position = d_position + dotx(d_grid, window, 1, 0)
                new.append((d_content, d_position))
            return tuple(new)

        first = tuple((jnp.zeros((TQ, HD), F32),) * 2 for _ in range(heads))
        final = lax.fori_loop(spans[0, qb], spans[1, qb], k_step, first)
        for h in range(heads):
            d_content, d_position = final[h]
            d_position = lax.dot_general(flip, d_position, (((1,), (0,)), ((), ())),
                                         precision=lax.Precision.HIGHEST, preferred_element_type=F32)
            all_ref[pl.ds(at, TQ), cols[h]] = (d_content + d_position).astype(B16)
            bias_ref[0:1, cols[h]] += jnp.sum(d_content, axis=0, keepdims=True)
            bias_ref[1:2, cols[h]] += jnp.sum(d_position, axis=0, keepdims=True)
        return 0

    lax.fori_loop(0, blocks, q_step, 0)
    width = dk_acc.shape[0]
    all_ref[:, width : 2 * width] = dk_acc[...].astype(B16).T
    all_ref[:, 2 * width :] = dv_acc[...].astype(B16).T
    drel_ref[...] = drel_acc[...].astype(B16).T

def sds(s, d): return jax.ShapeDtypeStruct(s, d)

def attend(spans, q_at, k_at, qc, qp, k, v, rel, code_q, code_k):
    slots, width = qc.shape
    heads = width // HD
    return pl.pallas_call(
        functools.partial(attend_kernel, heads),
        out_shape=(sds((slots, width), B16), sds((slots, width), F32), sds((slots, heads), F32)),
        in_specs=[SM] * 3 + [VM] * 7, out_specs=(VM,) * 3,
        compiler_params=pltpu.CompilerParams(vmem_limit_bytes=40 << 20),
        cost_estimate=pl.CostEstimate(flops=int(4e9), bytes_accessed=int(9e6), transcendentals=int(2e6)),
    )(spans, q_at, k_at, qc, qp, k, v, rel, code_q, code_k)

def attend_back(spans, q_at, k_at, qc, qp, k, v, rel, code_q, code_k, d_out, wide, lse):
    slots, width = qc.shape
    heads = width // HD
    return pl.pallas_call(
        functools.partial(attend_back_kernel, heads),
        out_shape=(sds((slots, 3 * width), B16), sds((2 * slots, width), B16), sds((8, width), F32)),
        in_specs=[SM] * 3 + [VM] * 10, out_specs=(VM,) * 3,
        scratch_shapes=[pltpu.VMEM((width, slots), F32), pltpu.VMEM((width, slots), F32), pltpu.VMEM((width, 2 * slots), F32)],
        compiler_params=pltpu.CompilerParams(vmem_limit_bytes=48 << 20),
        cost_estimate=pl.CostEstimate(flops=int(1e6), bytes_accessed=int(1e6), transcendentals=0),
    )(spans, q_at, k_at, qc, qp, k, v, rel, code_q, code_k, d_out, wide, lse)

def codes(segments, valid):
    slots = segments.shape[0]
    place = jnp.arange(slots, dtype=jnp.int32)
    code = jnp.where(valid == 1, segments, -1 - place)
    return code

def spans_of(code):
    slots = code.shape[0]
    same = code[:, None] == code[None, :]
    touch = jnp.any(same.reshape(slots // TQ, TQ, slots // TK, TK), axis=(1, 3))
    tiles = slots // TK
    idx = jnp.arange(tiles, dtype=jnp.int32)
    lo = jnp.min(jnp.where(touch, idx, tiles), axis=1)
    hi = jnp.max(jnp.where(touch, idx + 1, 0), axis=1)
    return jnp.stack([lo, hi], 0).astype(jnp.int32)


def normalize(values, gain):
    mean = jnp.mean(values, axis=-1, keepdims=True)
    centered = values - mean
    inverse = lax.rsqrt(jnp.mean(centered * centered, axis=-1, keepdims=True) + EPS)
    unit = centered * inverse
    return (unit * gain.astype(F32), unit, inverse)


def normalize_back(grad, unit, inverse, gain):
    scaled = grad * gain.astype(F32)
    first = jnp.mean(scaled, axis=-1, keepdims=True)
    second = jnp.mean(scaled * unit, axis=-1, keepdims=True)
    return (inverse * (scaled - first - unit * second), (grad, unit))


def gain_sums(pairs, gate):
    return jnp.stack([jnp.sum(grad * unit, axis=0) for grad, unit in after(pairs, gate)])


def swish_slope(values):
    gate = jax.nn.sigmoid(values)
    return gate * (1.0 + values * (1.0 - gate))


def distance_table(slots, width, first):
    column = jnp.arange(width)
    even = (column % 2 == 0)[None, :]
    rate = jnp.exp(-(column - column % 2).astype(F32) * (math.log(10000.0) / width))
    coarse = (slots - 1 - STEP * jnp.arange(2 * slots // STEP)).astype(F32)[:, None] * rate[None, :]
    fine = jnp.arange(STEP).astype(F32)[:, None] * rate[None, :]
    sin_c, cos_c = jnp.sin(coarse), jnp.cos(coarse)
    with_cos = jnp.where(even, sin_c, cos_c)
    with_sin = jnp.where(even, -cos_c, sin_c)
    with_cos, with_sin, sin_f, cos_f = after((with_cos, with_sin, jnp.sin(fine), jnp.cos(fine)), first)
    table = with_cos[:, None, :] * cos_f[None] + with_sin[:, None, :] * sin_f[None]
    return table.reshape(2 * slots, width).astype(B16)


def dot(left, right, contract=(1, 0)):
    return lax.dot_general(
        left, right, (((contract[0],), (contract[1],)), ((), ())), preferred_element_type=F32
    )


def swap(values, distance):
    size = lax.axis_size("tp")
    return lax.ppermute(values, "tp", [(i, i ^ distance) for i in range(size)])


def distances():
    size = lax.axis_size("tp")
    return [1 << bit for bit in range(size.bit_length() - 1)]


def same_kernel(block_ref, out_ref):
    pass


def arrived(block):
    spec = pl.BlockSpec(memory_space=pl.ANY)
    return pl.pallas_call(
        same_kernel,
        in_specs=[spec],
        out_specs=spec,
        out_shape=jax.ShapeDtypeStruct(block.shape, block.dtype),
        input_output_aliases={0: 0},
        cost_estimate=pl.CostEstimate(flops=0, bytes_accessed=LINK_BYTES, transcendentals=0),
    )(block)


def gather(own, first=False, late=()):
    slots = {0: own}
    for distance in reversed(distances()):
        for slot in list(slots):
            slots[slot ^ distance] = swap(slots[slot], distance)
    last = len(slots) - 1
    if first:
        slots[last] = after(arrived(slots[last]), late)
    return [slots[slot] for slot in range(len(slots))]


def scatter(parts, late=(), add=True):
    parts = dict(enumerate(parts))
    sent = got = None
    for distance in distances():
        for slot in sorted(parts, reverse=True):
            if slot & distance:
                sent = parts.pop(slot).astype(B16)
                if distance == distances()[-1]:
                    sent = after(sent, late)
                got = swap(sent, distance)
                if add or distance != distances()[-1]:
                    parts[slot ^ distance] = parts[slot ^ distance].astype(F32) + got.astype(F32)
    return parts[0], (sent, got)


def after(values, *others):
    return lax.optimization_barrier((values, others))[0]


def halves(slots):
    half = len(slots) // 2
    return jnp.concatenate(slots[:half], 0), jnp.concatenate(slots[half:], 0)


def pieces(near, far, weight, contract):
    count = lax.axis_size("tp") // 2
    rows = near.shape[0] // count
    outs = {}
    for slot in reversed(range(2 * count)):
        source, place = (near, slot) if slot < count else (far, slot - count)
        outs[slot] = dot(source[place * rows : (place + 1) * rows], weight, contract)
    return [outs[slot] for slot in range(2 * count)]


def ring():
    size, mine = lax.axis_size("rows"), lax.axis_index("rows")
    order = list(range(0, size, 2)) + list(range(size - 1, 0, -2))
    place = jnp.where(mine % 2 == 0, mine // 2, size - (mine + 1) // 2)
    right = [(order[i], order[(i + 1) % size]) for i in range(size)]
    return size, place, right, [(there, here) for here, there in right]


def plain(piece):
    return piece


def turned(piece):
    return piece.T


def first_kernel(at, *refs):
    count = (len(refs) - 2) // 2
    refs[-2][...] = jnp.concatenate([ref[...] for ref in refs[:count]], 1)
    refs[-1][...] = jnp.concatenate([ref[...] for ref in refs[count:-2]], 1)


def pass_kernel(second, at, *refs):
    count = (len(refs) - 4) // 2
    from_left, from_right = (ref[...].astype(F32) for ref in refs[-4:-2])
    if second:
        top = pl.program_id(0) == 0
        from_left = jnp.where(top, from_left, 0.0)
        from_right = jnp.where(top, 0.0, from_right)
    own = jnp.concatenate([ref[...] for ref in refs[:count]], 1).astype(F32)
    refs[-2][...] = (own + from_left).astype(B16)
    own = jnp.concatenate([ref[...] for ref in refs[count:-4]], 1).astype(F32)
    refs[-1][...] = (own + from_right).astype(B16)


def total_kernel(split, at, *refs):
    own = jnp.concatenate([ref[...] for ref in refs[:-3]], 1).astype(F32)
    from_left, from_right = (ref[...].astype(F32) for ref in refs[-3:-1])
    if split:
        refs[-1][...] = (own + jnp.concatenate([from_left, from_right], 0)).astype(B16)
    else:
        refs[-1][...] = (own + from_left + from_right).astype(B16)


def place_kernel(spots, spans, at, *refs):
    count = len(spots)
    outs, held = refs[count : count + len(spans)], refs[-1]
    half = refs[count - 1].shape[0]
    size = held.shape[0] // (2 * half)
    for ref, (k, bottom) in zip(refs[:count], spots):
        start = ((at[0] + k) % size) * (2 * half) + bottom * half
        start = pl.multiple_of(start, half)
        held[pl.ds(start, ref.shape[0]), :] = ref[...].astype(F32)
    for out, (low, high, form) in zip(outs, spans):
        here = (pl.program_id(0) >= low) & (pl.program_id(0) < high)

        @pl.when(here)
        def _(out=out, form=form):
            out[...] = form(held[...])


class RowSum:
    def __init__(self, arrays, parts):
        self.size, self.place, self.right, self.left = ring()
        self.arrays, self.parts = list(arrays), parts
        self.width = sum(item.shape[1] for item in arrays)
        self.rows = arrays[0].shape[0] // self.size
        self.half = self.rows // 2
        self.stages = self.size // 2
        self.steps = 2 * self.stages
        self.done = 0
        self.seen = []

    def call(self, kernel, at, blocks, extra, out_rows, grid, gate, out_blocks, count=2):
        arrays, extra = after((self.arrays, extra), gate)
        specs, operands = [], []
        for rows, index in blocks:
            for item in arrays:
                specs.append(pl.BlockSpec((rows, item.shape[1]), index))
                operands.append(item)
        for item, (rows, index) in zip(extra, out_blocks[1]):
            specs.append(pl.BlockSpec((rows, self.width), index))
            operands.append(item)
        rows, index = out_blocks[0]
        moved = sum(2 * rows * self.width for _ in range(4))
        return pl.pallas_call(
            kernel,
            grid_spec=pltpu.PrefetchScalarGridSpec(
                num_scalar_prefetch=1,
                grid=(grid,),
                in_specs=specs,
                out_specs=[pl.BlockSpec((rows, self.width), index)] * count,
            ),
            out_shape=(sds((out_rows, self.width), B16),) * count,
            cost_estimate=pl.CostEstimate(flops=moved, bytes_accessed=moved, transcendentals=0),
        )(at, *operands)

    def send(self, to_right, to_left):
        over = lambda items, way: [lax.ppermute(item, "rows", way) for item in items]
        self.from_left, self.from_right = over(to_right, self.right), over(to_left, self.left)
        return (to_right, to_left)

    def step(self, gate=()):
        stage, stages, half, rows = self.done, self.stages, self.half, self.rows
        self.done += 1
        ids = [(self.place + k) % self.size for k in (stages - stage, stage - stages)]
        at = jnp.stack(ids).astype(jnp.int32)
        whole = lambda i, at: (0, 0)
        if stage == 0:
            blocks = [(half, lambda i, at: (2 * at[0], 0)), (half, lambda i, at: (2 * at[1] + 1, 0))]
            out = self.call(first_kernel, at, blocks, [], half, 1, gate, ((half, whole), []))
            return self.send([out[0]], [out[1]])
        if stage < stages:
            blocks = [
                (half, lambda i, at: (2 * at[0] + i, 0)), (half, lambda i, at: (2 * at[1] + i, 0)),
            ]
            here = (half, lambda i, at: (i, 0))
            got = (half, whole) if stage == 1 else here
            kernel = functools.partial(pass_kernel, stage == 1)
            extra = self.from_left + self.from_right
            out = self.call(kernel, at, blocks, extra, rows, 2, gate, (here, [got, got]))
            return self.send([out[0]], [out[1]])
        if stage == stages:
            got = (half if stages == 1 else rows, whole)
            kernel = functools.partial(total_kernel, stages == 1)
            extra = self.from_left + self.from_right
            blocks = [(rows, lambda i, at: (at[0], 0))]
            blocks = [(half, lambda i, at: (2 * at[0] + i, 0))] if stages > 1 else blocks
            here = (half, lambda i, at: (i, 0)) if stages > 1 else (rows, whole)
            got = here if stages > 1 else got
            grid = 2 if stages > 1 else 1
            out = self.call(kernel, at, blocks, extra, rows, grid, gate, (here, [got, got]), 1)
            to_right = to_left = list(out)
            self.see(to_right, 0)
        else:
            to_right, to_left = after((self.from_left, self.from_right), gate)
            self.see(to_right, stages - stage)
            self.see(to_left, stage - stages)
        if stage == 2 * stages - 1:
            to_right, to_left = [to_right[0][:half]], [to_left[0][half:]]
        return self.send(to_right, to_left)

    def came(self):
        return self.from_left + self.from_right

    def see(self, items, k):
        self.seen.append((items[0], (k, 0)))

    def finish(self, gate=()):
        self.seen += [(self.from_left[0], (-self.stages, 0)), (self.from_right[0], (self.stages, 1))]
        items = after([item for item, _ in self.seen], gate)
        spots = [((k + self.size) % self.size, bottom) for _, (k, bottom) in self.seen]
        length = self.arrays[0].shape[0]
        step = math.gcd(*[width for width, _ in self.parts])
        spans, specs, shapes, low = [], [], [], 0
        for width, form in self.parts:
            count = width // step
            spans.append((low, low + count, form))

            def column(i, at, low=low, count=count):
                return jnp.clip(i - low, 0, count - 1)

            if form is turned:
                shapes.append((width, length))
                specs.append(pl.BlockSpec((step, length), lambda i, at, f=column: (f(i, at), 0)))
            else:
                shapes.append((length, width))
                specs.append(pl.BlockSpec((length, step), lambda i, at, f=column: (0, f(i, at))))
            low += count
        moved = 6 * length * self.width
        return pl.pallas_call(
            functools.partial(place_kernel, spots, spans),
            grid_spec=pltpu.PrefetchScalarGridSpec(
                num_scalar_prefetch=1,
                grid=(low,),
                in_specs=[pl.BlockSpec((item.shape[0], step), lambda i, at: (0, i)) for item in items],
                out_specs=specs,
                scratch_shapes=[pltpu.VMEM((length, step), F32)],
            ),
            out_shape=[sds(shape, F32) for shape in shapes],
            compiler_params=pltpu.CompilerParams(vmem_limit_bytes=60 << 20),
            cost_estimate=pl.CostEstimate(flops=moved, bytes_accessed=moved, transcendentals=0),
        )(self.place.reshape(1).astype(jnp.int32), *items)


class WholeSum:
    came = staticmethod(lambda: ())

    def __init__(self, arrays, parts):
        self.arrays, self.parts, self.steps, self.done = list(arrays), parts, 1, 0

    def step(self, gate=()):
        self.done += 1
        values = after(jnp.concatenate(self.arrays, 1), gate)
        self.total = lax.psum(values, "rows").astype(F32)
        return ()

    def finish(self, gate=()):
        edges = [sum(width for width, _ in self.parts[:k]) for k in range(len(self.parts) + 1)]
        return [
            form(self.total[:, edges[k] : edges[k + 1]]) for k, (_, form) in enumerate(self.parts)
        ]


def row_sum(arrays, parts):
    size = lax.axis_size("rows")
    fits = size % 2 == 0 and arrays[0].shape[0] % (16 * size) == 0
    return (RowSum if fits else WholeSum)(arrays, parts)


def start_sum(arrays):
    if arrays[0].shape[1] == arrays[1].shape[1]:
        arrays = [jnp.concatenate(arrays, 0)]
    sums = [lax.psum_scatter(item, "rows", scatter_dimension=0, tiled=True) for item in arrays]
    return sums, arrays


def end_sum(shares):
    return [lax.all_gather(item, "rows", axis=0, tiled=True) for item in shares]


def split_sum(whole, rows):
    if len(whole) == 1:
        whole = [whole[0][:rows], whole[0][rows:]]
    return [item.astype(F32) for item in whole]


class RowSums:
    def __init__(self, arrays, parts):
        if all(item.shape[0] == arrays[0].shape[0] for item in arrays):
            self.items = [row_sum(arrays, parts)]
        else:
            self.items = [row_sum([item], [part]) for item, part in zip(arrays, parts)]

    def came(self):
        return [item.came() for item in self.items]

    @property
    def done(self):
        return self.items[0].done

    @property
    def left(self):
        return max(item.steps - item.done for item in self.items)

    def step(self, gate=()):
        for item in self.items:
            if item.done < item.steps:
                gate = item.step(gate)
        return gate

    def finish(self, gate=()):
        while self.left:
            gate = self.step(gate)
        return [out for item in self.items for out in item.finish(gate)]


def sum_cube(values, axis, late=()):
    size = lax.axis_size(axis)
    if size & (size - 1):
        return lax.psum(values, axis)
    distance = 1
    while distance < size:
        values = values + lax.ppermute(values, axis, [(i, i ^ distance) for i in range(size)])
        values = after(values, late)
        distance *= 2
    return values


def halo(own, reach):
    size = lax.axis_size("tp")
    left = lax.ppermute(own[-reach:], "tp", [(i, i + 1) for i in range(size - 1)])
    right = lax.ppermute(own[:reach], "tp", [(i + 1, i) for i in range(size - 1)])
    return jnp.concatenate([left, own, right], 0)


def to_true(values):
    size, mine = lax.axis_size("tp"), lax.axis_index("tp")
    rows = values.shape[0] // size
    return jnp.concatenate(
        [lax.dynamic_slice_in_dim(values, (mine ^ k) * rows, rows, 0) for k in range(size)], 0
    )


def ffn_forward(values, gain, weight_up, weight_down):
    normed, unit, inverse = normalize(values, gain)
    near, far = halves(gather(normed.astype(B16)))
    pre, act = [], []
    for half in (near, far):
        pre.append(dot(after(half, act), weight_up))
        act.append((pre[-1] * jax.nn.sigmoid(pre[-1])).astype(B16))
    total, (sent, _) = scatter(pieces(act[0], act[1], weight_down, (1, 0)))
    pre = [item.astype(B16) for item in pre]
    return (values + 0.5 * total, (unit, inverse, (near, far), pre, act), sent)


def ffn_backward(grad, kept, gain, weight_up, weight_down, use=None, fill=None):
    unit, inverse, wide, pre, act = kept
    own = (0.5 * grad).astype(B16)
    cot = halves(gather(own) if fill is None else gather(own, True, fill(own)))
    d_pre = []
    for half in (0, 1):
        d_act = dot(after(cot[half], d_pre), weight_down, (1, 1))
        d_pre.append((d_act * swish_slope(pre[half].astype(F32))).astype(B16))
    d_norm, (sent, _) = scatter(pieces(d_pre[0], d_pre[1], weight_up, (1, 1)))
    cot, d_pre = after((cot, d_pre), sent)
    grad_down = dot(jnp.concatenate(act, 0), jnp.concatenate(cot, 0), (0, 0))
    grad_up = dot(jnp.concatenate(wide, 0), jnp.concatenate(d_pre, 0), (0, 0))
    grads = (grad_up.astype(B16), grad_down.astype(B16))
    if use is not None:
        d_norm = after(d_norm, use(grads))
    d_in, grad_gain = normalize_back(d_norm, unit, inverse, gain)
    return (grad + d_in, grad_gain, grads, (own, sent))


def places(slots):
    size, mine = lax.axis_size("tp"), lax.axis_index("tp")
    rows = slots // size
    if rows % TK:
        q_at = jnp.arange(slots // TQ, dtype=jnp.int32) * TQ
        k_at = jnp.arange(slots // TK, dtype=jnp.int32) * TK
        return q_at, k_at, True
    q_true = jnp.arange(slots // TQ, dtype=jnp.int32) * TQ
    k_true = jnp.arange(slots // TK, dtype=jnp.int32) * TK
    q_at = ((q_true // rows) ^ mine) * rows + q_true % rows
    k_at = ((k_true // rows) ^ mine) * rows + k_true % rows
    return q_at.astype(jnp.int32), k_at.astype(jnp.int32), False


def attend_forward(
    values, gain, weights, attend_out, content_bias, position_bias, code, spans, rel, prefetch
):
    slots = code.shape[0]
    width = attend_out.shape[0]
    q_at, k_at, reorder = places(slots)
    where = (spans, q_at, k_at)
    normed, unit, inverse = normalize(values, gain)
    near, far = halves(gather(normed.astype(B16)))
    mixed = [dot(near, weights)]
    far = after(far, rel, spans, mixed)
    fetched, arrived = prefetch(far)
    mixed.append(dot(far, weights))
    flat = lambda bias: bias.astype(F32).reshape(1, width)
    join = lambda items: jnp.concatenate(items, 0)
    q_content = join([(item[:, :width] + flat(content_bias)).astype(B16) for item in mixed])
    q_position = join([(item[:, :width] + flat(position_bias)).astype(B16) for item in mixed])
    key = join([item[:, width : 2 * width].astype(B16) for item in mixed])
    value = join([item[:, 2 * width :].astype(B16) for item in mixed])
    if reorder:
        q_content, q_position, key, value = map(to_true, (q_content, q_position, key, value))
    operands = (
        where
        + (q_content, q_position, key, value, rel)
        + (code.reshape(slots, 1), code.reshape(slots // TK, 1, TK))
    )
    heads_out, heads_wide, sums = attend(*operands)
    sent = after(to_true(heads_out) if reorder else heads_out, arrived)
    half = slots // 2
    total, _ = scatter(pieces(sent[:half], sent[half:], attend_out, (1, 0)))
    kept = (unit, inverse, (near, far), operands, heads_wide, sums, sent)
    return (values + total, kept, fetched)


def attend_backward(grad, cot, kept, gain, weights, attend_out, table, filler, use):
    unit, inverse, wide, operands, heads_wide, sums, sent = kept
    slots, width = sent.shape
    _, _, reorder = places(slots)
    cot = halves(cot)
    d_near = dot(cot[0], attend_out, (1, 1)).astype(B16)
    cot = (cot[0], after(cot[1], d_near))
    d_heads = jnp.concatenate([d_near, dot(cot[1], attend_out, (1, 1)).astype(B16)], 0)
    if reorder:
        d_heads = to_true(d_heads)
    d_heads = after(d_heads, filler[0])
    d_all, d_rel, d_bias = attend_back(*operands, d_heads, heads_wide, sums)
    if reorder:
        d_all = to_true(d_all)
    d_all = after(d_all, filler[1])
    half = slots // 2
    d_norm, (last, _) = scatter(pieces(d_all[:half], d_all[half:], weights, (1, 1)))
    cot, d_all, d_rel = after((cot, d_all, d_rel), last)
    grad_out = dot(jnp.concatenate(cot, 0), sent, (0, 0))
    grad_all = dot(jnp.concatenate(wide, 0), d_all, (0, 0))
    grad_pos = dot(table, d_rel, (0, 0))
    grads = [item.astype(B16) for item in (grad_all, grad_pos, grad_out)]
    d_norm = after(d_norm, use(grads, last))
    d_in, grad_gain = normalize_back(d_norm, unit, inverse, gain)
    return (grad + d_in, grad_gain, d_bias[:2])


def conv_weights(point_in, depth_kernel, gain_inner, point_out, first):
    taps = depth_kernel.shape[0]
    own = after((point_in[:, 0], point_in[:, 1], point_out), first)
    small = gather(jnp.concatenate([depth_kernel, gain_inner[None]], 0))
    small = jnp.concatenate(small, 1).astype(F32)
    in_a, in_b, out = map(gather, own)
    arrived = [item[2::2] for item in (in_a, in_b, out)]
    in_a, in_b = jnp.concatenate(in_a, 1), jnp.concatenate(in_b, 1)
    return (in_a, in_b, small[:taps], small[taps], jnp.concatenate(out, 0)), arrived


def conv_masks(segments, valid, rows, taps):
    edge = 8
    reach = taps // 2
    base = lax.axis_index("tp") * rows + edge - reach
    wide_segments = jnp.pad(segments, edge, constant_values=-1)
    wide_valid = jnp.pad(valid, edge)
    own = lax.dynamic_slice_in_dim(wide_segments, base, rows + 2 * reach)
    masks = []
    for tap in range(taps):
        other = lax.dynamic_slice_in_dim(wide_segments, base + tap - reach, rows + 2 * reach)
        good = lax.dynamic_slice_in_dim(wide_valid, base + tap - reach, rows + 2 * reach)
        masks.append(((other == own) & (good == 1)).astype(F32)[:, None])
    return masks


def conv_forward(values, gain, full, masks):
    in_a, in_b, kernel, gain_inner, out = full
    rows = values.shape[0]
    taps = kernel.shape[0]
    reach = taps // 2
    normed, unit, inverse = normalize(values, gain)
    low = normed.astype(B16)
    wide = halo(low, 2 * reach)
    mixed_a = dot(wide, in_a)
    gate = jax.nn.sigmoid(dot(wide, in_b))
    glu = mixed_a * gate
    depth = 0.0
    for tap in range(taps):
        depth = depth + kernel[tap] * masks[tap] * glu[tap : tap + rows + 2 * reach]
    depth_norm, inner_unit, inner_inverse = normalize(depth, gain_inner)
    inner = (depth_norm * jax.nn.sigmoid(depth_norm)).astype(B16)
    own = slice(2 * reach, 2 * reach + rows)
    kept = (unit, inverse, low, mixed_a[own], gate[own], glu, inner_unit, inner_inverse, depth_norm, inner)
    return (values + dot(inner[reach : reach + rows], out), kept)


def conv_backward(grad, kept, gain, full, masks):
    unit, inverse, low, mixed_a, gate, glu, inner_unit, inner_inverse, depth_norm, inner = kept
    in_a, in_b, kernel, gain_inner, out = full
    rows = grad.shape[0]
    taps = kernel.shape[0]
    reach = taps // 2
    mine = slice(reach, reach + rows)
    cot = grad.astype(B16)
    d_act = dot(halo(cot, reach), out, (1, 1))
    d_depth_norm = d_act * swish_slope(depth_norm)
    d_depth, _ = normalize_back(d_depth_norm, inner_unit, inner_inverse, gain_inner)
    d_glu = 0.0
    for tap in range(taps):
        weighted = d_depth * masks[tap]
        back = 2 * reach - tap
        d_glu = d_glu + kernel[tap] * weighted[back : back + rows]
    d_a = (d_glu * gate).astype(B16)
    d_b = (d_glu * mixed_a * gate * (1.0 - gate)).astype(B16)
    d_norm = dot(d_a, in_a, (1, 1)) + dot(d_b, in_b, (1, 1))
    d_in, grad_gain = normalize_back(d_norm, unit, inverse, gain)
    grad = grad + d_in
    slots = gather(grad.astype(B16), True)
    low, cot, d_a, d_b, inner = after((low, cot, d_a, d_b, inner), slots[1])
    size = lax.axis_size("tp")
    width = in_a.shape[1] // size
    parts = []
    grads = [
        dot(left, right, (0, 0)).astype(B16)
        for left, right in ((low, d_a), (low, d_b), (cot, inner[mine]))
    ]

    def small_grads(gate):
        d_own, norm_own = after((d_depth[mine], d_depth_norm[mine]), gate)
        sums = []
        for tap in range(taps):
            near = d_own * masks[tap][mine]
            sums.append(jnp.sum(near * glu[reach + tap : reach + tap + rows], axis=0))
        sums.append(jnp.sum(norm_own * inner_unit[mine], axis=0))
        small = jnp.stack(sums, 0)
        return scatter([small[:, k * width : (k + 1) * width] for k in range(size)])[0]

    for slot in range(size):
        cols = slice(slot * width, (slot + 1) * width)
        parts.append(jnp.concatenate([item[:, cols] for item in grads], 1))
    total, ends = scatter(parts, slots[-1], False)
    return (grad, slots, grad_gain, (total, small_grads), ends)


def body(
    layer_input,
    cotangent,
    segments,
    valid_frames,
    gain_first,
    up_first,
    down_first,
    gain_attend,
    query_weight,
    key_weight,
    value_weight,
    attend_out,
    pos_weight,
    content_bias,
    position_bias,
    gain_conv,
    point_in,
    depth_kernel,
    gain_inner,
    point_out,
    gain_second,
    up_second,
    down_second,
    gain_final,
):
    segment_row, valid_row = segments[0], valid_frames[0]
    weights = jnp.concatenate([query_weight, key_weight, value_weight], 1)
    width = query_weight.shape[1]
    taps = depth_kernel.shape[0]
    values = layer_input[0].astype(F32)
    rows = values.shape[0]
    slots = segment_row.shape[0]
    masks = conv_masks(segment_row, valid_row, rows, taps)
    code = codes(segment_row, valid_row)
    spans = spans_of(code)
    values, kept_first, sent = ffn_forward(values, gain_first, up_first, down_first)
    table = distance_table(slots, values.shape[1], sent)
    rel = dot(table, pos_weight).astype(B16)
    prefetch = functools.partial(conv_weights, point_in, depth_kernel, gain_inner, point_out)
    values, kept_attend, full = attend_forward(
        values, gain_attend, weights, attend_out, content_bias, position_bias, code, spans, rel, prefetch
    )
    values, kept_conv = conv_forward(values, gain_conv, full, masks)
    values, kept_second, _ = ffn_forward(values, gain_second, up_second, down_second)
    final, final_unit, final_inverse = normalize(values, gain_final)
    layer_output = final.astype(B16)
    grad, sum_final = normalize_back(cotangent[0].astype(F32), final_unit, final_inverse, gain_final)
    held = {}

    def start_second(grads):
        held["second"], arrays = start_sum(grads)
        return arrays

    grad, sum_second, _, _ = ffn_backward(
        grad, kept_second, gain_second, up_second, down_second, start_second
    )
    grad, cot, sum_conv, conv_grads, ends = conv_backward(grad, kept_conv, gain_conv, full, masks)
    ends = (ends[0], (ends, held["second"]))

    def start_middle(grads, last):
        own, got = after((conv_grads[0], ends[1][0][1]), last)
        total = (own.astype(F32) + got.astype(F32)).astype(B16)
        forms = [(width, plain)] * 4 + [(width, turned), (2 * width, plain), (width, turned)]
        held["middle"] = row_sum(grads + [total], forms)
        return held["middle"].step()

    grad, sum_attend, d_bias = attend_backward(
        grad, cot, kept_attend, gain_attend, weights, attend_out, table, ends, start_middle
    )
    middle = held["middle"]
    second_sum = end_sum(held["second"])
    grad, sum_first, first_grads, marks = ffn_backward(
        grad, kept_first, gain_first, up_first, down_first, None, middle.step
    )
    first = RowSums(first_grads, [(item.shape[1], plain) for item in first_grads])
    token = middle.step(marks[1])
    token = first.step(token)
    second_sum = after(second_sum, token)
    token = second_sum
    while middle.done < middle.steps:
        token = middle.step(token)
        if first.left > 1:
            token = first.step(token)
        if first.done == 3:
            token = (token, grad)
        if first.done == 5:
            second_up, second_down = split_sum(after(second_sum, token), up_second.shape[0])
            token = (token, second_up, second_down)
    attend_sum = None
    while first.left:
        if first.left == 2:
            token = (token, middle.came())
        if first.left == 1:
            attend_sum = middle.finish(token)
            token = (token, attend_sum)
        token = first.step(token)
    pairs = (sum_first, sum_attend, sum_conv, sum_second, sum_final)
    gains = sum_cube(gain_sums(pairs, marks[1]), "tp")
    small = jnp.concatenate([conv_grads[1](marks[1]), d_bias], 0)
    small_shape = small.shape
    pack = jnp.concatenate([gains.reshape(-1), small.reshape(-1)]).reshape(-1, width)
    pack = sum_cube(after(pack, token), "rows", first.came())
    if attend_sum is None:
        attend_sum = middle.finish(token)
    first_sum = first.finish()
    pack = pack.reshape(-1)
    gains, small = pack[: gains.size].reshape(gains.shape), pack[gains.size :].reshape(small_shape)
    bias_shape = content_bias.shape
    return (
        layer_output[None],
        grad[None],
        gains[0],
        first_sum[0],
        first_sum[1],
        gains[1],
        attend_sum[0],
        attend_sum[1],
        attend_sum[2],
        attend_sum[4],
        attend_sum[3],
        small[taps + 1].reshape(bias_shape),
        small[taps + 2].reshape(bias_shape),
        gains[2],
        attend_sum[5].reshape(attend_sum[5].shape[0], 2, width),
        small[:taps],
        small[taps],
        attend_sum[6],
        gains[3],
        second_up,
        second_down,
        gains[4],
    )


def solution(mesh):
    in_specs = (
        P("rows", "tp", None),
        P("rows", "tp", None),
        P("rows", None),
        P("rows", None),
        P(),
        P(None, "tp"),
        P("tp", None),
        P(),
        P(None, "tp"),
        P(None, "tp"),
        P(None, "tp"),
        P("tp", None),
        P(None, "tp"),
        P("tp", None),
        P("tp", None),
        P(),
        P(None, None, "tp"),
        P(None, "tp"),
        P("tp"),
        P("tp", None),
        P(),
        P(None, "tp"),
        P("tp", None),
        P(),
    )
    out_specs = (
        P("rows", "tp", None),
        P("rows", "tp", None),
        P(),
        P(None, "tp"),
        P("tp", None),
        P(),
        P(None, "tp"),
        P(None, "tp"),
        P(None, "tp"),
        P("tp", None),
        P(None, "tp"),
        P("tp", None),
        P("tp", None),
        P(),
        P(None, None, "tp"),
        P(None, "tp"),
        P("tp"),
        P("tp", None),
        P(),
        P(None, "tp"),
        P("tp", None),
        P(),
    )
    return jax.shard_map(body, mesh=mesh, in_specs=in_specs, out_specs=out_specs, check_vma=False)
```

```python
import functools
import math

import jax
import jax.numpy as jnp
from jax import lax
from jax.experimental import pallas as pl
from jax.experimental.pallas import tpu as pltpu
from jax.sharding import PartitionSpec as P

EPS = 1e-05
NEG = -1e30
F32 = jnp.float32
B16 = jnp.bfloat16
TQ = 384
TK = 384
HD = 128
STEP = 64
LINK_BYTES = 180_000_000
SM = pl.BlockSpec(memory_space=pltpu.SMEM)
VM = pl.BlockSpec(memory_space=pltpu.VMEM)

def dotx(a, b, ca, cb):
    return lax.dot_general(a, b, (((ca,), (cb,)), ((), ())), preferred_element_type=F32)

def skew_tile(grid):
    return pltpu.roll(grid, TK + 1, 1, stride=1, stride_axis=0)[:, :TK]

def unskew_flipped(flipped):
    wide = jnp.concatenate([flipped, jnp.zeros((TQ, TQ), F32)], axis=1)
    return pltpu.roll(wide, 0, 1, stride=1, stride_axis=0)

def attend_kernel(heads, spans, q_at, k_at, qc_ref, qp_ref, k_ref, v_ref, rel_ref, code_q_ref, code_k_ref,
                  out_ref, wide_ref, lse_ref):
    slots = qc_ref.shape[0]
    scale = HD ** -0.5
    blocks, tiles = slots // TQ, slots // TK

    def q_step(qb, _):
        at = pl.multiple_of(q_at[qb], TQ)
        true_at = pl.multiple_of(qb * TQ, TQ)
        code_q = code_q_ref[pl.ds(true_at, TQ), :]
        qc = [qc_ref[pl.ds(at, TQ), h * HD:(h + 1) * HD] for h in range(heads)]
        qp = [qp_ref[pl.ds(at, TQ), h * HD:(h + 1) * HD] for h in range(heads)]

        def k_step(kt, carry):
            ko = pl.multiple_of(k_at[kt], TQ)
            to = pl.multiple_of((blocks - 1 + kt * (TK // TQ) - qb) * TQ, TQ)
            mask = code_q == code_k_ref[kt]
            new = []
            for h in range(heads):
                lanes = slice(h * HD, (h + 1) * HD)
                top, total, acc = carry[h]
                grid = dotx(qp[h], rel_ref[pl.ds(to, TK + TQ), lanes], 1, 1)
                raw = dotx(qc[h], k_ref[pl.ds(ko, TK), lanes], 1, 1) + skew_tile(grid)
                scores = jnp.where(mask, raw * scale, NEG)
                top_new = jnp.maximum(top, jnp.max(scores, axis=1, keepdims=True))
                shrink = jnp.exp(top - top_new)
                weights = jnp.exp(scores - top_new)
                total = total * shrink + jnp.sum(weights, axis=1, keepdims=True)
                acc = acc * shrink + dotx(weights.astype(B16), v_ref[pl.ds(ko, TK), lanes], 1, 0)
                new.append((top_new, total, acc))
            return tuple(new)

        first = tuple((jnp.full((TQ, 1), NEG, F32), jnp.zeros((TQ, 1), F32), jnp.zeros((TQ, HD), F32))
                      for _ in range(heads))
        final = lax.fori_loop(spans[0, qb], spans[1, qb], k_step, first)
        for h in range(heads):
            lanes = slice(h * HD, (h + 1) * HD)
            top, total, acc = final[h]
            out = acc / total
            wide_ref[pl.ds(at, TQ), lanes] = out
            out_ref[pl.ds(at, TQ), lanes] = out.astype(B16)
            lse_ref[pl.ds(at, TQ), h:h + 1] = top + jnp.log(total)
        return 0

    lax.fori_loop(0, blocks, q_step, 0)

def attend_back_kernel(heads, spans, q_at, k_at, qc_ref, qp_ref, k_ref, v_ref, rel_ref, code_q_ref, code_k_ref,
                       d_out_ref, wide_ref, lse_ref,
                       all_ref, drel_ref, bias_ref, dk_acc, dv_acc, drel_acc):
    slots = qc_ref.shape[0]
    scale = HD ** -0.5
    blocks, tiles = slots // TQ, slots // TK
    dk_acc[...] = jnp.zeros_like(dk_acc)
    dv_acc[...] = jnp.zeros_like(dv_acc)
    drel_acc[...] = jnp.zeros_like(drel_acc)
    bias_ref[...] = jnp.zeros_like(bias_ref)
    row = lax.broadcasted_iota(jnp.int32, (TQ, TQ), 0)
    column = lax.broadcasted_iota(jnp.int32, (TQ, TQ), 1)
    flip = (row + column == TQ - 1).astype(F32)
    flip_low = flip.astype(B16)

    def q_step(qb, _):
        at = pl.multiple_of(q_at[qb], TQ)
        true_at = pl.multiple_of(qb * TQ, TQ)
        code_q = code_q_ref[pl.ds(true_at, TQ), :]
        cols = [slice(h * HD, (h + 1) * HD) for h in range(heads)]
        qc = [qc_ref[pl.ds(at, TQ), c] for c in cols]
        qp = [qp_ref[pl.ds(at, TQ), c] for c in cols]
        qp_turned = [dotx(item, flip_low, 0, 0).astype(B16) for item in qp]
        d_out = [d_out_ref[pl.ds(at, TQ), c] for c in cols]
        qc_turned = [item.T for item in qc]
        d_out_turned = [item.T for item in d_out]
        lse = [lse_ref[pl.ds(at, TQ), h:h + 1] for h in range(heads)]
        delta = [jnp.sum(d_out[h].astype(F32) * wide_ref[pl.ds(at, TQ), cols[h]], axis=1, keepdims=True)
                 for h in range(heads)]

        def k_step(kt, carry):
            ko = pl.multiple_of(k_at[kt], TQ)
            to = pl.multiple_of((blocks - 1 + kt * (TK // TQ) - qb) * TQ, TQ)
            mask = code_q == code_k_ref[kt]
            new = []
            for h in range(heads):
                lanes = cols[h]
                d_content, d_position = carry[h]
                window = rel_ref[pl.ds(to, TK + TQ), lanes]
                key = k_ref[pl.ds(ko, TK), lanes]
                grid = dotx(qp[h], window, 1, 1)
                raw = dotx(qc[h], key, 1, 1) + skew_tile(grid)
                probs = jnp.exp(jnp.where(mask, raw * scale - lse[h], NEG))
                d_probs = dotx(d_out[h], v_ref[pl.ds(ko, TK), lanes], 1, 1)
                d_raw = probs * (d_probs - delta[h]) * scale
                d_low = d_raw.astype(B16)
                d_grid = unskew_flipped(dotx(flip_low, d_low, 1, 0)).astype(B16)
                dv_acc[lanes, pl.ds(ko, TK)] += dotx(d_out_turned[h], probs.astype(B16), 1, 0)
                dk_acc[lanes, pl.ds(ko, TK)] += dotx(qc_turned[h], d_low, 1, 0)
                drel_acc[lanes, pl.ds(to, TK + TQ)] += dotx(qp_turned[h], d_grid, 1, 0)
                d_content = d_content + dotx(d_low, key, 1, 0)
                d_position = d_position + dotx(d_grid, window, 1, 0)
                new.append((d_content, d_position))
            return tuple(new)

        first = tuple((jnp.zeros((TQ, HD), F32),) * 2 for _ in range(heads))
        final = lax.fori_loop(spans[0, qb], spans[1, qb], k_step, first)
        for h in range(heads):
            d_content, d_position = final[h]
            d_position = lax.dot_general(flip, d_position, (((1,), (0,)), ((), ())),
                                         precision=lax.Precision.HIGHEST, preferred_element_type=F32)
            all_ref[pl.ds(at, TQ), cols[h]] = (d_content + d_position).astype(B16)
            bias_ref[0:1, cols[h]] += jnp.sum(d_content, axis=0, keepdims=True)
            bias_ref[1:2, cols[h]] += jnp.sum(d_position, axis=0, keepdims=True)
        return 0

    lax.fori_loop(0, blocks, q_step, 0)
    width = dk_acc.shape[0]
    all_ref[:, width : 2 * width] = dk_acc[...].astype(B16).T
    all_ref[:, 2 * width :] = dv_acc[...].astype(B16).T
    drel_ref[...] = drel_acc[...].astype(B16).T

def sds(s, d): return jax.ShapeDtypeStruct(s, d)

def attend(spans, q_at, k_at, qc, qp, k, v, rel, code_q, code_k):
    slots, width = qc.shape
    heads = width // HD
    return pl.pallas_call(
        functools.partial(attend_kernel, heads),
        out_shape=(sds((slots, width), B16), sds((slots, width), F32), sds((slots, heads), F32)),
        in_specs=[SM] * 3 + [VM] * 7, out_specs=(VM,) * 3,
        compiler_params=pltpu.CompilerParams(vmem_limit_bytes=40 << 20),
        cost_estimate=pl.CostEstimate(flops=int(4e9), bytes_accessed=int(9e6), transcendentals=int(2e6)),
    )(spans, q_at, k_at, qc, qp, k, v, rel, code_q, code_k)

def attend_back(spans, q_at, k_at, qc, qp, k, v, rel, code_q, code_k, d_out, wide, lse):
    slots, width = qc.shape
    heads = width // HD
    return pl.pallas_call(
        functools.partial(attend_back_kernel, heads),
        out_shape=(sds((slots, 3 * width), B16), sds((2 * slots, width), B16), sds((8, width), F32)),
        in_specs=[SM] * 3 + [VM] * 10, out_specs=(VM,) * 3,
        scratch_shapes=[pltpu.VMEM((width, slots), F32), pltpu.VMEM((width, slots), F32), pltpu.VMEM((width, 2 * slots), F32)],
        compiler_params=pltpu.CompilerParams(vmem_limit_bytes=48 << 20),
        cost_estimate=pl.CostEstimate(flops=int(1e6), bytes_accessed=int(1e6), transcendentals=0),
    )(spans, q_at, k_at, qc, qp, k, v, rel, code_q, code_k, d_out, wide, lse)

def codes(segments, valid):
    slots = segments.shape[0]
    place = jnp.arange(slots, dtype=jnp.int32)
    code = jnp.where(valid == 1, segments, -1 - place)
    return code

def spans_of(code):
    slots = code.shape[0]
    same = code[:, None] == code[None, :]
    touch = jnp.any(same.reshape(slots // TQ, TQ, slots // TK, TK), axis=(1, 3))
    tiles = slots // TK
    idx = jnp.arange(tiles, dtype=jnp.int32)
    lo = jnp.min(jnp.where(touch, idx, tiles), axis=1)
    hi = jnp.max(jnp.where(touch, idx + 1, 0), axis=1)
    return jnp.stack([lo, hi], 0).astype(jnp.int32)


def normalize(values, gain):
    mean = jnp.mean(values, axis=-1, keepdims=True)
    centered = values - mean
    inverse = lax.rsqrt(jnp.mean(centered * centered, axis=-1, keepdims=True) + EPS)
    unit = centered * inverse
    return (unit * gain.astype(F32), unit, inverse)


def normalize_back(grad, unit, inverse, gain):
    scaled = grad * gain.astype(F32)
    first = jnp.mean(scaled, axis=-1, keepdims=True)
    second = jnp.mean(scaled * unit, axis=-1, keepdims=True)
    return (inverse * (scaled - first - unit * second), (grad, unit))


def gain_sums(pairs, gate):
    return jnp.stack([jnp.sum(grad * unit, axis=0) for grad, unit in after(pairs, gate)])


def swish_slope(values):
    gate = jax.nn.sigmoid(values)
    return gate * (1.0 + values * (1.0 - gate))


def distance_table(slots, width, first):
    column = jnp.arange(width)
    even = (column % 2 == 0)[None, :]
    rate = jnp.exp(-(column - column % 2).astype(F32) * (math.log(10000.0) / width))
    coarse = (slots - 1 - STEP * jnp.arange(2 * slots // STEP)).astype(F32)[:, None] * rate[None, :]
    fine = jnp.arange(STEP).astype(F32)[:, None] * rate[None, :]
    sin_c, cos_c = jnp.sin(coarse), jnp.cos(coarse)
    with_cos = jnp.where(even, sin_c, cos_c)
    with_sin = jnp.where(even, -cos_c, sin_c)
    with_cos, with_sin, sin_f, cos_f = after((with_cos, with_sin, jnp.sin(fine), jnp.cos(fine)), first)
    table = with_cos[:, None, :] * cos_f[None] + with_sin[:, None, :] * sin_f[None]
    return table.reshape(2 * slots, width).astype(B16)


def dot(left, right, contract=(1, 0)):
    return lax.dot_general(
        left, right, (((contract[0],), (contract[1],)), ((), ())), preferred_element_type=F32
    )


def swap(values, distance):
    size = lax.axis_size("tp")
    return lax.ppermute(values, "tp", [(i, i ^ distance) for i in range(size)])


def distances():
    size = lax.axis_size("tp")
    return [1 << bit for bit in range(size.bit_length() - 1)]


def same_kernel(block_ref, out_ref):
    pass


def arrived(block):
    spec = pl.BlockSpec(memory_space=pl.ANY)
    return pl.pallas_call(
        same_kernel,
        in_specs=[spec],
        out_specs=spec,
        out_shape=jax.ShapeDtypeStruct(block.shape, block.dtype),
        input_output_aliases={0: 0},
        cost_estimate=pl.CostEstimate(flops=0, bytes_accessed=LINK_BYTES, transcendentals=0),
    )(block)


def gather(own, first=False, late=()):
    slots = {0: own}
    for distance in reversed(distances()):
        for slot in list(slots):
            slots[slot ^ distance] = swap(slots[slot], distance)
    last = len(slots) - 1
    if first:
        slots[last] = after(arrived(slots[last]), late)
    return [slots[slot] for slot in range(len(slots))]


def scatter(parts, late=(), add=True):
    parts = dict(enumerate(parts))
    sent = got = None
    for distance in distances():
        for slot in sorted(parts, reverse=True):
            if slot & distance:
                sent = parts.pop(slot).astype(B16)
                if distance == distances()[-1]:
                    sent = after(sent, late)
                got = swap(sent, distance)
                if add or distance != distances()[-1]:
                    parts[slot ^ distance] = parts[slot ^ distance].astype(F32) + got.astype(F32)
    return parts[0], (sent, got)


def after(values, *others):
    return lax.optimization_barrier((values, others))[0]


def halves(slots):
    half = len(slots) // 2
    return jnp.concatenate(slots[:half], 0), jnp.concatenate(slots[half:], 0)


def pieces(near, far, weight, contract):
    count = lax.axis_size("tp") // 2
    rows = near.shape[0] // count
    outs = {}
    for slot in reversed(range(2 * count)):
        source, place = (near, slot) if slot < count else (far, slot - count)
        outs[slot] = dot(source[place * rows : (place + 1) * rows], weight, contract)
    return [outs[slot] for slot in range(2 * count)]


def ring():
    size, mine = lax.axis_size("rows"), lax.axis_index("rows")
    order = list(range(0, size, 2)) + list(range(size - 1, 0, -2))
    place = jnp.where(mine % 2 == 0, mine // 2, size - (mine + 1) // 2)
    right = [(order[i], order[(i + 1) % size]) for i in range(size)]
    return size, place, right, [(there, here) for here, there in right]


def plain(piece):
    return piece


def turned(piece):
    return piece.T


def first_kernel(at, *refs):
    count = (len(refs) - 2) // 2
    refs[-2][...] = jnp.concatenate([ref[...] for ref in refs[:count]], 1)
    refs[-1][...] = jnp.concatenate([ref[...] for ref in refs[count:-2]], 1)


def pass_kernel(second, at, *refs):
    count = (len(refs) - 4) // 2
    from_left, from_right = (ref[...].astype(F32) for ref in refs[-4:-2])
    if second:
        top = pl.program_id(0) == 0
        from_left = jnp.where(top, from_left, 0.0)
        from_right = jnp.where(top, 0.0, from_right)
    own = jnp.concatenate([ref[...] for ref in refs[:count]], 1).astype(F32)
    refs[-2][...] = (own + from_left).astype(B16)
    own = jnp.concatenate([ref[...] for ref in refs[count:-4]], 1).astype(F32)
    refs[-1][...] = (own + from_right).astype(B16)


def total_kernel(split, at, *refs):
    own = jnp.concatenate([ref[...] for ref in refs[:-3]], 1).astype(F32)
    from_left, from_right = (ref[...].astype(F32) for ref in refs[-3:-1])
    if split:
        refs[-1][...] = (own + jnp.concatenate([from_left, from_right], 0)).astype(B16)
    else:
        refs[-1][...] = (own + from_left + from_right).astype(B16)


def place_kernel(spots, spans, at, *refs):
    count = len(spots)
    outs, held = refs[count : count + len(spans)], refs[-1]
    half = refs[count - 1].shape[0]
    size = held.shape[0] // (2 * half)
    for ref, (k, bottom) in zip(refs[:count], spots):
        start = ((at[0] + k) % size) * (2 * half) + bottom * half
        start = pl.multiple_of(start, half)
        held[pl.ds(start, ref.shape[0]), :] = ref[...].astype(F32)
    for out, (low, high, form) in zip(outs, spans):
        here = (pl.program_id(0) >= low) & (pl.program_id(0) < high)

        @pl.when(here)
        def _(out=out, form=form):
            out[...] = form(held[...])


class RowSum:
    def __init__(self, arrays, parts):
        self.size, self.place, self.right, self.left = ring()
        self.arrays, self.parts = list(arrays), parts
        self.width = sum(item.shape[1] for item in arrays)
        self.rows = arrays[0].shape[0] // self.size
        self.half = self.rows // 2
        self.stages = self.size // 2
        self.steps = 2 * self.stages
        self.done = 0
        self.seen = []

    def call(self, kernel, at, blocks, extra, out_rows, grid, gate, out_blocks, count=2):
        arrays, extra = after((self.arrays, extra), gate)
        specs, operands = [], []
        for rows, index in blocks:
            for item in arrays:
                specs.append(pl.BlockSpec((rows, item.shape[1]), index))
                operands.append(item)
        for item, (rows, index) in zip(extra, out_blocks[1]):
            specs.append(pl.BlockSpec((rows, self.width), index))
            operands.append(item)
        rows, index = out_blocks[0]
        moved = sum(2 * rows * self.width for _ in range(4))
        return pl.pallas_call(
            kernel,
            grid_spec=pltpu.PrefetchScalarGridSpec(
                num_scalar_prefetch=1,
                grid=(grid,),
                in_specs=specs,
                out_specs=[pl.BlockSpec((rows, self.width), index)] * count,
            ),
            out_shape=(sds((out_rows, self.width), B16),) * count,
            cost_estimate=pl.CostEstimate(flops=moved, bytes_accessed=moved, transcendentals=0),
        )(at, *operands)

    def send(self, to_right, to_left):
        over = lambda items, way: [lax.ppermute(item, "rows", way) for item in items]
        self.from_left, self.from_right = over(to_right, self.right), over(to_left, self.left)
        return (to_right, to_left)

    def step(self, gate=()):
        stage, stages, half, rows = self.done, self.stages, self.half, self.rows
        self.done += 1
        ids = [(self.place + k) % self.size for k in (stages - stage, stage - stages)]
        at = jnp.stack(ids).astype(jnp.int32)
        whole = lambda i, at: (0, 0)
        if stage == 0:
            blocks = [(half, lambda i, at: (2 * at[0], 0)), (half, lambda i, at: (2 * at[1] + 1, 0))]
            out = self.call(first_kernel, at, blocks, [], half, 1, gate, ((half, whole), []))
            return self.send([out[0]], [out[1]])
        if stage < stages:
            blocks = [
                (half, lambda i, at: (2 * at[0] + i, 0)), (half, lambda i, at: (2 * at[1] + i, 0)),
            ]
            here = (half, lambda i, at: (i, 0))
            got = (half, whole) if stage == 1 else here
            kernel = functools.partial(pass_kernel, stage == 1)
            extra = self.from_left + self.from_right
            out = self.call(kernel, at, blocks, extra, rows, 2, gate, (here, [got, got]))
            return self.send([out[0]], [out[1]])
        if stage == stages:
            got = (half if stages == 1 else rows, whole)
            kernel = functools.partial(total_kernel, stages == 1)
            extra = self.from_left + self.from_right
            blocks = [(rows, lambda i, at: (at[0], 0))]
            blocks = [(half, lambda i, at: (2 * at[0] + i, 0))] if stages > 1 else blocks
            here = (half, lambda i, at: (i, 0)) if stages > 1 else (rows, whole)
            got = here if stages > 1 else got
            grid = 2 if stages > 1 else 1
            out = self.call(kernel, at, blocks, extra, rows, grid, gate, (here, [got, got]), 1)
            to_right = to_left = list(out)
            self.see(to_right, 0)
        else:
            to_right, to_left = after((self.from_left, self.from_right), gate)
            self.see(to_right, stages - stage)
            self.see(to_left, stage - stages)
        if stage == 2 * stages - 1:
            to_right, to_left = [to_right[0][:half]], [to_left[0][half:]]
        return self.send(to_right, to_left)

    def came(self):
        return self.from_left + self.from_right

    def see(self, items, k):
        self.seen.append((items[0], (k, 0)))

    def finish(self, gate=()):
        self.seen += [(self.from_left[0], (-self.stages, 0)), (self.from_right[0], (self.stages, 1))]
        items = after([item for item, _ in self.seen], gate)
        spots = [((k + self.size) % self.size, bottom) for _, (k, bottom) in self.seen]
        length = self.arrays[0].shape[0]
        step = math.gcd(*[width for width, _ in self.parts])
        spans, specs, shapes, low = [], [], [], 0
        for width, form in self.parts:
            count = width // step
            spans.append((low, low + count, form))

            def column(i, at, low=low, count=count):
                return jnp.clip(i - low, 0, count - 1)

            if form is turned:
                shapes.append((width, length))
                specs.append(pl.BlockSpec((step, length), lambda i, at, f=column: (f(i, at), 0)))
            else:
                shapes.append((length, width))
                specs.append(pl.BlockSpec((length, step), lambda i, at, f=column: (0, f(i, at))))
            low += count
        moved = 6 * length * self.width
        return pl.pallas_call(
            functools.partial(place_kernel, spots, spans),
            grid_spec=pltpu.PrefetchScalarGridSpec(
                num_scalar_prefetch=1,
                grid=(low,),
                in_specs=[pl.BlockSpec((item.shape[0], step), lambda i, at: (0, i)) for item in items],
                out_specs=specs,
                scratch_shapes=[pltpu.VMEM((length, step), F32)],
            ),
            out_shape=[sds(shape, F32) for shape in shapes],
            compiler_params=pltpu.CompilerParams(vmem_limit_bytes=60 << 20),
            cost_estimate=pl.CostEstimate(flops=moved, bytes_accessed=moved, transcendentals=0),
        )(self.place.reshape(1).astype(jnp.int32), *items)


class WholeSum:
    came = staticmethod(lambda: ())

    def __init__(self, arrays, parts):
        self.arrays, self.parts, self.steps, self.done = list(arrays), parts, 1, 0

    def step(self, gate=()):
        self.done += 1
        values = after(jnp.concatenate(self.arrays, 1), gate)
        self.total = lax.psum(values, "rows").astype(F32)
        return ()

    def finish(self, gate=()):
        edges = [sum(width for width, _ in self.parts[:k]) for k in range(len(self.parts) + 1)]
        return [
            form(self.total[:, edges[k] : edges[k + 1]]) for k, (_, form) in enumerate(self.parts)
        ]


def row_sum(arrays, parts):
    size = lax.axis_size("rows")
    fits = size % 2 == 0 and arrays[0].shape[0] % (16 * size) == 0
    return (RowSum if fits else WholeSum)(arrays, parts)


def start_sum(arrays):
    if arrays[0].shape[1] == arrays[1].shape[1]:
        arrays = [jnp.concatenate(arrays, 0)]
    return [lax.psum_scatter(item, "rows", scatter_dimension=0, tiled=True) for item in arrays]


def end_sum(shares):
    return [lax.all_gather(item, "rows", axis=0, tiled=True) for item in shares]


def split_sum(whole, rows):
    if len(whole) == 1:
        whole = [whole[0][:rows], whole[0][rows:]]
    return [item.astype(F32) for item in whole]


class RowSums:
    def __init__(self, arrays, parts):
        if all(item.shape[0] == arrays[0].shape[0] for item in arrays):
            self.items = [row_sum(arrays, parts)]
        else:
            self.items = [row_sum([item], [part]) for item, part in zip(arrays, parts)]

    def came(self):
        return [item.came() for item in self.items]

    @property
    def done(self):
        return self.items[0].done

    @property
    def left(self):
        return max(item.steps - item.done for item in self.items)

    def step(self, gate=()):
        for item in self.items:
            if item.done < item.steps:
                gate = item.step(gate)
        return gate

    def finish(self, gate=()):
        while self.left:
            gate = self.step(gate)
        return [out for item in self.items for out in item.finish(gate)]


def sum_cube(values, axis, late=()):
    size = lax.axis_size(axis)
    if size & (size - 1):
        return lax.psum(values, axis)
    distance = 1
    while distance < size:
        values = values + lax.ppermute(values, axis, [(i, i ^ distance) for i in range(size)])
        values = after(values, late)
        distance *= 2
    return values


def halo(own, reach):
    size = lax.axis_size("tp")
    left = lax.ppermute(own[-reach:], "tp", [(i, i + 1) for i in range(size - 1)])
    right = lax.ppermute(own[:reach], "tp", [(i + 1, i) for i in range(size - 1)])
    return jnp.concatenate([left, own, right], 0)


def to_true(values):
    size, mine = lax.axis_size("tp"), lax.axis_index("tp")
    rows = values.shape[0] // size
    return jnp.concatenate(
        [lax.dynamic_slice_in_dim(values, (mine ^ k) * rows, rows, 0) for k in range(size)], 0
    )


def ffn_forward(values, gain, weight_up, weight_down):
    normed, unit, inverse = normalize(values, gain)
    near, far = halves(gather(normed.astype(B16)))
    pre, act = [], []
    for half in (near, far):
        pre.append(dot(after(half, act), weight_up))
        act.append((pre[-1] * jax.nn.sigmoid(pre[-1])).astype(B16))
    total, (sent, _) = scatter(pieces(act[0], act[1], weight_down, (1, 0)))
    pre = [item.astype(B16) for item in pre]
    return (values + 0.5 * total, (unit, inverse, (near, far), pre, act), sent)


def ffn_backward(grad, kept, gain, weight_up, weight_down, use=None, fill=None):
    unit, inverse, wide, pre, act = kept
    own = (0.5 * grad).astype(B16)
    cot = halves(gather(own) if fill is None else gather(own, True, fill(own)))
    d_pre = []
    for half in (0, 1):
        d_act = dot(after(cot[half], d_pre), weight_down, (1, 1))
        d_pre.append((d_act * swish_slope(pre[half].astype(F32))).astype(B16))
    d_norm, (sent, _) = scatter(pieces(d_pre[0], d_pre[1], weight_up, (1, 1)))
    cot, d_pre = after((cot, d_pre), sent)
    grad_down = dot(jnp.concatenate(act, 0), jnp.concatenate(cot, 0), (0, 0))
    grad_up = dot(jnp.concatenate(wide, 0), jnp.concatenate(d_pre, 0), (0, 0))
    grads = (grad_up.astype(B16), grad_down.astype(B16))
    if use is not None:
        d_norm = after(d_norm, use(grads))
    d_in, grad_gain = normalize_back(d_norm, unit, inverse, gain)
    return (grad + d_in, grad_gain, grads, (own, sent))


def places(slots):
    size, mine = lax.axis_size("tp"), lax.axis_index("tp")
    rows = slots // size
    if rows % TK:
        q_at = jnp.arange(slots // TQ, dtype=jnp.int32) * TQ
        k_at = jnp.arange(slots // TK, dtype=jnp.int32) * TK
        return q_at, k_at, True
    q_true = jnp.arange(slots // TQ, dtype=jnp.int32) * TQ
    k_true = jnp.arange(slots // TK, dtype=jnp.int32) * TK
    q_at = ((q_true // rows) ^ mine) * rows + q_true % rows
    k_at = ((k_true // rows) ^ mine) * rows + k_true % rows
    return q_at.astype(jnp.int32), k_at.astype(jnp.int32), False


def attend_forward(
    values, gain, weights, attend_out, content_bias, position_bias, code, spans, rel, prefetch
):
    slots = code.shape[0]
    width = attend_out.shape[0]
    q_at, k_at, reorder = places(slots)
    where = (spans, q_at, k_at)
    normed, unit, inverse = normalize(values, gain)
    near, far = halves(gather(normed.astype(B16)))
    mixed = [dot(near, weights)]
    far = after(far, rel, spans, mixed)
    fetched, arrived = prefetch(far)
    mixed.append(dot(far, weights))
    flat = lambda bias: bias.astype(F32).reshape(1, width)
    join = lambda items: jnp.concatenate(items, 0)
    q_content = join([(item[:, :width] + flat(content_bias)).astype(B16) for item in mixed])
    q_position = join([(item[:, :width] + flat(position_bias)).astype(B16) for item in mixed])
    key = join([item[:, width : 2 * width].astype(B16) for item in mixed])
    value = join([item[:, 2 * width :].astype(B16) for item in mixed])
    if reorder:
        q_content, q_position, key, value = map(to_true, (q_content, q_position, key, value))
    operands = (
        where
        + (q_content, q_position, key, value, rel)
        + (code.reshape(slots, 1), code.reshape(slots // TK, 1, TK))
    )
    heads_out, heads_wide, sums = attend(*operands)
    sent = after(to_true(heads_out) if reorder else heads_out, arrived)
    half = slots // 2
    total, _ = scatter(pieces(sent[:half], sent[half:], attend_out, (1, 0)))
    kept = (unit, inverse, (near, far), operands, heads_wide, sums, sent)
    return (values + total, kept, fetched)


def attend_backward(grad, cot, kept, gain, weights, attend_out, table, filler, use):
    unit, inverse, wide, operands, heads_wide, sums, sent = kept
    slots, width = sent.shape
    _, _, reorder = places(slots)
    cot = halves(cot)
    d_near = dot(cot[0], attend_out, (1, 1)).astype(B16)
    cot = (cot[0], after(cot[1], d_near))
    d_heads = jnp.concatenate([d_near, dot(cot[1], attend_out, (1, 1)).astype(B16)], 0)
    if reorder:
        d_heads = to_true(d_heads)
    d_heads = after(d_heads, filler[0])
    d_all, d_rel, d_bias = attend_back(*operands, d_heads, heads_wide, sums)
    if reorder:
        d_all = to_true(d_all)
    d_all = after(d_all, filler[1])
    half = slots // 2
    d_norm, (last, _) = scatter(pieces(d_all[:half], d_all[half:], weights, (1, 1)))
    cot, d_all, d_rel = after((cot, d_all, d_rel), last)
    grad_out = dot(jnp.concatenate(cot, 0), sent, (0, 0))
    grad_all = dot(jnp.concatenate(wide, 0), d_all, (0, 0))
    grad_pos = dot(table, d_rel, (0, 0))
    grads = [item.astype(B16) for item in (grad_all, grad_pos, grad_out)]
    d_norm = after(d_norm, use(grads, last))
    d_in, grad_gain = normalize_back(d_norm, unit, inverse, gain)
    return (grad + d_in, grad_gain, d_bias[:2])


def conv_weights(point_in, depth_kernel, gain_inner, point_out, first):
    taps = depth_kernel.shape[0]
    own = after((point_in[:, 0], point_in[:, 1], point_out), first)
    small = gather(jnp.concatenate([depth_kernel, gain_inner[None]], 0))
    small = jnp.concatenate(small, 1).astype(F32)
    in_a, in_b, out = map(gather, own)
    arrived = [item[2::2] for item in (in_a, in_b, out)]
    in_a, in_b = jnp.concatenate(in_a, 1), jnp.concatenate(in_b, 1)
    return (in_a, in_b, small[:taps], small[taps], jnp.concatenate(out, 0)), arrived


def conv_masks(segments, valid, rows, taps):
    edge = 8
    reach = taps // 2
    base = lax.axis_index("tp") * rows + edge - reach
    wide_segments = jnp.pad(segments, edge, constant_values=-1)
    wide_valid = jnp.pad(valid, edge)
    own = lax.dynamic_slice_in_dim(wide_segments, base, rows + 2 * reach)
    masks = []
    for tap in range(taps):
        other = lax.dynamic_slice_in_dim(wide_segments, base + tap - reach, rows + 2 * reach)
        good = lax.dynamic_slice_in_dim(wide_valid, base + tap - reach, rows + 2 * reach)
        masks.append(((other == own) & (good == 1)).astype(F32)[:, None])
    return masks


def conv_forward(values, gain, full, masks):
    in_a, in_b, kernel, gain_inner, out = full
    rows = values.shape[0]
    taps = kernel.shape[0]
    reach = taps // 2
    normed, unit, inverse = normalize(values, gain)
    low = normed.astype(B16)
    wide = halo(low, 2 * reach)
    mixed_a = dot(wide, in_a)
    gate = jax.nn.sigmoid(dot(wide, in_b))
    glu = mixed_a * gate
    depth = 0.0
    for tap in range(taps):
        depth = depth + kernel[tap] * masks[tap] * glu[tap : tap + rows + 2 * reach]
    depth_norm, inner_unit, inner_inverse = normalize(depth, gain_inner)
    inner = (depth_norm * jax.nn.sigmoid(depth_norm)).astype(B16)
    own = slice(2 * reach, 2 * reach + rows)
    kept = (unit, inverse, low, mixed_a[own], gate[own], glu, inner_unit, inner_inverse, depth_norm, inner)
    return (values + dot(inner[reach : reach + rows], out), kept)


def conv_backward(grad, kept, gain, full, masks):
    unit, inverse, low, mixed_a, gate, glu, inner_unit, inner_inverse, depth_norm, inner = kept
    in_a, in_b, kernel, gain_inner, out = full
    rows = grad.shape[0]
    taps = kernel.shape[0]
    reach = taps // 2
    mine = slice(reach, reach + rows)
    cot = grad.astype(B16)
    d_act = dot(halo(cot, reach), out, (1, 1))
    d_depth_norm = d_act * swish_slope(depth_norm)
    d_depth, _ = normalize_back(d_depth_norm, inner_unit, inner_inverse, gain_inner)
    d_glu = 0.0
    for tap in range(taps):
        weighted = d_depth * masks[tap]
        back = 2 * reach - tap
        d_glu = d_glu + kernel[tap] * weighted[back : back + rows]
    d_a = (d_glu * gate).astype(B16)
    d_b = (d_glu * mixed_a * gate * (1.0 - gate)).astype(B16)
    d_norm = dot(d_a, in_a, (1, 1)) + dot(d_b, in_b, (1, 1))
    d_in, grad_gain = normalize_back(d_norm, unit, inverse, gain)
    grad = grad + d_in
    slots = gather(grad.astype(B16), True)
    low, cot, d_a, d_b, inner = after((low, cot, d_a, d_b, inner), slots[1])
    size = lax.axis_size("tp")
    width = in_a.shape[1] // size
    parts = []
    grads = [
        dot(left, right, (0, 0)).astype(B16)
        for left, right in ((low, d_a), (low, d_b), (cot, inner[mine]))
    ]

    def small_grads(gate):
        d_own, norm_own = after((d_depth[mine], d_depth_norm[mine]), gate)
        sums = []
        for tap in range(taps):
            near = d_own * masks[tap][mine]
            sums.append(jnp.sum(near * glu[reach + tap : reach + tap + rows], axis=0))
        sums.append(jnp.sum(norm_own * inner_unit[mine], axis=0))
        small = jnp.stack(sums, 0)
        return scatter([small[:, k * width : (k + 1) * width] for k in range(size)])[0]

    for slot in range(size):
        cols = slice(slot * width, (slot + 1) * width)
        parts.append(jnp.concatenate([item[:, cols] for item in grads], 1))
    total, ends = scatter(parts, slots[-1], False)
    return (grad, slots, grad_gain, (total, small_grads), ends)


def body(
    layer_input,
    cotangent,
    segments,
    valid_frames,
    gain_first,
    up_first,
    down_first,
    gain_attend,
    query_weight,
    key_weight,
    value_weight,
    attend_out,
    pos_weight,
    content_bias,
    position_bias,
    gain_conv,
    point_in,
    depth_kernel,
    gain_inner,
    point_out,
    gain_second,
    up_second,
    down_second,
    gain_final,
):
    segment_row, valid_row = segments[0], valid_frames[0]
    weights = jnp.concatenate([query_weight, key_weight, value_weight], 1)
    width = query_weight.shape[1]
    taps = depth_kernel.shape[0]
    values = layer_input[0].astype(F32)
    rows = values.shape[0]
    slots = segment_row.shape[0]
    masks = conv_masks(segment_row, valid_row, rows, taps)
    code = codes(segment_row, valid_row)
    spans = spans_of(code)
    values, kept_first, sent = ffn_forward(values, gain_first, up_first, down_first)
    table = distance_table(slots, values.shape[1], sent)
    rel = dot(table, pos_weight).astype(B16)
    prefetch = functools.partial(conv_weights, point_in, depth_kernel, gain_inner, point_out)
    values, kept_attend, full = attend_forward(
        values, gain_attend, weights, attend_out, content_bias, position_bias, code, spans, rel, prefetch
    )
    values, kept_conv = conv_forward(values, gain_conv, full, masks)
    values, kept_second, _ = ffn_forward(values, gain_second, up_second, down_second)
    final, final_unit, final_inverse = normalize(values, gain_final)
    layer_output = final.astype(B16)
    grad, sum_final = normalize_back(cotangent[0].astype(F32), final_unit, final_inverse, gain_final)
    held = {}

    def start_second(grads):
        held["second"] = start_sum(grads)
        return grads

    grad, sum_second, _, _ = ffn_backward(
        grad, kept_second, gain_second, up_second, down_second, start_second
    )
    grad, cot, sum_conv, conv_grads, ends = conv_backward(grad, kept_conv, gain_conv, full, masks)
    ends = (ends[0], (ends, held["second"]))

    def start_middle(grads, last):
        own, got = after((conv_grads[0], ends[1][0][1]), last)
        total = (own.astype(F32) + got.astype(F32)).astype(B16)
        forms = [(width, plain)] * 4 + [(width, turned), (2 * width, plain), (width, turned)]
        held["middle"] = row_sum(grads + [total], forms)
        return held["middle"].step()

    grad, sum_attend, d_bias = attend_backward(
        grad, cot, kept_attend, gain_attend, weights, attend_out, table, ends, start_middle
    )
    middle = held["middle"]
    second_sum = end_sum(held["second"])
    grad, sum_first, first_grads, marks = ffn_backward(
        grad, kept_first, gain_first, up_first, down_first, None, middle.step
    )
    first = RowSums(first_grads, [(item.shape[1], plain) for item in first_grads])
    token = middle.step(marks[1])
    token = first.step(token)
    second_sum = after(second_sum, token)
    token = second_sum
    while middle.done < middle.steps:
        token = middle.step(token)
        if first.left > 1:
            token = first.step(token)
        if first.done == 3:
            token = (token, grad)
        if first.done == 5:
            second_up, second_down = split_sum(after(second_sum, token), up_second.shape[0])
            token = (token, second_up, second_down)
    while first.left:
        token = first.step(token)
    pairs = (sum_first, sum_attend, sum_conv, sum_second, sum_final)
    gains = sum_cube(gain_sums(pairs, marks[1]), "tp")
    small = jnp.concatenate([conv_grads[1](marks[1]), d_bias], 0)
    small_shape = small.shape
    pack = jnp.concatenate([gains.reshape(-1), small.reshape(-1)]).reshape(-1, width)
    pack = sum_cube(after(pack, token), "rows", first.came())
    attend_sum = middle.finish(token)
    first_sum = first.finish(attend_sum)
    pack = pack.reshape(-1)
    gains, small = pack[: gains.size].reshape(gains.shape), pack[gains.size :].reshape(small_shape)
    bias_shape = content_bias.shape
    return (
        layer_output[None],
        grad[None],
        gains[0],
        first_sum[0],
        first_sum[1],
        gains[1],
        attend_sum[0],
        attend_sum[1],
        attend_sum[2],
        attend_sum[4],
        attend_sum[3],
        small[taps + 1].reshape(bias_shape),
        small[taps + 2].reshape(bias_shape),
        gains[2],
        attend_sum[5].reshape(attend_sum[5].shape[0], 2, width),
        small[:taps],
        small[taps],
        attend_sum[6],
        gains[3],
        second_up,
        second_down,
        gains[4],
    )


def solution(mesh):
    in_specs = (
        P("rows", "tp", None),
        P("rows", "tp", None),
        P("rows", None),
        P("rows", None),
        P(),
        P(None, "tp"),
        P("tp", None),
        P(),
        P(None, "tp"),
        P(None, "tp"),
        P(None, "tp"),
        P("tp", None),
        P(None, "tp"),
        P("tp", None),
        P("tp", None),
        P(),
        P(None, None, "tp"),
        P(None, "tp"),
        P("tp"),
        P("tp", None),
        P(),
        P(None, "tp"),
        P("tp", None),
        P(),
    )
    out_specs = (
        P("rows", "tp", None),
        P("rows", "tp", None),
        P(),
        P(None, "tp"),
        P("tp", None),
        P(),
        P(None, "tp"),
        P(None, "tp"),
        P(None, "tp"),
        P("tp", None),
        P(None, "tp"),
        P("tp", None),
        P("tp", None),
        P(),
        P(None, None, "tp"),
        P(None, "tp"),
        P("tp"),
        P("tp", None),
        P(),
        P(None, "tp"),
        P("tp", None),
        P(),
    )
    return jax.shard_map(body, mesh=mesh, in_specs=in_specs, out_specs=out_specs, check_vma=False)
```

```python
import functools
import math

import jax
import jax.numpy as jnp
from jax import lax
from jax.experimental import pallas as pl
from jax.experimental.pallas import tpu as pltpu
from jax.sharding import PartitionSpec as P

EPS = 1e-05
NEG = -1e30
F32 = jnp.float32
B16 = jnp.bfloat16
TQ = 384
TK = 384
HD = 128
STEP = 64
LINK_BYTES = 180_000_000
SM = pl.BlockSpec(memory_space=pltpu.SMEM)
VM = pl.BlockSpec(memory_space=pltpu.VMEM)

def dotx(a, b, ca, cb):
    return lax.dot_general(a, b, (((ca,), (cb,)), ((), ())), preferred_element_type=F32)

def skew_tile(grid):
    return pltpu.roll(grid, TK + 1, 1, stride=1, stride_axis=0)[:, :TK]

def unskew_flipped(flipped):
    wide = jnp.concatenate([flipped, jnp.zeros((TQ, TQ), F32)], axis=1)
    return pltpu.roll(wide, 0, 1, stride=1, stride_axis=0)

def attend_kernel(heads, spans, q_at, k_at, qc_ref, qp_ref, k_ref, v_ref, rel_ref, code_q_ref, code_k_ref,
                  out_ref, wide_ref, lse_ref):
    slots = qc_ref.shape[0]
    scale = HD ** -0.5
    blocks, tiles = slots // TQ, slots // TK

    def q_step(qb, _):
        at = pl.multiple_of(q_at[qb], TQ)
        true_at = pl.multiple_of(qb * TQ, TQ)
        code_q = code_q_ref[pl.ds(true_at, TQ), :]
        qc = [qc_ref[pl.ds(at, TQ), h * HD:(h + 1) * HD] for h in range(heads)]
        qp = [qp_ref[pl.ds(at, TQ), h * HD:(h + 1) * HD] for h in range(heads)]

        def k_step(kt, carry):
            ko = pl.multiple_of(k_at[kt], TQ)
            to = pl.multiple_of((blocks - 1 + kt * (TK // TQ) - qb) * TQ, TQ)
            mask = code_q == code_k_ref[kt]
            new = []
            for h in range(heads):
                lanes = slice(h * HD, (h + 1) * HD)
                top, total, acc = carry[h]
                grid = dotx(qp[h], rel_ref[pl.ds(to, TK + TQ), lanes], 1, 1)
                raw = dotx(qc[h], k_ref[pl.ds(ko, TK), lanes], 1, 1) + skew_tile(grid)
                scores = jnp.where(mask, raw * scale, NEG)
                top_new = jnp.maximum(top, jnp.max(scores, axis=1, keepdims=True))
                shrink = jnp.exp(top - top_new)
                weights = jnp.exp(scores - top_new)
                total = total * shrink + jnp.sum(weights, axis=1, keepdims=True)
                acc = acc * shrink + dotx(weights.astype(B16), v_ref[pl.ds(ko, TK), lanes], 1, 0)
                new.append((top_new, total, acc))
            return tuple(new)

        first = tuple((jnp.full((TQ, 1), NEG, F32), jnp.zeros((TQ, 1), F32), jnp.zeros((TQ, HD), F32))
                      for _ in range(heads))
        final = lax.fori_loop(spans[0, qb], spans[1, qb], k_step, first)
        for h in range(heads):
            lanes = slice(h * HD, (h + 1) * HD)
            top, total, acc = final[h]
            out = acc / total
            wide_ref[pl.ds(at, TQ), lanes] = out
            out_ref[pl.ds(at, TQ), lanes] = out.astype(B16)
            lse_ref[pl.ds(at, TQ), h:h + 1] = top + jnp.log(total)
        return 0

    lax.fori_loop(0, blocks, q_step, 0)

def attend_back_kernel(heads, spans, q_at, k_at, qc_ref, qp_ref, k_ref, v_ref, rel_ref, code_q_ref, code_k_ref,
                       d_out_ref, wide_ref, lse_ref,
                       all_ref, drel_ref, bias_ref, dk_acc, dv_acc, drel_acc):
    slots = qc_ref.shape[0]
    scale = HD ** -0.5
    blocks, tiles = slots // TQ, slots // TK
    dk_acc[...] = jnp.zeros_like(dk_acc)
    dv_acc[...] = jnp.zeros_like(dv_acc)
    drel_acc[...] = jnp.zeros_like(drel_acc)
    bias_ref[...] = jnp.zeros_like(bias_ref)
    row = lax.broadcasted_iota(jnp.int32, (TQ, TQ), 0)
    column = lax.broadcasted_iota(jnp.int32, (TQ, TQ), 1)
    flip = (row + column == TQ - 1).astype(F32)
    flip_low = flip.astype(B16)

    def q_step(qb, _):
        at = pl.multiple_of(q_at[qb], TQ)
        true_at = pl.multiple_of(qb * TQ, TQ)
        code_q = code_q_ref[pl.ds(true_at, TQ), :]
        cols = [slice(h * HD, (h + 1) * HD) for h in range(heads)]
        qc = [qc_ref[pl.ds(at, TQ), c] for c in cols]
        qp = [qp_ref[pl.ds(at, TQ), c] for c in cols]
        qp_turned = [dotx(item, flip_low, 0, 0).astype(B16) for item in qp]
        d_out = [d_out_ref[pl.ds(at, TQ), c] for c in cols]
        qc_turned = [item.T for item in qc]
        d_out_turned = [item.T for item in d_out]
        lse = [lse_ref[pl.ds(at, TQ), h:h + 1] for h in range(heads)]
        delta = [jnp.sum(d_out[h].astype(F32) * wide_ref[pl.ds(at, TQ), cols[h]], axis=1, keepdims=True)
                 for h in range(heads)]

        def k_step(kt, carry):
            ko = pl.multiple_of(k_at[kt], TQ)
            to = pl.multiple_of((blocks - 1 + kt * (TK // TQ) - qb) * TQ, TQ)
            mask = code_q == code_k_ref[kt]
            new = []
            for h in range(heads):
                lanes = cols[h]
                d_content, d_position = carry[h]
                window = rel_ref[pl.ds(to, TK + TQ), lanes]
                key = k_ref[pl.ds(ko, TK), lanes]
                grid = dotx(qp[h], window, 1, 1)
                raw = dotx(qc[h], key, 1, 1) + skew_tile(grid)
                probs = jnp.exp(jnp.where(mask, raw * scale - lse[h], NEG))
                d_probs = dotx(d_out[h], v_ref[pl.ds(ko, TK), lanes], 1, 1)
                d_raw = probs * (d_probs - delta[h]) * scale
                d_low = d_raw.astype(B16)
                d_grid = unskew_flipped(dotx(flip_low, d_low, 1, 0)).astype(B16)
                dv_acc[lanes, pl.ds(ko, TK)] += dotx(d_out_turned[h], probs.astype(B16), 1, 0)
                dk_acc[lanes, pl.ds(ko, TK)] += dotx(qc_turned[h], d_low, 1, 0)
                drel_acc[lanes, pl.ds(to, TK + TQ)] += dotx(qp_turned[h], d_grid, 1, 0)
                d_content = d_content + dotx(d_low, key, 1, 0)
                d_position = d_position + dotx(d_grid, window, 1, 0)
                new.append((d_content, d_position))
            return tuple(new)

        first = tuple((jnp.zeros((TQ, HD), F32),) * 2 for _ in range(heads))
        final = lax.fori_loop(spans[0, qb], spans[1, qb], k_step, first)
        for h in range(heads):
            d_content, d_position = final[h]
            d_position = lax.dot_general(flip, d_position, (((1,), (0,)), ((), ())),
                                         precision=lax.Precision.HIGHEST, preferred_element_type=F32)
            all_ref[pl.ds(at, TQ), cols[h]] = (d_content + d_position).astype(B16)
            bias_ref[0:1, cols[h]] += jnp.sum(d_content, axis=0, keepdims=True)
            bias_ref[1:2, cols[h]] += jnp.sum(d_position, axis=0, keepdims=True)
        return 0

    lax.fori_loop(0, blocks, q_step, 0)
    width = dk_acc.shape[0]
    all_ref[:, width : 2 * width] = dk_acc[...].astype(B16).T
    all_ref[:, 2 * width :] = dv_acc[...].astype(B16).T
    drel_ref[...] = drel_acc[...].astype(B16).T

def sds(s, d): return jax.ShapeDtypeStruct(s, d)

def attend(spans, q_at, k_at, qc, qp, k, v, rel, code_q, code_k):
    slots, width = qc.shape
    heads = width // HD
    return pl.pallas_call(
        functools.partial(attend_kernel, heads),
        out_shape=(sds((slots, width), B16), sds((slots, width), F32), sds((slots, heads), F32)),
        in_specs=[SM] * 3 + [VM] * 7, out_specs=(VM,) * 3,
        compiler_params=pltpu.CompilerParams(vmem_limit_bytes=40 << 20),
        cost_estimate=pl.CostEstimate(flops=int(4e9), bytes_accessed=int(9e6), transcendentals=int(2e6)),
    )(spans, q_at, k_at, qc, qp, k, v, rel, code_q, code_k)

def attend_back(spans, q_at, k_at, qc, qp, k, v, rel, code_q, code_k, d_out, wide, lse):
    slots, width = qc.shape
    heads = width // HD
    return pl.pallas_call(
        functools.partial(attend_back_kernel, heads),
        out_shape=(sds((slots, 3 * width), B16), sds((2 * slots, width), B16), sds((8, width), F32)),
        in_specs=[SM] * 3 + [VM] * 10, out_specs=(VM,) * 3,
        scratch_shapes=[pltpu.VMEM((width, slots), F32), pltpu.VMEM((width, slots), F32), pltpu.VMEM((width, 2 * slots), F32)],
        compiler_params=pltpu.CompilerParams(vmem_limit_bytes=48 << 20),
        cost_estimate=pl.CostEstimate(flops=int(1e6), bytes_accessed=int(1e6), transcendentals=0),
    )(spans, q_at, k_at, qc, qp, k, v, rel, code_q, code_k, d_out, wide, lse)

def codes(segments, valid):
    slots = segments.shape[0]
    place = jnp.arange(slots, dtype=jnp.int32)
    code = jnp.where(valid == 1, segments, -1 - place)
    return code

def spans_of(code):
    slots = code.shape[0]
    same = code[:, None] == code[None, :]
    touch = jnp.any(same.reshape(slots // TQ, TQ, slots // TK, TK), axis=(1, 3))
    tiles = slots // TK
    idx = jnp.arange(tiles, dtype=jnp.int32)
    lo = jnp.min(jnp.where(touch, idx, tiles), axis=1)
    hi = jnp.max(jnp.where(touch, idx + 1, 0), axis=1)
    return jnp.stack([lo, hi], 0).astype(jnp.int32)


def normalize(values, gain):
    mean = jnp.mean(values, axis=-1, keepdims=True)
    centered = values - mean
    inverse = lax.rsqrt(jnp.mean(centered * centered, axis=-1, keepdims=True) + EPS)
    unit = centered * inverse
    return (unit * gain.astype(F32), unit, inverse)


def normalize_back(grad, unit, inverse, gain):
    scaled = grad * gain.astype(F32)
    first = jnp.mean(scaled, axis=-1, keepdims=True)
    second = jnp.mean(scaled * unit, axis=-1, keepdims=True)
    return (inverse * (scaled - first - unit * second), (grad, unit))


def gain_sums(pairs, gate):
    return jnp.stack([jnp.sum(grad * unit, axis=0) for grad, unit in after(pairs, gate)])


def swish_slope(values):
    gate = jax.nn.sigmoid(values)
    return gate * (1.0 + values * (1.0 - gate))


def distance_table(slots, width, first):
    column = jnp.arange(width)
    even = (column % 2 == 0)[None, :]
    rate = jnp.exp(-(column - column % 2).astype(F32) * (math.log(10000.0) / width))
    coarse = (slots - 1 - STEP * jnp.arange(2 * slots // STEP)).astype(F32)[:, None] * rate[None, :]
    fine = jnp.arange(STEP).astype(F32)[:, None] * rate[None, :]
    sin_c, cos_c = jnp.sin(coarse), jnp.cos(coarse)
    with_cos = jnp.where(even, sin_c, cos_c)
    with_sin = jnp.where(even, -cos_c, sin_c)
    with_cos, with_sin, sin_f, cos_f = after((with_cos, with_sin, jnp.sin(fine), jnp.cos(fine)), first)
    table = with_cos[:, None, :] * cos_f[None] + with_sin[:, None, :] * sin_f[None]
    return table.reshape(2 * slots, width).astype(B16)


def dot(left, right, contract=(1, 0)):
    return lax.dot_general(
        left, right, (((contract[0],), (contract[1],)), ((), ())), preferred_element_type=F32
    )


def swap(values, distance):
    size = lax.axis_size("tp")
    return lax.ppermute(values, "tp", [(i, i ^ distance) for i in range(size)])


def distances():
    size = lax.axis_size("tp")
    return [1 << bit for bit in range(size.bit_length() - 1)]


def same_kernel(block_ref, out_ref):
    pass


def arrived(block):
    spec = pl.BlockSpec(memory_space=pl.ANY)
    return pl.pallas_call(
        same_kernel,
        in_specs=[spec],
        out_specs=spec,
        out_shape=jax.ShapeDtypeStruct(block.shape, block.dtype),
        input_output_aliases={0: 0},
        cost_estimate=pl.CostEstimate(flops=0, bytes_accessed=LINK_BYTES, transcendentals=0),
    )(block)


def gather(own, first=False, late=()):
    slots = {0: own}
    for distance in reversed(distances()):
        for slot in list(slots):
            slots[slot ^ distance] = swap(slots[slot], distance)
    last = len(slots) - 1
    if first:
        slots[last] = after(arrived(slots[last]), late)
    return [slots[slot] for slot in range(len(slots))]


def scatter(parts, late=(), add=True):
    parts = dict(enumerate(parts))
    sent = got = None
    for distance in distances():
        for slot in sorted(parts, reverse=True):
            if slot & distance:
                sent = parts.pop(slot).astype(B16)
                if distance == distances()[-1]:
                    sent = after(sent, late)
                got = swap(sent, distance)
                if add or distance != distances()[-1]:
                    parts[slot ^ distance] = parts[slot ^ distance].astype(F32) + got.astype(F32)
    return parts[0], (sent, got)


def after(values, *others):
    return lax.optimization_barrier((values, others))[0]


def halves(slots):
    half = len(slots) // 2
    return jnp.concatenate(slots[:half], 0), jnp.concatenate(slots[half:], 0)


def pieces(near, far, weight, contract):
    count = lax.axis_size("tp") // 2
    rows = near.shape[0] // count
    outs = {}
    for slot in reversed(range(2 * count)):
        source, place = (near, slot) if slot < count else (far, slot - count)
        outs[slot] = dot(source[place * rows : (place + 1) * rows], weight, contract)
    return [outs[slot] for slot in range(2 * count)]


def ring():
    size, mine = lax.axis_size("rows"), lax.axis_index("rows")
    order = list(range(0, size, 2)) + list(range(size - 1, 0, -2))
    place = jnp.where(mine % 2 == 0, mine // 2, size - (mine + 1) // 2)
    right = [(order[i], order[(i + 1) % size]) for i in range(size)]
    return size, place, right, [(there, here) for here, there in right]


def plain(piece):
    return piece


def turned(piece):
    return piece.T


def first_kernel(at, *refs):
    count = (len(refs) - 2) // 2
    refs[-2][...] = jnp.concatenate([ref[...] for ref in refs[:count]], 1)
    refs[-1][...] = jnp.concatenate([ref[...] for ref in refs[count:-2]], 1)


def pass_kernel(second, at, *refs):
    count = (len(refs) - 4) // 2
    from_left, from_right = (ref[...].astype(F32) for ref in refs[-4:-2])
    if second:
        top = pl.program_id(0) == 0
        from_left = jnp.where(top, from_left, 0.0)
        from_right = jnp.where(top, 0.0, from_right)
    own = jnp.concatenate([ref[...] for ref in refs[:count]], 1).astype(F32)
    refs[-2][...] = (own + from_left).astype(B16)
    own = jnp.concatenate([ref[...] for ref in refs[count:-4]], 1).astype(F32)
    refs[-1][...] = (own + from_right).astype(B16)


def total_kernel(split, at, *refs):
    own = jnp.concatenate([ref[...] for ref in refs[:-3]], 1).astype(F32)
    from_left, from_right = (ref[...].astype(F32) for ref in refs[-3:-1])
    if split:
        refs[-1][...] = (own + jnp.concatenate([from_left, from_right], 0)).astype(B16)
    else:
        refs[-1][...] = (own + from_left + from_right).astype(B16)


def place_kernel(spots, spans, at, *refs):
    count = len(spots)
    outs, held = refs[count : count + len(spans)], refs[-1]
    half = refs[count - 1].shape[0]
    size = held.shape[0] // (2 * half)
    for ref, (k, bottom) in zip(refs[:count], spots):
        start = ((at[0] + k) % size) * (2 * half) + bottom * half
        start = pl.multiple_of(start, half)
        held[pl.ds(start, ref.shape[0]), :] = ref[...].astype(F32)
    for out, (low, high, form) in zip(outs, spans):
        here = (pl.program_id(0) >= low) & (pl.program_id(0) < high)

        @pl.when(here)
        def _(out=out, form=form):
            out[...] = form(held[...])


class RowSum:
    def __init__(self, arrays, parts):
        self.size, self.place, self.right, self.left = ring()
        self.arrays, self.parts = list(arrays), parts
        self.width = sum(item.shape[1] for item in arrays)
        self.rows = arrays[0].shape[0] // self.size
        self.half = self.rows // 2
        self.stages = self.size // 2
        self.steps = 2 * self.stages
        self.done = 0
        self.seen = []

    def call(self, kernel, at, blocks, extra, out_rows, grid, gate, out_blocks, count=2):
        arrays, extra = after((self.arrays, extra), gate)
        specs, operands = [], []
        for rows, index in blocks:
            for item in arrays:
                specs.append(pl.BlockSpec((rows, item.shape[1]), index))
                operands.append(item)
        for item, (rows, index) in zip(extra, out_blocks[1]):
            specs.append(pl.BlockSpec((rows, self.width), index))
            operands.append(item)
        rows, index = out_blocks[0]
        moved = sum(2 * rows * self.width for _ in range(4))
        return pl.pallas_call(
            kernel,
            grid_spec=pltpu.PrefetchScalarGridSpec(
                num_scalar_prefetch=1,
                grid=(grid,),
                in_specs=specs,
                out_specs=[pl.BlockSpec((rows, self.width), index)] * count,
            ),
            out_shape=(sds((out_rows, self.width), B16),) * count,
            cost_estimate=pl.CostEstimate(flops=moved, bytes_accessed=moved, transcendentals=0),
        )(at, *operands)

    def send(self, to_right, to_left):
        over = lambda items, way: [lax.ppermute(item, "rows", way) for item in items]
        self.from_left, self.from_right = over(to_right, self.right), over(to_left, self.left)
        return (to_right, to_left)

    def step(self, gate=()):
        stage, stages, half, rows = self.done, self.stages, self.half, self.rows
        self.done += 1
        ids = [(self.place + k) % self.size for k in (stages - stage, stage - stages)]
        at = jnp.stack(ids).astype(jnp.int32)
        whole = lambda i, at: (0, 0)
        if stage == 0:
            blocks = [(half, lambda i, at: (2 * at[0], 0)), (half, lambda i, at: (2 * at[1] + 1, 0))]
            out = self.call(first_kernel, at, blocks, [], half, 1, gate, ((half, whole), []))
            return self.send([out[0]], [out[1]])
        if stage < stages:
            blocks = [
                (half, lambda i, at: (2 * at[0] + i, 0)), (half, lambda i, at: (2 * at[1] + i, 0)),
            ]
            here = (half, lambda i, at: (i, 0))
            got = (half, whole) if stage == 1 else here
            kernel = functools.partial(pass_kernel, stage == 1)
            extra = self.from_left + self.from_right
            out = self.call(kernel, at, blocks, extra, rows, 2, gate, (here, [got, got]))
            return self.send([out[0]], [out[1]])
        if stage == stages:
            got = (half if stages == 1 else rows, whole)
            kernel = functools.partial(total_kernel, stages == 1)
            extra = self.from_left + self.from_right
            blocks = [(rows, lambda i, at: (at[0], 0))]
            blocks = [(half, lambda i, at: (2 * at[0] + i, 0))] if stages > 1 else blocks
            here = (half, lambda i, at: (i, 0)) if stages > 1 else (rows, whole)
            got = here if stages > 1 else got
            grid = 2 if stages > 1 else 1
            out = self.call(kernel, at, blocks, extra, rows, grid, gate, (here, [got, got]), 1)
            to_right = to_left = list(out)
            self.see(to_right, 0)
        else:
            to_right, to_left = after((self.from_left, self.from_right), gate)
            self.see(to_right, stages - stage)
            self.see(to_left, stage - stages)
        if stage == 2 * stages - 1:
            to_right, to_left = [to_right[0][:half]], [to_left[0][half:]]
        return self.send(to_right, to_left)

    def came(self):
        return self.from_left + self.from_right

    def see(self, items, k):
        self.seen.append((items[0], (k, 0)))

    def finish(self, gate=()):
        self.seen += [(self.from_left[0], (-self.stages, 0)), (self.from_right[0], (self.stages, 1))]
        items = after([item for item, _ in self.seen], gate)
        spots = [((k + self.size) % self.size, bottom) for _, (k, bottom) in self.seen]
        length = self.arrays[0].shape[0]
        step = math.gcd(*[width for width, _ in self.parts])
        spans, specs, shapes, low = [], [], [], 0
        for width, form in self.parts:
            count = width // step
            spans.append((low, low + count, form))

            def column(i, at, low=low, count=count):
                return jnp.clip(i - low, 0, count - 1)

            if form is turned:
                shapes.append((width, length))
                specs.append(pl.BlockSpec((step, length), lambda i, at, f=column: (f(i, at), 0)))
            else:
                shapes.append((length, width))
                specs.append(pl.BlockSpec((length, step), lambda i, at, f=column: (0, f(i, at))))
            low += count
        moved = 6 * length * self.width
        return pl.pallas_call(
            functools.partial(place_kernel, spots, spans),
            grid_spec=pltpu.PrefetchScalarGridSpec(
                num_scalar_prefetch=1,
                grid=(low,),
                in_specs=[pl.BlockSpec((item.shape[0], step), lambda i, at: (0, i)) for item in items],
                out_specs=specs,
                scratch_shapes=[pltpu.VMEM((length, step), F32)],
            ),
            out_shape=[sds(shape, F32) for shape in shapes],
            compiler_params=pltpu.CompilerParams(vmem_limit_bytes=60 << 20),
            cost_estimate=pl.CostEstimate(flops=moved, bytes_accessed=moved, transcendentals=0),
        )(self.place.reshape(1).astype(jnp.int32), *items)


class WholeSum:
    came = staticmethod(lambda: ())

    def __init__(self, arrays, parts):
        self.arrays, self.parts, self.steps, self.done = list(arrays), parts, 1, 0

    def step(self, gate=()):
        self.done += 1
        values = after(jnp.concatenate(self.arrays, 1), gate)
        self.total = lax.psum(values, "rows").astype(F32)
        return ()

    def finish(self, gate=()):
        edges = [sum(width for width, _ in self.parts[:k]) for k in range(len(self.parts) + 1)]
        return [
            form(self.total[:, edges[k] : edges[k + 1]]) for k, (_, form) in enumerate(self.parts)
        ]


def row_sum(arrays, parts):
    size = lax.axis_size("rows")
    fits = size % 2 == 0 and arrays[0].shape[0] % (16 * size) == 0
    return (RowSum if fits else WholeSum)(arrays, parts)


def start_sum(arrays):
    if arrays[0].shape[1] == arrays[1].shape[1]:
        arrays = [jnp.concatenate(arrays, 0)]
    return [lax.psum_scatter(item, "rows", scatter_dimension=0, tiled=True) for item in arrays]


def end_sum(shares):
    return [lax.all_gather(item, "rows", axis=0, tiled=True) for item in shares]


def split_sum(whole, rows):
    if len(whole) == 1:
        whole = [whole[0][:rows], whole[0][rows:]]
    return [item.astype(F32) for item in whole]


class RowSums:
    def __init__(self, arrays, parts):
        if all(item.shape[0] == arrays[0].shape[0] for item in arrays):
            self.items = [row_sum(arrays, parts)]
        else:
            self.items = [row_sum([item], [part]) for item, part in zip(arrays, parts)]

    def came(self):
        return [item.came() for item in self.items]

    @property
    def done(self):
        return self.items[0].done

    @property
    def left(self):
        return max(item.steps - item.done for item in self.items)

    def step(self, gate=()):
        for item in self.items:
            if item.done < item.steps:
                gate = item.step(gate)
        return gate

    def finish(self, gate=()):
        while self.left:
            gate = self.step(gate)
        return [out for item in self.items for out in item.finish(gate)]


def sum_cube(values, axis, late=()):
    size = lax.axis_size(axis)
    if size & (size - 1):
        return lax.psum(values, axis)
    distance = 1
    while distance < size:
        values = values + lax.ppermute(values, axis, [(i, i ^ distance) for i in range(size)])
        values = after(values, late)
        distance *= 2
    return values


def halo(own, reach):
    size = lax.axis_size("tp")
    left = lax.ppermute(own[-reach:], "tp", [(i, i + 1) for i in range(size - 1)])
    right = lax.ppermute(own[:reach], "tp", [(i + 1, i) for i in range(size - 1)])
    return jnp.concatenate([left, own, right], 0)


def to_true(values):
    size, mine = lax.axis_size("tp"), lax.axis_index("tp")
    rows = values.shape[0] // size
    return jnp.concatenate(
        [lax.dynamic_slice_in_dim(values, (mine ^ k) * rows, rows, 0) for k in range(size)], 0
    )


def ffn_forward(values, gain, weight_up, weight_down):
    normed, unit, inverse = normalize(values, gain)
    near, far = halves(gather(normed.astype(B16)))
    pre, act = [], []
    for half in (near, far):
        pre.append(dot(after(half, act), weight_up))
        act.append((pre[-1] * jax.nn.sigmoid(pre[-1])).astype(B16))
    total, (sent, _) = scatter(pieces(act[0], act[1], weight_down, (1, 0)))
    pre = [item.astype(B16) for item in pre]
    return (values + 0.5 * total, (unit, inverse, (near, far), pre, act), sent)


def ffn_backward(grad, kept, gain, weight_up, weight_down, use=None, fill=None):
    unit, inverse, wide, pre, act = kept
    own = (0.5 * grad).astype(B16)
    cot = halves(gather(own) if fill is None else gather(own, True, fill(own)))
    d_pre = []
    for half in (0, 1):
        d_act = dot(after(cot[half], d_pre), weight_down, (1, 1))
        d_pre.append((d_act * swish_slope(pre[half].astype(F32))).astype(B16))
    d_norm, (sent, _) = scatter(pieces(d_pre[0], d_pre[1], weight_up, (1, 1)))
    cot, d_pre = after((cot, d_pre), sent)
    grad_down = dot(jnp.concatenate(act, 0), jnp.concatenate(cot, 0), (0, 0))
    grad_up = dot(jnp.concatenate(wide, 0), jnp.concatenate(d_pre, 0), (0, 0))
    grads = (grad_up.astype(B16), grad_down.astype(B16))
    if use is not None:
        d_norm = after(d_norm, use(grads))
    d_in, grad_gain = normalize_back(d_norm, unit, inverse, gain)
    return (grad + d_in, grad_gain, grads, (own, sent))


def places(slots):
    size, mine = lax.axis_size("tp"), lax.axis_index("tp")
    rows = slots // size
    if rows % TK:
        q_at = jnp.arange(slots // TQ, dtype=jnp.int32) * TQ
        k_at = jnp.arange(slots // TK, dtype=jnp.int32) * TK
        return q_at, k_at, True
    q_true = jnp.arange(slots // TQ, dtype=jnp.int32) * TQ
    k_true = jnp.arange(slots // TK, dtype=jnp.int32) * TK
    q_at = ((q_true // rows) ^ mine) * rows + q_true % rows
    k_at = ((k_true // rows) ^ mine) * rows + k_true % rows
    return q_at.astype(jnp.int32), k_at.astype(jnp.int32), False


def attend_forward(
    values, gain, weights, attend_out, content_bias, position_bias, code, spans, rel, prefetch
):
    slots = code.shape[0]
    width = attend_out.shape[0]
    q_at, k_at, reorder = places(slots)
    where = (spans, q_at, k_at)
    normed, unit, inverse = normalize(values, gain)
    near, far = halves(gather(normed.astype(B16)))
    mixed = [dot(near, weights)]
    far = after(far, rel, spans, mixed)
    fetched, arrived = prefetch(far)
    mixed.append(dot(far, weights))
    flat = lambda bias: bias.astype(F32).reshape(1, width)
    join = lambda items: jnp.concatenate(items, 0)
    q_content = join([(item[:, :width] + flat(content_bias)).astype(B16) for item in mixed])
    q_position = join([(item[:, :width] + flat(position_bias)).astype(B16) for item in mixed])
    key = join([item[:, width : 2 * width].astype(B16) for item in mixed])
    value = join([item[:, 2 * width :].astype(B16) for item in mixed])
    if reorder:
        q_content, q_position, key, value = map(to_true, (q_content, q_position, key, value))
    operands = (
        where
        + (q_content, q_position, key, value, rel)
        + (code.reshape(slots, 1), code.reshape(slots // TK, 1, TK))
    )
    heads_out, heads_wide, sums = attend(*operands)
    sent = after(to_true(heads_out) if reorder else heads_out, arrived)
    half = slots // 2
    total, _ = scatter(pieces(sent[:half], sent[half:], attend_out, (1, 0)))
    kept = (unit, inverse, (near, far), operands, heads_wide, sums, sent)
    return (values + total, kept, fetched)


def attend_backward(grad, cot, kept, gain, weights, attend_out, table, filler, use):
    unit, inverse, wide, operands, heads_wide, sums, sent = kept
    slots, width = sent.shape
    _, _, reorder = places(slots)
    cot = halves(cot)
    d_near = dot(cot[0], attend_out, (1, 1)).astype(B16)
    cot = (cot[0], after(cot[1], d_near))
    d_heads = jnp.concatenate([d_near, dot(cot[1], attend_out, (1, 1)).astype(B16)], 0)
    if reorder:
        d_heads = to_true(d_heads)
    d_heads = after(d_heads, filler[0])
    d_all, d_rel, d_bias = attend_back(*operands, d_heads, heads_wide, sums)
    if reorder:
        d_all = to_true(d_all)
    d_all = after(d_all, filler[1])
    half = slots // 2
    d_norm, (last, _) = scatter(pieces(d_all[:half], d_all[half:], weights, (1, 1)))
    cot, d_all, d_rel = after((cot, d_all, d_rel), last)
    grad_out = dot(jnp.concatenate(cot, 0), sent, (0, 0))
    grad_all = dot(jnp.concatenate(wide, 0), d_all, (0, 0))
    grad_pos = dot(table, d_rel, (0, 0))
    grads = [item.astype(B16) for item in (grad_all, grad_pos, grad_out)]
    d_norm = after(d_norm, use(grads, last))
    d_in, grad_gain = normalize_back(d_norm, unit, inverse, gain)
    return (grad + d_in, grad_gain, d_bias[:2])


def conv_weights(point_in, depth_kernel, gain_inner, point_out, first):
    taps = depth_kernel.shape[0]
    own = after((point_in[:, 0], point_in[:, 1], point_out), first)
    small = gather(jnp.concatenate([depth_kernel, gain_inner[None]], 0))
    small = jnp.concatenate(small, 1).astype(F32)
    in_a, in_b, out = map(gather, own)
    arrived = [item[2::2] for item in (in_a, in_b, out)]
    in_a, in_b = jnp.concatenate(in_a, 1), jnp.concatenate(in_b, 1)
    return (in_a, in_b, small[:taps], small[taps], jnp.concatenate(out, 0)), arrived


def conv_masks(segments, valid, rows, taps):
    edge = 8
    reach = taps // 2
    base = lax.axis_index("tp") * rows + edge - reach
    wide_segments = jnp.pad(segments, edge, constant_values=-1)
    wide_valid = jnp.pad(valid, edge)
    own = lax.dynamic_slice_in_dim(wide_segments, base, rows + 2 * reach)
    masks = []
    for tap in range(taps):
        other = lax.dynamic_slice_in_dim(wide_segments, base + tap - reach, rows + 2 * reach)
        good = lax.dynamic_slice_in_dim(wide_valid, base + tap - reach, rows + 2 * reach)
        masks.append(((other == own) & (good == 1)).astype(F32)[:, None])
    return masks


def conv_forward(values, gain, full, masks):
    in_a, in_b, kernel, gain_inner, out = full
    rows = values.shape[0]
    taps = kernel.shape[0]
    reach = taps // 2
    normed, unit, inverse = normalize(values, gain)
    low = normed.astype(B16)
    wide = halo(low, 2 * reach)
    mixed_a = dot(wide, in_a)
    gate = jax.nn.sigmoid(dot(wide, in_b))
    glu = mixed_a * gate
    depth = 0.0
    for tap in range(taps):
        depth = depth + kernel[tap] * masks[tap] * glu[tap : tap + rows + 2 * reach]
    depth_norm, inner_unit, inner_inverse = normalize(depth, gain_inner)
    inner = (depth_norm * jax.nn.sigmoid(depth_norm)).astype(B16)
    own = slice(2 * reach, 2 * reach + rows)
    kept = (unit, inverse, low, mixed_a[own], gate[own], glu, inner_unit, inner_inverse, depth_norm, inner)
    return (values + dot(inner[reach : reach + rows], out), kept)


def conv_backward(grad, kept, gain, full, masks):
    unit, inverse, low, mixed_a, gate, glu, inner_unit, inner_inverse, depth_norm, inner = kept
    in_a, in_b, kernel, gain_inner, out = full
    rows = grad.shape[0]
    taps = kernel.shape[0]
    reach = taps // 2
    mine = slice(reach, reach + rows)
    cot = grad.astype(B16)
    d_act = dot(halo(cot, reach), out, (1, 1))
    d_depth_norm = d_act * swish_slope(depth_norm)
    d_depth, _ = normalize_back(d_depth_norm, inner_unit, inner_inverse, gain_inner)
    d_glu = 0.0
    for tap in range(taps):
        weighted = d_depth * masks[tap]
        back = 2 * reach - tap
        d_glu = d_glu + kernel[tap] * weighted[back : back + rows]
    d_a = (d_glu * gate).astype(B16)
    d_b = (d_glu * mixed_a * gate * (1.0 - gate)).astype(B16)
    d_norm = dot(d_a, in_a, (1, 1)) + dot(d_b, in_b, (1, 1))
    d_in, grad_gain = normalize_back(d_norm, unit, inverse, gain)
    grad = grad + d_in
    slots = gather(grad.astype(B16), True)
    low, cot, d_a, d_b, inner = after((low, cot, d_a, d_b, inner), slots[1])
    size = lax.axis_size("tp")
    width = in_a.shape[1] // size
    parts = []
    grads = [
        dot(left, right, (0, 0)).astype(B16)
        for left, right in ((low, d_a), (low, d_b), (cot, inner[mine]))
    ]

    def small_grads(gate):
        d_own, norm_own = after((d_depth[mine], d_depth_norm[mine]), gate)
        sums = []
        for tap in range(taps):
            near = d_own * masks[tap][mine]
            sums.append(jnp.sum(near * glu[reach + tap : reach + tap + rows], axis=0))
        sums.append(jnp.sum(norm_own * inner_unit[mine], axis=0))
        small = jnp.stack(sums, 0)
        return scatter([small[:, k * width : (k + 1) * width] for k in range(size)])[0]

    for slot in range(size):
        cols = slice(slot * width, (slot + 1) * width)
        parts.append(jnp.concatenate([item[:, cols] for item in grads], 1))
    total, ends = scatter(parts, slots[-1], False)
    return (grad, slots, grad_gain, (total, small_grads), ends)


def body(
    layer_input,
    cotangent,
    segments,
    valid_frames,
    gain_first,
    up_first,
    down_first,
    gain_attend,
    query_weight,
    key_weight,
    value_weight,
    attend_out,
    pos_weight,
    content_bias,
    position_bias,
    gain_conv,
    point_in,
    depth_kernel,
    gain_inner,
    point_out,
    gain_second,
    up_second,
    down_second,
    gain_final,
):
    segment_row, valid_row = segments[0], valid_frames[0]
    weights = jnp.concatenate([query_weight, key_weight, value_weight], 1)
    width = query_weight.shape[1]
    taps = depth_kernel.shape[0]
    values = layer_input[0].astype(F32)
    rows = values.shape[0]
    slots = segment_row.shape[0]
    masks = conv_masks(segment_row, valid_row, rows, taps)
    code = codes(segment_row, valid_row)
    spans = spans_of(code)
    values, kept_first, sent = ffn_forward(values, gain_first, up_first, down_first)
    table = distance_table(slots, values.shape[1], sent)
    rel = dot(table, pos_weight).astype(B16)
    prefetch = functools.partial(conv_weights, point_in, depth_kernel, gain_inner, point_out)
    values, kept_attend, full = attend_forward(
        values, gain_attend, weights, attend_out, content_bias, position_bias, code, spans, rel, prefetch
    )
    values, kept_conv = conv_forward(values, gain_conv, full, masks)
    values, kept_second, _ = ffn_forward(values, gain_second, up_second, down_second)
    final, final_unit, final_inverse = normalize(values, gain_final)
    layer_output = final.astype(B16)
    grad, sum_final = normalize_back(cotangent[0].astype(F32), final_unit, final_inverse, gain_final)
    held = {}

    def start_second(grads):
        held["second"] = start_sum(grads)
        return grads

    grad, sum_second, _, _ = ffn_backward(
        grad, kept_second, gain_second, up_second, down_second, start_second
    )
    grad, cot, sum_conv, conv_grads, ends = conv_backward(grad, kept_conv, gain_conv, full, masks)
    ends = (ends[0], (ends, held["second"]))

    def start_middle(grads, last):
        own, got = after((conv_grads[0], ends[1][0][1]), last)
        total = (own.astype(F32) + got.astype(F32)).astype(B16)
        forms = [(width, plain)] * 4 + [(width, turned), (2 * width, plain), (width, turned)]
        held["middle"] = row_sum(grads + [total], forms)
        return held["middle"].step()

    grad, sum_attend, d_bias = attend_backward(
        grad, cot, kept_attend, gain_attend, weights, attend_out, table, ends, start_middle
    )
    middle = held["middle"]
    second_sum = end_sum(held["second"])
    grad, sum_first, first_grads, marks = ffn_backward(
        grad, kept_first, gain_first, up_first, down_first, None, middle.step
    )
    first = RowSums(first_grads, [(item.shape[1], plain) for item in first_grads])
    token = middle.step(marks[1])
    token = first.step(token)
    second_sum = after(second_sum, token)
    token = second_sum
    while middle.done < middle.steps:
        token = middle.step(token)
        if middle.done == middle.steps:
            token = (token, middle.came())
        if first.left > 1:
            token = first.step(token)
        if first.done == 3:
            token = (token, grad)
        if first.done == 5:
            second_up, second_down = split_sum(after(second_sum, token), up_second.shape[0])
            token = (token, second_up, second_down)
    attend_sum = middle.finish(token)
    token = (token, attend_sum)
    while first.left:
        token = first.step(token)
    pairs = (sum_first, sum_attend, sum_conv, sum_second, sum_final)
    gains = sum_cube(gain_sums(pairs, marks[1]), "tp")
    small = jnp.concatenate([conv_grads[1](marks[1]), d_bias], 0)
    small_shape = small.shape
    pack = jnp.concatenate([gains.reshape(-1), small.reshape(-1)]).reshape(-1, width)
    pack = sum_cube(after(pack, token), "rows", first.came())
    first_sum = first.finish()
    pack = pack.reshape(-1)
    gains, small = pack[: gains.size].reshape(gains.shape), pack[gains.size :].reshape(small_shape)
    bias_shape = content_bias.shape
    return (
        layer_output[None],
        grad[None],
        gains[0],
        first_sum[0],
        first_sum[1],
        gains[1],
        attend_sum[0],
        attend_sum[1],
        attend_sum[2],
        attend_sum[4],
        attend_sum[3],
        small[taps + 1].reshape(bias_shape),
        small[taps + 2].reshape(bias_shape),
        gains[2],
        attend_sum[5].reshape(attend_sum[5].shape[0], 2, width),
        small[:taps],
        small[taps],
        attend_sum[6],
        gains[3],
        second_up,
        second_down,
        gains[4],
    )


def solution(mesh):
    in_specs = (
        P("rows", "tp", None),
        P("rows", "tp", None),
        P("rows", None),
        P("rows", None),
        P(),
        P(None, "tp"),
        P("tp", None),
        P(),
        P(None, "tp"),
        P(None, "tp"),
        P(None, "tp"),
        P("tp", None),
        P(None, "tp"),
        P("tp", None),
        P("tp", None),
        P(),
        P(None, None, "tp"),
        P(None, "tp"),
        P("tp"),
        P("tp", None),
        P(),
        P(None, "tp"),
        P("tp", None),
        P(),
    )
    out_specs = (
        P("rows", "tp", None),
        P("rows", "tp", None),
        P(),
        P(None, "tp"),
        P("tp", None),
        P(),
        P(None, "tp"),
        P(None, "tp"),
        P(None, "tp"),
        P("tp", None),
        P(None, "tp"),
        P("tp", None),
        P("tp", None),
        P(),
        P(None, None, "tp"),
        P(None, "tp"),
        P("tp"),
        P("tp", None),
        P(),
        P(None, "tp"),
        P("tp", None),
        P(),
    )
    return jax.shard_map(body, mesh=mesh, in_specs=in_specs, out_specs=out_specs, check_vma=False)
```
